32 devices in a mesh: ctx: 4 (over y, x), fsdp: 8 (over z, core).
Axes of the slice: x: 2, y: 2, z: 4, core: 2. Of those that a mesh axis runs over, the one named last changes fastest.
Arguments:
- tokens: bfloat16 [8, 768, 1536], P('fsdp', 'ctx'), may hold values from -6 to 6
- block_order: int32 [8, 8], P('fsdp'), may hold values from 0 to 7, each once within a row
- segment_ids: int32 [8, 768], P('fsdp'), may hold values from -1 to 7, as said below
- norm_gains: bfloat16 [2, 1536], P(None, 'fsdp'), may hold values from 0.5 to 1.5
- attn_in_weight: bfloat16 [1536, 6144], P('fsdp'), may hold values from -0.15625 to 0.15625
- forget_weight: bfloat16 [1536, 24], P('fsdp'), may hold values from -0.15625 to 0.15625
- forget_bias: float32 [24], replicated, may hold values from 0 to 8, as said below
- qk_gains: float32 [2, 64], replicated, may hold values from 0.5 to 1.5
- out_weight: bfloat16 [1536, 1536], P('fsdp'), may hold values from -0.625 to 0.625
- gate_up_weight: bfloat16 [1536, 8192], P('fsdp'), may hold values from -0.15625 to 0.15625
- down_weight: bfloat16 [4096, 1536], P('fsdp'), may hold values from -0.09375 to 0.09375
- out_grad: bfloat16 [8, 768, 1536], P('fsdp', 'ctx'), may hold values from -6 to 6
Outputs:
- block_out: bfloat16 [8, 768, 1536], P('fsdp', 'ctx')
- tokens_grad: bfloat16 [8, 768, 1536], P('fsdp', 'ctx')
- norm_gains_grad: float32 [2, 1536], P(None, 'fsdp')
- attn_in_grad: float32 [1536, 6144], P('fsdp')
- forget_weight_grad: float32 [1536, 24], P('fsdp')
- forget_bias_grad: float32 [24], replicated
- qk_gains_grad: float32 [2, 64], replicated
- out_weight_grad: float32 [1536, 1536], P('fsdp')
- gate_up_grad: float32 [1536, 8192], P('fsdp')
- down_grad: float32 [4096, 1536], P('fsdp')
- rms_stats: float32 [8, 2], P('fsdp')
The draws below stay inside these ranges and needn't reach their ends.
Inputs may be any that keep to these rules, and one draw needn't show every extreme that they name: `block_order`: each row names every block of its sequence once; context index c holds storage blocks 2c and 2c + 1. `segment_ids`: in true order a sequence's non-negative ids start at 0, never fall and rise by one at each new document, so every sequence holds exactly 8 documents, ids 0 to 7, each contiguous and of uneven length; -1 marks a padding tail of 1 to 96 tokens at the end of every sequence. `forget_bias`: one bias for each head.
All inputs are finite; a program needn't handle non-finite values.
Results may differ from the reference program's by a relative error of at most 0.018.
Values may be sent and summed in bfloat16 or wider, within the bound.
A program may use at most 384 MiB of HBM per device.

```python
import jax
import jax.numpy as jnp
from jax import lax

D = 1536
HEADS = 24
HEAD = 64
FF = 4096
BLK = 96
NBLK = 8
SEQ_LEN = 768
SEQS = 8


def draw_segment_ids(key, part):
    first_key, second_key, third_key = jax.random.split(key, 3)
    places = jnp.arange(SEQ_LEN, dtype=jnp.int32)
    region_weight = jax.random.randint(first_key, (SEQS, NBLK), 1, 17)
    weight_rows = jnp.repeat(region_weight, BLK, axis=1)
    raw_scores = jax.random.randint(second_key, (SEQS, SEQ_LEN), 0, 1024)
    scores = raw_scores * weight_rows * SEQ_LEN + places[None, :]
    usable = (places >= 1) & (places < SEQ_LEN - BLK)
    scores = jnp.where(usable[None, :], scores, -1)
    cut_scores, cuts = lax.top_k(scores, NBLK - 1)
    doc_ids = jnp.sum((cuts[:, None, :] <= places[None, :, None]).astype(jnp.int32), axis=-1)
    padding = jax.random.randint(third_key, (SEQS, 1), 1, BLK + 1)
    return jnp.where(places[None, :] >= SEQ_LEN - padding, -1, doc_ids).astype(jnp.int32)


def draw_forget_bias(key, part):
    base = jax.random.uniform(jax.random.fold_in(key, 7), (HEADS,), jnp.float32)
    return (8.0 * base).astype(jnp.float32)


def block_scale(key, shape, shards, smallest, top_value):
    level = 1.0
    for position, shards_of in shards:
        steps = jax.random.uniform(jax.random.fold_in(jax.random.fold_in(key, 6), position), (shards_of,), jnp.float32, smallest / len(shards), top_value / len(shards))
        level = level * jnp.repeat(jnp.exp(steps), shape[position] // shards_of).reshape((-1,) + (1,) * (len(shape) - 1 - position))
    return level


def centred(own_key, extent, deviation, bound, shards=(), kind=jnp.bfloat16):
    array = jax.random.normal(own_key, extent, jnp.float32) * deviation
    if len(shards) > 0:
        array = block_scale(own_key, extent, shards, -0.22, 0.18) * array
    return jnp.clip(array, min=-bound, max=bound).astype(kind)


def setup_inputs(seed: int = 0) -> dict:
    splits = jax.random.split(jax.random.key(seed), 13)
    tokens = centred(splits[0], (SEQS, SEQ_LEN, D), 1.0, 6.0, ((0, 8), (1, 4)))
    block_order = jax.vmap(lambda own: jax.random.permutation(own, NBLK))(jax.random.split(splits[1], SEQS)).reshape((SEQS, NBLK)).astype(jnp.int32)
    segment_ids = draw_segment_ids(jax.random.fold_in(splits[12], 71), 0)
    norm_gains = jnp.clip(1.0 + 0.1 * jax.random.normal(splits[3], (2, D), jnp.float32), 0.5, 1.5).astype(jnp.bfloat16)
    attn_in_weight = centred(splits[4], (D, 4 * D), D ** -0.5, 0.15625, ((0, 8),))
    forget_weight = centred(splits[5], (D, HEADS), D ** -0.5, 0.15625, ((0, 8),))
    forget_bias = draw_forget_bias(jax.random.fold_in(splits[12], 71), 0)
    qk_gains = jnp.clip(1.0 + 0.1 * jax.random.normal(splits[7], (2, HEAD), jnp.float32), 0.5, 1.5)
    out_weight = centred(splits[8], (D, D), (D // 16) ** -0.5, 0.625, ((0, 8),))
    gate_up_weight = centred(splits[9], (D, 2 * FF), D ** -0.5, 0.15625, ((0, 8),))
    down_weight = centred(splits[10], (FF, D), FF ** -0.5, 0.09375, ((0, 8),))
    out_grad = centred(splits[11], (SEQS, SEQ_LEN, D), 1.0, 6.0, ((0, 8), (1, 4)))
    return dict(tokens=tokens, block_order=block_order, segment_ids=segment_ids, norm_gains=norm_gains, attn_in_weight=attn_in_weight, forget_weight=forget_weight, forget_bias=forget_bias, qk_gains=qk_gains, out_weight=out_weight, gate_up_weight=gate_up_weight, down_weight=down_weight, out_grad=out_grad)


EPS = 1e-06
SCALE = 0.125

@jax.custom_vjp
def low(v):
    return lax.optimization_barrier(v.astype(jnp.bfloat16)).astype(jnp.float32)

@jax.custom_vjp
def low_back(v):
    return v

def low_keep(v):
    return (low(v), None)

def low_pass(kept, grad):
    return (grad,)

def back_keep(v):
    return (v, None)

def back_low(kept, grad):
    return (low(grad),)
low.defvjp(low_keep, low_pass)
low_back.defvjp(back_keep, back_low)

def matmul(left, right):
    return jnp.dot(left, right, precision=lax.Precision.HIGHEST, preferred_element_type=jnp.float32)

def rms_scale(values):
    return lax.rsqrt(lax.optimization_barrier(jnp.mean(values * values, axis=-1, keepdims=True)) + EPS)

def head_norm(values, head_gain):
    split_up = values.reshape(SEQ_LEN, HEADS, HEAD)
    return (split_up * rms_scale(split_up) * head_gain).reshape(SEQ_LEN, D)

def by_head(values):
    return values.reshape(SEQ_LEN, HEADS, HEAD).transpose(1, 0, 2)

def forward(inputs, segment, gain_pair, in_proj, forget_proj, bias_forget, gains_qk, out_proj, gate_up_proj, down_proj):
    normed = low(inputs * rms_scale(inputs) * gain_pair[0])
    project = matmul(normed, in_proj)
    query_raw = low_back(project[:, :D])
    key_raw = low_back(project[:, D:2 * D])
    values = low(low_back(project[:, 2 * D:3 * D]))
    gate_logit = low_back(project[:, 3 * D:])
    forget_logit = low_back(matmul(normed, forget_proj) + bias_forget)
    prefix = jnp.cumsum(jax.nn.log_sigmoid(forget_logit), axis=0)
    query_norm = low(head_norm(query_raw, gains_qk[0]))
    key_norm = low(head_norm(key_raw, gains_qk[1]))
    places = jnp.arange(SEQ_LEN, dtype=jnp.int32)
    allowed = (places[None, :] <= places[:, None]) & (segment[None, :] == segment[:, None])

    def one_head(pieces):
        query_head, key_head, value_head, prefix_head = pieces
        scores = low_back(matmul(query_head, key_head.T) * SCALE + prefix_head[:, None] - prefix_head[None, :])
        probs = jax.nn.softmax(jnp.where(allowed, scores, -jnp.inf), axis=-1)
        return low_back(matmul(low(probs), value_head))
    attended = lax.map(jax.checkpoint(one_head), (by_head(query_norm), by_head(key_norm), by_head(values), prefix.T))
    attended = attended.transpose(1, 0, 2).reshape(SEQ_LEN, D)
    gated = low(attended * jax.nn.sigmoid(gate_logit))
    mixed = inputs + low_back(matmul(gated, out_proj))
    normed_two = low(mixed * rms_scale(mixed) * gain_pair[1])
    gate_up = low_back(matmul(normed_two, gate_up_proj))
    hidden = low(jax.nn.silu(gate_up[:, :FF]) * gate_up[:, FF:])
    return mixed + low_back(matmul(hidden, down_proj))

def reference(tokens, block_order, segment_ids, norm_gains, attn_in_weight, forget_weight, forget_bias, qk_gains, out_weight, gate_up_weight, down_weight, out_grad):
    params = (norm_gains.astype(jnp.float32), attn_in_weight.astype(jnp.float32), forget_weight.astype(jnp.float32), forget_bias.astype(jnp.float32), qk_gains.astype(jnp.float32), out_weight.astype(jnp.float32), gate_up_weight.astype(jnp.float32), down_weight.astype(jnp.float32))
    offsets = jnp.arange(BLK, dtype=jnp.int32)

    def one_sequence(totals, sequence):
        seq_rows, seq_grads, seq_order, segment = sequence
        places = (seq_order[:, None].astype(jnp.int32) * BLK + offsets[None, :]).reshape(SEQ_LEN)
        inputs = jnp.zeros((SEQ_LEN, D), jnp.float32).at[places].set(seq_rows.astype(jnp.float32))
        cotangent = jnp.zeros((SEQ_LEN, D), jnp.float32).at[places].set(seq_grads.astype(jnp.float32))

        def one_layer(inputs_in, gain_pair, in_proj, forget_proj, bias_forget, gains_qk, out_proj, gate_up_proj, down_proj):
            return forward(inputs_in, segment, gain_pair, in_proj, forget_proj, bias_forget, gains_qk, out_proj, gate_up_proj, down_proj)
        result, pullback = jax.vjp(one_layer, inputs, params[0], params[1], params[2], params[3], params[4], params[5], params[6], params[7])
        gradients = pullback(cotangent)
        valid_rows = (segment >= 0).astype(jnp.float32)
        denominator = jnp.sum(valid_rows) * D
        branch = result - inputs
        rms_pair = jnp.sqrt(jnp.stack([jnp.sum(valid_rows * lax.optimization_barrier(jnp.sum(result * result, axis=-1))), jnp.sum(valid_rows * lax.optimization_barrier(jnp.sum(branch * branch, axis=-1)))]) / denominator)
        totals = tuple((jnp.add(total, grad_part) for total, grad_part in zip(totals, gradients[1:])))
        return (totals, (result[places].astype(jnp.bfloat16), gradients[0][places].astype(jnp.bfloat16), rms_pair))
    initial = tuple((jnp.zeros_like(param) for param in params))
    sums, (outputs, input_grads, rms_all) = lax.scan(one_sequence, initial, (tokens, out_grad, block_order, segment_ids))
    return (outputs, input_grads, sums[0], sums[1], sums[2], sums[3], sums[4], sums[5], sums[6], sums[7], rms_all)
```

```python
import functools

import jax
import jax.numpy as jnp
from jax import lax
from jax.experimental import pallas as pl
from jax.experimental.pallas import tpu as pltpu
from jax.sharding import PartitionSpec as P

EPS = 1e-06
SCALE = 0.125
LANES = 128
F32 = jnp.float32
BF16 = jnp.bfloat16


def rms_scale(values):
    return lax.rsqrt(jnp.mean(values * values, axis=-1, keepdims=True) + EPS)


def norm_back(grad_normed, values, scale_values, gain_values):
    scaled = grad_normed * gain_values
    cubed = scale_values * scale_values * scale_values
    return scale_values * scaled - values * cubed * jnp.mean(
        scaled * values, axis=-1, keepdims=True
    )


def dot(left, right):
    return lax.dot_general(
        left, right, (((1,), (0,)), ((), ())), preferred_element_type=F32
    )


def left_product(left, right):
    return lax.dot_general(
        left, right, (((0,), (0,)), ((), ())), preferred_element_type=F32
    )


def right_product(left, right):
    return lax.dot_general(
        left, right, (((1,), (1,)), ((), ())), preferred_element_type=F32
    )


def split_three(values):
    high = values.astype(BF16).astype(F32)
    rest = values - high
    middle = rest.astype(BF16).astype(F32)
    return high, middle, rest - middle


def precise_left(zero_one, values):
    high, middle, low = split_three(values)
    total = dot(zero_one, high.astype(BF16))
    total = total + dot(zero_one, middle.astype(BF16))
    return total + dot(zero_one, low.astype(BF16))


def lane_ids(rows, lanes=LANES):
    return lax.broadcasted_iota(jnp.int32, (rows, lanes), 1)


def pick_lane(values, lanes, index):
    return jnp.sum(jnp.where(lanes == index, values, 0.0), axis=-1, keepdims=True)


def attend_kernel(
    head, chunk,
    pos_row, pos_col, seg_row, seg_col, bias, gains, query, key, value, gate, forget,
    gated, attended, wide_query, wide_key, wide_value,
    mask, prefix,
):
    step = pl.program_id(0)
    rows = query.shape[0]
    lanes = lane_ids(rows)
    half = lane_ids(rows, head)

    @pl.when(step == 0)
    def _():
        log_forget = jax.nn.log_sigmoid(forget[...] + bias[0:1, :])
        high, middle, low = split_three(log_forget)
        for start in range(0, rows, chunk):
            part = pl.ds(start, chunk)
            before = pos_row[0:1, :] <= pos_col[part, :]
            same = seg_row[0:1, :] == seg_col[part, :]
            mask[part, :] = jnp.where(before & same, 0.0, -jnp.inf)
            before = jnp.where(before, 1.0, 0.0).astype(BF16)
            prefix[part, :] = (
                dot(before, high.astype(BF16))
                + dot(before, middle.astype(BF16))
                + dot(before, low.astype(BF16))
            )

    for side in range(LANES // head):
        here = pl.ds(side * head, head)
        column = pick_lane(prefix[...], lanes, (LANES // head) * step + side)
        high, middle, low = split_three(column)
        wide = jnp.where(half == 1, high, 0.0)
        wide = jnp.where(half == 2, middle, wide)
        wide = jnp.where(half == 3, low, wide)
        query_rest = jnp.where((half >= 4) & (half < 7), 1.0, wide)
        wide = jnp.where(half == 4, -high, 0.0)
        wide = jnp.where(half == 5, -middle, wide)
        wide = jnp.where(half == 6, -low, wide)
        ones = ((half >= 1) & (half < 4)) | ((half >= 7) & (half < 10))
        key_rest = jnp.where(ones, 1.0, wide)
        raw = query[:, here]
        normed = (raw * rms_scale(raw) * gains[0:1, here]).astype(BF16)
        wide_query[side, :, 0:head] = (normed.astype(F32) * SCALE).astype(BF16)
        wide_query[side, :, head:LANES] = query_rest.astype(BF16)
        raw = key[:, here]
        wide_key[side, :, 0:head] = (raw * rms_scale(raw) * gains[1:2, here]).astype(BF16)
        wide_key[side, :, head:LANES] = key_rest.astype(BF16)
        wide_value[side, :, 0:head] = value[:, here].astype(BF16)
        wide_value[side, :, head:LANES] = jnp.where(half < 3, 1.0, 0.0).astype(BF16)
        for start in range(0, rows, chunk):
            part = pl.ds(start, chunk)
            scores = right_product(wide_query[side, part, :], wide_key[side]) + mask[part, :]
            expos = jnp.exp(scores)
            total = jnp.sum(expos, axis=-1, keepdims=True)
            result = dot(expos.astype(BF16), wide_value[side])[:, 0:head] / total
            attended[part, here] = result
            gated[part, here] = (result * jax.nn.sigmoid(gate[part, here])).astype(BF16)
            high, middle, low = split_three(-jnp.log(total))
            short = half[start : start + chunk]
            rest = query_rest[start : start + chunk]
            rest = jnp.where(short == 7, high, rest)
            rest = jnp.where(short == 8, middle, rest)
            rest = jnp.where(short == 9, low, rest)
            wide_query[side, part, head:LANES] = rest.astype(BF16)


def attend_back_kernel(
    head, chunk, width,
    pos_row, pos_col, seg_row, seg_col, bias, gains, query, key, gate, forget,
    attended, wide_query, wide_key, wide_value, grad_gated,
    grad_project, small,
    mask, wide_grad, grad_query, grad_key, grad_value, grad_prefix,
):
    step = pl.program_id(0)
    steps = pl.num_programs(0)
    rows = query.shape[0]
    lanes = lane_ids(rows)
    half = lane_ids(rows, head)

    @pl.when(step == 0)
    def _():
        for start in range(0, rows, chunk):
            part = pl.ds(start, chunk)
            after = pos_row[0:1, :] >= pos_col[part, :]
            same = seg_row[0:1, :] == seg_col[part, :]
            mask[part, :] = jnp.where(after & same, 0.0, -jnp.inf)
        grad_prefix[...] = jnp.zeros_like(grad_prefix)
        small[...] = jnp.zeros_like(small)

    for side in range(LANES // head):
        here = pl.ds(side * head, head)

        def column(part):
            return pl.ds(pl.multiple_of(part * width + step * LANES, LANES), LANES)

        sig = jax.nn.sigmoid(gate[:, here])
        grad_in = grad_gated[:, here]
        result = attended[:, here]
        grad_result = (grad_in * sig).astype(BF16)
        grad_gate = (grad_in * result * sig * (1.0 - sig)).astype(BF16)
        inner = -jnp.sum(grad_result.astype(F32) * result, axis=-1, keepdims=True)
        high, middle, low = split_three(inner)
        rest = jnp.where(half == 0, high, 0.0)
        rest = jnp.where(half == 1, middle, rest)
        rest = jnp.where(half == 2, low, rest)
        wide_grad[:, 0:head] = grad_result
        wide_grad[:, head:LANES] = rest.astype(BF16)
        grad_query[...] = jnp.zeros_like(grad_query)
        for start in range(0, rows, chunk):
            part = pl.ds(start, chunk)
            scores = right_product(wide_key[side, part, :], wide_query[side]) + mask[part, :]
            probs = jnp.exp(scores)
            outer = right_product(wide_value[side, part, :], wide_grad[...])
            grad_scores = (probs * outer).astype(BF16)
            grad_key[part, :] = dot(grad_scores, wide_query[side])
            grad_value[part, :] = dot(probs.astype(BF16), wide_grad[...])
            grad_query[...] += left_product(grad_scores, wide_key[side, part, :])
        from_query = grad_query[...]
        from_key = grad_key[...]
        change = pick_lane(from_query, lanes, head + 1) - pick_lane(from_key, lanes, head + 4)
        grad_prefix[...] += jnp.where(lanes == (LANES // head) * step + side, change, 0.0)

        raw = query[:, here]
        scale_raw = rms_scale(raw)
        grad_normed = from_query[:, 0:head] * SCALE
        grad_raw_query = norm_back(grad_normed, raw, scale_raw, gains[0:1, here])
        small[0:1, here] += jnp.sum(grad_normed * raw * scale_raw, axis=0, keepdims=True)
        raw = key[:, here]
        scale_raw = rms_scale(raw)
        grad_normed = from_key[:, 0:head]
        grad_raw_key = norm_back(grad_normed, raw, scale_raw, gains[1:2, here])
        small[1:2, here] += jnp.sum(grad_normed * raw * scale_raw, axis=0, keepdims=True)
        wide_grad[:, here] = grad_gate
        for part_id, piece in enumerate(
            (grad_raw_query.astype(BF16), grad_raw_key.astype(BF16), grad_value[:, 0:head].astype(BF16), grad_gate)
        ):
            if side == 0:
                grad_project[:, column(part_id)] = jnp.concatenate([piece, piece], axis=1)
            else:
                keep = grad_project[:, column(part_id)]
                both = jnp.concatenate([piece, piece], axis=1)
                grad_project[:, column(part_id)] = jnp.where(lanes < head, keep, both)

    @pl.when(step == steps - 1)
    def _():
        high, middle, low = split_three(grad_prefix[...])
        logits = forget[...] + bias[0:1, :]
        heads = steps * (LANES // head)
        for start in range(0, rows, chunk):
            part = pl.ds(start, chunk)
            after = jnp.where(pos_row[0:1, :] >= pos_col[part, :], 1.0, 0.0).astype(BF16)
            total = dot(after, high.astype(BF16)) + dot(after, middle.astype(BF16)) + dot(after, low.astype(BF16))
            grad_logit = total * jax.nn.sigmoid(-logits[start : start + chunk])
            grad_logit = jnp.where(lanes[start : start + chunk] < heads, grad_logit, 0.0).astype(BF16)
            grad_project[part, 4 * width : 4 * width + LANES] = grad_logit
            small[2:3, :] += jnp.sum(grad_logit.astype(F32), axis=0, keepdims=True)


def pick_chunk(rows):
    return 256 if rows % 256 == 0 else 192


def whole(shape):
    return pl.BlockSpec(shape, lambda step: tuple(0 for _ in shape))


def attend(project, places, bias, gains, head, width):
    rows = project.shape[0]
    steps = width // LANES
    per = LANES // head
    chunk = pick_chunk(rows)

    def part(index):
        return pl.BlockSpec((rows, LANES), lambda step: (0, index * steps + step))

    own = pl.BlockSpec((rows, LANES), lambda step: (0, step))
    wide = pl.BlockSpec((per, rows, LANES), lambda step: (step, 0, 0))
    forget = pl.BlockSpec((rows, LANES), lambda step: (0, 4 * steps))
    wide_shape = jax.ShapeDtypeStruct((per * steps, rows, LANES), BF16)
    return pl.pallas_call(
        functools.partial(attend_kernel, head, chunk),
        grid=(steps,),
        in_specs=[whole(p.shape) for p in places] + [whole(bias.shape), whole(gains.shape)]
        + [part(0), part(1), part(2), part(3), forget],
        out_specs=[own, own, wide, wide, wide],
        out_shape=[
            jax.ShapeDtypeStruct((rows, width), BF16),
            jax.ShapeDtypeStruct((rows, width), F32),
            wide_shape, wide_shape, wide_shape,
        ],
        scratch_shapes=[pltpu.VMEM((rows, rows), F32), pltpu.VMEM((rows, LANES), F32)],
        compiler_params=pltpu.CompilerParams(vmem_limit_bytes=48 << 20),
        name="attend",
    )(*places, bias, gains, project, project, project, project, project)


def attend_back(project, places, bias, gains, attended, wides, grad_gated, head, width):
    rows = project.shape[0]
    steps = width // LANES
    per = LANES // head
    chunk = pick_chunk(rows)

    def part(index):
        return pl.BlockSpec((rows, LANES), lambda step: (0, index * steps + step))

    own = pl.BlockSpec((rows, LANES), lambda step: (0, step))
    wide = pl.BlockSpec((per, rows, LANES), lambda step: (step, 0, 0))
    forget = pl.BlockSpec((rows, LANES), lambda step: (0, 4 * steps))
    total = 4 * width + LANES
    return pl.pallas_call(
        functools.partial(attend_back_kernel, head, chunk, width),
        grid=(steps,),
        in_specs=[whole(p.shape) for p in places] + [whole(bias.shape), whole(gains.shape)]
        + [part(0), part(1), part(3), forget, own, wide, wide, wide, own],
        out_specs=[whole((rows, total)), whole((8, LANES))],
        out_shape=[
            jax.ShapeDtypeStruct((rows, total), BF16),
            jax.ShapeDtypeStruct((8, LANES), F32),
        ],
        scratch_shapes=[
            pltpu.VMEM((rows, rows), F32),
            pltpu.VMEM((rows, LANES), BF16),
            pltpu.VMEM((rows, LANES), F32),
            pltpu.VMEM((rows, LANES), F32),
            pltpu.VMEM((rows, LANES), F32),
            pltpu.VMEM((rows, LANES), F32),
        ],
        compiler_params=pltpu.CompilerParams(vmem_limit_bytes=48 << 20),
        name="attend_back",
    )(*places, bias, gains, project, project, project, project, attended, *wides, grad_gated)


def body(
    tokens, block_order, segment_ids, norm_gains, attn_in_weight, forget_weight, forget_bias,
    qk_gains, out_weight, gate_up_weight, down_weight, out_grad,
):
    ranks = lax.axis_size("ctx")
    shards = lax.axis_size("fsdp")
    rank = lax.axis_index("ctx")
    row_count, model_width = tokens.shape[1], tokens.shape[2]
    head_count, head_dim = forget_bias.shape[0], qk_gains.shape[1]
    local_heads = head_count // ranks
    width = local_heads * head_dim
    seq_order = block_order[0]
    seq_len = segment_ids.shape[1]
    block_len = seq_len // seq_order.shape[0]
    hidden_all = down_weight.shape[0] * shards
    hidden_piece = down_weight.shape[0] // ranks
    hidden = hidden_piece * shards

    def slab(array, start, size, axis):
        return lax.dynamic_slice_in_dim(array, start, size, axis)

    spare = LANES - local_heads - 2
    in_piece = jnp.concatenate(
        [slab(attn_in_weight, i * model_width + rank * width, width, 1) for i in range(4)]
        + [
            slab(forget_weight, rank * local_heads, local_heads, 1),
            norm_gains.T,
            jnp.zeros((attn_in_weight.shape[0], spare), BF16),
        ],
        axis=1,
    )
    out_piece = slab(out_weight, rank * width, width, 1)
    gate_up_piece = jnp.concatenate(
        [
            slab(gate_up_weight, (i * shards + f) * hidden_piece * ranks + rank * hidden_piece, hidden_piece, 1)
            for i in range(2)
            for f in range(shards)
        ],
        axis=1,
    )
    down_piece = slab(down_weight, rank * hidden_piece, hidden_piece, 0)

    def gather_shards(array):
        return lax.all_gather(array, "fsdp", axis=0, tiled=True)

    w_in = gather_shards(in_piece)
    w_out = gather_shards(out_piece)
    w_gate_up = gather_shards(gate_up_piece)
    w_down = gather_shards(down_piece)

    inputs = lax.all_gather(tokens[0], "ctx", axis=0, tiled=True)
    grad_low = lax.all_gather(out_grad[0], "ctx", axis=0, tiled=True)

    offsets = jnp.arange(seq_len, dtype=jnp.int32)
    places = jnp.take(seq_order, offsets // block_len) * block_len + offsets % block_len
    segments = jnp.take(segment_ids[0], places)
    places_all = (places[None, :], places[:, None], segments[None, :], segments[:, None])
    valid = (segments >= 0).astype(F32)

    bias = jnp.pad(slab(forget_bias, rank * local_heads, local_heads, 0), (0, LANES - local_heads))[None]
    head_gains = jnp.tile(qk_gains, (1, LANES // head_dim))

    gain_cols = w_in[:, 4 * width : 4 * width + LANES].astype(F32).T
    gain_one = gain_cols[local_heads]
    gain_two = gain_cols[local_heads + 1]

    wide_inputs = inputs.astype(F32)
    scale_one = rms_scale(wide_inputs)
    normed = (wide_inputs * scale_one * gain_one).astype(BF16)
    project = dot(normed, w_in)
    gated, attended, wide_query, wide_key, wide_value = attend(
        project, places_all, bias, head_gains, head_dim, width
    )
    gated_all = lax.all_gather(gated, "ctx", axis=1, tiled=True)
    mixed_cols = slab(inputs, rank * width, width, 1).astype(F32) + dot(gated_all, w_out)
    mixed = lax.all_gather(mixed_cols.astype(BF16), "ctx", axis=1, tiled=True).astype(F32)
    scale_two = rms_scale(mixed)
    normed_two = (mixed * scale_two * gain_two).astype(BF16)
    gate_up = dot(normed_two, w_gate_up)
    gate_part, up_part = gate_up[:, :hidden], gate_up[:, hidden:]
    gate_sigmoid = jax.nn.sigmoid(gate_part)
    silu = gate_part * gate_sigmoid
    hidden_act = (silu * up_part).astype(BF16)
    down_sum = lax.psum_scatter(
        dot(hidden_act, w_down).astype(BF16), "ctx", scatter_dimension=0, tiled=True
    ).astype(F32)

    def own_rows(array):
        return slab(array, rank * row_count, row_count, 0)

    result = own_rows(mixed) + down_sum
    block_out = result.astype(BF16)[None]
    branch = result - own_rows(wide_inputs)
    own_valid = own_rows(valid)
    partial_sums = jnp.stack(
        [
            jnp.sum(own_valid * jnp.sum(result * result, axis=-1)),
            jnp.sum(own_valid * jnp.sum(branch * branch, axis=-1)),
        ]
    )
    valid_count = jnp.sum(valid) * model_width

    grad_hidden = right_product(grad_low, w_down)
    grad_gate = grad_hidden * up_part * gate_sigmoid * (1.0 + gate_part * (1.0 - gate_sigmoid))
    grad_gate_up = jnp.concatenate([grad_gate, grad_hidden * silu], axis=1).astype(BF16)
    grad_normed_two = right_product(grad_gate_up, w_gate_up)
    gain_two_grad = jnp.sum(grad_normed_two * mixed * scale_two, axis=0)
    grad_mixed_part = norm_back(grad_normed_two, mixed, scale_two, gain_two).astype(BF16)
    grad_mixed_cols = slab(grad_low, rank * width, width, 1).astype(F32) + lax.psum_scatter(
        grad_mixed_part, "ctx", scatter_dimension=1, tiled=True
    ).astype(F32)
    grad_branch = grad_mixed_cols.astype(BF16)
    grad_gated = lax.psum_scatter(
        right_product(grad_branch, w_out).astype(BF16), "ctx", scatter_dimension=1, tiled=True
    ).astype(F32)
    grad_project, small = attend_back(
        project, places_all, bias, head_gains, attended, (wide_query, wide_key, wide_value),
        grad_gated, head_dim, width,
    )
    grad_normed = right_product(grad_project, w_in)
    gain_one_grad = jnp.sum(grad_normed * wide_inputs * scale_one, axis=0)
    in_own = jnp.arange(model_width, dtype=jnp.int32) // width == rank
    grad_inputs = norm_back(grad_normed, wide_inputs, scale_one, gain_one) + jnp.where(
        in_own[None], jnp.tile(grad_mixed_cols, (1, ranks)), 0.0
    )
    tokens_grad = lax.psum_scatter(grad_inputs.astype(BF16), "ctx", scatter_dimension=0, tiled=True)[None]

    def reduce_shards(array):
        return lax.psum_scatter(array.astype(BF16), "fsdp", scatter_dimension=0, tiled=True)

    def gather_ranks(array):
        return lax.all_gather(array, "ctx", axis=0, tiled=False).astype(F32)

    down_own = gather_ranks(reduce_shards(left_product(hidden_act, grad_low)))
    down_out = down_own.reshape(down_weight.shape)
    gate_up_own = gather_ranks(reduce_shards(left_product(normed_two, grad_gate_up)))
    gate_up_out = jnp.concatenate(
        [
            gate_up_own[c, :, (i * shards + f) * hidden_piece : (i * shards + f + 1) * hidden_piece]
            for i in range(2)
            for f in range(shards)
            for c in range(ranks)
        ],
        axis=1,
    )
    out_own = gather_ranks(reduce_shards(left_product(gated_all, grad_branch)))
    out_out = jnp.concatenate([out_own[c] for c in range(ranks)], axis=1)
    in_own = gather_ranks(reduce_shards(left_product(normed, grad_project)))
    in_out = jnp.concatenate(
        [in_own[c, :, i * width : (i + 1) * width] for i in range(4) for c in range(ranks)], axis=1
    )
    forget_out = jnp.concatenate([in_own[c, :, 4 * width : 4 * width + local_heads] for c in range(ranks)], axis=1)
    gains_sum = lax.psum_scatter(
        jnp.stack([gain_one_grad, gain_two_grad]), "fsdp", scatter_dimension=1, tiled=True
    )
    gains_sum, partial_sums = lax.psum((gains_sum, partial_sums), "ctx")
    bias_slots = jnp.where(
        jnp.arange(ranks, dtype=jnp.int32)[:, None] == rank, small[2, :local_heads][None], 0.0
    ).reshape(-1)
    qk_sum = small[0:2].reshape(2, LANES // head_dim, head_dim).sum(axis=1)
    bias_sum, qk_sum = lax.psum((bias_slots, qk_sum), ("ctx", "fsdp"))
    return (
        block_out, tokens_grad, gains_sum, in_out, forget_out, bias_sum, qk_sum,
        out_out, gate_up_out, down_out, jnp.sqrt(partial_sums / valid_count)[None],
    )


def solution(mesh):
    rows = P("fsdp", "ctx", None)
    return jax.shard_map(
        body,
        mesh=mesh,
        in_specs=(
            rows, P("fsdp", None), P("fsdp", None), P(None, "fsdp"), P("fsdp", None), P("fsdp", None),
            P(), P(), P("fsdp", None), P("fsdp", None), P("fsdp", None), rows,
        ),
        out_specs=(
            rows, rows, P(None, "fsdp"), P("fsdp", None), P("fsdp", None), P(), P(),
            P("fsdp", None), P("fsdp", None), P("fsdp", None), P("fsdp", None),
        ),
        check_vma=False,
    )
```

```python
import functools

import jax
import jax.numpy as jnp
from jax import lax
from jax.experimental import pallas as pl
from jax.experimental.pallas import tpu as pltpu
from jax.sharding import PartitionSpec as P

EPS = 1e-06
SCALE = 0.125
LANES = 128
F32 = jnp.float32
BF16 = jnp.bfloat16


def rms_scale(values):
    return lax.rsqrt(jnp.mean(values * values, axis=-1, keepdims=True) + EPS)


def norm_back(grad_normed, values, scale_values, gain_values):
    scaled = grad_normed * gain_values
    cubed = scale_values * scale_values * scale_values
    return scale_values * scaled - values * cubed * jnp.mean(
        scaled * values, axis=-1, keepdims=True
    )


def dot(left, right):
    return lax.dot_general(
        left, right, (((1,), (0,)), ((), ())), preferred_element_type=F32
    )


def left_product(left, right):
    return lax.dot_general(
        left, right, (((0,), (0,)), ((), ())), preferred_element_type=F32
    )


def right_product(left, right):
    return lax.dot_general(
        left, right, (((1,), (1,)), ((), ())), preferred_element_type=F32
    )


def split_three(values):
    high = values.astype(BF16).astype(F32)
    rest = values - high
    middle = rest.astype(BF16).astype(F32)
    return high, middle, rest - middle


def precise_left(zero_one, values):
    high, middle, low = split_three(values)
    total = dot(zero_one, high.astype(BF16))
    total = total + dot(zero_one, middle.astype(BF16))
    return total + dot(zero_one, low.astype(BF16))


def lane_ids(rows, lanes=LANES):
    return lax.broadcasted_iota(jnp.int32, (rows, lanes), 1)


def pick_lane(values, lanes, index):
    return jnp.sum(jnp.where(lanes == index, values, 0.0), axis=-1, keepdims=True)


def attend_kernel(
    head, chunk, heads,
    pos_row, pos_col, seg_row, seg_col, bias, gains, query, key, value, gate, forget,
    gated, attended, wide_query, wide_key, wide_value,
    mask, prefix,
):
    step = pl.program_id(0)
    rows = query.shape[0]
    lanes = lane_ids(rows)
    half = lane_ids(rows, head)

    @pl.when(step == 0)
    def _():
        log_forget = jax.nn.log_sigmoid(jnp.where(lanes < heads, forget[...] + bias[0:1, :], 0.0))
        high, middle, low = split_three(log_forget)
        @pl.loop(0, rows // chunk)
        def _(turn):
            part = pl.ds(pl.multiple_of(turn * chunk, chunk), chunk)
            before = pos_row[0:1, :] <= pos_col[part, :]
            same = seg_row[0:1, :] == seg_col[part, :]
            mask[part, :] = jnp.where(before & same, 0.0, -jnp.inf)
            before = jnp.where(before, 1.0, 0.0).astype(BF16)
            prefix[part, :] = (
                dot(before, high.astype(BF16))
                + dot(before, middle.astype(BF16))
                + dot(before, low.astype(BF16))
            )

    for side in range(LANES // head):
        here = pl.ds(side * head, head)
        column = pick_lane(prefix[...], lanes, (LANES // head) * step + side)
        high, middle, low = split_three(column)
        wide = jnp.where(half == 1, high, 0.0)
        wide = jnp.where(half == 2, middle, wide)
        wide = jnp.where(half == 3, low, wide)
        query_rest = jnp.where((half >= 4) & (half < 7), 1.0, wide)
        wide = jnp.where(half == 4, -high, 0.0)
        wide = jnp.where(half == 5, -middle, wide)
        wide = jnp.where(half == 6, -low, wide)
        ones = ((half >= 1) & (half < 4)) | ((half >= 7) & (half < 10))
        key_rest = jnp.where(ones, 1.0, wide)
        raw = query[:, here]
        normed = (raw * rms_scale(raw) * gains[0:1, here]).astype(BF16)
        wide_query[side, :, 0:head] = (normed.astype(F32) * SCALE).astype(BF16)
        wide_query[side, :, head:LANES] = query_rest.astype(BF16)
        raw = key[:, here]
        wide_key[side, :, 0:head] = (raw * rms_scale(raw) * gains[1:2, here]).astype(BF16)
        wide_key[side, :, head:LANES] = key_rest.astype(BF16)
        wide_value[side, :, 0:head] = value[:, here].astype(BF16)
        wide_value[side, :, head:LANES] = jnp.where(half < 3, 1.0, 0.0).astype(BF16)
        short = lane_ids(chunk, head)

        @pl.loop(0, rows // chunk)
        def _(turn):
            part = pl.ds(pl.multiple_of(turn * chunk, chunk), chunk)
            scores = right_product(wide_query[side, part, :], wide_key[side]) + mask[part, :]
            expos = jnp.exp(scores)
            total = jnp.sum(expos, axis=-1, keepdims=True)
            result = dot(expos.astype(BF16), wide_value[side])[:, 0:head] / total
            attended[part, here] = result
            gated[part, here] = (result * jax.nn.sigmoid(gate[part, here])).astype(BF16)
            high, middle, low = split_three(-jnp.log(total))
            rest = wide_query[side, part, head:LANES].astype(F32)
            rest = jnp.where(short == 7, high, rest)
            rest = jnp.where(short == 8, middle, rest)
            rest = jnp.where(short == 9, low, rest)
            wide_query[side, part, head:LANES] = rest.astype(BF16)


def attend_back_kernel(
    head, chunk, width, heads,
    pos_row, pos_col, seg_row, seg_col, bias, gains, query, key, gate, forget,
    attended, wide_query, wide_key, wide_value, grad_gated,
    grad_project, small,
    mask, wide_grad, grad_query, grad_key, grad_value, grad_prefix,
):
    step = pl.program_id(0)
    steps = pl.num_programs(0)
    rows = query.shape[0]
    lanes = lane_ids(rows)
    half = lane_ids(rows, head)

    @pl.when(step == 0)
    def _():
        @pl.loop(0, rows // chunk)
        def _(turn):
            part = pl.ds(pl.multiple_of(turn * chunk, chunk), chunk)
            after = pos_row[0:1, :] >= pos_col[part, :]
            same = seg_row[0:1, :] == seg_col[part, :]
            mask[part, :] = jnp.where(after & same, 0.0, -jnp.inf)
        grad_prefix[...] = jnp.zeros_like(grad_prefix)
        small[...] = jnp.zeros_like(small)

    for side in range(LANES // head):
        here = pl.ds(side * head, head)

        def column(part):
            return pl.ds(pl.multiple_of(part * width + step * LANES, LANES), LANES)

        sig = jax.nn.sigmoid(gate[:, here])
        grad_in = grad_gated[:, here]
        result = attended[:, here]
        grad_result = (grad_in * sig).astype(BF16)
        grad_gate = (grad_in * result * sig * (1.0 - sig)).astype(BF16)
        inner = -jnp.sum(grad_result.astype(F32) * result, axis=-1, keepdims=True)
        high, middle, low = split_three(inner)
        rest = jnp.where(half == 0, high, 0.0)
        rest = jnp.where(half == 1, middle, rest)
        rest = jnp.where(half == 2, low, rest)
        wide_grad[:, 0:head] = grad_result
        wide_grad[:, head:LANES] = rest.astype(BF16)
        grad_query[...] = jnp.zeros_like(grad_query)
        @pl.loop(0, rows // chunk)
        def _(turn):
            part = pl.ds(pl.multiple_of(turn * chunk, chunk), chunk)
            scores = right_product(wide_key[side, part, :], wide_query[side]) + mask[part, :]
            probs = jnp.exp(scores)
            outer = right_product(wide_value[side, part, :], wide_grad[...])
            grad_scores = (probs * outer).astype(BF16)
            grad_key[part, :] = dot(grad_scores, wide_query[side])
            grad_value[part, :] = dot(probs.astype(BF16), wide_grad[...])
            grad_query[...] += left_product(grad_scores, wide_key[side, part, :])
        from_query = grad_query[...]
        from_key = grad_key[...]
        change = pick_lane(from_query, lanes, head + 1) - pick_lane(from_key, lanes, head + 4)
        grad_prefix[...] += jnp.where(lanes == (LANES // head) * step + side, change, 0.0)

        raw = query[:, here]
        scale_raw = rms_scale(raw)
        grad_normed = from_query[:, 0:head] * SCALE
        grad_raw_query = norm_back(grad_normed, raw, scale_raw, gains[0:1, here])
        small[0:1, here] += jnp.sum(grad_normed * raw * scale_raw, axis=0, keepdims=True)
        raw = key[:, here]
        scale_raw = rms_scale(raw)
        grad_normed = from_key[:, 0:head]
        grad_raw_key = norm_back(grad_normed, raw, scale_raw, gains[1:2, here])
        small[1:2, here] += jnp.sum(grad_normed * raw * scale_raw, axis=0, keepdims=True)
        wide_grad[:, here] = grad_gate
        for part_id, piece in enumerate(
            (grad_raw_query.astype(BF16), grad_raw_key.astype(BF16), grad_value[:, 0:head].astype(BF16), grad_gate)
        ):
            if side == 0:
                grad_project[:, column(part_id)] = jnp.concatenate([piece, piece], axis=1)
            else:
                keep = grad_project[:, column(part_id)]
                both = jnp.concatenate([piece, piece], axis=1)
                grad_project[:, column(part_id)] = jnp.where(lanes < head, keep, both)

    @pl.when(step == steps - 1)
    def _():
        high, middle, low = split_three(grad_prefix[...])
        short = lane_ids(chunk)

        @pl.loop(0, rows // chunk)
        def _(turn):
            part = pl.ds(pl.multiple_of(turn * chunk, chunk), chunk)
            after = jnp.where(pos_row[0:1, :] >= pos_col[part, :], 1.0, 0.0).astype(BF16)
            total = dot(after, high.astype(BF16)) + dot(after, middle.astype(BF16)) + dot(after, low.astype(BF16))
            grad_logit = total * jax.nn.sigmoid(-(forget[part, :] + bias[0:1, :]))
            grad_logit = jnp.where(short < heads, grad_logit, 0.0).astype(BF16)
            grad_project[part, 4 * width : 4 * width + LANES] = grad_logit
            small[2:3, :] += jnp.sum(grad_logit.astype(F32), axis=0, keepdims=True)


def pick_chunk(rows):
    return 256 if rows % 256 == 0 else 128


def whole(shape):
    return pl.BlockSpec(shape, lambda step: tuple(0 for _ in shape))


def attend(project, places, bias, gains, head, width, heads):
    rows = project.shape[0]
    steps = width // LANES
    per = LANES // head
    chunk = pick_chunk(rows)

    def part(index):
        return pl.BlockSpec((rows, LANES), lambda step: (0, index * steps + step))

    own = pl.BlockSpec((rows, LANES), lambda step: (0, step))
    wide = pl.BlockSpec((per, rows, LANES), lambda step: (step, 0, 0))
    forget = pl.BlockSpec((rows, LANES), lambda step: (0, 4 * steps))
    wide_shape = jax.ShapeDtypeStruct((per * steps, rows, LANES), BF16)
    return pl.pallas_call(
        functools.partial(attend_kernel, head, chunk, heads),
        grid=(steps,),
        in_specs=[whole(p.shape) for p in places] + [whole(bias.shape), whole(gains.shape)]
        + [part(0), part(1), part(2), part(3), forget],
        out_specs=[own, own, wide, wide, wide],
        out_shape=[
            jax.ShapeDtypeStruct((rows, width), BF16),
            jax.ShapeDtypeStruct((rows, width), F32),
            wide_shape, wide_shape, wide_shape,
        ],
        scratch_shapes=[pltpu.VMEM((rows, rows), F32), pltpu.VMEM((rows, LANES), F32)],
        compiler_params=pltpu.CompilerParams(vmem_limit_bytes=48 << 20),
        name="attend",
    )(*places, bias, gains, project, project, project, project, project)


def attend_back(project, places, bias, gains, attended, wides, grad_gated, head, width, heads):
    rows = project.shape[0]
    steps = width // LANES
    per = LANES // head
    chunk = pick_chunk(rows)

    def part(index):
        return pl.BlockSpec((rows, LANES), lambda step: (0, index * steps + step))

    own = pl.BlockSpec((rows, LANES), lambda step: (0, step))
    wide = pl.BlockSpec((per, rows, LANES), lambda step: (step, 0, 0))
    forget = pl.BlockSpec((rows, LANES), lambda step: (0, 4 * steps))
    total = 4 * width + LANES
    return pl.pallas_call(
        functools.partial(attend_back_kernel, head, chunk, width, heads),
        grid=(steps,),
        in_specs=[whole(p.shape) for p in places] + [whole(bias.shape), whole(gains.shape)]
        + [part(0), part(1), part(3), forget, own, wide, wide, wide, own],
        out_specs=[whole((rows, total)), whole((8, LANES))],
        out_shape=[
            jax.ShapeDtypeStruct((rows, total), BF16),
            jax.ShapeDtypeStruct((8, LANES), F32),
        ],
        scratch_shapes=[
            pltpu.VMEM((rows, rows), F32),
            pltpu.VMEM((rows, LANES), BF16),
            pltpu.VMEM((rows, LANES), F32),
            pltpu.VMEM((rows, LANES), F32),
            pltpu.VMEM((rows, LANES), F32),
            pltpu.VMEM((rows, LANES), F32),
        ],
        compiler_params=pltpu.CompilerParams(vmem_limit_bytes=48 << 20),
        name="attend_back",
    )(*places, bias, gains, project, project, project, project, attended, *wides, grad_gated)


MESH = pl.DeviceIdType.MESH
ANY = pl.BlockSpec(memory_space=pltpu.HBM)


def greet(peers, line=None):
    barrier = pltpu.get_barrier_semaphore()
    if line is not None:
        peers = peers + [line.sibling]
    for peer in peers:
        pl.semaphore_signal(barrier, inc=1, device_id=peer, device_id_type=MESH)
    if line is not None:
        for there, peer in ((line.has_above, line.above), (line.has_below, line.below)):

            @pl.when(there)
            def _():
                pl.semaphore_signal(barrier, inc=1, device_id=peer, device_id_type=MESH)

    count = len(peers)
    if line is not None:
        last = line.layers - 1
        count = count + (1 - line.layer // last) + (line.layer + last) // line.layers
    pl.semaphore_wait(barrier, count)


class Line:
    def __init__(self, shards, source, target, sems):
        self.shard = lax.axis_index("fsdp")
        self.layers = shards // 2
        self.layer, self.core = self.shard // 2, self.shard % 2
        self.sibling = {"fsdp": self.shard ^ 1}
        self.above, self.below = {"fsdp": self.shard + 2}, {"fsdp": self.shard - 2}
        self.has_above, self.has_below = self.layer < self.layers - 1, self.layer > 0
        self.source, self.target = source, target
        self.rows = target.shape[0] // shards
        self.line_send, self.line_recv, self.side_send, self.side_recv, self.own_sem = sems

    def block(self, owner):
        return rows_of(self.target, owner, self.rows)

    def line(self, owner_layer, peer, way, own=False):
        here = self.block(owner_layer * 2 + self.core)
        return pltpu.make_async_remote_copy(
            self.source if own else here, here, self.line_send.at[way, owner_layer], self.line_recv.at[owner_layer],
            device_id=peer, device_id_type=MESH,
        )

    def side(self, owner_layer, owner_core, own=False):
        here = self.block(owner_layer * 2 + owner_core)
        return pltpu.make_async_remote_copy(
            self.source if own else here, here, self.side_send.at[owner_layer], self.side_recv.at[owner_layer],
            device_id=self.sibling, device_id_type=MESH,
        )

    def start(self):
        own = self.source is not None

        @pl.when(self.has_above)
        def _():
            self.line(self.layer, self.above, 0, own).start()

        @pl.when(self.has_below)
        def _():
            self.line(self.layer, self.below, 1, own).start()

        self.side(self.layer, self.core, own).start()
        if own:
            self.keep = pltpu.make_async_copy(self.source, self.block(self.shard), self.own_sem)
            self.keep.start()

    def step(self, distance):
        lower, upper = self.layer - distance, self.layer + distance

        @pl.when(lower >= 0)
        def _():
            self.line(lower, self.below, 1).wait_recv()

            @pl.when(self.has_above)
            def _():
                self.line(lower, self.above, 0).start()

            self.side(lower, self.core).start()

        @pl.when(upper < self.layers)
        def _():
            self.line(upper, self.above, 0).wait_recv()

            @pl.when(self.has_below)
            def _():
                self.line(upper, self.below, 1).start()

            self.side(upper, self.core).start()

    def finish(self):
        if self.source is not None:
            self.keep.wait()
        for owner_layer in range(self.layers):
            self.side(owner_layer, 1 - self.core).wait_recv()
            self.side(owner_layer, self.core).wait_send()

            @pl.when(self.has_above & (owner_layer <= self.layer))
            def _():
                self.line(owner_layer, self.above, 0).wait_send()

            @pl.when(self.has_below & (owner_layer >= self.layer))
            def _():
                self.line(owner_layer, self.below, 1).wait_send()


def line_scratch(shards):
    layers = shards // 2
    return [
        pltpu.SemaphoreType.DMA((2, layers)),
        pltpu.SemaphoreType.DMA((layers,)),
        pltpu.SemaphoreType.DMA((layers,)),
        pltpu.SemaphoreType.DMA((layers,)),
        pltpu.SemaphoreType.DMA,
    ]


class Relay:
    def __init__(self, rank, source, place, send_sem, recv_sem, own_sem):
        self.rank, self.source, self.place = rank, source, place
        self.send_sem, self.recv_sem, self.own_sem = send_sem, recv_sem, own_sem
        self.copies = []

    def send(self, number, source, place, distance):
        copy = pltpu.make_async_remote_copy(
            source, place, self.send_sem.at[number], self.recv_sem.at[number],
            device_id={"ctx": self.rank ^ distance}, device_id_type=MESH,
        )
        copy.start()
        self.copies.append(copy)

    def start(self):
        me = self.rank
        self.send(0, self.source(0), self.place(me, 0), 1)
        self.send(1, self.source(1), self.place(me, 1), 2)
        self.send(2, self.source(1), self.place(me, 1), 1)
        self.send(3, self.source(0), self.place(me, 0), 2)
        self.own = [
            pltpu.make_async_copy(self.source(h), self.place(me, h), self.own_sem.at[h]) for h in range(2)
        ]
        for copy in self.own:
            copy.start()

    def forward(self):
        near, below = self.rank ^ 1, self.rank ^ 2
        self.copies[0].wait_recv()
        self.send(4, self.place(near, 0), self.place(near, 0), 2)
        self.copies[1].wait_recv()
        self.send(5, self.place(below, 1), self.place(below, 1), 1)

    def finish(self):
        for copy in self.own:
            copy.wait()
        for number, copy in enumerate(self.copies):
            if number >= 2:
                copy.wait_recv()
        for copy in self.copies:
            copy.wait_send()


def rows_of(ref, index, size):
    return ref.at[pl.ds(pl.multiple_of(index * size, 16), size), :]


def cols_of(ref, index, size):
    return ref.at[:, pl.ds(pl.multiple_of(index * size, LANES), size)]


def relay_ops(mode, rank, source, target, sems):
    rows, cols = source.shape
    half = rows // 2

    def part(h):
        return source.at[pl.ds(h * half, half), :]

    def place(block, h):
        if mode == "gather_rows":
            return target.at[pl.ds(pl.multiple_of(block * rows + h * half, 16), half), :]
        if mode == "gather_cols":
            return target.at[pl.ds(h * half, half), pl.ds(pl.multiple_of(block * cols, LANES), cols)]
        return target.at[block, pl.ds(h * half, half), :]

    return Relay(rank, part, place, *sems)


def exchange_kernel(modes, ranks, across, shards, *refs):
    count = len(modes)
    sources, targets = refs[:count], refs[count : 2 * count]
    send_sem, recv_sem, own_sem = refs[2 * count : 2 * count + 3]
    rank = lax.axis_index("ctx")
    shard = lax.axis_index("fsdp")
    line = None
    if "line" in modes:
        at = modes.index("line")
        line = Line(shards, sources[at], targets[at], refs[2 * count + 3 :])
    far = any(mode not in ("gather_rows", "gather_cols", "stack", "line") for mode in modes)
    peers = [{"ctx": rank ^ distance} for distance in range(1, ranks if far else ranks - 1)]
    if across:
        peers += [{"fsdp": shard ^ distance} for distance in range(1, across)]
    greet(peers, line)
    copies, relays = [], []
    for op, (mode, source, target) in enumerate(zip(modes, sources, targets)):
        if mode == "line":
            line.start()
            continue
        if mode in ("gather_rows", "gather_cols", "stack"):
            relay = relay_ops(mode, rank, source, target, (send_sem.at[op], recv_sem.at[op], own_sem.at[op]))
            relay.start()
            relays.append(relay)
            continue
        axis, me, members = ("fsdp", shard, across) if mode == "shards" else ("ctx", rank, ranks)
        for distance in range(members):
            other = me ^ distance if distance else me
            place = target.at[me]
            if mode == "scatter_rows":
                piece = rows_of(source, other, target.shape[1])
            elif mode == "scatter_cols":
                piece = cols_of(source, other, target.shape[2])
            elif mode == "shards":
                piece = source.at[other]
            else:
                piece = source
            if distance == 0:
                copy = pltpu.make_async_copy(piece, place, own_sem.at[op, 0])
            else:
                copy = pltpu.make_async_remote_copy(
                    piece, place, send_sem.at[op, distance - 1], recv_sem.at[op, distance - 1],
                    device_id={axis: other}, device_id_type=MESH,
                )
            copy.start()
            copies.append(copy)
    for index in range(max(len(relays), shards // 2 - 1 if line is not None else 0)):
        if line is not None and 0 < index < shards // 2:
            line.step(index)
        if index < len(relays):
            relays[index].forward()
    if line is not None:
        line.step(shards // 2 - 1)
        line.finish()
    for relay in relays:
        relay.finish()
    for copy in copies:
        copy.wait()


def exchange(collective_id, ranks, across, shards, *ops):
    shapes = []
    for mode, source in ops:
        shape = source.shape
        if mode == "gather_rows":
            shape = (ranks * shape[0], shape[1])
        elif mode == "gather_cols":
            shape = (shape[0], ranks * shape[1])
        elif mode == "scatter_rows":
            shape = (ranks, shape[0] // ranks, shape[1])
        elif mode == "scatter_cols":
            shape = (ranks, shape[0], shape[1] // ranks)
        elif mode in ("stack", "each"):
            shape = (ranks,) + shape
        elif mode == "line":
            shape = (shards * shape[0], shape[1])
        shapes.append(jax.ShapeDtypeStruct(shape, source.dtype))
    count = len(ops)
    most = max(6, across - 1)
    moved = sum(s.size * s.dtype.itemsize for s in shapes)
    return pl.pallas_call(
        functools.partial(exchange_kernel, [mode for mode, _ in ops], ranks, across, shards),
        in_specs=[ANY] * count,
        out_specs=[ANY] * count,
        out_shape=shapes,
        scratch_shapes=[
            pltpu.SemaphoreType.DMA((count, most)),
            pltpu.SemaphoreType.DMA((count, most)),
            pltpu.SemaphoreType.DMA((count, 2)),
        ]
        + (line_scratch(shards) if any(mode == "line" for mode, _ in ops) else []),
        compiler_params=pltpu.CompilerParams(collective_id=collective_id, has_side_effects=True),
        cost_estimate=pl.CostEstimate(flops=0, bytes_accessed=moved * 20, transcendentals=0),
        name="exchange",
    )(*[source for _, source in ops])


def start_kernel(
    shards, width, piece,
    tokens, cotangent, weight, tail, other, inputs, grad_low, gathered, picked,
    weight_all, other_all, own_cols, own_pick,
    send_sem, recv_sem, own_sem, load_sem, *line_sems,
):
    rank = lax.axis_index("ctx")
    ranks = lax.axis_size("ctx")
    model = weight.shape[1] // 4
    loads = [
        pltpu.make_async_copy(weight, weight_all, load_sem.at[0]),
        pltpu.make_async_copy(other, other_all, load_sem.at[1]),
    ]
    for copy in loads:
        copy.start()
    line = Line(shards, own_cols, gathered, line_sems)
    greet([{"ctx": rank ^ 1}, {"ctx": rank ^ 2}], line)
    first = relay_ops("gather_rows", rank, tokens, inputs, (send_sem.at[0], recv_sem.at[0], own_sem.at[0]))
    second = relay_ops("gather_rows", rank, cotangent, grad_low, (send_sem.at[1], recv_sem.at[1], own_sem.at[1]))
    loads[0].wait()
    for i in range(4):
        own_cols[:, i * width : (i + 1) * width] = weight_all[
            :, pl.ds(pl.multiple_of(i * model + rank * width, LANES), width)
        ]
    own_cols[:, 4 * width : 4 * width + LANES] = tail[...]
    line.start()
    first.start()
    loads[1].wait()
    for i in range(picked.shape[1] // piece):
        own_pick[:, i * piece : (i + 1) * piece] = other_all[
            :, pl.ds(pl.multiple_of((i * ranks + rank) * piece, LANES), piece)
        ]
    keep = pltpu.make_async_copy(own_pick, picked, load_sem.at[2])
    keep.start()
    first.forward()
    second.start()
    for distance in range(1, line.layers):
        line.step(distance)
        if distance == 1:
            second.forward()
    first.finish()
    second.finish()
    line.finish()
    keep.wait()


def start_moves(collective_id, ranks, shards, width, piece, tokens, cotangent, weight, tail, other):
    rows, model = tokens.shape
    return pl.pallas_call(
        functools.partial(start_kernel, shards, width, piece),
        in_specs=[ANY] * 3 + [pl.BlockSpec(memory_space=pltpu.VMEM), ANY],
        out_specs=[ANY] * 4,
        out_shape=[
            jax.ShapeDtypeStruct((ranks * rows, model), BF16),
            jax.ShapeDtypeStruct((ranks * rows, model), BF16),
            jax.ShapeDtypeStruct((shards * weight.shape[0], 4 * width + LANES), BF16),
            jax.ShapeDtypeStruct((other.shape[0], other.shape[1] // ranks), BF16),
        ],
        scratch_shapes=[
            pltpu.VMEM(weight.shape, BF16),
            pltpu.VMEM(other.shape, BF16),
            pltpu.VMEM((weight.shape[0], 4 * width + LANES), BF16),
            pltpu.VMEM((other.shape[0], other.shape[1] // ranks), BF16),
            pltpu.SemaphoreType.DMA((2, 6)),
            pltpu.SemaphoreType.DMA((2, 6)),
            pltpu.SemaphoreType.DMA((2, 2)),
            pltpu.SemaphoreType.DMA((3,)),
        ]
        + line_scratch(shards),
        compiler_params=pltpu.CompilerParams(
            collective_id=collective_id, has_side_effects=True, vmem_limit_bytes=24 << 20
        ),
        cost_estimate=pl.CostEstimate(flops=0, bytes_accessed=150 << 20, transcendentals=0),
        name="start_moves",
    )(tokens, cotangent, weight, tail, other)


def spread_kernel(pieces, *refs):
    source, targets = refs[0], refs[1:]
    ranks = source.shape[0]
    for target, (piece, first, count) in zip(targets, pieces):
        for block in range(count):
            for index in range(ranks):
                target[:, pl.ds((block * ranks + index) * piece, piece)] = source[
                    index, :, pl.ds(first + block * piece, piece)
                ].astype(F32)


def spread_cols(source, *pieces):
    ranks, rows, cols = source.shape
    if any(piece % LANES or first % LANES for piece, first, _ in pieces):
        return [
            jnp.concatenate(
                [
                    source[c, :, first + i * piece : first + (i + 1) * piece]
                    for i in range(count)
                    for c in range(ranks)
                ],
                axis=1,
            ).astype(F32)
            for piece, first, count in pieces
        ]
    part = rows // 4 if rows % 64 == 0 else rows
    widths = [count * ranks * piece for piece, _, count in pieces]
    return pl.pallas_call(
        functools.partial(spread_kernel, pieces),
        grid=(rows // part,),
        in_specs=[pl.BlockSpec((ranks, part, cols), lambda step: (0, step, 0))],
        out_specs=[pl.BlockSpec((part, w), lambda step: (step, 0)) for w in widths],
        out_shape=[jax.ShapeDtypeStruct((rows, w), F32) for w in widths],
        compiler_params=pltpu.CompilerParams(vmem_limit_bytes=32 << 20),
        cost_estimate=pl.CostEstimate(flops=0, bytes_accessed=rows * sum(widths) * 6, transcendentals=0),
        name="spread_cols",
    )(source)


class Native:
    def __init__(self, ranks):
        self.ranks = ranks

    def begin(self, number, tokens, cotangent, weight, tail, other, piece, width, padded):
        rank, model = lax.axis_index("ctx"), tokens.shape[1]
        parts = [lax.dynamic_slice_in_dim(weight, i * model + rank * width, width, 1) for i in range(4)]
        parts = [jnp.pad(part, ((0, 0), (0, padded - width))) for part in parts]
        cols = other.shape[1] // self.ranks
        picks = [
            lax.dynamic_slice_in_dim(other, (i * self.ranks + rank) * piece, piece, 1) for i in range(cols // piece)
        ]
        return (
            lax.all_gather(tokens, "ctx", axis=0, tiled=True),
            lax.all_gather(cotangent, "ctx", axis=0, tiled=True),
            lax.all_gather(jnp.concatenate(parts + [tail], axis=1), "fsdp", axis=0, tiled=True),
            jnp.concatenate(picks, axis=1),
        )

    def gather_cols(self, number, array, piece):
        return lax.all_gather(array, "ctx", axis=1, tiled=True), lax.all_gather(piece, "fsdp", axis=0, tiled=True)

    def scatter_cols(self, number, array):
        return lax.psum_scatter(array, "ctx", scatter_dimension=1, tiled=True).astype(F32)

    def finish_rows(self, number, first, second, sums):
        pair = [
            lax.psum_scatter(a, "ctx", scatter_dimension=0, tiled=True).astype(F32) for a in (first, second)
        ]
        return pair + [lax.psum(sums, "ctx")]

    def stack(self, number, *arrays):
        return [lax.all_gather(a, "ctx", axis=0, tiled=False) for a in arrays]

    def finish(self, number, array, pieces):
        return lax.all_gather(array, "ctx", axis=0, tiled=False), lax.psum_scatter(
            pieces, "fsdp", scatter_dimension=0, tiled=False
        )


class Direct:
    def __init__(self, ranks, shards):
        self.ranks, self.shards = ranks, shards

    def run(self, number, *ops):
        return exchange(number, self.ranks, 0, self.shards, *ops)

    def begin(self, number, tokens, cotangent, weight, tail, other, piece, width, padded):
        return start_moves(
            number, self.ranks, self.shards, width, piece, tokens, cotangent, weight, tail, other
        )

    def gather_cols(self, number, array, piece):
        return self.run(number, ("gather_cols", array), ("line", piece))

    def scatter_cols(self, number, array):
        return self.run(number, ("scatter_cols", array))[0].astype(F32).sum(axis=0)

    def finish_rows(self, number, first, second, sums):
        out = self.run(number, ("scatter_rows", first), ("scatter_rows", second), ("each", sums))
        return [a.astype(F32).sum(axis=0) for a in out]

    def stack(self, number, *arrays):
        return self.run(number, *[("stack" if a.dtype == BF16 else "each", a) for a in arrays])

    def finish(self, number, array, pieces):
        out = exchange(number, self.ranks, self.shards, self.shards, ("stack", array), ("shards", pieces))
        return out[0], out[1].sum(axis=0)


def body(
    tokens, block_order, segment_ids, norm_gains, attn_in_weight, forget_weight, forget_bias,
    qk_gains, out_weight, gate_up_weight, down_weight, out_grad,
):
    ranks = lax.axis_size("ctx")
    shards = lax.axis_size("fsdp")
    rank = lax.axis_index("ctx")
    row_count, model_width = tokens.shape[1], tokens.shape[2]
    head_count, head_dim = forget_bias.shape[0], qk_gains.shape[1]
    local_heads = head_count // ranks
    width = local_heads * head_dim
    padded = -(-width // LANES) * LANES
    seq_order = block_order[0]
    seq_len = segment_ids.shape[1]
    block_len = seq_len // seq_order.shape[0]
    hidden_piece = down_weight.shape[0] // ranks
    hidden = hidden_piece * shards
    plain = ranks == 4 and shards & (shards - 1) == 0 and width == padded
    comm = Direct(ranks, shards) if plain else Native(ranks)

    def slab(array, start, size, axis):
        return lax.dynamic_slice_in_dim(array, start, size, axis)

    def widen(array):
        return jnp.pad(array, ((0, 0), (0, padded - width))) if padded > width else array

    tail = jnp.concatenate(
        [
            slab(forget_weight, rank * local_heads, local_heads, 1),
            norm_gains.T,
            jnp.zeros((attn_in_weight.shape[0], LANES - local_heads - 2), BF16),
        ],
        axis=1,
    )
    inputs, grad_low, w_in, gate_up_piece = comm.begin(
        0, tokens[0], out_grad[0], attn_in_weight, tail, gate_up_weight, hidden_piece, width, padded
    )
    w_gate_up = lax.all_gather(gate_up_piece, "fsdp", axis=0, tiled=True)

    offsets = jnp.arange(seq_len, dtype=jnp.int32)
    blocks = jnp.arange(seq_order.shape[0], dtype=jnp.int32)
    places = (seq_order[:, None] * block_len + offsets[None, :block_len]).reshape(-1)
    by_block = segment_ids[0].reshape(-1, block_len)
    chosen = seq_order[:, None, None] == blocks[None, :, None]
    segments = jnp.sum(jnp.where(chosen, by_block[None], 0), axis=1).reshape(-1)
    places_all = (places[None, :], places[:, None], segments[None, :], segments[:, None])
    valid = (segments >= 0).astype(F32)

    bias = jnp.pad(slab(forget_bias, rank * local_heads, local_heads, 0), (0, LANES - local_heads))[None]
    head_gains = jnp.tile(qk_gains, (1, LANES // head_dim))

    gain_cols = w_in[:, 4 * padded : 4 * padded + LANES].astype(F32).T
    gain_one = gain_cols[local_heads]
    gain_two = gain_cols[local_heads + 1]

    wide_inputs = inputs.astype(F32)
    scale_one = rms_scale(wide_inputs)
    normed = (wide_inputs * scale_one * gain_one).astype(BF16)
    project = dot(normed, w_in)
    gated, attended, wide_query, wide_key, wide_value = attend(
        project, places_all, bias, head_gains, head_dim, padded, local_heads
    )
    gated_all, w_out = comm.gather_cols(1, gated[:, :width], slab(out_weight, rank * width, width, 1))
    mixed_cols = slab(inputs, rank * width, width, 1).astype(F32) + dot(gated_all, w_out)
    mixed, w_down = comm.gather_cols(
        2, mixed_cols.astype(BF16), slab(down_weight, rank * hidden_piece, hidden_piece, 0)
    )
    mixed = mixed.astype(F32)
    scale_two = rms_scale(mixed)
    normed_two = (mixed * scale_two * gain_two).astype(BF16)
    gate_up = dot(normed_two, w_gate_up)
    gate_part, up_part = gate_up[:, :hidden], gate_up[:, hidden:]
    gate_sigmoid = jax.nn.sigmoid(gate_part)
    silu = gate_part * gate_sigmoid
    hidden_act = (silu * up_part).astype(BF16)
    down_part = dot(hidden_act, w_down).astype(BF16)

    def own_rows(array):
        return slab(array, rank * row_count, row_count, 0)

    grad_hidden = right_product(grad_low, w_down)
    grad_gate = grad_hidden * up_part * gate_sigmoid * (1.0 + gate_part * (1.0 - gate_sigmoid))
    grad_gate_up = jnp.concatenate([grad_gate, grad_hidden * silu], axis=1).astype(BF16)
    grad_normed_two = right_product(grad_gate_up, w_gate_up)
    gain_two_grad = jnp.sum(grad_normed_two * mixed * scale_two, axis=0)
    grad_mixed_part = norm_back(grad_normed_two, mixed, scale_two, gain_two).astype(BF16)

    def reduce_shards(array):
        return lax.psum_scatter(array.astype(BF16), "fsdp", scatter_dimension=0, tiled=True)

    down_part_grad = left_product(hidden_act, grad_low).astype(BF16)
    grad_mixed_part, down_part_grad = lax.optimization_barrier((grad_mixed_part, down_part_grad))
    down_share = reduce_shards(down_part_grad)
    grad_mixed_cols = slab(grad_low, rank * width, width, 1).astype(F32) + comm.scatter_cols(3, grad_mixed_part)
    grad_branch = grad_mixed_cols.astype(BF16)
    gate_up_grad = left_product(normed_two, grad_gate_up).astype(BF16)
    grad_branch, gate_up_grad = lax.optimization_barrier((grad_branch, gate_up_grad))
    gate_up_share = reduce_shards(gate_up_grad)
    grad_gated = widen(comm.scatter_cols(4, right_product(grad_branch, w_out).astype(BF16)))
    grad_gated, down_share = lax.optimization_barrier((grad_gated, down_share))
    grad_project, small = attend_back(
        project, places_all, bias, head_gains, attended, (wide_query, wide_key, wide_value),
        grad_gated, head_dim, padded, local_heads,
    )

    in_part = left_product(normed, grad_project).astype(BF16)
    out_part = left_product(gated_all, grad_branch).astype(BF16)
    late = jnp.concatenate([in_part[:, : 4 * padded], out_part, in_part[:, 4 * padded :]], axis=1)
    late, gate_up_share = lax.optimization_barrier((late, gate_up_share))
    late_share = reduce_shards(late)

    grad_normed = right_product(grad_project, w_in)
    gain_one_grad = jnp.sum(grad_normed * wide_inputs * scale_one, axis=0)
    in_own = jnp.arange(model_width, dtype=jnp.int32) // width == rank
    grad_inputs = norm_back(grad_normed, wide_inputs, scale_one, gain_one) + jnp.where(
        in_own[None], jnp.tile(grad_mixed_cols, (1, ranks)), 0.0
    )
    bias_slots = jnp.where(
        jnp.arange(ranks, dtype=jnp.int32)[:, None] == rank, small[2, :local_heads][None], 0.0
    ).reshape(-1)
    qk_sum = small[0:2].reshape(2, LANES // head_dim, head_dim).sum(axis=1).reshape(-1)
    others = jnp.concatenate([bias_slots, qk_sum])
    sums = jnp.stack(
        [gain_one_grad, gain_two_grad, jnp.pad(others, (0, model_width - others.shape[0]))]
        + [jnp.zeros((model_width,), F32)] * 5
    )
    down_sum, tokens_grad, sums = comm.finish_rows(5, down_part, grad_inputs.astype(BF16), sums)
    tokens_grad = tokens_grad.astype(BF16)[None]
    result = own_rows(mixed) + down_sum
    block_out = result.astype(BF16)[None]
    branch = result - own_rows(wide_inputs)
    own_valid = own_rows(valid)
    partial_sums = jnp.stack(
        [
            jnp.sum(own_valid * jnp.sum(result * result, axis=-1)),
            jnp.sum(own_valid * jnp.sum(branch * branch, axis=-1)),
        ]
    )
    valid_count = jnp.sum(valid) * model_width

    down_own, gate_up_own, stats = comm.stack(
        6, down_share, gate_up_share, jnp.broadcast_to(jnp.pad(partial_sums, (0, LANES - 2)), (8, LANES))
    )
    down_out = down_own.astype(F32).reshape(down_weight.shape)
    gate_up_out = spread_cols(gate_up_own, (hidden_piece, 0, 2 * shards))[0]
    share = model_width // shards
    room = -(-share // LANES) * LANES
    gain_pieces = jnp.pad(sums[0:2].reshape(2, shards, share).transpose(1, 0, 2), ((0, 0), (0, 0), (0, room - share)))
    tail = jnp.pad(sums[2, : others.shape[0]], (0, 2 * room - others.shape[0])).reshape(1, 2, room)
    pieces = jnp.concatenate(
        [gain_pieces, jnp.broadcast_to(tail, (shards, 2, room)), jnp.zeros((shards, 4, room), F32)], axis=1
    )
    late_own, piece_sum = comm.finish(7, late_share, pieces)
    if plain:
        in_out, out_out = spread_cols(late_own, (width, 0, 4), (width, 4 * width, 1))
    else:
        in_out = jnp.concatenate(
            [late_own[c, :, i * padded : i * padded + width] for i in range(4) for c in range(ranks)], axis=1
        ).astype(F32)
        out_out = jnp.concatenate(
            [late_own[c, :, 4 * padded : 4 * padded + width] for c in range(ranks)], axis=1
        ).astype(F32)
    last = 4 * padded + width
    forget_out = jnp.concatenate([late_own[c, :, last : last + local_heads] for c in range(ranks)], axis=1).astype(F32)
    gains_sum = piece_sum[0:2, :share]
    tail_sum = piece_sum[2:4].reshape(-1)
    bias_sum = tail_sum[:head_count]
    qk_sum = tail_sum[head_count : head_count + 2 * head_dim].reshape(2, head_dim)
    totals = stats[:, 0, :2].sum(axis=0)
    return (
        block_out, tokens_grad, gains_sum, in_out, forget_out, bias_sum, qk_sum,
        out_out, gate_up_out, down_out, jnp.sqrt(totals / valid_count)[None],
    )


def solution(mesh):
    rows = P("fsdp", "ctx", None)
    return jax.shard_map(
        body,
        mesh=mesh,
        in_specs=(
            rows, P("fsdp", None), P("fsdp", None), P(None, "fsdp"), P("fsdp", None), P("fsdp", None),
            P(), P(), P("fsdp", None), P("fsdp", None), P("fsdp", None), rows,
        ),
        out_specs=(
            rows, rows, P(None, "fsdp"), P("fsdp", None), P("fsdp", None), P(), P(),
            P("fsdp", None), P("fsdp", None), P("fsdp", None), P("fsdp", None),
        ),
        check_vma=False,
    )
```

```python
import functools

import jax
import jax.numpy as jnp
from jax import lax
from jax.experimental import pallas as pl
from jax.experimental.pallas import tpu as pltpu
from jax.sharding import PartitionSpec as P

EPS = 1e-06
SCALE = 0.125
LANES = 128
VMEM_LIMIT = 60 << 20
F32 = jnp.float32
BF16 = jnp.bfloat16


MESH = pl.DeviceIdType.MESH
ANY = pl.BlockSpec(memory_space=pltpu.HBM)


def rms_scale(values):
    return lax.rsqrt(jnp.mean(values * values, axis=-1, keepdims=True) + EPS)


def norm_back(grad_normed, values, scale_values, gain_values):
    scaled = grad_normed * gain_values
    cubed = scale_values * scale_values * scale_values
    return scale_values * scaled - values * cubed * jnp.mean(
        scaled * values, axis=-1, keepdims=True
    )


def dot(left, right):
    return lax.dot_general(
        left, right, (((1,), (0,)), ((), ())), preferred_element_type=F32
    )


def left_product(left, right):
    return lax.dot_general(
        left, right, (((0,), (0,)), ((), ())), preferred_element_type=F32
    )


def right_product(left, right):
    return lax.dot_general(
        left, right, (((1,), (1,)), ((), ())), preferred_element_type=F32
    )


def split_three(values):
    high = values.astype(BF16).astype(F32)
    rest = values - high
    middle = rest.astype(BF16).astype(F32)
    return high, middle, rest - middle


def precise_left(zero_one, values):
    high, middle, low = split_three(values)
    total = dot(zero_one, high.astype(BF16))
    total = total + dot(zero_one, middle.astype(BF16))
    return total + dot(zero_one, low.astype(BF16))


def lane_ids(rows, lanes=LANES):
    return lax.broadcasted_iota(jnp.int32, (rows, lanes), 1)


def pick_lane(values, lanes, index):
    return jnp.sum(jnp.where(lanes == index, values, 0.0), axis=-1, keepdims=True)


def attend_kernel(
    head, chunk, heads,
    pos_row, pos_col, seg_row, seg_col, bias, gains, query, key, value, gate, forget,
    gated, attended, wide_query, wide_key, wide_value,
    mask, prefix,
):
    step = pl.program_id(0)
    rows = query.shape[0]
    lanes = lane_ids(rows)
    half = lane_ids(rows, head)

    @pl.when(step == 0)
    def _():
        log_forget = jax.nn.log_sigmoid(jnp.where(lanes < heads, forget[...] + bias[0:1, :], 0.0))
        high, middle, low = split_three(log_forget)
        @pl.loop(0, rows // chunk)
        def _(turn):
            part = pl.ds(pl.multiple_of(turn * chunk, chunk), chunk)
            before = pos_row[0:1, :] <= pos_col[part, :]
            same = seg_row[0:1, :] == seg_col[part, :]
            mask[part, :] = jnp.where(before & same, 0.0, -jnp.inf)
            before = jnp.where(before, 1.0, 0.0).astype(BF16)
            prefix[part, :] = (
                dot(before, high.astype(BF16))
                + dot(before, middle.astype(BF16))
                + dot(before, low.astype(BF16))
            )

    for side in range(LANES // head):
        here = pl.ds(side * head, head)
        column = pick_lane(prefix[...], lanes, (LANES // head) * step + side)
        high, middle, low = split_three(column)
        wide = jnp.where(half == 1, high, 0.0)
        wide = jnp.where(half == 2, middle, wide)
        wide = jnp.where(half == 3, low, wide)
        query_rest = jnp.where((half >= 4) & (half < 7), 1.0, wide)
        wide = jnp.where(half == 4, -high, 0.0)
        wide = jnp.where(half == 5, -middle, wide)
        wide = jnp.where(half == 6, -low, wide)
        ones = ((half >= 1) & (half < 4)) | ((half >= 7) & (half < 10))
        key_rest = jnp.where(ones, 1.0, wide)
        raw = query[:, here]
        normed = (raw * rms_scale(raw) * gains[0:1, here]).astype(BF16)
        wide_query[side, :, 0:head] = (normed.astype(F32) * SCALE).astype(BF16)
        wide_query[side, :, head:LANES] = query_rest.astype(BF16)
        raw = key[:, here]
        wide_key[side, :, 0:head] = (raw * rms_scale(raw) * gains[1:2, here]).astype(BF16)
        wide_key[side, :, head:LANES] = key_rest.astype(BF16)
        wide_value[side, :, 0:head] = value[:, here].astype(BF16)
        wide_value[side, :, head:LANES] = jnp.where(half < 3, 1.0, 0.0).astype(BF16)
        short = lane_ids(chunk, head)

        @pl.loop(0, rows // chunk)
        def _(turn):
            part = pl.ds(pl.multiple_of(turn * chunk, chunk), chunk)
            scores = right_product(wide_query[side, part, :], wide_key[side]) + mask[part, :]
            expos = jnp.exp(scores)
            total = jnp.sum(expos, axis=-1, keepdims=True)
            result = dot(expos.astype(BF16), wide_value[side])[:, 0:head] / total
            attended[part, here] = result
            gated[part, here] = (result * jax.nn.sigmoid(gate[part, here])).astype(BF16)
            high, middle, low = split_three(-jnp.log(total))
            rest = wide_query[side, part, head:LANES].astype(F32)
            rest = jnp.where(short == 7, high, rest)
            rest = jnp.where(short == 8, middle, rest)
            rest = jnp.where(short == 9, low, rest)
            wide_query[side, part, head:LANES] = rest.astype(BF16)


def attend_back_kernel(
    head, chunk, width, heads, ranks,
    pos_row, pos_col, seg_row, seg_col, bias, gains, query, key, gate, forget,
    attended, wide_query, wide_key, wide_value, grad_gated, aside,
    grad_project, small, aside_in,
    mask, wide_grad, grad_query, grad_key, grad_value, grad_prefix, *sems,
):
    step = pl.program_id(0)
    steps = pl.num_programs(0)

    def aside_copies():
        send_sem, recv_sem, own_sem = sems
        rank = lax.axis_index("ctx")
        size = aside_in.shape[1]
        yield pltpu.make_async_copy(rows_of(aside, rank, size), aside_in.at[rank], own_sem)
        for distance in range(1, ranks):
            other = rank ^ distance
            yield to_rank(
                rows_of(aside, other, size), aside_in.at[rank],
                send_sem.at[distance - 1], recv_sem.at[distance - 1], other,
            )

    if ranks:

        @pl.when(step == 0)
        def _():
            rank = lax.axis_index("ctx")
            greet([{"ctx": rank ^ distance} for distance in range(1, ranks)])
            for copy in aside_copies():
                copy.start()

    rows = query.shape[0]
    lanes = lane_ids(rows)
    half = lane_ids(rows, head)

    @pl.when(step == 0)
    def _():
        @pl.loop(0, rows // chunk)
        def _(turn):
            part = pl.ds(pl.multiple_of(turn * chunk, chunk), chunk)
            after = pos_row[0:1, :] >= pos_col[part, :]
            same = seg_row[0:1, :] == seg_col[part, :]
            mask[part, :] = jnp.where(after & same, 0.0, -jnp.inf)
        grad_prefix[...] = jnp.zeros_like(grad_prefix)
        small[...] = jnp.zeros_like(small)

    for side in range(LANES // head):
        here = pl.ds(side * head, head)

        def column(part):
            return pl.ds(pl.multiple_of(part * width + step * LANES, LANES), LANES)

        sig = jax.nn.sigmoid(gate[:, here])
        grad_in = grad_gated[:, here]
        result = attended[:, here]
        grad_result = (grad_in * sig).astype(BF16)
        grad_gate = (grad_in * result * sig * (1.0 - sig)).astype(BF16)
        inner = -jnp.sum(grad_result.astype(F32) * result, axis=-1, keepdims=True)
        high, middle, low = split_three(inner)
        rest = jnp.where(half == 0, high, 0.0)
        rest = jnp.where(half == 1, middle, rest)
        rest = jnp.where(half == 2, low, rest)
        wide_grad[:, 0:head] = grad_result
        wide_grad[:, head:LANES] = rest.astype(BF16)
        grad_query[...] = jnp.zeros_like(grad_query)
        @pl.loop(0, rows // chunk)
        def _(turn):
            part = pl.ds(pl.multiple_of(turn * chunk, chunk), chunk)
            scores = right_product(wide_key[side, part, :], wide_query[side]) + mask[part, :]
            probs = jnp.exp(scores)
            outer = right_product(wide_value[side, part, :], wide_grad[...])
            grad_scores = (probs * outer).astype(BF16)
            grad_key[part, :] = dot(grad_scores, wide_query[side])
            grad_value[part, :] = dot(probs.astype(BF16), wide_grad[...])
            grad_query[...] += left_product(grad_scores, wide_key[side, part, :])
        from_query = grad_query[...]
        from_key = grad_key[...]
        change = pick_lane(from_query, lanes, head + 1) - pick_lane(from_key, lanes, head + 4)
        grad_prefix[...] += jnp.where(lanes == (LANES // head) * step + side, change, 0.0)

        raw = query[:, here]
        scale_raw = rms_scale(raw)
        grad_normed = from_query[:, 0:head] * SCALE
        grad_raw_query = norm_back(grad_normed, raw, scale_raw, gains[0:1, here])
        small[0:1, here] += jnp.sum(grad_normed * raw * scale_raw, axis=0, keepdims=True)
        raw = key[:, here]
        scale_raw = rms_scale(raw)
        grad_normed = from_key[:, 0:head]
        grad_raw_key = norm_back(grad_normed, raw, scale_raw, gains[1:2, here])
        small[1:2, here] += jnp.sum(grad_normed * raw * scale_raw, axis=0, keepdims=True)
        wide_grad[:, here] = grad_gate
        for part_id, piece in enumerate(
            (grad_raw_query.astype(BF16), grad_raw_key.astype(BF16), grad_value[:, 0:head].astype(BF16), grad_gate)
        ):
            if side == 0:
                grad_project[:, column(part_id)] = jnp.concatenate([piece, piece], axis=1)
            else:
                keep = grad_project[:, column(part_id)]
                both = jnp.concatenate([piece, piece], axis=1)
                grad_project[:, column(part_id)] = jnp.where(lanes < head, keep, both)

    @pl.when(step == steps - 1)
    def _():
        high, middle, low = split_three(grad_prefix[...])
        short = lane_ids(chunk)

        @pl.loop(0, rows // chunk)
        def _(turn):
            part = pl.ds(pl.multiple_of(turn * chunk, chunk), chunk)
            after = jnp.where(pos_row[0:1, :] >= pos_col[part, :], 1.0, 0.0).astype(BF16)
            total = dot(after, high.astype(BF16)) + dot(after, middle.astype(BF16)) + dot(after, low.astype(BF16))
            grad_logit = total * jax.nn.sigmoid(-(forget[part, :] + bias[0:1, :]))
            grad_logit = jnp.where(short < heads, grad_logit, 0.0).astype(BF16)
            grad_project[part, 4 * width : 4 * width + LANES] = grad_logit
            small[2:3, :] += jnp.sum(grad_logit.astype(F32), axis=0, keepdims=True)

        if ranks:
            for copy in aside_copies():
                copy.wait()


def pick_chunk(rows):
    return 256 if rows % 256 == 0 else 128


def whole(shape):
    return pl.BlockSpec(shape, lambda step: tuple(0 for _ in shape))


def attend(project, places, bias, gains, head, width, heads):
    rows = project.shape[0]
    steps = width // LANES
    per = LANES // head
    chunk = pick_chunk(rows)

    def part(index):
        return pl.BlockSpec((rows, LANES), lambda step: (0, index * steps + step))

    own = pl.BlockSpec((rows, LANES), lambda step: (0, step))
    wide = pl.BlockSpec((per, rows, LANES), lambda step: (step, 0, 0))
    forget = pl.BlockSpec((rows, LANES), lambda step: (0, 4 * steps))
    wide_shape = jax.ShapeDtypeStruct((per * steps, rows, LANES), BF16)
    return pl.pallas_call(
        functools.partial(attend_kernel, head, chunk, heads),
        grid=(steps,),
        in_specs=[whole(p.shape) for p in places] + [whole(bias.shape), whole(gains.shape)]
        + [part(0), part(1), part(2), part(3), forget],
        out_specs=[own, own, wide, wide, wide],
        out_shape=[
            jax.ShapeDtypeStruct((rows, width), BF16),
            jax.ShapeDtypeStruct((rows, width), F32),
            wide_shape, wide_shape, wide_shape,
        ],
        scratch_shapes=[pltpu.VMEM((rows, rows), F32), pltpu.VMEM((rows, LANES), F32)],
        compiler_params=pltpu.CompilerParams(vmem_limit_bytes=VMEM_LIMIT),
        name="attend",
    )(*places, bias, gains, project, project, project, project, project)


def attend_back(project, places, bias, gains, attended, wides, grad_gated, aside, ranks, head, width, heads):
    rows = project.shape[0]
    steps = width // LANES
    per = LANES // head
    chunk = pick_chunk(rows)

    def part(index):
        return pl.BlockSpec((rows, LANES), lambda step: (0, index * steps + step))

    own = pl.BlockSpec((rows, LANES), lambda step: (0, step))
    wide = pl.BlockSpec((per, rows, LANES), lambda step: (step, 0, 0))
    forget = pl.BlockSpec((rows, LANES), lambda step: (0, 4 * steps))
    total = 4 * width + LANES
    return pl.pallas_call(
        functools.partial(attend_back_kernel, head, chunk, width, heads, ranks),
        grid=(steps,),
        in_specs=[whole(p.shape) for p in places] + [whole(bias.shape), whole(gains.shape)]
        + [part(0), part(1), part(3), forget, own, wide, wide, wide, own, ANY],
        out_specs=[whole((rows, total)), whole((8, LANES)), ANY],
        out_shape=[
            jax.ShapeDtypeStruct((rows, total), BF16),
            jax.ShapeDtypeStruct((8, LANES), F32),
            jax.ShapeDtypeStruct((max(ranks, 1), aside.shape[0] // max(ranks, 1), aside.shape[1]), BF16),
        ],
        scratch_shapes=[
            pltpu.VMEM((rows, rows), F32),
            pltpu.VMEM((rows, LANES), BF16),
            pltpu.VMEM((rows, LANES), F32),
            pltpu.VMEM((rows, LANES), F32),
            pltpu.VMEM((rows, LANES), F32),
            pltpu.VMEM((rows, LANES), F32),
        ]
        + (
            [pltpu.SemaphoreType.DMA((ranks - 1,)), pltpu.SemaphoreType.DMA((ranks - 1,)), pltpu.SemaphoreType.DMA]
            if ranks
            else []
        ),
        compiler_params=pltpu.CompilerParams(
            collective_id=5 if ranks else None, has_side_effects=ranks > 0, vmem_limit_bytes=VMEM_LIMIT
        ),
        name="attend_back",
    )(*places, bias, gains, project, project, project, project, attended, *wides, grad_gated, aside)


def greet(peers, line=None):
    barrier = pltpu.get_barrier_semaphore()
    if line is not None:
        peers = peers + [line.sibling]
    for peer in peers:
        pl.semaphore_signal(barrier, inc=1, device_id=peer, device_id_type=MESH)
    if line is not None:
        for there, peer in ((line.has_above, line.above), (line.has_below, line.below)):

            @pl.when(there)
            def _():
                pl.semaphore_signal(barrier, inc=1, device_id=peer, device_id_type=MESH)

    count = len(peers)
    if line is not None:
        last = line.layers - 1
        count = count + (1 - line.layer // last) + (line.layer + last) // line.layers
    pl.semaphore_wait(barrier, count)


class Line:
    def __init__(self, shards, source, target, sems):
        self.shard = lax.axis_index("fsdp")
        self.layers = shards // 2
        self.layer, self.core = self.shard // 2, self.shard % 2
        self.sibling = {"fsdp": self.shard ^ 1}
        self.above, self.below = {"fsdp": self.shard + 2}, {"fsdp": self.shard - 2}
        self.has_above, self.has_below = self.layer < self.layers - 1, self.layer > 0
        self.source, self.target = source, target
        self.rows = target.shape[0] // shards
        self.line_send, self.line_recv, self.side_send, self.side_recv, self.own_sem = sems

    def block(self, owner):
        return rows_of(self.target, owner, self.rows)

    def line(self, owner_layer, peer, way, own=False):
        here = self.block(owner_layer * 2 + self.core)
        return pltpu.make_async_remote_copy(
            self.source if own else here, here, self.line_send.at[way, owner_layer], self.line_recv.at[owner_layer],
            device_id=peer, device_id_type=MESH,
        )

    def side(self, owner_layer, owner_core, own=False):
        here = self.block(owner_layer * 2 + owner_core)
        return pltpu.make_async_remote_copy(
            self.source if own else here, here, self.side_send.at[owner_layer], self.side_recv.at[owner_layer],
            device_id=self.sibling, device_id_type=MESH,
        )

    def start(self):
        own = self.source is not None

        @pl.when(self.has_above)
        def _():
            self.line(self.layer, self.above, 0, own).start()

        @pl.when(self.has_below)
        def _():
            self.line(self.layer, self.below, 1, own).start()

        self.side(self.layer, self.core, own).start()
        if own:
            self.keep = pltpu.make_async_copy(self.source, self.block(self.shard), self.own_sem)
            self.keep.start()

    def step(self, distance):
        lower, upper = self.layer - distance, self.layer + distance

        @pl.when(lower >= 0)
        def _():
            self.line(lower, self.below, 1).wait_recv()

            @pl.when(self.has_above)
            def _():
                self.line(lower, self.above, 0).start()

            self.side(lower, self.core).start()

        @pl.when(upper < self.layers)
        def _():
            self.line(upper, self.above, 0).wait_recv()

            @pl.when(self.has_below)
            def _():
                self.line(upper, self.below, 1).start()

            self.side(upper, self.core).start()

    def finish(self):
        if self.source is not None:
            self.keep.wait()
        for owner_layer in range(self.layers):
            self.side(owner_layer, 1 - self.core).wait_recv()
            self.side(owner_layer, self.core).wait_send()

            @pl.when(self.has_above & (owner_layer <= self.layer))
            def _():
                self.line(owner_layer, self.above, 0).wait_send()

            @pl.when(self.has_below & (owner_layer >= self.layer))
            def _():
                self.line(owner_layer, self.below, 1).wait_send()


def line_scratch(shards):
    layers = shards // 2
    return [
        pltpu.SemaphoreType.DMA((2, layers)),
        pltpu.SemaphoreType.DMA((layers,)),
        pltpu.SemaphoreType.DMA((layers,)),
        pltpu.SemaphoreType.DMA((layers,)),
        pltpu.SemaphoreType.DMA,
    ]


class Relay:
    def __init__(self, rank, source, place, send_sem, recv_sem, own_sem):
        self.rank, self.source, self.place = rank, source, place
        self.send_sem, self.recv_sem, self.own_sem = send_sem, recv_sem, own_sem
        self.copies = []

    def send(self, number, source, place, distance):
        copy = pltpu.make_async_remote_copy(
            source, place, self.send_sem.at[number], self.recv_sem.at[number],
            device_id={"ctx": self.rank ^ distance}, device_id_type=MESH,
        )
        copy.start()
        self.copies.append(copy)

    def start(self):
        me = self.rank
        self.send(0, self.source(0), self.place(me, 0), 1)
        self.send(1, self.source(1), self.place(me, 1), 2)
        self.send(2, self.source(1), self.place(me, 1), 1)
        self.send(3, self.source(0), self.place(me, 0), 2)
        self.own = [
            pltpu.make_async_copy(self.source(h), self.place(me, h), self.own_sem.at[h]) for h in range(2)
        ]
        for copy in self.own:
            copy.start()

    def forward(self):
        near, below = self.rank ^ 1, self.rank ^ 2
        self.copies[0].wait_recv()
        self.send(4, self.place(near, 0), self.place(near, 0), 2)
        self.copies[1].wait_recv()
        self.send(5, self.place(below, 1), self.place(below, 1), 1)

    def finish(self):
        for copy in self.own:
            copy.wait()
        for number, copy in enumerate(self.copies):
            if number >= 2:
                copy.wait_recv()
        for copy in self.copies:
            copy.wait_send()


def rows_of(ref, index, size):
    return ref.at[pl.ds(pl.multiple_of(index * size, 16), size), :]


def cols_of(ref, index, size):
    return ref.at[:, pl.ds(pl.multiple_of(index * size, LANES), size)]


def relay_ops(mode, rank, source, target, sems):
    rows, cols = source.shape
    half = rows // 2

    def part(h):
        return source.at[pl.ds(h * half, half), :]

    def place(block, h):
        if mode == "gather_rows":
            return target.at[pl.ds(pl.multiple_of(block * rows + h * half, 16), half), :]
        if mode == "gather_cols":
            return target.at[pl.ds(h * half, half), pl.ds(pl.multiple_of(block * cols, LANES), cols)]
        return target.at[block, pl.ds(h * half, half), :]

    return Relay(rank, part, place, *sems)


def exchange_kernel(modes, ranks, across, shards, *refs):
    count = len(modes)
    sources, targets = refs[:count], refs[count : 2 * count]
    send_sem, recv_sem, own_sem = refs[2 * count : 2 * count + 3]
    rank = lax.axis_index("ctx")
    shard = lax.axis_index("fsdp")
    line = None
    if "line" in modes:
        at = modes.index("line")
        line = Line(shards, sources[at], targets[at], refs[2 * count + 3 :])
    far = any(mode not in ("gather_rows", "gather_cols", "stack", "line") for mode in modes)
    peers = [{"ctx": rank ^ distance} for distance in range(1, ranks if far else ranks - 1)]
    if across:
        peers += [{"fsdp": shard ^ distance} for distance in range(1, across)]
    greet(peers, line)
    copies, relays = [], []
    for op, (mode, source, target) in enumerate(zip(modes, sources, targets)):
        if mode == "line":
            line.start()
            continue
        if mode in ("gather_rows", "gather_cols", "stack"):
            relay = relay_ops(mode, rank, source, target, (send_sem.at[op], recv_sem.at[op], own_sem.at[op]))
            relay.start()
            relays.append(relay)
            continue
        axis, me, members = ("fsdp", shard, across) if mode == "shards" else ("ctx", rank, ranks)
        for distance in range(members):
            other = me ^ distance if distance else me
            place = target.at[me]
            if mode == "scatter_rows":
                piece = rows_of(source, other, target.shape[1])
            elif mode == "scatter_cols":
                piece = cols_of(source, other, target.shape[2])
            elif mode == "shards":
                piece = source.at[other]
            else:
                piece = source
            if distance == 0:
                copy = pltpu.make_async_copy(piece, place, own_sem.at[op, 0])
            else:
                copy = pltpu.make_async_remote_copy(
                    piece, place, send_sem.at[op, distance - 1], recv_sem.at[op, distance - 1],
                    device_id={axis: other}, device_id_type=MESH,
                )
            copy.start()
            copies.append(copy)
    for index in range(max(len(relays), shards // 2 - 1 if line is not None else 0)):
        if line is not None and 0 < index < shards // 2:
            line.step(index)
        if index < len(relays):
            relays[index].forward()
    if line is not None:
        line.step(shards // 2 - 1)
        line.finish()
    for relay in relays:
        relay.finish()
    for copy in copies:
        copy.wait()


def exchange(collective_id, ranks, across, shards, *ops):
    shapes = []
    for mode, source in ops:
        shape = source.shape
        if mode == "gather_rows":
            shape = (ranks * shape[0], shape[1])
        elif mode == "gather_cols":
            shape = (shape[0], ranks * shape[1])
        elif mode == "scatter_rows":
            shape = (ranks, shape[0] // ranks, shape[1])
        elif mode == "scatter_cols":
            shape = (ranks, shape[0], shape[1] // ranks)
        elif mode in ("stack", "each"):
            shape = (ranks,) + shape
        elif mode == "line":
            shape = (shards * shape[0], shape[1])
        shapes.append(jax.ShapeDtypeStruct(shape, source.dtype))
    count = len(ops)
    most = max(6, across - 1)
    moved = sum(s.size * s.dtype.itemsize for s in shapes)
    return pl.pallas_call(
        functools.partial(exchange_kernel, [mode for mode, _ in ops], ranks, across, shards),
        in_specs=[ANY] * count,
        out_specs=[ANY] * count,
        out_shape=shapes,
        scratch_shapes=[
            pltpu.SemaphoreType.DMA((count, most)),
            pltpu.SemaphoreType.DMA((count, most)),
            pltpu.SemaphoreType.DMA((count, 2)),
        ]
        + (line_scratch(shards) if any(mode == "line" for mode, _ in ops) else []),
        compiler_params=pltpu.CompilerParams(collective_id=collective_id, has_side_effects=True),
        cost_estimate=pl.CostEstimate(flops=0, bytes_accessed=moved * 20, transcendentals=0),
        name="exchange",
    )(*[source for _, source in ops])


def start_kernel(
    shards, width, piece,
    tokens, cotangent, weight, tail, other, inputs, grad_low, gathered, picked,
    weight_all, other_all, own_cols, own_pick,
    send_sem, recv_sem, own_sem, load_sem, *line_sems,
):
    rank = lax.axis_index("ctx")
    ranks = lax.axis_size("ctx")
    model = weight.shape[1] // 4
    loads = [
        pltpu.make_async_copy(weight, weight_all, load_sem.at[0]),
        pltpu.make_async_copy(other, other_all, load_sem.at[1]),
    ]
    for copy in loads:
        copy.start()
    line = Line(shards, own_cols, gathered, line_sems)
    greet([{"ctx": rank ^ 1}, {"ctx": rank ^ 2}], line)
    first = relay_ops("gather_rows", rank, tokens, inputs, (send_sem.at[0], recv_sem.at[0], own_sem.at[0]))
    second = relay_ops("gather_rows", rank, cotangent, grad_low, (send_sem.at[1], recv_sem.at[1], own_sem.at[1]))
    loads[0].wait()
    for i in range(4):
        own_cols[:, i * width : (i + 1) * width] = weight_all[
            :, pl.ds(pl.multiple_of(i * model + rank * width, LANES), width)
        ]
    own_cols[:, 4 * width : 4 * width + LANES] = tail[...]
    line.start()
    first.start()
    loads[1].wait()
    for i in range(picked.shape[1] // piece):
        own_pick[:, i * piece : (i + 1) * piece] = other_all[
            :, pl.ds(pl.multiple_of((i * ranks + rank) * piece, LANES), piece)
        ]
    keep = pltpu.make_async_copy(own_pick, picked, load_sem.at[2])
    keep.start()
    first.forward()
    second.start()
    for distance in range(1, line.layers):
        line.step(distance)
        if distance == 1:
            second.forward()
    first.finish()
    second.finish()
    line.finish()
    keep.wait()


def start_moves(collective_id, ranks, shards, width, piece, tokens, cotangent, weight, tail, other):
    rows, model = tokens.shape
    return pl.pallas_call(
        functools.partial(start_kernel, shards, width, piece),
        in_specs=[ANY] * 3 + [pl.BlockSpec(memory_space=pltpu.VMEM), ANY],
        out_specs=[ANY] * 4,
        out_shape=[
            jax.ShapeDtypeStruct((ranks * rows, model), BF16),
            jax.ShapeDtypeStruct((ranks * rows, model), BF16),
            jax.ShapeDtypeStruct((shards * weight.shape[0], 4 * width + LANES), BF16),
            jax.ShapeDtypeStruct((other.shape[0], other.shape[1] // ranks), BF16),
        ],
        scratch_shapes=[
            pltpu.VMEM(weight.shape, BF16),
            pltpu.VMEM(other.shape, BF16),
            pltpu.VMEM((weight.shape[0], 4 * width + LANES), BF16),
            pltpu.VMEM((other.shape[0], other.shape[1] // ranks), BF16),
            pltpu.SemaphoreType.DMA((2, 6)),
            pltpu.SemaphoreType.DMA((2, 6)),
            pltpu.SemaphoreType.DMA((2, 2)),
            pltpu.SemaphoreType.DMA((3,)),
        ]
        + line_scratch(shards),
        compiler_params=pltpu.CompilerParams(
            collective_id=collective_id, has_side_effects=True, vmem_limit_bytes=VMEM_LIMIT
        ),
        cost_estimate=pl.CostEstimate(flops=0, bytes_accessed=150 << 20, transcendentals=0),
        name="start_moves",
    )(tokens, cotangent, weight, tail, other)


VMEM_WHOLE = pl.BlockSpec(memory_space=pltpu.VMEM)


def to_rank(source, target, send, recv, other):
    return pltpu.make_async_remote_copy(
        source, target, send, recv, device_id={"ctx": other}, device_id_type=MESH
    )


def middle_kernel(
    ranks,
    grad_gate_up, w_gate_up, mixed, cotangent, w_out, gain, mixed_grad, gated_grad, gain_grad,
    grad_in, weight_in, mixed_in, cotangent_in, out_in, wide, first_out, first_in, second_out, second_in,
    load_sem, first_send, first_recv, second_send, second_recv,
):
    rank = lax.axis_index("ctx")
    rows = mixed.shape[0] // ranks
    model, width = w_out.shape
    tile = 256
    loads = [
        pltpu.make_async_copy(a, b, load_sem.at[n])
        for n, (a, b) in enumerate(
            (
                (w_gate_up, weight_in), (grad_gate_up, grad_in), (mixed, mixed_in), (cotangent, cotangent_in),
                (w_out, out_in),
            )
        )
    ]
    for copy in loads:
        copy.start()
    greet([{"ctx": rank ^ distance} for distance in range(1, ranks)])
    gain_grad[...] = jnp.zeros_like(gain_grad)
    for copy in loads:
        copy.wait()

    def part(turn):
        return pl.ds(pl.multiple_of(turn * rows, 16), rows)

    def send(out, into, send_sem, recv_sem, turn, distance):
        other = rank ^ distance
        return to_rank(
            out.at[other, part(turn), :], into.at[distance, part(turn), :],
            send_sem.at[distance - 1, turn], recv_sem.at[distance - 1, turn], other,
        )

    def arrived(out, into, send_sem, recv_sem, turn):
        total = out[rank, part(turn), :].astype(F32)
        for distance in range(1, ranks):
            send(out, into, send_sem, recv_sem, turn, distance).wait_recv()
            total = total + into[distance, part(turn), :].astype(F32)
        return total

    first = (first_out, first_in, first_send, first_recv)
    second = (second_out, second_in, second_send, second_recv)

    def project(turn):
        here = part(turn)
        total = cotangent_in[here, pl.ds(pl.multiple_of(rank * width, LANES), width)].astype(F32)
        total = total + arrived(*first, turn)
        mixed_grad[here, :] = total
        low = total.astype(BF16)
        for index in range(ranks):
            second_out[index, here, :] = right_product(low, out_in[index * width : (index + 1) * width, :]).astype(BF16)
        for distance in range(1, ranks):
            send(*second, turn, distance).start()

    @pl.loop(0, ranks)
    def _(turn):
        here = part(turn)

        @pl.loop(0, model // tile)
        def _(step):
            cols = pl.ds(pl.multiple_of(step * tile, tile), tile)
            wide[:, cols] = right_product(grad_in[here, :], weight_in[cols, :])

        values = mixed_in[here, :].astype(F32)
        scale = rms_scale(values)
        grad = wide[...]
        gain_grad[0:1, :] += jnp.sum(grad * values * scale, axis=0, keepdims=True)
        back = norm_back(grad, values, scale, gain[0:1, :]).astype(BF16)
        for index in range(ranks):
            first_out[index, here, :] = back[:, index * width : (index + 1) * width]
        for distance in range(1, ranks):
            send(*first, turn, distance).start()

        @pl.when(turn > 0)
        def _():
            project(turn - 1)

    project(ranks - 1)

    @pl.loop(0, ranks)
    def _(turn):
        gated_grad[part(turn), :] = arrived(*second, turn)

    @pl.loop(0, ranks)
    def _(turn):
        for distance in range(1, ranks):
            send(*first, turn, distance).wait_send()
            send(*second, turn, distance).wait_send()


def middle(collective_id, ranks, grad_gate_up, w_gate_up, mixed, cotangent, w_out, gain):
    rows, model = mixed.shape
    width = w_out.shape[1]
    blocks = pltpu.VMEM((ranks, rows, width), BF16)
    sems = pltpu.SemaphoreType.DMA((ranks - 1, ranks))
    return pl.pallas_call(
        functools.partial(middle_kernel, ranks),
        in_specs=[ANY] * 5 + [VMEM_WHOLE],
        out_specs=[VMEM_WHOLE] * 3,
        out_shape=[
            jax.ShapeDtypeStruct((rows, width), F32),
            jax.ShapeDtypeStruct((rows, width), F32),
            jax.ShapeDtypeStruct((8, model), F32),
        ],
        scratch_shapes=[
            pltpu.VMEM(grad_gate_up.shape, BF16),
            pltpu.VMEM(w_gate_up.shape, BF16),
            pltpu.VMEM(mixed.shape, BF16),
            pltpu.VMEM(cotangent.shape, BF16),
            pltpu.VMEM(w_out.shape, BF16),
            pltpu.VMEM((rows // ranks, model), F32),
            blocks, blocks, blocks, blocks,
            pltpu.SemaphoreType.DMA((5,)),
            sems, sems, sems, sems,
        ],
        compiler_params=pltpu.CompilerParams(
            collective_id=collective_id, has_side_effects=True, vmem_limit_bytes=VMEM_LIMIT
        ),
        cost_estimate=pl.CostEstimate(flops=0, bytes_accessed=150 << 20, transcendentals=0),
        name="middle",
    )(grad_gate_up, w_gate_up, mixed, cotangent, w_out, gain)


def last_kernel(
    ranks,
    grad_project, w_in, inputs, mixed_grad, gain, sums, tokens_grad, total_sums,
    grad_in, weight_in, inputs_in, wide, out, into, sums_out, sums_in,
    load_sem, send_sem, recv_sem, sums_send, sums_recv,
):
    rank = lax.axis_index("ctx")
    rows = inputs.shape[0] // ranks
    model, width = inputs.shape[1], mixed_grad.shape[1]
    tile = 256
    loads = [
        pltpu.make_async_copy(a, b, load_sem.at[n])
        for n, (a, b) in enumerate(((w_in, weight_in), (grad_project, grad_in), (inputs, inputs_in)))
    ]
    for copy in loads:
        copy.start()
    greet([{"ctx": rank ^ distance} for distance in range(1, ranks)])
    sums_out[...] = sums[...]
    for copy in loads:
        copy.wait()

    def send(distance):
        other = rank ^ distance
        return to_rank(out.at[other], into.at[distance], send_sem.at[distance - 1], recv_sem.at[distance - 1], other)

    def send_sums(distance):
        return to_rank(
            sums_out, sums_in.at[distance], sums_send.at[distance - 1], sums_recv.at[distance - 1], rank ^ distance
        )

    def compute(other):
        here = pl.ds(pl.multiple_of(other * rows, 16), rows)

        @pl.loop(0, model // tile)
        def _(step):
            cols = pl.ds(pl.multiple_of(step * tile, tile), tile)
            wide[:, cols] = right_product(grad_in[here, :], weight_in[cols, :])

        values = inputs_in[here, :].astype(F32)
        scale = rms_scale(values)
        grad = wide[...]
        sums_out[0:1, :] += jnp.sum(grad * values * scale, axis=0, keepdims=True)
        wide[...] = norm_back(grad, values, scale, gain[0:1, :])
        own = pl.ds(pl.multiple_of(rank * width, LANES), width)
        wide[:, own] += mixed_grad[here, :]
        out[other] = wide[...].astype(BF16)

    @pl.loop(1, ranks)
    def _(distance):
        compute(rank ^ distance)
        send(distance).start()

    compute(rank)
    for distance in range(1, ranks):
        send_sums(distance).start()
    total = out[rank].astype(F32)
    for distance in range(1, ranks):
        send(distance).wait_recv()
        total = total + into[distance].astype(F32)
    tokens_grad[...] = total.astype(BF16)
    total = sums_out[...]
    for distance in range(1, ranks):
        send_sums(distance).wait_recv()
        total = total + sums_in[distance]
    total_sums[...] = total
    for distance in range(1, ranks):
        send(distance).wait_send()
        send_sums(distance).wait_send()


def last_moves(collective_id, ranks, grad_project, w_in, inputs, mixed_grad, gain, sums):
    rows, model = inputs.shape
    blocks = pltpu.VMEM((ranks, rows // ranks, model), BF16)
    sems = pltpu.SemaphoreType.DMA((ranks - 1,))
    return pl.pallas_call(
        functools.partial(last_kernel, ranks),
        in_specs=[ANY] * 3 + [VMEM_WHOLE] * 3,
        out_specs=[VMEM_WHOLE] * 2,
        out_shape=[
            jax.ShapeDtypeStruct((rows // ranks, model), BF16),
            jax.ShapeDtypeStruct((8, model), F32),
        ],
        scratch_shapes=[
            pltpu.VMEM(grad_project.shape, BF16),
            pltpu.VMEM(w_in.shape, BF16),
            pltpu.VMEM(inputs.shape, BF16),
            pltpu.VMEM((rows // ranks, model), F32),
            blocks, blocks,
            pltpu.VMEM((8, model), F32),
            pltpu.VMEM((ranks, 8, model), F32),
            pltpu.SemaphoreType.DMA((3,)),
            sems, sems, sems, sems,
        ],
        compiler_params=pltpu.CompilerParams(
            collective_id=collective_id, has_side_effects=True, vmem_limit_bytes=VMEM_LIMIT
        ),
        cost_estimate=pl.CostEstimate(flops=0, bytes_accessed=150 << 20, transcendentals=0),
        name="last_moves",
    )(grad_project, w_in, inputs, mixed_grad, gain, sums)


def spread_kernel(pieces, *refs):
    source, targets = refs[0], refs[1:]
    ranks = source.shape[0]
    for target, (piece, first, count) in zip(targets, pieces):
        for block in range(count):
            for index in range(ranks):
                target[:, pl.ds((block * ranks + index) * piece, piece)] = source[
                    index, :, pl.ds(first + block * piece, piece)
                ].astype(F32)


def spread_cols(source, *pieces):
    ranks, rows, cols = source.shape
    if any(piece % LANES or first % LANES for piece, first, _ in pieces):
        return [
            jnp.concatenate(
                [
                    source[c, :, first + i * piece : first + (i + 1) * piece]
                    for i in range(count)
                    for c in range(ranks)
                ],
                axis=1,
            ).astype(F32)
            for piece, first, count in pieces
        ]
    part = rows // 4 if rows % 64 == 0 else rows
    widths = [count * ranks * piece for piece, _, count in pieces]
    return pl.pallas_call(
        functools.partial(spread_kernel, pieces),
        grid=(rows // part,),
        in_specs=[pl.BlockSpec((ranks, part, cols), lambda step: (0, step, 0))],
        out_specs=[pl.BlockSpec((part, w), lambda step: (step, 0)) for w in widths],
        out_shape=[jax.ShapeDtypeStruct((rows, w), F32) for w in widths],
        compiler_params=pltpu.CompilerParams(vmem_limit_bytes=VMEM_LIMIT),
        cost_estimate=pl.CostEstimate(flops=0, bytes_accessed=rows * sum(widths) * 6, transcendentals=0),
        name="spread_cols",
    )(source)


class Native:
    def __init__(self, ranks):
        self.ranks = ranks

    def begin(self, number, tokens, cotangent, weight, tail, other, piece, width, padded):
        rank, model = lax.axis_index("ctx"), tokens.shape[1]
        parts = [lax.dynamic_slice_in_dim(weight, i * model + rank * width, width, 1) for i in range(4)]
        parts = [jnp.pad(part, ((0, 0), (0, padded - width))) for part in parts]
        cols = other.shape[1] // self.ranks
        picks = [
            lax.dynamic_slice_in_dim(other, (i * self.ranks + rank) * piece, piece, 1) for i in range(cols // piece)
        ]
        return (
            lax.all_gather(tokens, "ctx", axis=0, tiled=True),
            lax.all_gather(cotangent, "ctx", axis=0, tiled=True),
            lax.all_gather(jnp.concatenate(parts + [tail], axis=1), "fsdp", axis=0, tiled=True),
            jnp.concatenate(picks, axis=1),
        )

    def gather_cols(self, number, array, piece):
        return lax.all_gather(array, "ctx", axis=1, tiled=True), lax.all_gather(piece, "fsdp", axis=0, tiled=True)

    def stack(self, number, *arrays):
        return [lax.all_gather(a, "ctx", axis=0, tiled=False) for a in arrays]

    def finish(self, number, array, pieces):
        return lax.all_gather(array, "ctx", axis=0, tiled=False), lax.psum_scatter(
            pieces, "fsdp", scatter_dimension=0, tiled=False
        )


class Direct:
    def __init__(self, ranks, shards):
        self.ranks, self.shards = ranks, shards

    def run(self, number, *ops):
        return exchange(number, self.ranks, 0, self.shards, *ops)

    def begin(self, number, tokens, cotangent, weight, tail, other, piece, width, padded):
        return start_moves(
            number, self.ranks, self.shards, width, piece, tokens, cotangent, weight, tail, other
        )

    def gather_cols(self, number, array, piece):
        return self.run(number, ("gather_cols", array), ("line", piece))

    def stack(self, number, *arrays):
        return self.run(number, *[("stack" if a.dtype == BF16 else "each", a) for a in arrays])

    def finish(self, number, array, pieces):
        out = exchange(number, self.ranks, self.shards, self.shards, ("stack", array), ("shards", pieces))
        return out[0], out[1].sum(axis=0)


def body(
    tokens, block_order, segment_ids, norm_gains, attn_in_weight, forget_weight, forget_bias,
    qk_gains, out_weight, gate_up_weight, down_weight, out_grad,
):
    ranks = lax.axis_size("ctx")
    shards = lax.axis_size("fsdp")
    rank = lax.axis_index("ctx")
    row_count, model_width = tokens.shape[1], tokens.shape[2]
    head_count, head_dim = forget_bias.shape[0], qk_gains.shape[1]
    local_heads = head_count // ranks
    width = local_heads * head_dim
    padded = -(-width // LANES) * LANES
    seq_order = block_order[0]
    seq_len = segment_ids.shape[1]
    block_len = seq_len // seq_order.shape[0]
    hidden_piece = down_weight.shape[0] // ranks
    hidden = hidden_piece * shards
    plain = ranks == 4 and shards & (shards - 1) == 0 and width == padded
    comm = Direct(ranks, shards) if plain else Native(ranks)

    def slab(array, start, size, axis):
        return lax.dynamic_slice_in_dim(array, start, size, axis)

    def widen(array):
        return jnp.pad(array, ((0, 0), (0, padded - width))) if padded > width else array

    tail = jnp.concatenate(
        [
            slab(forget_weight, rank * local_heads, local_heads, 1),
            norm_gains.T,
            jnp.zeros((attn_in_weight.shape[0], LANES - local_heads - 2), BF16),
        ],
        axis=1,
    )
    inputs, grad_low, w_in, gate_up_piece = comm.begin(
        0, tokens[0], out_grad[0], attn_in_weight, tail, gate_up_weight, hidden_piece, width, padded
    )
    w_gate_up = lax.all_gather(gate_up_piece, "fsdp", axis=0, tiled=True)

    offsets = jnp.arange(seq_len, dtype=jnp.int32)
    blocks = jnp.arange(seq_order.shape[0], dtype=jnp.int32)
    places = (seq_order[:, None] * block_len + offsets[None, :block_len]).reshape(-1)
    by_block = segment_ids[0].reshape(-1, block_len)
    chosen = seq_order[:, None, None] == blocks[None, :, None]
    segments = jnp.sum(jnp.where(chosen, by_block[None], 0), axis=1).reshape(-1)
    places_all = (places[None, :], places[:, None], segments[None, :], segments[:, None])
    valid = (segments >= 0).astype(F32)

    bias = jnp.pad(slab(forget_bias, rank * local_heads, local_heads, 0), (0, LANES - local_heads))[None]
    head_gains = jnp.tile(qk_gains, (1, LANES // head_dim))

    gain_cols = lax.optimization_barrier(w_in[:, 4 * padded : 4 * padded + LANES]).astype(F32).T
    gain_one = gain_cols[local_heads]
    gain_two = gain_cols[local_heads + 1]

    wide_inputs = inputs.astype(F32)
    scale_one = rms_scale(wide_inputs)
    normed = (wide_inputs * scale_one * gain_one).astype(BF16)
    project = dot(normed, w_in)
    gated, attended, wide_query, wide_key, wide_value = attend(
        project, places_all, bias, head_gains, head_dim, padded, local_heads
    )
    gated_all, w_out = comm.gather_cols(1, gated[:, :width], slab(out_weight, rank * width, width, 1))
    mixed_cols = slab(inputs, rank * width, width, 1).astype(F32) + dot(gated_all, w_out)
    mixed_low, w_down = comm.gather_cols(
        2, mixed_cols.astype(BF16), slab(down_weight, rank * hidden_piece, hidden_piece, 0)
    )
    mixed = mixed_low.astype(F32)
    scale_two = rms_scale(mixed)
    normed_two = (mixed * scale_two * gain_two).astype(BF16)
    gate_up = dot(normed_two, w_gate_up)
    gate_part, up_part = gate_up[:, :hidden], gate_up[:, hidden:]
    gate_sigmoid = jax.nn.sigmoid(gate_part)
    silu = gate_part * gate_sigmoid
    hidden_act = (silu * up_part).astype(BF16)
    down_part = dot(hidden_act, w_down).astype(BF16)

    def own_rows(array):
        return slab(array, rank * row_count, row_count, 0)

    grad_hidden = right_product(grad_low, w_down)
    grad_gate = grad_hidden * up_part * gate_sigmoid * (1.0 + gate_part * (1.0 - gate_sigmoid))
    grad_gate_up = jnp.concatenate([grad_gate, grad_hidden * silu], axis=1).astype(BF16)

    def reduce_shards(array):
        return lax.psum_scatter(array.astype(BF16), "fsdp", scatter_dimension=0, tiled=True)

    down_part_grad = left_product(hidden_act, grad_low).astype(BF16)
    gate_up_grad = left_product(normed_two, grad_gate_up).astype(BF16)
    grad_gate_up, down_part_grad, gate_up_grad = lax.optimization_barrier(
        (grad_gate_up, down_part_grad, gate_up_grad)
    )
    down_share = reduce_shards(down_part_grad)
    gate_up_share = reduce_shards(gate_up_grad)
    if plain:
        grad_mixed_cols, grad_gated, gain_two_grad = middle(
            3, ranks, grad_gate_up, w_gate_up, mixed_low, grad_low, w_out, gain_two[None]
        )
        gain_two_grad = gain_two_grad[0]
        grad_branch = grad_mixed_cols.astype(BF16)
    else:
        grad_normed_two = right_product(grad_gate_up, w_gate_up)
        gain_two_grad = jnp.sum(grad_normed_two * mixed * scale_two, axis=0)
        grad_mixed_part = norm_back(grad_normed_two, mixed, scale_two, gain_two).astype(BF16)
        grad_mixed_cols = slab(grad_low, rank * width, width, 1).astype(F32) + lax.psum_scatter(
            grad_mixed_part, "ctx", scatter_dimension=1, tiled=True
        ).astype(F32)
        grad_branch = grad_mixed_cols.astype(BF16)
        grad_gated = widen(
            lax.psum_scatter(
                right_product(grad_branch, w_out).astype(BF16), "ctx", scatter_dimension=1, tiled=True
            ).astype(F32)
        )
    grad_gated, down_share = lax.optimization_barrier((grad_gated, down_share))
    grad_project, small, down_pieces = attend_back(
        project, places_all, bias, head_gains, attended, (wide_query, wide_key, wide_value),
        grad_gated, down_part, ranks if plain else 0, head_dim, padded, local_heads,
    )

    in_part = left_product(normed, grad_project).astype(BF16)
    out_part = left_product(gated_all, grad_branch).astype(BF16)
    late = jnp.concatenate([in_part[:, : 4 * padded], out_part, in_part[:, 4 * padded :]], axis=1)
    late, gate_up_share = lax.optimization_barrier((late, gate_up_share))
    late_share = reduce_shards(late)

    bias_slots = jnp.where(
        jnp.arange(ranks, dtype=jnp.int32)[:, None] == rank, small[2, :local_heads][None], 0.0
    ).reshape(-1)
    qk_sum = small[0:2].reshape(2, LANES // head_dim, head_dim).sum(axis=1).reshape(-1)
    others = jnp.concatenate([bias_slots, qk_sum])
    others = jnp.pad(others, (0, model_width - others.shape[0]))
    if plain:
        down_sum = down_pieces.astype(F32).sum(axis=0)
        sums = jnp.stack([jnp.zeros_like(others), gain_two_grad, others] + [jnp.zeros_like(others)] * 5)
        tokens_grad, sums = last_moves(4, ranks, grad_project, w_in, inputs, grad_mixed_cols, gain_one[None], sums)
        tokens_grad = tokens_grad[None]
    else:
        grad_normed = right_product(grad_project, w_in)
        gain_one_grad = jnp.sum(grad_normed * wide_inputs * scale_one, axis=0)
        in_own = jnp.arange(model_width, dtype=jnp.int32) // width == rank
        grad_inputs = norm_back(grad_normed, wide_inputs, scale_one, gain_one) + jnp.where(
            in_own[None], jnp.tile(grad_mixed_cols, (1, ranks)), 0.0
        )
        down_sum = lax.psum_scatter(down_part, "ctx", scatter_dimension=0, tiled=True).astype(F32)
        tokens_grad = lax.psum_scatter(grad_inputs.astype(BF16), "ctx", scatter_dimension=0, tiled=True)[None]
        sums = lax.psum(jnp.stack([gain_one_grad, gain_two_grad, others]), "ctx")
    result = own_rows(mixed_low).astype(F32) + down_sum
    block_out = result.astype(BF16)[None]
    branch = result - own_rows(inputs).astype(F32)
    own_valid = own_rows(valid)
    partial_sums = jnp.stack(
        [
            jnp.sum(own_valid * jnp.sum(result * result, axis=-1)),
            jnp.sum(own_valid * jnp.sum(branch * branch, axis=-1)),
        ]
    )
    valid_count = jnp.sum(valid) * model_width

    down_own, gate_up_own, stats = comm.stack(
        6, down_share, gate_up_share, jnp.broadcast_to(jnp.pad(partial_sums, (0, LANES - 2)), (8, LANES))
    )
    down_out = down_own.astype(F32).reshape(down_weight.shape)
    gate_up_out = spread_cols(gate_up_own, (hidden_piece, 0, 2 * shards))[0]
    share = model_width // shards
    room = -(-share // LANES) * LANES
    gain_pieces = jnp.pad(sums[0:2].reshape(2, shards, share).transpose(1, 0, 2), ((0, 0), (0, 0), (0, room - share)))
    tail = sums[2, : 2 * room].reshape(1, 2, room)
    pieces = jnp.concatenate(
        [gain_pieces, jnp.broadcast_to(tail, (shards, 2, room)), jnp.zeros((shards, 4, room), F32)], axis=1
    )
    late_own, piece_sum = comm.finish(7, late_share, pieces)
    if plain:
        in_out, out_out = spread_cols(late_own, (width, 0, 4), (width, 4 * width, 1))
    else:
        in_out = jnp.concatenate(
            [late_own[c, :, i * padded : i * padded + width] for i in range(4) for c in range(ranks)], axis=1
        ).astype(F32)
        out_out = jnp.concatenate(
            [late_own[c, :, 4 * padded : 4 * padded + width] for c in range(ranks)], axis=1
        ).astype(F32)
    last = 4 * padded + width
    forget_out = jnp.concatenate([late_own[c, :, last : last + local_heads] for c in range(ranks)], axis=1).astype(F32)
    gains_sum = piece_sum[0:2, :share]
    tail_sum = piece_sum[2:4].reshape(-1)
    bias_sum = tail_sum[:head_count]
    qk_sum = tail_sum[head_count : head_count + 2 * head_dim].reshape(2, head_dim)
    totals = stats[:, 0, :2].sum(axis=0)
    return (
        block_out, tokens_grad, gains_sum, in_out, forget_out, bias_sum, qk_sum,
        out_out, gate_up_out, down_out, jnp.sqrt(totals / valid_count)[None],
    )


def solution(mesh):
    rows = P("fsdp", "ctx", None)
    return jax.shard_map(
        body,
        mesh=mesh,
        in_specs=(
            rows, P("fsdp", None), P("fsdp", None), P(None, "fsdp"), P("fsdp", None), P("fsdp", None),
            P(), P(), P("fsdp", None), P("fsdp", None), P("fsdp", None), rows,
        ),
        out_specs=(
            rows, rows, P(None, "fsdp"), P("fsdp", None), P("fsdp", None), P(), P(),
            P("fsdp", None), P("fsdp", None), P("fsdp", None), P("fsdp", None),
        ),
        check_vma=False,
    )
```

```python
import functools

import jax
import jax.numpy as jnp
from jax import lax
from jax.experimental import pallas as pl
from jax.experimental.pallas import tpu as pltpu
from jax.sharding import PartitionSpec as P

EPS = 1e-06
SCALE = 0.125
LANES = 128
VMEM_LIMIT = 60 << 20
F32 = jnp.float32
BF16 = jnp.bfloat16


MESH = pl.DeviceIdType.MESH
ANY = pl.BlockSpec(memory_space=pltpu.HBM)


def rms_scale(values):
    return lax.rsqrt(jnp.mean(values * values, axis=-1, keepdims=True) + EPS)


def norm_back(grad_normed, values, scale_values, gain_values):
    scaled = grad_normed * gain_values
    cubed = scale_values * scale_values * scale_values
    return scale_values * scaled - values * cubed * jnp.mean(
        scaled * values, axis=-1, keepdims=True
    )


def dot(left, right):
    return lax.dot_general(
        left, right, (((1,), (0,)), ((), ())), preferred_element_type=F32
    )


def left_product(left, right):
    return lax.dot_general(
        left, right, (((0,), (0,)), ((), ())), preferred_element_type=F32
    )


def right_product(left, right):
    return lax.dot_general(
        left, right, (((1,), (1,)), ((), ())), preferred_element_type=F32
    )


def split_three(values):
    high = values.astype(BF16).astype(F32)
    rest = values - high
    middle = rest.astype(BF16).astype(F32)
    return high, middle, rest - middle


def lane_ids(rows, lanes=LANES):
    return lax.broadcasted_iota(jnp.int32, (rows, lanes), 1)


def pick_lane(values, lanes, index):
    return jnp.sum(jnp.where(lanes == index, values, 0.0), axis=-1, keepdims=True)


def turns(rows, chunk, unroll=False):
    def decorate(body):
        @pl.loop(0, rows // chunk, unroll=rows // chunk if unroll else None)
        def _(turn):
            body(pl.ds(pl.multiple_of(turn * chunk, chunk), chunk))

    return decorate


def fill_mask(chunk, pos_row, pos_col, seg_row, seg_col, mask):
    @turns(mask.shape[0], chunk)
    def _(part):
        allowed = (pos_row[0:1, :] <= pos_col[part, :]) & (seg_row[0:1, :] == seg_col[part, :])
        mask[part, :] = jnp.where(allowed, 0.0, -jnp.inf)


def fill_prefix(chunk, heads, pos_row, pos_col, logits, prefix):
    rows = prefix.shape[0]
    log_forget = jax.nn.log_sigmoid(jnp.where(lane_ids(rows) < heads, logits, 0.0))
    high, middle, low = split_three(log_forget)

    @turns(rows, chunk)
    def _(part):
        before = jnp.where(pos_row[0:1, :] <= pos_col[part, :], 1.0, 0.0).astype(BF16)
        prefix[part, :] = (
            dot(before, high.astype(BF16)) + dot(before, middle.astype(BF16)) + dot(before, low.astype(BF16))
        )


def attend_block(
    head, chunk, index, query, key, value, gate, gains, mask, prefix,
    gated, attended, wide_query, wide_key, wide_value,
):
    rows = mask.shape[0]
    lanes = lane_ids(rows)
    half = lane_ids(rows, head)
    short = lane_ids(chunk, head)
    for side in range(LANES // head):
        here = slice(side * head, (side + 1) * head)
        column = pick_lane(prefix[...], lanes, (LANES // head) * index + side)
        high, middle, low = split_three(column)
        wide = jnp.where(half == 1, high, 0.0)
        wide = jnp.where(half == 2, middle, wide)
        wide = jnp.where(half == 3, low, wide)
        query_rest = jnp.where((half >= 4) & (half < 7), 1.0, wide)
        wide = jnp.where(half == 4, -high, 0.0)
        wide = jnp.where(half == 5, -middle, wide)
        wide = jnp.where(half == 6, -low, wide)
        ones = ((half >= 1) & (half < 4)) | ((half >= 7) & (half < 10))
        key_rest = jnp.where(ones, 1.0, wide)
        raw = query[:, here]
        normed = (raw * rms_scale(raw) * gains[0:1, here]).astype(BF16)
        wide_query[side, :, 0:head] = (normed.astype(F32) * SCALE).astype(BF16)
        wide_query[side, :, head:LANES] = query_rest.astype(BF16)
        raw = key[:, here]
        wide_key[side, :, 0:head] = (raw * rms_scale(raw) * gains[1:2, here]).astype(BF16)
        wide_key[side, :, head:LANES] = key_rest.astype(BF16)
        wide_value[side, :, 0:head] = value[:, here].astype(BF16)
        wide_value[side, :, head:LANES] = jnp.where(half < 3, 1.0, 0.0).astype(BF16)

        @turns(rows, chunk, unroll=True)
        def _(part):
            scores = right_product(wide_query[side, part, :], wide_key[side]) + mask[part, :]
            expos = jnp.exp(scores)
            total = jnp.sum(expos, axis=-1, keepdims=True)
            result = dot(expos.astype(BF16), wide_value[side])[:, 0:head] / total
            attended[part, here] = result
            gated[part, here] = (result * jax.nn.sigmoid(gate(part)[:, here])).astype(BF16)
            high, middle, low = split_three(-jnp.log(total))
            rest = wide_query[side, part, head:LANES].astype(F32)
            rest = jnp.where(short == 7, high, rest)
            rest = jnp.where(short == 8, middle, rest)
            rest = jnp.where(short == 9, low, rest)
            wide_query[side, part, head:LANES] = rest.astype(BF16)


def attend_kernel(
    head, chunk, heads,
    pos_row, pos_col, seg_row, seg_col, bias, gains, query, key, value, gate, forget,
    gated, attended, wide_query, wide_key, wide_value,
    mask, prefix,
):
    @pl.when(pl.program_id(0) == 0)
    def _():
        fill_mask(chunk, pos_row, pos_col, seg_row, seg_col, mask)
        fill_prefix(chunk, heads, pos_row, pos_col, forget[...] + bias[0:1, :], prefix)

    attend_block(
        head, chunk, pl.program_id(0), query, key, value, lambda part: gate[part, :], gains, mask, prefix,
        gated, attended.at[0], wide_query, wide_key, wide_value,
    )


def attend_back_kernel(
    head, chunk, width, heads, ranks,
    pos_row, pos_col, seg_row, seg_col, bias, gains, query, key, gate, forget,
    attended, wide_query, wide_key, wide_value, grad_gated, *rest,
):
    if ranks:
        aside, normed, out_grad, grad_project, small, aside_in, late = rest[:7]
        mask, wide_grad, grad_query, grad_key, grad_value, grad_prefix = rest[7:13]
        normed_in, out_in, late_all, load_sem, save_sem = rest[13:18]
        sems = rest[18:]
    else:
        grad_project, small, mask, wide_grad, grad_query, grad_key, grad_value, grad_prefix = rest
    step = pl.program_id(0)
    steps = pl.num_programs(0)

    def aside_copies():
        send_sem, recv_sem, own_sem = sems
        rank = lax.axis_index("ctx")
        size = aside_in.shape[1]
        yield pltpu.make_async_copy(rows_of(aside, rank, size), aside_in.at[rank], own_sem)
        for distance in range(1, ranks):
            other = rank ^ distance
            yield to_rank(
                rows_of(aside, other, size), aside_in.at[rank],
                send_sem.at[distance - 1], recv_sem.at[distance - 1], other,
            )

    if ranks:

        @pl.when(step == 0)
        def _():
            rank = lax.axis_index("ctx")
            greet([{"ctx": rank ^ distance} for distance in range(1, ranks)])
            for copy in aside_copies():
                copy.start()
            pltpu.make_async_copy(normed, normed_in, load_sem.at[0]).start()
            pltpu.make_async_copy(out_grad, out_in, load_sem.at[1]).start()

    rows = query.shape[0]
    lanes = lane_ids(rows)
    half = lane_ids(rows, head)

    @pl.when(step == 0)
    def _():
        @pl.loop(0, rows // chunk)
        def _(turn):
            part = pl.ds(pl.multiple_of(turn * chunk, chunk), chunk)
            after = pos_row[0:1, :] >= pos_col[part, :]
            same = seg_row[0:1, :] == seg_col[part, :]
            mask[part, :] = jnp.where(after & same, 0.0, -jnp.inf)
        grad_prefix[...] = jnp.zeros_like(grad_prefix)
        small[...] = jnp.zeros_like(small)

    for side in range(LANES // head):
        here = pl.ds(side * head, head)

        def column(part):
            return pl.ds(pl.multiple_of(part * width + step * LANES, LANES), LANES)

        sig = jax.nn.sigmoid(gate[:, here])
        grad_in = grad_gated[:, here]
        result = attended[0, :, here]
        grad_result = (grad_in * sig).astype(BF16)
        grad_gate = (grad_in * result * sig * (1.0 - sig)).astype(BF16)
        inner = -jnp.sum(grad_result.astype(F32) * result, axis=-1, keepdims=True)
        high, middle, low = split_three(inner)
        rest = jnp.where(half == 0, high, 0.0)
        rest = jnp.where(half == 1, middle, rest)
        rest = jnp.where(half == 2, low, rest)
        wide_grad[:, 0:head] = grad_result
        wide_grad[:, head:LANES] = rest.astype(BF16)
        grad_query[...] = jnp.zeros_like(grad_query)
        @pl.loop(0, rows // chunk)
        def _(turn):
            part = pl.ds(pl.multiple_of(turn * chunk, chunk), chunk)
            scores = right_product(wide_key[side, part, :], wide_query[side]) + mask[part, :]
            probs = jnp.exp(scores)
            outer = right_product(wide_value[side, part, :], wide_grad[...])
            grad_scores = (probs * outer).astype(BF16)
            grad_key[part, :] = dot(grad_scores, wide_query[side])
            grad_value[part, :] = dot(probs.astype(BF16), wide_grad[...])
            grad_query[...] += left_product(grad_scores, wide_key[side, part, :])
        from_query = grad_query[...]
        from_key = grad_key[...]
        change = pick_lane(from_query, lanes, head + 1) - pick_lane(from_key, lanes, head + 4)
        grad_prefix[...] += jnp.where(lanes == (LANES // head) * step + side, change, 0.0)

        raw = query[:, here]
        scale_raw = rms_scale(raw)
        grad_normed = from_query[:, 0:head] * SCALE
        grad_raw_query = norm_back(grad_normed, raw, scale_raw, gains[0:1, here])
        small[0:1, here] += jnp.sum(grad_normed * raw * scale_raw, axis=0, keepdims=True)
        raw = key[:, here]
        scale_raw = rms_scale(raw)
        grad_normed = from_key[:, 0:head]
        grad_raw_key = norm_back(grad_normed, raw, scale_raw, gains[1:2, here])
        small[1:2, here] += jnp.sum(grad_normed * raw * scale_raw, axis=0, keepdims=True)
        wide_grad[:, here] = grad_gate
        for part_id, piece in enumerate(
            (grad_raw_query.astype(BF16), grad_raw_key.astype(BF16), grad_value[:, 0:head].astype(BF16), grad_gate)
        ):
            if side == 0:
                grad_project[:, column(part_id)] = jnp.concatenate([piece, piece], axis=1)
            else:
                keep = grad_project[:, column(part_id)]
                both = jnp.concatenate([piece, piece], axis=1)
                grad_project[:, column(part_id)] = jnp.where(lanes < head, keep, both)

    @pl.when(step == steps - 1)
    def _():
        high, middle, low = split_three(grad_prefix[...])
        short = lane_ids(chunk)

        @pl.loop(0, rows // chunk)
        def _(turn):
            part = pl.ds(pl.multiple_of(turn * chunk, chunk), chunk)
            after = jnp.where(pos_row[0:1, :] >= pos_col[part, :], 1.0, 0.0).astype(BF16)
            total = dot(after, high.astype(BF16)) + dot(after, middle.astype(BF16)) + dot(after, low.astype(BF16))
            grad_logit = total * jax.nn.sigmoid(-(forget[part, :] + bias[0:1, :]))
            grad_logit = jnp.where(short < heads, grad_logit, 0.0).astype(BF16)
            grad_project[part, 4 * width : 4 * width + LANES] = grad_logit
            small[2:3, :] += jnp.sum(grad_logit.astype(F32), axis=0, keepdims=True)

        if ranks:
            pltpu.make_async_copy(normed, normed_in, load_sem.at[0]).wait()
            pltpu.make_async_copy(out_grad, out_in, load_sem.at[1]).wait()
            ends = 4 * width, 4 * width + out_grad.shape[1]

            def save(turn):
                part = pl.ds(pl.multiple_of(turn * chunk, chunk), chunk)
                return pltpu.make_async_copy(late_all.at[part, :], late.at[part, :], save_sem.at[turn])

            @pl.loop(0, late.shape[0] // chunk)
            def _(turn):
                part = pl.ds(pl.multiple_of(turn * chunk, chunk), chunk)
                product = left_product(normed_in[:, part], grad_project[...]).astype(BF16)
                late_all[part, 0 : ends[0]] = product[:, 0 : ends[0]]
                late_all[part, ends[0] : ends[1]] = out_in[part, :]
                late_all[part, ends[1] : ends[1] + LANES] = product[:, ends[0] :]
                save(turn).start()

            for copy in aside_copies():
                copy.wait()

            @pl.loop(0, late.shape[0] // chunk)
            def _(turn):
                save(turn).wait()


def pick_chunk(rows):
    return 256 if rows % 256 == 0 else 128


def whole(shape):
    return pl.BlockSpec(shape, lambda step: tuple(0 for _ in shape))


def attend(project, places, bias, gains, head, width, heads):
    rows = project.shape[0]
    steps = width // LANES
    per = LANES // head
    chunk = pick_chunk(rows)

    def part(index):
        return pl.BlockSpec((rows, LANES), lambda step: (0, index * steps + step))

    own = pl.BlockSpec((rows, LANES), lambda step: (0, step))
    wide = pl.BlockSpec((per, rows, LANES), lambda step: (step, 0, 0))
    forget = pl.BlockSpec((rows, LANES), lambda step: (0, 4 * steps))
    wide_shape = jax.ShapeDtypeStruct((per * steps, rows, LANES), BF16)
    return pl.pallas_call(
        functools.partial(attend_kernel, head, chunk, heads),
        grid=(steps,),
        in_specs=[whole(p.shape) for p in places] + [whole(bias.shape), whole(gains.shape)]
        + [part(0), part(1), part(2), part(3), forget],
        out_specs=[own, pl.BlockSpec((1, rows, LANES), lambda step: (step, 0, 0)), wide, wide, wide],
        out_shape=[
            jax.ShapeDtypeStruct((rows, width), BF16),
            jax.ShapeDtypeStruct((steps, rows, LANES), F32),
            wide_shape, wide_shape, wide_shape,
        ],
        scratch_shapes=[pltpu.VMEM((rows, rows), F32), pltpu.VMEM((rows, LANES), F32)],
        compiler_params=pltpu.CompilerParams(vmem_limit_bytes=VMEM_LIMIT),
        name="attend",
    )(*places, bias, gains, project, project, project, project, project)


def attend_back(project, places, bias, gains, attended, wides, grad_gated, beside, ranks, head, width, heads):
    rows = project.shape[0]
    steps = width // LANES
    per = LANES // head
    chunk = pick_chunk(rows)

    def part(index):
        return pl.BlockSpec((rows, LANES), lambda step: (0, index * steps + step))

    own = pl.BlockSpec((rows, LANES), lambda step: (0, step))
    block = pl.BlockSpec((1, rows, LANES), lambda step: (step, 0, 0))
    wide = pl.BlockSpec((per, rows, LANES), lambda step: (step, 0, 0))
    forget = pl.BlockSpec((rows, LANES), lambda step: (0, 4 * steps))
    total = 4 * width + LANES
    out_specs = [whole((rows, total)), whole((8, LANES))]
    out_shape = [jax.ShapeDtypeStruct((rows, total), BF16), jax.ShapeDtypeStruct((8, LANES), F32)]
    scratch = [
        pltpu.VMEM((rows, rows), F32),
        pltpu.VMEM((rows, LANES), BF16),
        pltpu.VMEM((rows, LANES), F32),
        pltpu.VMEM((rows, LANES), F32),
        pltpu.VMEM((rows, LANES), F32),
        pltpu.VMEM((rows, LANES), F32),
    ]
    if ranks:
        aside, normed, out_grad = beside
        model, late_cols = normed.shape[1], total + out_grad.shape[1]
        out_specs += [ANY, ANY]
        out_shape += [
            jax.ShapeDtypeStruct((ranks, aside.shape[0] // ranks, aside.shape[1]), BF16),
            jax.ShapeDtypeStruct((model, late_cols), BF16),
        ]
        scratch += [
            pltpu.VMEM(normed.shape, BF16),
            pltpu.VMEM(out_grad.shape, BF16),
            pltpu.VMEM((model, late_cols), BF16),
            pltpu.SemaphoreType.DMA((2,)),
            pltpu.SemaphoreType.DMA((model // chunk,)),
            pltpu.SemaphoreType.DMA((ranks - 1,)),
            pltpu.SemaphoreType.DMA((ranks - 1,)),
            pltpu.SemaphoreType.DMA,
        ]
    return pl.pallas_call(
        functools.partial(attend_back_kernel, head, chunk, width, heads, ranks),
        grid=(steps,),
        in_specs=[whole(p.shape) for p in places] + [whole(bias.shape), whole(gains.shape)]
        + [part(0), part(1), part(3), forget, block, wide, wide, wide, own] + [ANY] * len(beside),
        out_specs=out_specs,
        out_shape=out_shape,
        scratch_shapes=scratch,
        compiler_params=pltpu.CompilerParams(
            collective_id=5 if ranks else None, has_side_effects=ranks > 0, vmem_limit_bytes=VMEM_LIMIT
        ),
        name="attend_back",
    )(*places, bias, gains, project, project, project, project, attended, *wides, grad_gated, *beside)


def greet(peers, line=None):
    barrier = pltpu.get_barrier_semaphore()
    if line is not None:
        peers = peers + [line.sibling]
    for peer in peers:
        pl.semaphore_signal(barrier, inc=1, device_id=peer, device_id_type=MESH)
    if line is not None:
        for there, peer in ((line.has_above, line.above), (line.has_below, line.below)):

            @pl.when(there)
            def _():
                pl.semaphore_signal(barrier, inc=1, device_id=peer, device_id_type=MESH)

    count = len(peers)
    if line is not None:
        last = line.layers - 1
        count = count + (1 - line.layer // last) + (line.layer + last) // line.layers
    pl.semaphore_wait(barrier, count)


class Line:
    def __init__(self, shards, source, target, sems):
        self.shard = lax.axis_index("fsdp")
        self.layers = shards // 2
        self.layer, self.core = self.shard // 2, self.shard % 2
        self.sibling = {"fsdp": self.shard ^ 1}
        self.above, self.below = {"fsdp": self.shard + 2}, {"fsdp": self.shard - 2}
        self.has_above, self.has_below = self.layer < self.layers - 1, self.layer > 0
        self.source, self.target = source, target
        self.rows = target.shape[0] // shards
        self.line_send, self.line_recv, self.side_send, self.side_recv, self.own_sem = sems

    def block(self, owner):
        return rows_of(self.target, owner, self.rows)

    def line(self, owner_layer, peer, way, own=False):
        here = self.block(owner_layer * 2 + self.core)
        return pltpu.make_async_remote_copy(
            self.source if own else here, here, self.line_send.at[way, owner_layer], self.line_recv.at[owner_layer],
            device_id=peer, device_id_type=MESH,
        )

    def side(self, owner_layer, owner_core, own=False):
        here = self.block(owner_layer * 2 + owner_core)
        return pltpu.make_async_remote_copy(
            self.source if own else here, here, self.side_send.at[owner_layer], self.side_recv.at[owner_layer],
            device_id=self.sibling, device_id_type=MESH,
        )

    def start(self):
        own = self.source is not None

        @pl.when(self.has_above)
        def _():
            self.line(self.layer, self.above, 0, own).start()

        @pl.when(self.has_below)
        def _():
            self.line(self.layer, self.below, 1, own).start()

        self.side(self.layer, self.core, own).start()
        if own:
            self.keep = pltpu.make_async_copy(self.source, self.block(self.shard), self.own_sem)
            self.keep.start()

    def step(self, distance):
        lower, upper = self.layer - distance, self.layer + distance

        @pl.when(lower >= 0)
        def _():
            self.line(lower, self.below, 1).wait_recv()

            @pl.when(self.has_above)
            def _():
                self.line(lower, self.above, 0).start()

            self.side(lower, self.core).start()

        @pl.when(upper < self.layers)
        def _():
            self.line(upper, self.above, 0).wait_recv()

            @pl.when(self.has_below)
            def _():
                self.line(upper, self.below, 1).start()

            self.side(upper, self.core).start()

    def from_side(self, owner_layer):
        self.side(owner_layer, 1 - self.core).wait_recv()

    def finish(self):
        self.keep.wait()
        for owner_layer in range(self.layers):
            self.from_side(owner_layer)
        self.sent()

    def sent(self):
        for owner_layer in range(self.layers):
            self.side(owner_layer, self.core).wait_send()

            @pl.when(self.has_above & (owner_layer <= self.layer))
            def _():
                self.line(owner_layer, self.above, 0).wait_send()

            @pl.when(self.has_below & (owner_layer >= self.layer))
            def _():
                self.line(owner_layer, self.below, 1).wait_send()


def line_scratch(shards):
    layers = shards // 2
    return [
        pltpu.SemaphoreType.DMA((2, layers)),
        pltpu.SemaphoreType.DMA((layers,)),
        pltpu.SemaphoreType.DMA((layers,)),
        pltpu.SemaphoreType.DMA((layers,)),
        pltpu.SemaphoreType.DMA,
    ]


class Relay:
    def __init__(self, rank, source, place, send_sem, recv_sem, own_sem):
        self.rank, self.source, self.place = rank, source, place
        self.send_sem, self.recv_sem, self.own_sem = send_sem, recv_sem, own_sem

    def copy(self, number):
        me = self.rank
        source, place, distance = (
            lambda: (self.source(0), self.place(me, 0), 1),
            lambda: (self.source(1), self.place(me, 1), 2),
            lambda: (self.source(1), self.place(me, 1), 1),
            lambda: (self.source(0), self.place(me, 0), 2),
            lambda: (self.place(me ^ 1, 0), self.place(me ^ 1, 0), 2),
            lambda: (self.place(me ^ 2, 1), self.place(me ^ 2, 1), 1),
        )[number]()
        return pltpu.make_async_remote_copy(
            source, place, self.send_sem.at[number], self.recv_sem.at[number],
            device_id={"ctx": me ^ distance}, device_id_type=MESH,
        )

    def own(self, h):
        return pltpu.make_async_copy(self.source(h), self.place(self.rank, h), self.own_sem.at[h])

    def start(self, keep=True):
        for number in range(4):
            self.copy(number).start()
        if keep:
            for h in range(2):
                self.own(h).start()

    def forward(self):
        for number in range(2):
            self.copy(number).wait_recv()
            self.copy(number + 4).start()

    def arrive(self):
        for number in range(2, 6):
            self.copy(number).wait_recv()

    def finish(self, arrive=True, keep=True):
        if keep:
            for h in range(2):
                self.own(h).wait()
        if arrive:
            self.arrive()
        for number in range(6):
            self.copy(number).wait_send()


def rows_of(ref, index, size):
    return ref.at[pl.ds(pl.multiple_of(index * size, 16), size), :]


def cols_of(ref, index, size):
    return ref.at[:, pl.ds(pl.multiple_of(index * size, LANES), size)]


def relay_ops(mode, rank, source, target, sems):
    rows, cols = source.shape
    half = rows // 2

    def part(h):
        return source.at[pl.ds(h * half, half), :]

    def place(block, h):
        if mode == "gather_rows":
            return target.at[pl.ds(pl.multiple_of(block * rows + h * half, 16), half), :]
        if mode == "gather_cols":
            return target.at[pl.ds(h * half, half), pl.ds(pl.multiple_of(block * cols, LANES), cols)]
        return target.at[block, pl.ds(h * half, half), :]

    return Relay(rank, part, place, *sems)


def exchange_kernel(modes, ranks, across, shards, *refs):
    count = len(modes)
    sources, targets = refs[:count], refs[count : 2 * count]
    send_sem, recv_sem, own_sem = refs[2 * count : 2 * count + 3]
    rank = lax.axis_index("ctx")
    shard = lax.axis_index("fsdp")
    line = None
    if "line" in modes:
        at = modes.index("line")
        line = Line(shards, sources[at], targets[at], refs[2 * count + 3 :])
    far = any(mode not in ("gather_rows", "gather_cols", "stack", "line") for mode in modes)
    peers = [{"ctx": rank ^ distance} for distance in range(1, ranks if far else ranks - 1)]
    if across:
        peers += [{"fsdp": shard ^ distance} for distance in range(1, across)]
    greet(peers, line)
    copies, relays = [], []
    for op, (mode, source, target) in enumerate(zip(modes, sources, targets)):
        if mode == "line":
            line.start()
            continue
        if mode in ("gather_rows", "gather_cols", "stack"):
            relay = relay_ops(mode, rank, source, target, (send_sem.at[op], recv_sem.at[op], own_sem.at[op]))
            relay.start()
            relays.append(relay)
            continue
        axis, me, members = ("fsdp", shard, across) if mode == "shards" else ("ctx", rank, ranks)
        for distance in range(members):
            other = me ^ distance if distance else me
            place = target.at[me]
            if mode == "scatter_rows":
                piece = rows_of(source, other, target.shape[1])
            elif mode == "scatter_cols":
                piece = cols_of(source, other, target.shape[2])
            elif mode == "shards":
                piece = source.at[other]
            else:
                piece = source
            if distance == 0:
                copy = pltpu.make_async_copy(piece, place, own_sem.at[op, 0])
            else:
                copy = pltpu.make_async_remote_copy(
                    piece, place, send_sem.at[op, distance - 1], recv_sem.at[op, distance - 1],
                    device_id={axis: other}, device_id_type=MESH,
                )
            copy.start()
            copies.append(copy)
    for index in range(max(len(relays), shards // 2 - 1 if line is not None else 0)):
        if line is not None and 0 < index < shards // 2:
            line.step(index)
        if index < len(relays):
            relays[index].forward()
    if line is not None:
        line.step(shards // 2 - 1)
        line.finish()
    for relay in relays:
        relay.finish()
    for copy in copies:
        copy.wait()


def exchange(collective_id, ranks, across, shards, *ops):
    shapes = []
    for mode, source in ops:
        shape = source.shape
        if mode == "gather_rows":
            shape = (ranks * shape[0], shape[1])
        elif mode == "gather_cols":
            shape = (shape[0], ranks * shape[1])
        elif mode == "scatter_rows":
            shape = (ranks, shape[0] // ranks, shape[1])
        elif mode == "scatter_cols":
            shape = (ranks, shape[0], shape[1] // ranks)
        elif mode in ("stack", "each"):
            shape = (ranks,) + shape
        elif mode == "line":
            shape = (shards * shape[0], shape[1])
        shapes.append(jax.ShapeDtypeStruct(shape, source.dtype))
    count = len(ops)
    most = max(6, across - 1)
    moved = sum(s.size * s.dtype.itemsize for s in shapes)
    return pl.pallas_call(
        functools.partial(exchange_kernel, [mode for mode, _ in ops], ranks, across, shards),
        in_specs=[ANY] * count,
        out_specs=[ANY] * count,
        out_shape=shapes,
        scratch_shapes=[
            pltpu.SemaphoreType.DMA((count, most)),
            pltpu.SemaphoreType.DMA((count, most)),
            pltpu.SemaphoreType.DMA((count, 2)),
        ]
        + (line_scratch(shards) if any(mode == "line" for mode, _ in ops) else []),
        compiler_params=pltpu.CompilerParams(collective_id=collective_id, has_side_effects=True),
        cost_estimate=pl.CostEstimate(flops=0, bytes_accessed=moved * 20, transcendentals=0),
        name="exchange",
    )(*[source for _, source in ops])


VMEM_WHOLE = pl.BlockSpec(memory_space=pltpu.VMEM)


def to_rank(source, target, send, recv, other):
    return pltpu.make_async_remote_copy(
        source, target, send, recv, device_id={"ctx": other}, device_id_type=MESH
    )


FRONT_LOADS = 3
FRONT_SAVES = 9


def front_kernel(
    shards, head, heads, width, piece, chunk,
    tokens, cotangent, weight, weight_out, other, forget_weight, norm_gains, qk_gains, segments, order, forget_bias,
    inputs, grad_low, w_in, w_out, w_gate_up, normed, project, gated, attended, wide_query, wide_key, wide_value,
    mixed, gain_rows, pos_row, pos_col, seg_row, seg_col, bias, gains,
    weight_all, other_all, out_all, own_in, own_pick, own_out, x_all, in_all, hn_all, proj_all, mask, prefix,
    gated_all, attended_all, query_all, key_all, value_all, out_cols, scale_one, y_own,
    send_sem, recv_sem, own_sem, load_sem, save_sem, *line_sems,
):
    rank = lax.axis_index("ctx")
    ranks = lax.axis_size("ctx")
    model = weight.shape[1] // 4
    rows = x_all.shape[0]
    steps = width // LANES
    tail_at = 4 * width
    loads = [
        pltpu.make_async_copy(a, b, load_sem.at[n])
        for n, (a, b) in enumerate(((weight, weight_all), (other, other_all), (weight_out, out_all)))
    ]
    saves = [
        pltpu.make_async_copy(a, b, save_sem.at[n])
        for n, (a, b) in enumerate(
            (
                (x_all, inputs), (in_all, w_in), (hn_all, normed), (proj_all, project), (query_all, wide_query),
                (key_all, wide_key), (value_all, wide_value), (attended_all, attended), (gated_all, gated),
            )
        )
    ]
    for copy in loads:
        copy.start()
    per = len(line_sems) // 3
    in_line = Line(shards, own_in, in_all, line_sems[:per])
    out_line = Line(shards, own_out, out_cols, line_sems[per : 2 * per])
    up_line = Line(shards, own_pick, w_gate_up, line_sems[2 * per :])
    greet([{"ctx": rank ^ 1}, {"ctx": rank ^ 2}], in_line)

    def sems(n):
        return send_sem.at[n], recv_sem.at[n], own_sem.at[n]

    first = relay_ops("gather_rows", rank, tokens, x_all, sems(0))
    second = relay_ops("gather_rows", rank, cotangent, grad_low, sems(1))

    def cols(start, size):
        return pl.ds(pl.multiple_of(start, LANES), size)

    loads[0].wait()
    for i in range(4):
        own_in[:, i * width : (i + 1) * width] = weight_all[:, cols(i * model + rank * width, width)]
    total_heads = forget_weight.shape[1]
    from_head = lax.broadcasted_iota(jnp.int32, (total_heads, LANES), 0)
    to_lane = lax.broadcasted_iota(jnp.int32, (total_heads, LANES), 1)
    chosen = jnp.where((to_lane < heads) & (from_head == rank * heads + to_lane), 1.0, 0.0).astype(BF16)
    from_gain = lax.broadcasted_iota(jnp.int32, (2, LANES), 0)
    to_lane = lax.broadcasted_iota(jnp.int32, (2, LANES), 1)
    chosen_gain = jnp.where(to_lane == heads + from_gain, 1.0, 0.0).astype(BF16)
    tail = dot(forget_weight[...], chosen) + left_product(norm_gains[...], chosen_gain)
    own_in[:, tail_at : tail_at + LANES] = tail.astype(BF16)
    in_line.start()
    first.start()
    loads[1].wait()
    for i in range(own_pick.shape[1] // piece):
        own_pick[:, i * piece : (i + 1) * piece] = other_all[:, cols((i * ranks + rank) * piece, piece)]
    loads[2].wait()
    own_out[...] = out_all[:, cols(rank * width, width)]
    count = order.shape[1]
    length = rows // count
    row_ids = lax.broadcasted_iota(jnp.int32, (rows, LANES), 0)
    lane_id = lax.broadcasted_iota(jnp.int32, (8, rows), 1)
    tall = jnp.zeros((rows, LANES), jnp.int32)
    flat = jnp.zeros((8, rows), jnp.int32)
    for block in range(count):
        start = order[0, block] * length - block * length
        tall = jnp.where((row_ids >= block * length) & (row_ids < (block + 1) * length), row_ids + start, tall)
        flat = jnp.where((lane_id >= block * length) & (lane_id < (block + 1) * length), lane_id + start, flat)
    pos_col[...] = tall[:, 0:1].astype(F32)
    pos_row[...] = flat[0:1, :].astype(F32)
    true_segments = segments[0:1, :].astype(F32)

    @turns(rows, chunk)
    def _(part):
        true_place = lax.broadcasted_iota(jnp.int32, (chunk, rows), 1).astype(F32)
        own_place = true_place == pos_col[part, :]
        seg_col[part, :] = jnp.sum(jnp.where(own_place, true_segments, 0.0), axis=-1, keepdims=True)

    seg_row[...] = jnp.broadcast_to(seg_col[...], (rows, LANES)).T[0:1, :]
    lane = lax.broadcasted_iota(jnp.int32, (1, LANES), 1)
    bias_row = jnp.zeros((1, LANES), F32)
    for index in range(heads):
        bias_row = jnp.where(lane == index, forget_bias[0, rank * heads + index], bias_row)
    bias[...] = bias_row
    for side in range(LANES // head):
        gains[:, side * head : (side + 1) * head] = qk_gains[...]
    fill_mask(chunk, pos_row, pos_col, seg_row, seg_col, mask)
    proj_all[...] = jnp.zeros_like(proj_all)
    gain_rows[...] = jnp.zeros_like(gain_rows)
    first.forward()
    second.start()
    in_line.step(1)
    first.finish()
    saves[0].start()

    @turns(rows, chunk)
    def _(part):
        values = x_all[part, :].astype(F32)
        scale_one[part, :] = jnp.broadcast_to(rms_scale(values), (chunk, LANES))

    def consume(layer):
        in_line.from_side(layer)
        size = 2 * in_line.rows
        here = cols(layer * size, size)
        tail_block = in_all[here, tail_at : tail_at + LANES].astype(F32).T
        gain_rows[0:1, here] = tail_block[heads : heads + 1, :]
        gain_rows[1:2, here] = tail_block[heads + 1 : heads + 2, :]

        @turns(rows, chunk)
        def _(part):
            values = x_all[part, here].astype(F32) * scale_one[part, 0:1] * gain_rows[0:1, here]
            hn_all[part, here] = values.astype(BF16)
            proj_all[part, :] += dot(values.astype(BF16), in_all[here, :])

    def consume_at(distance):
        lower, upper = in_line.layer - distance, in_line.layer + distance

        @pl.when(lower >= 0)
        def _():
            consume(lower)

        @pl.when(upper < in_line.layers)
        def _():
            consume(upper)

    in_line.keep.wait()
    consume(in_line.layer)
    consume_at(1)
    second.forward()
    for distance in range(2, in_line.layers):
        in_line.step(distance)
        if distance == in_line.layers - 1:
            out_line.start()
        consume_at(distance)

    for n in (1, 2, 3):
        saves[n].start()
    up_line.start()
    out_line.step(1)
    fill_prefix(chunk, heads, pos_row, pos_col, proj_all[:, tail_at : tail_at + LANES] + bias[0:1, :], prefix)

    def share(index):
        block = rank * steps + index
        half = rows // 2

        def source(h):
            return gated_all.at[block, pl.ds(h * half, half), :]

        def place(owner, h):
            return gated_all.at[owner * steps + index, pl.ds(h * half, half), :]

        return Relay(rank, source, place, send_sem.at[2 + index], recv_sem.at[2 + index], None)

    per_block = LANES // head

    @pl.loop(0, steps)
    def _(index):
        def lanes_of(part_id):
            return proj_all[:, cols(part_id * width + index * LANES, LANES)]

        def gate(part):
            return proj_all[part, cols(3 * width + index * LANES, LANES)]

        group = pl.ds(index * per_block, per_block)
        attend_block(
            head, chunk, index, lanes_of(0), lanes_of(1), lanes_of(2), gate, gains, mask, prefix,
            gated_all.at[rank * steps + index], attended_all.at[index],
            query_all.at[group], key_all.at[group], value_all.at[group],
        )
        share(index).start(keep=False)

        @pl.when(index == 0)
        def _():
            out_line.step(2)

        @pl.when(index > 0)
        def _():
            share(index - 1).forward()

    up_line.step(1)
    out_line.step(3)
    share(steps - 1).forward()
    for n in (4, 5, 6, 7):
        saves[n].start()
    for index in range(steps):
        share(index).arrive()
    saves[8].start()
    out_line.keep.wait()
    for layer in range(out_line.layers):
        out_line.from_side(layer)
    save_out = pltpu.make_async_copy(out_cols, w_out, save_sem.at[len(saves)])
    save_out.start()

    third = relay_ops("gather_cols", rank, y_own, mixed, sems(2 + steps))

    @turns(rows, chunk)
    def _(part):
        total = x_all[part, cols(rank * width, width)].astype(F32)
        for block in range(gated_all.shape[0]):
            total = total + dot(gated_all[block, part, :], out_cols[block * LANES : (block + 1) * LANES, :])
        y_own[part, :] = total.astype(BF16)

    third.start()
    third.forward()
    up_line.step(2)
    up_line.step(3)
    third.finish()
    up_line.finish()
    out_line.sent()
    in_line.sent()
    second.finish()
    for index in range(steps):
        share(index).finish(arrive=False, keep=False)
    for copy in saves:
        copy.wait()
    save_out.wait()


def front(
    collective_id, ranks, shards, head, heads, width, piece,
    tokens, cotangent, weight, weight_out, other, forget_weight, norm_gains, qk_gains, segments, order, forget_bias,
):
    own_rows, model = tokens.shape
    rows = ranks * own_rows
    chunk = pick_chunk(rows)
    steps, shard_rows = width // LANES, weight.shape[0]
    wide_in = 4 * width + LANES
    other_cols = other.shape[1] // ranks
    wide = (heads, rows, LANES)
    shape, vmem = jax.ShapeDtypeStruct, pltpu.VMEM
    return pl.pallas_call(
        functools.partial(front_kernel, shards, head, heads, width, piece, chunk),
        in_specs=[ANY] * 5 + [VMEM_WHOLE] * 4 + [pl.BlockSpec(memory_space=pltpu.SMEM)] * 2,
        out_specs=[ANY] * 13 + [VMEM_WHOLE] * 7,
        out_shape=[
            shape((rows, model), BF16),
            shape((rows, model), BF16),
            shape((model, wide_in), BF16),
            shape((model, width), BF16),
            shape((model, other_cols), BF16),
            shape((rows, model), BF16),
            shape((rows, wide_in), F32),
            shape((ranks * steps, rows, LANES), BF16),
            shape((steps, rows, LANES), F32),
            shape(wide, BF16), shape(wide, BF16), shape(wide, BF16),
            shape((rows, model), BF16),
            shape((8, model), F32),
            shape((1, rows), F32), shape((rows, 1), F32), shape((1, rows), F32), shape((rows, 1), F32),
            shape((1, LANES), F32),
            shape((2, LANES), F32),
        ],
        scratch_shapes=[
            vmem(weight.shape, BF16),
            vmem(other.shape, BF16),
            vmem(weight_out.shape, BF16),
            vmem((shard_rows, wide_in), BF16),
            vmem((shard_rows, other_cols), BF16),
            vmem((shard_rows, width), BF16),
            vmem((rows, model), BF16),
            vmem((model, wide_in), BF16),
            vmem((rows, model), BF16),
            vmem((rows, wide_in), F32),
            vmem((rows, rows), F32),
            vmem((rows, LANES), F32),
            vmem((ranks * steps, rows, LANES), BF16),
            vmem((steps, rows, LANES), F32),
            vmem(wide, BF16), vmem(wide, BF16), vmem(wide, BF16),
            vmem((model, width), BF16),
            vmem((rows, LANES), F32),
            vmem((rows, width), BF16),
            pltpu.SemaphoreType.DMA((3 + steps, 6)),
            pltpu.SemaphoreType.DMA((3 + steps, 6)),
            pltpu.SemaphoreType.DMA((3 + steps, 2)),
            pltpu.SemaphoreType.DMA((FRONT_LOADS,)),
            pltpu.SemaphoreType.DMA((FRONT_SAVES + 1,)),
        ]
        + 3 * line_scratch(shards),
        compiler_params=pltpu.CompilerParams(
            collective_id=collective_id, has_side_effects=True, vmem_limit_bytes=VMEM_LIMIT
        ),
        cost_estimate=pl.CostEstimate(flops=0, bytes_accessed=300 << 20, transcendentals=0),
        name="front",
    )(
        tokens, cotangent, weight, weight_out, other, forget_weight, norm_gains, qk_gains, segments, order, forget_bias
    )


def ffn_kernel(
    shards, chunk,
    mixed, w_gate_up, cotangent, down_weight, gain,
    w_down, normed, hidden, grad_gate_up, grad_down, grad_weight,
    mixed_in, weight_in, cotangent_in, own_in, gates, ups, hn, turned, acts, grads, down_out, weight_out,
    load_sem, save_sem, *line_sems,
):
    size = gates.shape[1]
    rows, model = mixed.shape
    tile = 2 * own_in.shape[0]
    rank = lax.axis_index("ctx")
    loads = [
        pltpu.make_async_copy(a, b, load_sem.at[n])
        for n, (a, b) in enumerate(
            (
                (rows_of(down_weight, rank, own_in.shape[0]), own_in), (mixed, mixed_in), (w_gate_up, weight_in),
                (cotangent, cotangent_in),
            )
        )
    ]
    saves = [
        pltpu.make_async_copy(a, b, save_sem.at[n])
        for n, (a, b) in enumerate(
            ((hn, normed), (acts, hidden), (down_out, grad_down), (grads, grad_gate_up), (weight_out, grad_weight))
        )
    ]
    for copy in loads:
        copy.start()
    line = Line(shards, own_in, w_down, line_sems)
    greet([], line)
    loads[0].wait()
    line.start()
    loads[1].wait()

    @turns(rows, chunk)
    def _(part):
        values = mixed_in[part, :].astype(F32)
        low = values * rms_scale(values) * gain[1:2, :]
        hn[part, :] = low.astype(BF16)
        turned[:, part] = low.T.astype(BF16)

    saves[0].start()
    loads[2].wait()

    def span(turn, start=0):
        return pl.ds(pl.multiple_of(start + turn * tile, LANES), tile)

    @pl.loop(0, size // tile)
    def _(turn):
        @turns(rows, chunk)
        def _(part):
            gate = dot(hn[part, :], weight_in[:, span(turn)])
            up = dot(hn[part, :], weight_in[:, span(turn, size)])
            gates[part, span(turn)] = gate
            ups[part, span(turn)] = up
            acts[part, span(turn)] = (jax.nn.silu(gate) * up).astype(BF16)

    saves[1].start()
    line.step(1)
    loads[3].wait()

    def consume(turn):
        line.from_side(turn)

        @turns(rows, chunk)
        def _(part):
            grad = right_product(cotangent_in[part, :], w_down[span(turn), :])
            gate, up = gates[part, span(turn)], ups[part, span(turn)]
            sig = jax.nn.sigmoid(gate)
            grads[part, span(turn)] = (grad * up * sig * (1.0 + gate * (1.0 - sig))).astype(BF16)
            grads[part, span(turn, size)] = (grad * gate * sig).astype(BF16)

        for start in (0, size):
            here = span(turn, start)

            @turns(model, 3 * chunk if model % (3 * chunk) == 0 else chunk)
            def _(part):
                weight_out[part, here] = dot(turned[part, :], grads[:, here]).astype(BF16)

    def consume_at(distance):
        lower, upper = line.layer - distance, line.layer + distance

        @pl.when(lower >= 0)
        def _():
            consume(lower)

        @pl.when(upper < line.layers)
        def _():
            consume(upper)

    line.keep.wait()
    consume(line.layer)
    consume_at(1)
    line.step(2)

    @pl.loop(0, size // tile)
    def _(turn):
        down_out[span(turn), :] = left_product(acts[:, span(turn)], cotangent_in[...]).astype(BF16)

    saves[2].start()
    consume_at(2)
    for distance in range(3, line.layers):
        line.step(distance)
        consume_at(distance)
    saves[3].start()
    saves[4].start()
    line.sent()
    for copy in saves:
        copy.wait()


def ffn(collective_id, ranks, shards, mixed, w_gate_up, cotangent, down_weight, gain):
    rows, model = mixed.shape
    size = w_gate_up.shape[1] // 2
    shape, vmem = jax.ShapeDtypeStruct, pltpu.VMEM
    return pl.pallas_call(
        functools.partial(ffn_kernel, shards, pick_chunk(rows)),
        in_specs=[ANY] * 4 + [VMEM_WHOLE],
        out_specs=[VMEM_WHOLE] + [ANY] * 5,
        out_shape=[
            shape((size, model), BF16),
            shape((rows, model), BF16),
            shape((rows, size), BF16),
            shape((rows, 2 * size), BF16),
            shape((size, model), BF16),
            shape((model, 2 * size), BF16),
        ],
        scratch_shapes=[
            vmem((rows, model), BF16),
            vmem(w_gate_up.shape, BF16),
            vmem((rows, model), BF16),
            vmem((down_weight.shape[0] // ranks, model), BF16),
            vmem((rows, size), F32),
            vmem((rows, size), F32),
            vmem((rows, model), BF16),
            vmem((model, rows), BF16),
            vmem((rows, size), BF16),
            vmem((rows, 2 * size), BF16),
            vmem((size, model), BF16),
            vmem((model, 2 * size), BF16),
            pltpu.SemaphoreType.DMA((4,)),
            pltpu.SemaphoreType.DMA((5,)),
        ]
        + line_scratch(shards),
        compiler_params=pltpu.CompilerParams(
            collective_id=collective_id, has_side_effects=True, vmem_limit_bytes=VMEM_LIMIT
        ),
        cost_estimate=pl.CostEstimate(flops=0, bytes_accessed=100 << 20, transcendentals=0),
        name="ffn",
    )(mixed, w_gate_up, cotangent, down_weight, gain)


def middle_kernel(
    ranks,
    grad_gate_up, w_gate_up, mixed, cotangent, w_out, hidden, w_down, gated, gain,
    mixed_grad, gated_grad, gain_grad, down_part, out_grad,
    grad_in, weight_in, mixed_in, cotangent_in, out_in, hidden_in, down_in, gated_in, low_grad, down_all, out_all,
    wide, first_out, first_in, second_out, second_in,
    load_sem, save_sem, first_send, first_recv, second_send, second_recv,
):
    rank = lax.axis_index("ctx")
    rows = mixed.shape[0] // ranks
    model, width = w_out.shape
    tile = 256
    loads = [
        pltpu.make_async_copy(a, b, load_sem.at[n])
        for n, (a, b) in enumerate(
            (
                (w_gate_up, weight_in), (grad_gate_up, grad_in), (mixed, mixed_in), (cotangent, cotangent_in),
                (w_out, out_in), (hidden, hidden_in), (w_down, down_in), (gated, gated_in),
            )
        )
    ]
    saves = [
        pltpu.make_async_copy(down_all, down_part, save_sem.at[0]),
        pltpu.make_async_copy(out_all, out_grad, save_sem.at[1]),
    ]
    for copy in loads:
        copy.start()
    greet([{"ctx": rank ^ distance} for distance in range(1, ranks)])
    gain_grad[...] = jnp.zeros_like(gain_grad)
    for copy in loads[:5]:
        copy.wait()

    def part(turn):
        return pl.ds(pl.multiple_of(turn * rows, 16), rows)

    def send(out, into, send_sem, recv_sem, turn, distance):
        other = rank ^ distance
        return to_rank(
            out.at[other, part(turn), :], into.at[distance, part(turn), :],
            send_sem.at[distance - 1, turn], recv_sem.at[distance - 1, turn], other,
        )

    def arrived(out, into, send_sem, recv_sem, turn):
        total = out[rank, part(turn), :].astype(F32)
        for distance in range(1, ranks):
            send(out, into, send_sem, recv_sem, turn, distance).wait_recv()
            total = total + into[distance, part(turn), :].astype(F32)
        return total

    first = (first_out, first_in, first_send, first_recv)
    second = (second_out, second_in, second_send, second_recv)

    def project(turn):
        here = part(turn)
        total = cotangent_in[here, pl.ds(pl.multiple_of(rank * width, LANES), width)].astype(F32)
        total = total + arrived(*first, turn)
        mixed_grad[here, :] = total
        low = total.astype(BF16)
        low_grad[here, :] = low
        for index in range(ranks):
            second_out[index, here, :] = right_product(low, out_in[index * width : (index + 1) * width, :]).astype(BF16)
        for distance in range(1, ranks):
            send(*second, turn, distance).start()

    @pl.loop(0, ranks)
    def _(turn):
        here = part(turn)

        @pl.loop(0, model // tile)
        def _(step):
            cols = pl.ds(pl.multiple_of(step * tile, tile), tile)
            wide[:, cols] = right_product(grad_in[here, :], weight_in[cols, :])

        values = mixed_in[here, :].astype(F32)
        scale = rms_scale(values)
        grad = wide[...]
        gain_grad[0:1, :] += jnp.sum(grad * values * scale, axis=0, keepdims=True)
        back = norm_back(grad, values, scale, gain[0:1, :]).astype(BF16)
        for index in range(ranks):
            first_out[index, here, :] = back[:, index * width : (index + 1) * width]
        for distance in range(1, ranks):
            send(*first, turn, distance).start()

        @pl.when(turn > 0)
        def _():
            project(turn - 1)

    for copy in loads[5:]:
        copy.wait()

    @pl.loop(0, model // tile)
    def _(step):
        cols = pl.ds(pl.multiple_of(step * tile, tile), tile)
        down_all[:, cols] = dot(hidden_in[...], down_in[:, cols]).astype(BF16)

    saves[0].start()
    project(ranks - 1)

    @pl.loop(0, gated_in.shape[0])
    def _(block):
        out_all[pl.ds(pl.multiple_of(block * LANES, LANES), LANES), :] = left_product(
            gated_in[block], low_grad[...]
        ).astype(BF16)

    saves[1].start()

    @pl.loop(0, ranks)
    def _(turn):
        gated_grad[part(turn), :] = arrived(*second, turn)

    @pl.loop(0, ranks)
    def _(turn):
        for distance in range(1, ranks):
            send(*first, turn, distance).wait_send()
            send(*second, turn, distance).wait_send()

    for copy in saves:
        copy.wait()


def middle(collective_id, ranks, grad_gate_up, w_gate_up, mixed, cotangent, w_out, hidden, w_down, gated, gain):
    rows, model = mixed.shape
    width = w_out.shape[1]
    blocks = pltpu.VMEM((ranks, rows, width), BF16)
    sems = pltpu.SemaphoreType.DMA((ranks - 1, ranks))
    return pl.pallas_call(
        functools.partial(middle_kernel, ranks),
        in_specs=[ANY] * 8 + [VMEM_WHOLE],
        out_specs=[VMEM_WHOLE] * 3 + [ANY] * 2,
        out_shape=[
            jax.ShapeDtypeStruct((rows, width), F32),
            jax.ShapeDtypeStruct((rows, width), F32),
            jax.ShapeDtypeStruct((8, model), F32),
            jax.ShapeDtypeStruct((rows, model), BF16),
            jax.ShapeDtypeStruct((model, width), BF16),
        ],
        scratch_shapes=[
            pltpu.VMEM(grad_gate_up.shape, BF16),
            pltpu.VMEM(w_gate_up.shape, BF16),
            pltpu.VMEM(mixed.shape, BF16),
            pltpu.VMEM(cotangent.shape, BF16),
            pltpu.VMEM(w_out.shape, BF16),
            pltpu.VMEM(hidden.shape, BF16),
            pltpu.VMEM(w_down.shape, BF16),
            pltpu.VMEM(gated.shape, BF16),
            pltpu.VMEM((rows, width), BF16),
            pltpu.VMEM((rows, model), BF16),
            pltpu.VMEM((model, width), BF16),
            pltpu.VMEM((rows // ranks, model), F32),
            blocks, blocks, blocks, blocks,
            pltpu.SemaphoreType.DMA((8,)),
            pltpu.SemaphoreType.DMA((2,)),
            sems, sems, sems, sems,
        ],
        compiler_params=pltpu.CompilerParams(
            collective_id=collective_id, has_side_effects=True, vmem_limit_bytes=VMEM_LIMIT
        ),
        cost_estimate=pl.CostEstimate(flops=0, bytes_accessed=150 << 20, transcendentals=0),
        name="middle",
    )(grad_gate_up, w_gate_up, mixed, cotangent, w_out, hidden, w_down, gated, gain)


def last_kernel(
    ranks,
    grad_project, w_in, inputs, aside, other, mixed_grad, gain, gain_two_grad, small,
    tokens_grad, total_sums, aside_all, other_all,
    grad_in, weight_in, inputs_in, wide, out, into, sums_out, sums_in,
    load_sem, send_sem, recv_sem, sums_send, sums_recv, aside_send, aside_recv, aside_own,
):
    rank = lax.axis_index("ctx")
    rows = inputs.shape[0] // ranks
    model, width = inputs.shape[1], mixed_grad.shape[1]
    tile = 256
    loads = [
        pltpu.make_async_copy(a, b, load_sem.at[n])
        for n, (a, b) in enumerate(((w_in, weight_in), (grad_project, grad_in), (inputs, inputs_in)))
    ]
    for copy in loads:
        copy.start()
    greet([{"ctx": rank ^ distance} for distance in range(1, ranks)])
    relays = [
        relay_ops("stack", rank, a, b, (aside_send.at[n], aside_recv.at[n], aside_own.at[n]))
        for n, (a, b) in enumerate(((aside, aside_all), (other, other_all)))
    ]
    relays[0].start()
    sums_out[...] = jnp.zeros_like(sums_out)
    sums_out[1:2, :] = gain_two_grad[0:1, :]
    sums_out[2:3, 0:LANES] = small[0:1, :]
    sums_out[2:3, LANES : 2 * LANES] = small[1:2, :]
    for index in range(ranks):
        sums_out[3 + index : 4 + index, 0:LANES] = jnp.where(rank == index, small[2:3, :], 0.0)
    for copy in loads:
        copy.wait()

    def send(distance):
        other = rank ^ distance
        return to_rank(out.at[other], into.at[distance], send_sem.at[distance - 1], recv_sem.at[distance - 1], other)

    def send_sums(distance):
        return to_rank(
            sums_out, sums_in.at[distance], sums_send.at[distance - 1], sums_recv.at[distance - 1], rank ^ distance
        )

    def compute(other):
        here = pl.ds(pl.multiple_of(other * rows, 16), rows)

        @pl.loop(0, model // tile)
        def _(step):
            cols = pl.ds(pl.multiple_of(step * tile, tile), tile)
            wide[:, cols] = right_product(grad_in[here, :], weight_in[cols, :])

        values = inputs_in[here, :].astype(F32)
        scale = rms_scale(values)
        grad = wide[...]
        sums_out[0:1, :] += jnp.sum(grad * values * scale, axis=0, keepdims=True)
        wide[...] = norm_back(grad, values, scale, gain[0:1, :])
        own = pl.ds(pl.multiple_of(rank * width, LANES), width)
        wide[:, own] += mixed_grad[here, :]
        out[other] = wide[...].astype(BF16)

    @pl.loop(1, ranks)
    def _(distance):
        compute(rank ^ distance)
        send(distance).start()

        @pl.when(distance == 1)
        def _():
            relays[0].forward()

        @pl.when(distance == 2)
        def _():
            relays[1].start()

    compute(rank)
    for distance in range(1, ranks):
        send_sums(distance).start()
    total = out[rank].astype(F32)
    for distance in range(1, ranks):
        send(distance).wait_recv()
        total = total + into[distance].astype(F32)
    tokens_grad[...] = total.astype(BF16)
    relays[1].forward()
    total = sums_out[...]
    for distance in range(1, ranks):
        send_sums(distance).wait_recv()
        total = total + sums_in[distance]
    total_sums[...] = total
    for distance in range(1, ranks):
        send(distance).wait_send()
        send_sums(distance).wait_send()
    for relay in relays:
        relay.finish()


def last_moves(
    collective_id, ranks, grad_project, w_in, inputs, aside, other, mixed_grad, gain, gain_two_grad, small
):
    rows, model = inputs.shape
    blocks = pltpu.VMEM((ranks, rows // ranks, model), BF16)
    sems = pltpu.SemaphoreType.DMA((ranks - 1,))
    return pl.pallas_call(
        functools.partial(last_kernel, ranks),
        in_specs=[ANY] * 5 + [VMEM_WHOLE] * 4,
        out_specs=[VMEM_WHOLE] * 2 + [ANY] * 2,
        out_shape=[
            jax.ShapeDtypeStruct((rows // ranks, model), BF16),
            jax.ShapeDtypeStruct((8, model), F32),
            jax.ShapeDtypeStruct((ranks,) + aside.shape, BF16),
            jax.ShapeDtypeStruct((ranks,) + other.shape, BF16),
        ],
        scratch_shapes=[
            pltpu.VMEM(grad_project.shape, BF16),
            pltpu.VMEM(w_in.shape, BF16),
            pltpu.VMEM(inputs.shape, BF16),
            pltpu.VMEM((rows // ranks, model), F32),
            blocks, blocks,
            pltpu.VMEM((8, model), F32),
            pltpu.VMEM((ranks, 8, model), F32),
            pltpu.SemaphoreType.DMA((3,)),
            sems, sems, sems, sems,
            pltpu.SemaphoreType.DMA((2, 6)),
            pltpu.SemaphoreType.DMA((2, 6)),
            pltpu.SemaphoreType.DMA((2, 2)),
        ],
        compiler_params=pltpu.CompilerParams(
            collective_id=collective_id, has_side_effects=True, vmem_limit_bytes=VMEM_LIMIT
        ),
        cost_estimate=pl.CostEstimate(flops=0, bytes_accessed=150 << 20, transcendentals=0),
        name="last_moves",
    )(grad_project, w_in, inputs, aside, other, mixed_grad, gain, gain_two_grad, small)


def spread_kernel(pieces, *refs):
    source, targets = refs[0], refs[1:]
    ranks = source.shape[0]
    for target, (piece, first, count) in zip(targets, pieces):
        for block in range(count):
            for index in range(ranks):
                target[:, pl.ds((block * ranks + index) * piece, piece)] = source[
                    index, :, pl.ds(first + block * piece, piece)
                ].astype(F32)


def spread_cols(source, *pieces):
    ranks, rows, cols = source.shape
    if any(piece % LANES or first % LANES for piece, first, _ in pieces):
        return [
            jnp.concatenate(
                [
                    source[c, :, first + i * piece : first + (i + 1) * piece]
                    for i in range(count)
                    for c in range(ranks)
                ],
                axis=1,
            ).astype(F32)
            for piece, first, count in pieces
        ]
    part = rows // 4 if rows % 64 == 0 else rows
    widths = [count * ranks * piece for piece, _, count in pieces]
    return pl.pallas_call(
        functools.partial(spread_kernel, pieces),
        grid=(rows // part,),
        in_specs=[pl.BlockSpec((ranks, part, cols), lambda step: (0, step, 0))],
        out_specs=[pl.BlockSpec((part, w), lambda step: (step, 0)) for w in widths],
        out_shape=[jax.ShapeDtypeStruct((rows, w), F32) for w in widths],
        compiler_params=pltpu.CompilerParams(vmem_limit_bytes=VMEM_LIMIT),
        cost_estimate=pl.CostEstimate(flops=0, bytes_accessed=rows * sum(widths) * 6, transcendentals=0),
        name="spread_cols",
    )(source)


class Native:
    def __init__(self, ranks):
        self.ranks = ranks

    def begin(self, tokens, cotangent, weight, tail, other, piece, width, padded):
        rank, model = lax.axis_index("ctx"), tokens.shape[1]
        parts = [lax.dynamic_slice_in_dim(weight, i * model + rank * width, width, 1) for i in range(4)]
        parts = [jnp.pad(part, ((0, 0), (0, padded - width))) for part in parts]
        cols = other.shape[1] // self.ranks
        picks = [
            lax.dynamic_slice_in_dim(other, (i * self.ranks + rank) * piece, piece, 1) for i in range(cols // piece)
        ]
        return (
            lax.all_gather(tokens, "ctx", axis=0, tiled=True),
            lax.all_gather(cotangent, "ctx", axis=0, tiled=True),
            lax.all_gather(jnp.concatenate(parts + [tail], axis=1), "fsdp", axis=0, tiled=True),
            jnp.concatenate(picks, axis=1),
        )

    def gather_cols(self, array, piece):
        return lax.all_gather(array, "ctx", axis=1, tiled=True), lax.all_gather(piece, "fsdp", axis=0, tiled=True)

    def stack(self, number, *arrays):
        return [lax.all_gather(a, "ctx", axis=0, tiled=False) for a in arrays]

    def finish(self, number, array, pieces, stats):
        return (
            lax.all_gather(array, "ctx", axis=0, tiled=False),
            lax.psum_scatter(pieces, "fsdp", scatter_dimension=0, tiled=False),
            lax.psum(stats, "ctx"),
        )


class Direct:
    def __init__(self, ranks, shards):
        self.ranks, self.shards = ranks, shards

    def run(self, number, *ops):
        return exchange(number, self.ranks, 0, self.shards, *ops)

    def stack(self, number, *arrays):
        return self.run(number, *[("stack" if a.dtype == BF16 else "each", a) for a in arrays])

    def finish(self, number, array, pieces, stats):
        out = exchange(
            number, self.ranks, self.shards, self.shards, ("stack", array), ("shards", pieces), ("each", stats)
        )
        return out[0], out[1].sum(axis=0), out[2].sum(axis=0)


def body(
    tokens, block_order, segment_ids, norm_gains, attn_in_weight, forget_weight, forget_bias,
    qk_gains, out_weight, gate_up_weight, down_weight, out_grad,
):
    ranks = lax.axis_size("ctx")
    shards = lax.axis_size("fsdp")
    rank = lax.axis_index("ctx")
    row_count, model_width = tokens.shape[1], tokens.shape[2]
    head_count, head_dim = forget_bias.shape[0], qk_gains.shape[1]
    local_heads = head_count // ranks
    width = local_heads * head_dim
    padded = -(-width // LANES) * LANES
    seq_order = block_order[0]
    seq_len = segment_ids.shape[1]
    block_len = seq_len // seq_order.shape[0]
    hidden_piece = down_weight.shape[0] // ranks
    hidden = hidden_piece * shards
    plain = ranks == 4 and shards & (shards - 1) == 0 and width == padded
    comm = Direct(ranks, shards) if plain else Native(ranks)

    def slab(array, start, size, axis):
        return lax.dynamic_slice_in_dim(array, start, size, axis)

    def widen(array):
        return jnp.pad(array, ((0, 0), (0, padded - width))) if padded > width else array

    if plain:
        (
            inputs, grad_low, w_in, w_out, w_gate_up, normed, project, gated_all, attended,
            wide_query, wide_key, wide_value, mixed_low, gain_rows, *places_all, bias, head_gains,
        ) = front(
            0, ranks, shards, head_dim, local_heads, width, hidden_piece,
            tokens[0], out_grad[0], attn_in_weight, out_weight, gate_up_weight, forget_weight, norm_gains, qk_gains,
            segment_ids, block_order, forget_bias[None],
        )
        gain_one, gain_two = gain_rows[0], gain_rows[1]
        w_down, normed_two, hidden_act, grad_gate_up, down_part_grad, gate_up_grad = ffn(
            1, ranks, shards, mixed_low, w_gate_up, grad_low, down_weight, gain_rows
        )
    else:
        tail = jnp.concatenate(
            [
                slab(forget_weight, rank * local_heads, local_heads, 1),
                norm_gains.T,
                jnp.zeros((attn_in_weight.shape[0], LANES - local_heads - 2), BF16),
            ],
            axis=1,
        )
        offsets = jnp.arange(block_len, dtype=jnp.int32)
        blocks = jnp.arange(seq_order.shape[0], dtype=jnp.int32)
        places = (seq_order[:, None] * block_len + offsets[None]).reshape(-1)
        by_block = segment_ids[0].reshape(-1, block_len)
        chosen = seq_order[:, None, None] == blocks[None, :, None]
        segments = jnp.sum(jnp.where(chosen, by_block[None], 0), axis=1).reshape(-1)
        places, segments = places.astype(F32), segments.astype(F32)
        places_all = (places[None, :], places[:, None], segments[None, :], segments[:, None])
        bias = jnp.pad(slab(forget_bias, rank * local_heads, local_heads, 0), (0, LANES - local_heads))[None]
        head_gains = jnp.tile(qk_gains, (1, LANES // head_dim))
        down_piece = slab(down_weight, rank * hidden_piece, hidden_piece, 0)
        inputs, grad_low, w_in, gate_up_piece = comm.begin(
            tokens[0], out_grad[0], attn_in_weight, tail, gate_up_weight, hidden_piece, width, padded
        )
        w_gate_up = lax.all_gather(gate_up_piece, "fsdp", axis=0, tiled=True)
        gain_cols = w_in[:, 4 * padded : 4 * padded + LANES].astype(F32).T
        gain_one = gain_cols[local_heads]
        gain_two = gain_cols[local_heads + 1]
        wide_inputs = inputs.astype(F32)
        scale_one = rms_scale(wide_inputs)
        normed = (wide_inputs * scale_one * gain_one).astype(BF16)
        project = dot(normed, w_in)
        gated, attended, wide_query, wide_key, wide_value = attend(
            project, places_all, bias, head_gains, head_dim, padded, local_heads
        )
        gated_all, w_out = comm.gather_cols(gated[:, :width], slab(out_weight, rank * width, width, 1))
        mixed_cols = slab(inputs, rank * width, width, 1).astype(F32) + dot(gated_all, w_out)
        mixed_low, w_down = comm.gather_cols(mixed_cols.astype(BF16), down_piece)
        mixed = mixed_low.astype(F32)
        scale_two = rms_scale(mixed)
        normed_two = (mixed * scale_two * gain_two).astype(BF16)
        gate_up = dot(normed_two, w_gate_up)
        gate_part, up_part = gate_up[:, :hidden], gate_up[:, hidden:]
        gate_sigmoid = jax.nn.sigmoid(gate_part)
        silu = gate_part * gate_sigmoid
        hidden_act = (silu * up_part).astype(BF16)
        grad_hidden = right_product(grad_low, w_down)
        grad_gate = grad_hidden * up_part * gate_sigmoid * (1.0 + gate_part * (1.0 - gate_sigmoid))
        grad_gate_up = jnp.concatenate([grad_gate, grad_hidden * silu], axis=1).astype(BF16)
        down_part_grad = left_product(hidden_act, grad_low).astype(BF16)
        gate_up_grad = left_product(normed_two, grad_gate_up).astype(BF16)
        down_part = dot(hidden_act, w_down).astype(BF16)

    def own_rows(array):
        return slab(array, rank * row_count, row_count, 0)

    def reduce_shards(array):
        return lax.psum_scatter(array.astype(BF16), "fsdp", scatter_dimension=0, tiled=True)

    grad_gate_up, down_part_grad, gate_up_grad = lax.optimization_barrier(
        (grad_gate_up, down_part_grad, gate_up_grad)
    )
    down_share = reduce_shards(down_part_grad)
    gate_up_share = reduce_shards(gate_up_grad)
    if plain:
        grad_mixed_cols, grad_gated, gain_two_grad, down_part, out_part = middle(
            3, ranks, grad_gate_up, w_gate_up, mixed_low, grad_low, w_out, hidden_act, w_down, gated_all, gain_two[None]
        )
    else:
        grad_normed_two = right_product(grad_gate_up, w_gate_up)
        gain_two_grad = jnp.sum(grad_normed_two * mixed * scale_two, axis=0)
        grad_mixed_part = norm_back(grad_normed_two, mixed, scale_two, gain_two).astype(BF16)
        grad_mixed_cols = slab(grad_low, rank * width, width, 1).astype(F32) + lax.psum_scatter(
            grad_mixed_part, "ctx", scatter_dimension=1, tiled=True
        ).astype(F32)
        grad_branch = grad_mixed_cols.astype(BF16)
        grad_gated = widen(
            lax.psum_scatter(
                right_product(grad_branch, w_out).astype(BF16), "ctx", scatter_dimension=1, tiled=True
            ).astype(F32)
        )
    grad_gated, down_share = lax.optimization_barrier((grad_gated, down_share))
    grad_project, small, *rest = attend_back(
        project, places_all, bias, head_gains, attended, (wide_query, wide_key, wide_value),
        grad_gated, (down_part, normed, out_part) if plain else (), ranks if plain else 0, head_dim, padded, local_heads,
    )
    if plain:
        down_pieces, late = rest
    else:
        in_part = left_product(normed, grad_project).astype(BF16)
        out_part = left_product(gated_all, grad_branch).astype(BF16)
        late = jnp.concatenate([in_part[:, : 4 * padded], out_part, in_part[:, 4 * padded :]], axis=1)
    late, gate_up_share = lax.optimization_barrier((late, gate_up_share))
    late_share = reduce_shards(late)

    if plain:
        down_sum = down_pieces.astype(F32).sum(axis=0)
        tokens_grad, sums, down_own, gate_up_own = last_moves(
            4, ranks, grad_project, w_in, inputs, down_share, gate_up_share, grad_mixed_cols, gain_one[None],
            gain_two_grad, small,
        )
        tokens_grad = tokens_grad[None]
    else:
        grad_normed = right_product(grad_project, w_in)
        gain_one_grad = jnp.sum(grad_normed * wide_inputs * scale_one, axis=0)
        in_own = jnp.arange(model_width, dtype=jnp.int32) // width == rank
        grad_inputs = norm_back(grad_normed, wide_inputs, scale_one, gain_one) + jnp.where(
            in_own[None], jnp.tile(grad_mixed_cols, (1, ranks)), 0.0
        )
        down_sum = lax.psum_scatter(down_part, "ctx", scatter_dimension=0, tiled=True).astype(F32)
        tokens_grad = lax.psum_scatter(grad_inputs.astype(BF16), "ctx", scatter_dimension=0, tiled=True)[None]
        own_bias = jnp.where(jnp.arange(ranks, dtype=jnp.int32)[:, None] == rank, small[2:3], 0.0)
        small_rows = jnp.concatenate([small[0:2].reshape(1, -1), jnp.pad(own_bias, ((0, 0), (0, LANES)))], axis=0)
        sums = jnp.concatenate(
            [
                jnp.stack([gain_one_grad, gain_two_grad]),
                jnp.pad(small_rows, ((0, 0), (0, model_width - 2 * LANES))),
            ],
            axis=0,
        )
        sums = lax.psum(sums, "ctx")
        down_own = lax.all_gather(down_share, "ctx", axis=0, tiled=False)
        gate_up_own = lax.all_gather(gate_up_share, "ctx", axis=0, tiled=False)
    result = own_rows(mixed_low).astype(F32) + down_sum
    block_out = result.astype(BF16)[None]
    branch = result - own_rows(inputs).astype(F32)
    own_valid = own_rows(places_all[3][:, 0] >= 0).astype(F32)
    partial_sums = jnp.stack(
        [
            jnp.sum(own_valid * jnp.sum(result * result, axis=-1)),
            jnp.sum(own_valid * jnp.sum(branch * branch, axis=-1)),
        ]
    )
    valid_count = jnp.sum((segment_ids[0] >= 0).astype(F32)) * model_width

    down_out = down_own.astype(F32).reshape(down_weight.shape)
    gate_up_out = spread_cols(gate_up_own, (hidden_piece, 0, 2 * shards))[0]
    share = model_width // shards
    room = -(-share // LANES) * LANES
    gain_pieces = jnp.pad(sums[0:2].reshape(2, shards, share).transpose(1, 0, 2), ((0, 0), (0, 0), (0, room - share)))
    tail = jnp.broadcast_to(sums[None, 2 : 3 + ranks, : 2 * LANES], (shards, 1 + ranks, 2 * LANES))
    tail = jnp.pad(tail, ((0, 0), (0, 0), (0, max(room - 2 * LANES, 0))))
    gain_pieces = jnp.pad(gain_pieces, ((0, 0), (0, 0), (0, max(2 * LANES - room, 0))))
    pieces = jnp.concatenate([gain_pieces, tail], axis=1)
    pieces = jnp.pad(pieces, ((0, 0), (0, -pieces.shape[1] % 8), (0, 0)))
    stats = jnp.broadcast_to(jnp.pad(partial_sums, (0, LANES - 2)), (8, LANES))
    late_own, piece_sum, stats = comm.finish(7, late_share, pieces, stats)
    if plain:
        in_out, out_out = spread_cols(late_own, (width, 0, 4), (width, 4 * width, 1))
    else:
        in_out = jnp.concatenate(
            [late_own[c, :, i * padded : i * padded + width] for i in range(4) for c in range(ranks)], axis=1
        ).astype(F32)
        out_out = jnp.concatenate(
            [late_own[c, :, 4 * padded : 4 * padded + width] for c in range(ranks)], axis=1
        ).astype(F32)
    last = 4 * padded + width
    forget_out = jnp.concatenate([late_own[c, :, last : last + local_heads] for c in range(ranks)], axis=1).astype(F32)
    gains_sum = piece_sum[0:2, :share]
    bias_sum = piece_sum[3 : 3 + ranks, :local_heads].reshape(-1)
    qk_sum = piece_sum[2, : 2 * LANES].reshape(2, LANES // head_dim, head_dim).sum(axis=1)
    totals = stats[0, :2]
    return (
        block_out, tokens_grad, gains_sum, in_out, forget_out, bias_sum, qk_sum,
        out_out, gate_up_out, down_out, jnp.sqrt(totals / valid_count)[None],
    )


def solution(mesh):
    rows = P("fsdp", "ctx", None)
    return jax.shard_map(
        body,
        mesh=mesh,
        in_specs=(
            rows, P("fsdp", None), P("fsdp", None), P(None, "fsdp"), P("fsdp", None), P("fsdp", None),
            P(), P(), P("fsdp", None), P("fsdp", None), P("fsdp", None), rows,
        ),
        out_specs=(
            rows, rows, P(None, "fsdp"), P("fsdp", None), P("fsdp", None), P(), P(),
            P("fsdp", None), P("fsdp", None), P("fsdp", None), P("fsdp", None),
        ),
        check_vma=False,
    )
```

```python
import functools
import math

import jax
import jax.numpy as jnp
from jax import lax
from jax.experimental import pallas as pl
from jax.experimental.pallas import tpu as pltpu
from jax.sharding import PartitionSpec as P

EPS = 1e-06
SCALE = 0.125
LANES = 128
VMEM_LIMIT = 60 << 20
F32 = jnp.float32
BF16 = jnp.bfloat16


MESH = pl.DeviceIdType.MESH
ANY = pl.BlockSpec(memory_space=pltpu.HBM)


def rms_scale(values):
    return lax.rsqrt(jnp.mean(values * values, axis=-1, keepdims=True) + EPS)


def norm_back(grad_normed, values, scale_values, gain_values):
    scaled = grad_normed * gain_values
    cubed = scale_values * scale_values * scale_values
    return scale_values * scaled - values * cubed * jnp.mean(
        scaled * values, axis=-1, keepdims=True
    )


def dot(left, right):
    return lax.dot_general(
        left, right, (((1,), (0,)), ((), ())), preferred_element_type=F32
    )


def left_product(left, right):
    return lax.dot_general(
        left, right, (((0,), (0,)), ((), ())), preferred_element_type=F32
    )


def right_product(left, right):
    return lax.dot_general(
        left, right, (((1,), (1,)), ((), ())), preferred_element_type=F32
    )


def split_three(values):
    high = values.astype(BF16).astype(F32)
    rest = values - high
    middle = rest.astype(BF16).astype(F32)
    return high, middle, rest - middle


def lane_ids(rows, lanes=LANES):
    return lax.broadcasted_iota(jnp.int32, (rows, lanes), 1)


def pick_lane(values, lanes, index):
    return jnp.sum(jnp.where(lanes == index, values, 0.0), axis=-1, keepdims=True)


def turns(rows, chunk, unroll=False):
    def decorate(body):
        @pl.loop(0, rows // chunk, unroll=rows // chunk if unroll else None)
        def _(turn):
            body(pl.ds(pl.multiple_of(turn * chunk, chunk), chunk))

    return decorate


def fill_mask(chunk, pos_row, pos_col, seg_row, seg_col, mask):
    @turns(mask.shape[0], chunk)
    def _(part):
        allowed = (pos_row[0:1, :] <= pos_col[part, :]) & (seg_row[0:1, :] == seg_col[part, :])
        mask[part, :] = jnp.where(allowed, 0.0, -jnp.inf)


def fill_prefix(chunk, heads, pos_row, pos_col, logits, prefix):
    rows = prefix.shape[0]
    log_forget = jax.nn.log_sigmoid(jnp.where(lane_ids(rows) < heads, logits, 0.0))
    high, middle, low = split_three(log_forget)

    @turns(rows, chunk)
    def _(part):
        before = jnp.where(pos_row[0:1, :] <= pos_col[part, :], 1.0, 0.0).astype(BF16)
        prefix[part, :] = (
            dot(before, high.astype(BF16)) + dot(before, middle.astype(BF16)) + dot(before, low.astype(BF16))
        )


def attend_block(
    head, chunk, index, query, key, value, gate, gains, mask, prefix,
    gated, attended, wide_query, wide_key, wide_value,
):
    rows = mask.shape[0]
    lanes = lane_ids(rows)
    half = lane_ids(rows, head)
    short = lane_ids(chunk, head)
    for side in range(LANES // head):
        here = slice(side * head, (side + 1) * head)
        column = pick_lane(prefix[...], lanes, (LANES // head) * index + side)
        high, middle, low = split_three(column)
        wide = jnp.where(half == 1, high, 0.0)
        wide = jnp.where(half == 2, middle, wide)
        wide = jnp.where(half == 3, low, wide)
        query_rest = jnp.where((half >= 4) & (half < 7), 1.0, wide)
        wide = jnp.where(half == 4, -high, 0.0)
        wide = jnp.where(half == 5, -middle, wide)
        wide = jnp.where(half == 6, -low, wide)
        ones = ((half >= 1) & (half < 4)) | ((half >= 7) & (half < 10))
        key_rest = jnp.where(ones, 1.0, wide)
        raw = query[:, here]
        normed = (raw * rms_scale(raw) * gains[0:1, here]).astype(BF16)
        wide_query[side, :, 0:head] = (normed.astype(F32) * SCALE).astype(BF16)
        wide_query[side, :, head:LANES] = query_rest.astype(BF16)
        raw = key[:, here]
        wide_key[side, :, 0:head] = (raw * rms_scale(raw) * gains[1:2, here]).astype(BF16)
        wide_key[side, :, head:LANES] = key_rest.astype(BF16)
        wide_value[side, :, 0:head] = value[:, here].astype(BF16)
        wide_value[side, :, head:LANES] = jnp.where(half < 3, 1.0, 0.0).astype(BF16)

        @turns(rows, chunk, unroll=True)
        def _(part):
            scores = right_product(wide_query[side, part, :], wide_key[side]) + mask[part, :]
            expos = jnp.exp(scores)
            total = jnp.sum(expos, axis=-1, keepdims=True)
            result = dot(expos.astype(BF16), wide_value[side])[:, 0:head] / total
            attended[part, here] = result
            gated[part, here] = (result * jax.nn.sigmoid(gate(part)[:, here])).astype(BF16)
            high, middle, low = split_three(-jnp.log(total))
            rest = wide_query[side, part, head:LANES].astype(F32)
            rest = jnp.where(short == 7, high, rest)
            rest = jnp.where(short == 8, middle, rest)
            rest = jnp.where(short == 9, low, rest)
            wide_query[side, part, head:LANES] = rest.astype(BF16)


def attend_kernel(
    head, chunk, heads,
    pos_row, pos_col, seg_row, seg_col, bias, gains, query, key, value, gate, forget,
    gated, attended, wide_query, wide_key, wide_value,
    mask, prefix,
):
    @pl.when(pl.program_id(0) == 0)
    def _():
        fill_mask(chunk, pos_row, pos_col, seg_row, seg_col, mask)
        fill_prefix(chunk, heads, pos_row, pos_col, forget[...] + bias[0:1, :], prefix)

    attend_block(
        head, chunk, pl.program_id(0), query, key, value, lambda part: gate[part, :], gains, mask, prefix,
        gated, attended.at[0], wide_query, wide_key, wide_value,
    )


def attend_back_kernel(
    head, chunk, width, heads, ranks,
    pos_row, pos_col, seg_row, seg_col, bias, gains, query, key, gate, forget,
    attended, wide_query, wide_key, wide_value, grad_gated, *rest,
):
    if ranks:
        aside, normed, out_grad, grad_project, small, aside_in, late = rest[:7]
        mask, wide_grad, grad_query, grad_key, grad_value, grad_prefix = rest[7:13]
        normed_in, out_in, aside_own, late_all, load_sem, save_sem = rest[13:19]
        sems = rest[19:]

        def loads():
            own = rows_of(aside, lax.axis_index("ctx"), aside_in.shape[1])
            for n, pair in enumerate(((normed, normed_in), (out_grad, out_in), (own, aside_own))):
                yield pltpu.make_async_copy(*pair, load_sem.at[n])

    else:
        grad_project, small, mask, wide_grad, grad_query, grad_key, grad_value, grad_prefix = rest
    step = pl.program_id(0)
    steps = pl.num_programs(0)

    def aside_copies():
        send_sem, recv_sem = sems
        rank = lax.axis_index("ctx")
        size = aside_in.shape[1]
        for distance in range(1, ranks):
            other = rank ^ distance
            yield to_rank(
                rows_of(aside, other, size), aside_in.at[rank],
                send_sem.at[distance - 1], recv_sem.at[distance - 1], other,
            )

    if ranks:

        @pl.when(step == 0)
        def _():
            rank = lax.axis_index("ctx")
            greet([{"ctx": rank ^ distance} for distance in range(1, ranks)])
            for copy in aside_copies():
                copy.start()
            for copy in loads():
                copy.start()

    rows = query.shape[0]
    lanes = lane_ids(rows)
    half = lane_ids(rows, head)

    @pl.when(step == 0)
    def _():
        @pl.loop(0, rows // chunk)
        def _(turn):
            part = pl.ds(pl.multiple_of(turn * chunk, chunk), chunk)
            after = pos_row[0:1, :] >= pos_col[part, :]
            same = seg_row[0:1, :] == seg_col[part, :]
            mask[part, :] = jnp.where(after & same, 0.0, -jnp.inf)
        grad_prefix[...] = jnp.zeros_like(grad_prefix)
        small[...] = jnp.zeros_like(small)

    for side in range(LANES // head):
        here = pl.ds(side * head, head)

        def column(part):
            return pl.ds(pl.multiple_of(part * width + step * LANES, LANES), LANES)

        sig = jax.nn.sigmoid(gate[:, here])
        grad_in = grad_gated[:, here]
        result = attended[0, :, here]
        grad_result = (grad_in * sig).astype(BF16)
        grad_gate = (grad_in * result * sig * (1.0 - sig)).astype(BF16)
        inner = -jnp.sum(grad_result.astype(F32) * result, axis=-1, keepdims=True)
        high, middle, low = split_three(inner)
        rest = jnp.where(half == 0, high, 0.0)
        rest = jnp.where(half == 1, middle, rest)
        rest = jnp.where(half == 2, low, rest)
        wide_grad[:, 0:head] = grad_result
        wide_grad[:, head:LANES] = rest.astype(BF16)
        grad_query[...] = jnp.zeros_like(grad_query)
        @turns(rows, chunk, unroll=True)
        def _(part):
            scores = right_product(wide_key[side, part, :], wide_query[side]) + mask[part, :]
            probs = jnp.exp(scores)
            outer = right_product(wide_value[side, part, :], wide_grad[...])
            grad_scores = (probs * outer).astype(BF16)
            grad_key[part, :] = dot(grad_scores, wide_query[side])
            grad_value[part, :] = dot(probs.astype(BF16), wide_grad[...])
            grad_query[...] += left_product(grad_scores, wide_key[side, part, :])
        from_query = grad_query[...]
        from_key = grad_key[...]
        change = pick_lane(from_query, lanes, head + 1) - pick_lane(from_key, lanes, head + 4)
        grad_prefix[...] += jnp.where(lanes == (LANES // head) * step + side, change, 0.0)

        raw = query[:, here]
        scale_raw = rms_scale(raw)
        grad_normed = from_query[:, 0:head] * SCALE
        grad_raw_query = norm_back(grad_normed, raw, scale_raw, gains[0:1, here])
        small[0:1, here] += jnp.sum(grad_normed * raw * scale_raw, axis=0, keepdims=True)
        raw = key[:, here]
        scale_raw = rms_scale(raw)
        grad_normed = from_key[:, 0:head]
        grad_raw_key = norm_back(grad_normed, raw, scale_raw, gains[1:2, here])
        small[1:2, here] += jnp.sum(grad_normed * raw * scale_raw, axis=0, keepdims=True)
        wide_grad[:, here] = grad_gate
        for part_id, piece in enumerate(
            (grad_raw_query.astype(BF16), grad_raw_key.astype(BF16), grad_value[:, 0:head].astype(BF16), grad_gate)
        ):
            if side == 0:
                grad_project[:, column(part_id)] = jnp.concatenate([piece, piece], axis=1)
            else:
                keep = grad_project[:, column(part_id)]
                both = jnp.concatenate([piece, piece], axis=1)
                grad_project[:, column(part_id)] = jnp.where(lanes < head, keep, both)

    @pl.when(step == steps - 1)
    def _():
        high, middle, low = split_three(grad_prefix[...])
        short = lane_ids(chunk)

        @pl.loop(0, rows // chunk)
        def _(turn):
            part = pl.ds(pl.multiple_of(turn * chunk, chunk), chunk)
            after = jnp.where(pos_row[0:1, :] >= pos_col[part, :], 1.0, 0.0).astype(BF16)
            total = dot(after, high.astype(BF16)) + dot(after, middle.astype(BF16)) + dot(after, low.astype(BF16))
            grad_logit = total * jax.nn.sigmoid(-(forget[part, :] + bias[0:1, :]))
            grad_logit = jnp.where(short < heads, grad_logit, 0.0).astype(BF16)
            grad_project[part, 4 * width : 4 * width + LANES] = grad_logit
            small[2:3, :] += jnp.sum(grad_logit.astype(F32), axis=0, keepdims=True)

        if ranks:
            for copy in loads():
                copy.wait()
            keep = pltpu.make_async_copy(aside_own, aside_in.at[lax.axis_index("ctx")], load_sem.at[3])
            keep.start()
            ends = 4 * width, 4 * width + out_grad.shape[1]
            late_all[:, ends[0] : ends[1]] = out_in[...]
            piece = 2 * LANES

            def save(turn, size=piece):
                cols = pl.ds(pl.multiple_of(turn * piece, LANES), size)
                return pltpu.make_async_copy(late_all.at[:, cols], late.at[:, cols], save_sem.at[turn])

            count = 4 * width // piece
            rest_save = pltpu.make_async_copy(
                late_all.at[:, pl.ds(ends[0], late.shape[1] - ends[0])],
                late.at[:, pl.ds(ends[0], late.shape[1] - ends[0])],
                save_sem.at[count],
            )

            def product(into, cols):
                @turns(late.shape[0], 3 * chunk if late.shape[0] % (3 * chunk) == 0 else chunk)
                def _(part):
                    late_all[part, into] = dot(normed_in[part, :], grad_project[:, cols]).astype(BF16)

            product(slice(ends[1], ends[1] + LANES), slice(ends[0], ends[0] + LANES))
            rest_save.start()

            @pl.loop(0, count)
            def _(turn):
                cols = pl.ds(pl.multiple_of(turn * piece, LANES), piece)
                product(cols, cols)
                save(turn).start()

            for copy in aside_copies():
                copy.wait()
            keep.wait()
            rest_save.wait()

            @pl.loop(0, count)
            def _(turn):
                save(turn).wait()


def pick_chunk(rows):
    return 256 if rows % 256 == 0 else 128


def whole(shape):
    return pl.BlockSpec(shape, lambda step: tuple(0 for _ in shape))


def attend(project, places, bias, gains, head, width, heads):
    rows = project.shape[0]
    steps = width // LANES
    per = LANES // head
    chunk = pick_chunk(rows)

    def part(index):
        return pl.BlockSpec((rows, LANES), lambda step: (0, index * steps + step))

    own = pl.BlockSpec((rows, LANES), lambda step: (0, step))
    wide = pl.BlockSpec((per, rows, LANES), lambda step: (step, 0, 0))
    forget = pl.BlockSpec((rows, LANES), lambda step: (0, 4 * steps))
    wide_shape = jax.ShapeDtypeStruct((per * steps, rows, LANES), BF16)
    return pl.pallas_call(
        functools.partial(attend_kernel, head, chunk, heads),
        grid=(steps,),
        in_specs=[whole(p.shape) for p in places] + [whole(bias.shape), whole(gains.shape)]
        + [part(0), part(1), part(2), part(3), forget],
        out_specs=[own, pl.BlockSpec((1, rows, LANES), lambda step: (step, 0, 0)), wide, wide, wide],
        out_shape=[
            jax.ShapeDtypeStruct((rows, width), BF16),
            jax.ShapeDtypeStruct((steps, rows, LANES), F32),
            wide_shape, wide_shape, wide_shape,
        ],
        scratch_shapes=[pltpu.VMEM((rows, rows), F32), pltpu.VMEM((rows, LANES), F32)],
        compiler_params=pltpu.CompilerParams(vmem_limit_bytes=VMEM_LIMIT),
        name="attend",
    )(*places, bias, gains, project, project, project, project, project)


def attend_back(project, places, bias, gains, attended, wides, grad_gated, beside, ranks, head, width, heads):
    rows = project.shape[0]
    steps = width // LANES
    per = LANES // head
    chunk = pick_chunk(rows)

    def part(index):
        return pl.BlockSpec((rows, LANES), lambda step: (0, index * steps + step))

    own = pl.BlockSpec((rows, LANES), lambda step: (0, step))
    block = pl.BlockSpec((1, rows, LANES), lambda step: (step, 0, 0))
    wide = pl.BlockSpec((per, rows, LANES), lambda step: (step, 0, 0))
    forget = pl.BlockSpec((rows, LANES), lambda step: (0, 4 * steps))
    total = 4 * width + LANES
    out_specs = [whole((rows, total)), whole((8, LANES))]
    out_shape = [jax.ShapeDtypeStruct((rows, total), BF16), jax.ShapeDtypeStruct((8, LANES), F32)]
    scratch = [
        pltpu.VMEM((rows, rows), F32),
        pltpu.VMEM((rows, LANES), BF16),
        pltpu.VMEM((rows, LANES), F32),
        pltpu.VMEM((rows, LANES), F32),
        pltpu.VMEM((rows, LANES), F32),
        pltpu.VMEM((rows, LANES), F32),
    ]
    if ranks:
        aside, normed, out_grad = beside
        model, late_cols = normed.shape[0], total + out_grad.shape[1]
        out_specs += [ANY, ANY]
        out_shape += [
            jax.ShapeDtypeStruct((ranks, aside.shape[0] // ranks, aside.shape[1]), BF16),
            jax.ShapeDtypeStruct((model, late_cols), BF16),
        ]
        scratch += [
            pltpu.VMEM(normed.shape, BF16),
            pltpu.VMEM(out_grad.shape, BF16),
            pltpu.VMEM((aside.shape[0] // ranks, aside.shape[1]), BF16),
            pltpu.VMEM((model, late_cols), BF16),
            pltpu.SemaphoreType.DMA((4,)),
            pltpu.SemaphoreType.DMA((4 * width // (2 * LANES) + 1,)),
            pltpu.SemaphoreType.DMA((ranks - 1,)),
            pltpu.SemaphoreType.DMA((ranks - 1,)),
        ]
    return pl.pallas_call(
        functools.partial(attend_back_kernel, head, chunk, width, heads, ranks),
        grid=(steps,),
        in_specs=[whole(p.shape) for p in places] + [whole(bias.shape), whole(gains.shape)]
        + [part(0), part(1), part(3), forget, block, wide, wide, wide, own] + [ANY] * len(beside),
        out_specs=out_specs,
        out_shape=out_shape,
        scratch_shapes=scratch,
        compiler_params=pltpu.CompilerParams(
            collective_id=5 if ranks else None, has_side_effects=ranks > 0, vmem_limit_bytes=VMEM_LIMIT
        ),
        name="attend_back",
    )(*places, bias, gains, project, project, project, project, attended, *wides, grad_gated, *beside)


def greet(peers, line=None):
    barrier = pltpu.get_barrier_semaphore()
    if line is not None:
        peers = peers + [line.sibling]
    for peer in peers:
        pl.semaphore_signal(barrier, inc=1, device_id=peer, device_id_type=MESH)
    if line is not None:
        for there, peer in ((line.has_above, line.above), (line.has_below, line.below)):

            @pl.when(there)
            def _():
                pl.semaphore_signal(barrier, inc=1, device_id=peer, device_id_type=MESH)

    count = len(peers)
    if line is not None:
        last = line.layers - 1
        count = count + (1 - line.layer // last) + (line.layer + last) // line.layers
    pl.semaphore_wait(barrier, count)


class Line:
    def __init__(self, shards, source, target, sems):
        self.shard = lax.axis_index("fsdp")
        self.layers = shards // 2
        self.layer, self.core = self.shard // 2, self.shard % 2
        self.sibling = {"fsdp": self.shard ^ 1}
        self.above, self.below = {"fsdp": self.shard + 2}, {"fsdp": self.shard - 2}
        self.has_above, self.has_below = self.layer < self.layers - 1, self.layer > 0
        self.source, self.target = source, target
        self.rows = target.shape[0] // shards
        self.line_send, self.line_recv, self.side_send, self.side_recv, self.own_sem = sems

    def block(self, owner):
        return rows_of(self.target, owner, self.rows)

    def line(self, owner_layer, peer, way, own=False):
        here = self.block(owner_layer * 2 + self.core)
        return pltpu.make_async_remote_copy(
            self.source if own else here, here, self.line_send.at[way, owner_layer], self.line_recv.at[owner_layer],
            device_id=peer, device_id_type=MESH,
        )

    def side(self, owner_layer, owner_core, own=False):
        here = self.block(owner_layer * 2 + owner_core)
        return pltpu.make_async_remote_copy(
            self.source if own else here, here, self.side_send.at[owner_layer], self.side_recv.at[owner_layer],
            device_id=self.sibling, device_id_type=MESH,
        )

    def start(self):
        own = self.source is not None

        @pl.when(self.has_above)
        def _():
            self.line(self.layer, self.above, 0, own).start()

        @pl.when(self.has_below)
        def _():
            self.line(self.layer, self.below, 1, own).start()

        self.side(self.layer, self.core, own).start()
        if own:
            self.keep = pltpu.make_async_copy(self.source, self.block(self.shard), self.own_sem)
            self.keep.start()

    def step(self, distance):
        lower, upper = self.layer - distance, self.layer + distance

        @pl.when(lower >= 0)
        def _():
            self.line(lower, self.below, 1).wait_recv()

            @pl.when(self.has_above)
            def _():
                self.line(lower, self.above, 0).start()

            self.side(lower, self.core).start()

        @pl.when(upper < self.layers)
        def _():
            self.line(upper, self.above, 0).wait_recv()

            @pl.when(self.has_below)
            def _():
                self.line(upper, self.below, 1).start()

            self.side(upper, self.core).start()

    def from_side(self, owner_layer):
        self.side(owner_layer, 1 - self.core).wait_recv()

    def finish(self):
        self.keep.wait()
        for owner_layer in range(self.layers):
            self.from_side(owner_layer)
        self.sent()

    def sent(self):
        for owner_layer in range(self.layers):
            self.side(owner_layer, self.core).wait_send()

            @pl.when(self.has_above & (owner_layer <= self.layer))
            def _():
                self.line(owner_layer, self.above, 0).wait_send()

            @pl.when(self.has_below & (owner_layer >= self.layer))
            def _():
                self.line(owner_layer, self.below, 1).wait_send()

    def near_finish(self):
        self.keep.wait()
        self.from_side(self.layer)
        self.side(self.layer, self.core).wait_send()

        @pl.when(self.has_below)
        def _():
            self.line(self.layer - 1, self.below, 1).wait_recv()
            self.line(self.layer, self.below, 1).wait_send()

        @pl.when(self.has_above)
        def _():
            self.line(self.layer + 1, self.above, 0).wait_recv()
            self.line(self.layer, self.above, 0).wait_send()

    def near_load(self, near, sems, number):
        if number == 0:
            chip = 2 * self.rows
            source, target = rows_of(near, self.layer, chip), rows_of(self.target, self.layer, chip)
        else:
            owner = self.shard + (-2, 2)[number - 1]
            source, target = rows_of(near, owner, self.rows), self.block(owner)
        return pltpu.make_async_copy(source, target, sems.at[number])

    def near_start(self, near, sems):
        self.near_load(near, sems, 0).start()

        @pl.when(self.has_below)
        def _():
            self.near_load(near, sems, 1).start()

        @pl.when(self.has_above)
        def _():
            self.near_load(near, sems, 2).start()

    def resume(self, near, sems):
        @pl.when(self.has_below)
        def _():
            self.near_load(near, sems, 1).wait()

            @pl.when(self.has_above)
            def _():
                self.line(self.layer - 1, self.above, 0).start()

            self.side(self.layer - 1, self.core).start()

        @pl.when(self.has_above)
        def _():
            self.near_load(near, sems, 2).wait()

            @pl.when(self.has_below)
            def _():
                self.line(self.layer + 1, self.below, 1).start()

            self.side(self.layer + 1, self.core).start()

    def resumed_sent(self):
        for owner_layer in range(self.layers):

            @pl.when(owner_layer != self.layer)
            def _():
                self.side(owner_layer, self.core).wait_send()

            @pl.when(self.has_above & (owner_layer < self.layer))
            def _():
                self.line(owner_layer, self.above, 0).wait_send()

            @pl.when(self.has_below & (owner_layer > self.layer))
            def _():
                self.line(owner_layer, self.below, 1).wait_send()


def line_scratch(shards):
    layers = shards // 2
    return [
        pltpu.SemaphoreType.DMA((2, layers)),
        pltpu.SemaphoreType.DMA((layers,)),
        pltpu.SemaphoreType.DMA((layers,)),
        pltpu.SemaphoreType.DMA((layers,)),
        pltpu.SemaphoreType.DMA,
    ]


class Relay:
    def __init__(self, rank, source, place, send_sem, recv_sem, own_sem):
        self.rank, self.source, self.place = rank, source, place
        self.send_sem, self.recv_sem, self.own_sem = send_sem, recv_sem, own_sem

    def copy(self, number):
        me = self.rank
        source, place, distance = (
            lambda: (self.source(0), self.place(me, 0), 1),
            lambda: (self.source(1), self.place(me, 1), 2),
            lambda: (self.source(1), self.place(me, 1), 1),
            lambda: (self.source(0), self.place(me, 0), 2),
            lambda: (self.place(me ^ 1, 0), self.place(me ^ 1, 0), 2),
            lambda: (self.place(me ^ 2, 1), self.place(me ^ 2, 1), 1),
        )[number]()
        return pltpu.make_async_remote_copy(
            source, place, self.send_sem.at[number], self.recv_sem.at[number],
            device_id={"ctx": me ^ distance}, device_id_type=MESH,
        )

    def own(self, h):
        return pltpu.make_async_copy(self.source(h), self.place(self.rank, h), self.own_sem.at[h])

    def start(self, keep=True):
        for number in range(4):
            self.copy(number).start()
        if keep:
            for h in range(2):
                self.own(h).start()

    def forward(self):
        for number in range(2):
            self.copy(number).wait_recv()
            self.copy(number + 4).start()

    def arrive(self):
        for number in range(2, 6):
            self.copy(number).wait_recv()

    def finish(self, arrive=True, keep=True):
        if keep:
            for h in range(2):
                self.own(h).wait()
        if arrive:
            self.arrive()
        for number in range(6):
            self.copy(number).wait_send()


def rows_of(ref, index, size):
    return ref.at[pl.ds(pl.multiple_of(index * size, 16), size), :]


def cols_of(ref, index, size):
    return ref.at[:, pl.ds(pl.multiple_of(index * size, LANES), size)]


def relay_ops(mode, rank, source, target, sems):
    rows, cols = source.shape
    half = rows // 2

    def part(h):
        return source.at[pl.ds(h * half, half), :]

    def place(block, h):
        if mode == "gather_rows":
            return target.at[pl.ds(pl.multiple_of(block * rows + h * half, 16), half), :]
        if mode == "gather_cols":
            return target.at[pl.ds(h * half, half), pl.ds(pl.multiple_of(block * cols, LANES), cols)]
        return target.at[block, pl.ds(h * half, half), :]

    return Relay(rank, part, place, *sems)


VMEM_WHOLE = pl.BlockSpec(memory_space=pltpu.VMEM)


def to_rank(source, target, send, recv, other):
    return pltpu.make_async_remote_copy(
        source, target, send, recv, device_id={"ctx": other}, device_id_type=MESH
    )


FRONT_LOADS = 6
FRONT_SAVES = 12


def front_kernel(
    shards, head, heads, width, piece, chunk,
    tokens, cotangent, weight, weight_out, other, down, forget_weight, norm_gains, qk_gains, segments, order, forget_bias,
    inputs, grad_low, w_in, w_out, w_gate_up, normed, project, gated, attended, wide_query, wide_key, wide_value,
    mixed, down_near, normed_two, turned, gain_rows, pos_row, pos_col, seg_row, seg_col, bias, gains,
    weight_all, other_all, out_all, own_x, own_g, own_in, own_pick, own_out, x_all, in_all, hn_all, proj_all, mask, prefix,
    gated_all, attended_all, query_all, key_all, value_all, out_cols, scale_one, y_own, own_down,
    mixed_all, h2_all, turned_all,
    send_sem, recv_sem, own_sem, load_sem, save_sem, *line_sems,
):
    rank = lax.axis_index("ctx")
    ranks = lax.axis_size("ctx")
    model = weight.shape[1] // 4
    rows = x_all.shape[0]
    steps = width // LANES
    tail_at = 4 * width
    loads = [
        pltpu.make_async_copy(a, b, load_sem.at[n])
        for n, (a, b) in enumerate(
            (
                (weight, weight_all), (other, other_all), (weight_out, out_all), (tokens, own_x), (cotangent, own_g),
                (rows_of(down, rank, own_down.shape[0]), own_down),
            )
        )
    ]
    saves = [
        pltpu.make_async_copy(a, b, save_sem.at[n])
        for n, (a, b) in enumerate(
            (
                (x_all, inputs), (in_all, w_in), (hn_all, normed), (proj_all, project), (query_all, wide_query),
                (key_all, wide_key), (value_all, wide_value), (attended_all, attended), (gated_all, gated),
                (mixed_all, mixed), (h2_all, normed_two), (turned_all, turned),
            )
        )
    ]
    for copy in loads:
        copy.start()
    per = len(line_sems) // 4
    in_line = Line(shards, own_in, in_all, line_sems[:per])
    out_line = Line(shards, own_out, out_cols, line_sems[per : 2 * per])
    up_line = Line(shards, own_pick, w_gate_up, line_sems[2 * per : 3 * per])
    down_line = Line(shards, own_down, down_near, line_sems[3 * per :])
    greet([{"ctx": rank ^ 1}, {"ctx": rank ^ 2}], in_line)

    def sems(n):
        return send_sem.at[n], recv_sem.at[n], own_sem.at[n]

    first = relay_ops("gather_rows", rank, own_x, x_all, sems(0))
    second = relay_ops("gather_rows", rank, own_g, grad_low, sems(1))

    def cols(start, size):
        return pl.ds(pl.multiple_of(start, LANES), size)

    loads[0].wait()
    for i in range(4):
        own_in[:, i * width : (i + 1) * width] = weight_all[:, cols(i * model + rank * width, width)]
    total_heads = forget_weight.shape[0]
    from_head = lax.broadcasted_iota(jnp.int32, (total_heads, LANES), 0)
    to_lane = lax.broadcasted_iota(jnp.int32, (total_heads, LANES), 1)
    chosen = jnp.where((to_lane < heads) & (from_head == rank * heads + to_lane), 1.0, 0.0).astype(BF16)
    from_gain = lax.broadcasted_iota(jnp.int32, (2, LANES), 0)
    to_lane = lax.broadcasted_iota(jnp.int32, (2, LANES), 1)
    chosen_gain = jnp.where(to_lane == heads + from_gain, 1.0, 0.0).astype(BF16)
    tail = left_product(forget_weight[...], chosen) + left_product(norm_gains[...], chosen_gain)
    own_in[:, tail_at : tail_at + LANES] = tail.astype(BF16)
    in_line.start()
    loads[3].wait()
    first.start()
    loads[1].wait()
    for i in range(own_pick.shape[1] // piece):
        own_pick[:, i * piece : (i + 1) * piece] = other_all[:, cols((i * ranks + rank) * piece, piece)]
    loads[2].wait()
    own_out[...] = out_all[:, cols(rank * width, width)]
    count = order.shape[1]
    length = rows // count
    row_ids = lax.broadcasted_iota(jnp.int32, (rows, LANES), 0)
    lane_id = lax.broadcasted_iota(jnp.int32, (8, rows), 1)
    tall = jnp.zeros((rows, LANES), jnp.int32)
    flat = jnp.zeros((8, rows), jnp.int32)
    for block in range(count):
        start = order[0, block] * length - block * length
        tall = jnp.where((row_ids >= block * length) & (row_ids < (block + 1) * length), row_ids + start, tall)
        flat = jnp.where((lane_id >= block * length) & (lane_id < (block + 1) * length), lane_id + start, flat)
    pos_col[...] = tall[:, 0:1].astype(F32)
    pos_row[...] = flat[0:1, :].astype(F32)
    true_segments = segments[0:1, :].astype(F32)

    @turns(rows, chunk)
    def _(part):
        true_place = lax.broadcasted_iota(jnp.int32, (chunk, rows), 1).astype(F32)
        own_place = true_place == pos_col[part, :]
        seg_col[part, :] = jnp.sum(jnp.where(own_place, true_segments, 0.0), axis=-1, keepdims=True)

    seg_row[...] = jnp.broadcast_to(seg_col[...], (rows, LANES)).T[0:1, :]
    lane = lax.broadcasted_iota(jnp.int32, (1, LANES), 1)
    bias_row = jnp.zeros((1, LANES), F32)
    for index in range(heads):
        bias_row = jnp.where(lane == index, forget_bias[0, rank * heads + index], bias_row)
    bias[...] = bias_row
    for side in range(LANES // head):
        gains[:, side * head : (side + 1) * head] = qk_gains[...]
    fill_mask(chunk, pos_row, pos_col, seg_row, seg_col, mask)
    proj_all[...] = jnp.zeros_like(proj_all)
    gain_rows[...] = jnp.zeros_like(gain_rows)
    first.forward()
    loads[4].wait()
    second.start()
    in_line.step(1)
    first.finish()
    saves[0].start()

    @turns(rows, chunk)
    def _(part):
        values = x_all[part, :].astype(F32)
        scale_one[part, :] = jnp.broadcast_to(rms_scale(values), (chunk, LANES))

    def consume(layer):
        in_line.from_side(layer)
        size = 2 * in_line.rows
        here = cols(layer * size, size)
        tail_block = in_all[here, tail_at : tail_at + LANES].astype(F32).T
        gain_rows[0:1, here] = tail_block[heads : heads + 1, :]
        gain_rows[1:2, here] = tail_block[heads + 1 : heads + 2, :]

        @turns(rows, chunk)
        def _(part):
            values = x_all[part, here].astype(F32) * scale_one[part, 0:1] * gain_rows[0:1, here]
            hn_all[here, part] = values.T.astype(BF16)
            proj_all[part, :] += dot(values.astype(BF16), in_all[here, :])

    def consume_at(distance):
        lower, upper = in_line.layer - distance, in_line.layer + distance

        @pl.when(lower >= 0)
        def _():
            consume(lower)

        @pl.when(upper < in_line.layers)
        def _():
            consume(upper)

    in_line.keep.wait()
    consume(in_line.layer)
    consume_at(1)
    second.forward()
    for distance in range(2, in_line.layers):
        in_line.step(distance)
        if distance == in_line.layers - 1:
            out_line.start()
            up_line.start()
        consume_at(distance)

    for n in (1, 2, 3):
        saves[n].start()
    out_line.step(1)
    fill_prefix(chunk, heads, pos_row, pos_col, proj_all[:, tail_at : tail_at + LANES] + bias[0:1, :], prefix)

    def share(index):
        block = rank * steps + index
        half = rows // 2

        def source(h):
            return gated_all.at[block, pl.ds(h * half, half), :]

        def place(owner, h):
            return gated_all.at[owner * steps + index, pl.ds(h * half, half), :]

        return Relay(rank, source, place, send_sem.at[2 + index], recv_sem.at[2 + index], None)

    per_block = LANES // head

    @pl.loop(0, steps)
    def _(index):
        def lanes_of(part_id):
            return proj_all[:, cols(part_id * width + index * LANES, LANES)]

        def gate(part):
            return proj_all[part, cols(3 * width + index * LANES, LANES)]

        group = pl.ds(index * per_block, per_block)
        attend_block(
            head, chunk, index, lanes_of(0), lanes_of(1), lanes_of(2), gate, gains, mask, prefix,
            gated_all.at[rank * steps + index], attended_all.at[index],
            query_all.at[group], key_all.at[group], value_all.at[group],
        )
        share(index).start(keep=False)

        @pl.when(index == 0)
        def _():
            out_line.step(2)

        @pl.when(index > 0)
        def _():
            share(index - 1).forward()

    up_line.step(1)
    out_line.step(3)
    share(steps - 1).forward()
    for n in (4, 5, 6, 7):
        saves[n].start()
    for index in range(steps):
        share(index).arrive()
    saves[8].start()
    out_line.keep.wait()
    for layer in range(out_line.layers):
        out_line.from_side(layer)
    save_out = pltpu.make_async_copy(out_cols, w_out, save_sem.at[len(saves)])
    save_out.start()

    third = relay_ops("gather_cols", rank, y_own, mixed_all, sems(2 + steps))

    @turns(rows, chunk)
    def _(part):
        total = x_all[part, cols(rank * width, width)].astype(F32)
        for block in range(gated_all.shape[0]):
            total = total + dot(gated_all[block, part, :], out_cols[block * LANES : (block + 1) * LANES, :])
        y_own[part, :] = total.astype(BF16)

    third.start()
    third.forward()
    up_line.step(2)
    loads[5].wait()
    down_line.start()
    third.finish()
    saves[9].start()

    @turns(rows, chunk)
    def _(part):
        values = mixed_all[part, :].astype(F32)
        low = values * rms_scale(values) * gain_rows[1:2, :]
        h2_all[part, :] = low.astype(BF16)
        turned_all[:, part] = low.T.astype(BF16)

    saves[10].start()
    saves[11].start()
    for distance in range(3, up_line.layers):
        up_line.step(distance)
    up_line.finish()
    down_line.near_finish()
    out_line.sent()
    in_line.sent()
    second.finish()
    for index in range(steps):
        share(index).finish(arrive=False, keep=False)
    for copy in saves:
        copy.wait()
    save_out.wait()


def front(
    collective_id, ranks, shards, head, heads, width, piece,
    tokens, cotangent, weight, weight_out, other, down, forget_weight, norm_gains, qk_gains, segments, order, forget_bias,
):
    own_rows, model = tokens.shape
    rows = ranks * own_rows
    chunk = pick_chunk(rows)
    steps, shard_rows = width // LANES, weight.shape[0]
    wide_in = 4 * width + LANES
    other_cols = other.shape[1] // ranks
    wide = (heads, rows, LANES)
    shape, vmem = jax.ShapeDtypeStruct, pltpu.VMEM
    return pl.pallas_call(
        functools.partial(front_kernel, shards, head, heads, width, piece, chunk),
        in_specs=[ANY] * 6 + [VMEM_WHOLE] * 4 + [pl.BlockSpec(memory_space=pltpu.SMEM)] * 2,
        out_specs=[ANY] * 16 + [VMEM_WHOLE] * 7,
        out_shape=[
            shape((rows, model), BF16),
            shape((rows, model), BF16),
            shape((model, wide_in), BF16),
            shape((model, width), BF16),
            shape((model, other_cols), BF16),
            shape((model, rows), BF16),
            shape((rows, wide_in), F32),
            shape((ranks * steps, rows, LANES), BF16),
            shape((steps, rows, LANES), F32),
            shape(wide, BF16), shape(wide, BF16), shape(wide, BF16),
            shape((rows, model), BF16),
            shape((shards * (down.shape[0] // ranks), model), BF16),
            shape((rows, model), BF16),
            shape((model, rows), BF16),
            shape((8, model), F32),
            shape((1, rows), F32), shape((rows, 1), F32), shape((1, rows), F32), shape((rows, 1), F32),
            shape((1, LANES), F32),
            shape((2, LANES), F32),
        ],
        scratch_shapes=[
            vmem(weight.shape, BF16),
            vmem(other.shape, BF16),
            vmem(weight_out.shape, BF16),
            vmem(tokens.shape, BF16),
            vmem(cotangent.shape, BF16),
            vmem((shard_rows, wide_in), BF16),
            vmem((shard_rows, other_cols), BF16),
            vmem((shard_rows, width), BF16),
            vmem((rows, model), BF16),
            vmem((model, wide_in), BF16),
            vmem((model, rows), BF16),
            vmem((rows, wide_in), F32),
            vmem((rows, rows), F32),
            vmem((rows, LANES), F32),
            vmem((ranks * steps, rows, LANES), BF16),
            vmem((steps, rows, LANES), F32),
            vmem(wide, BF16), vmem(wide, BF16), vmem(wide, BF16),
            vmem((model, width), BF16),
            vmem((rows, LANES), F32),
            vmem((rows, width), BF16),
            vmem((down.shape[0] // ranks, model), BF16),
            vmem((rows, model), BF16),
            vmem((rows, model), BF16),
            vmem((model, rows), BF16),
            pltpu.SemaphoreType.DMA((3 + steps, 6)),
            pltpu.SemaphoreType.DMA((3 + steps, 6)),
            pltpu.SemaphoreType.DMA((3 + steps, 2)),
            pltpu.SemaphoreType.DMA((FRONT_LOADS,)),
            pltpu.SemaphoreType.DMA((FRONT_SAVES + 1,)),
        ]
        + 4 * line_scratch(shards),
        compiler_params=pltpu.CompilerParams(
            collective_id=collective_id, has_side_effects=True, vmem_limit_bytes=VMEM_LIMIT
        ),
        cost_estimate=pl.CostEstimate(flops=0, bytes_accessed=300 << 20, transcendentals=0),
        name="front",
    )(
        tokens, cotangent, weight, weight_out, other, down, forget_weight, norm_gains, qk_gains, segments, order, forget_bias
    )


def fold_tiles(rows, cols, share_rows):
    extra = rows * cols // share_rows
    high, wide = math.gcd(rows, share_rows), math.gcd(cols, extra)
    tiles = []
    for row in range(rows // high):
        for col in range(cols // wide):
            k = row * (cols // wide) + col
            tiles.append((row * high, col * wide, k // (extra // wide) * high, k % (extra // wide) * wide))
    return tiles, high, wide, extra


def ffn_kernel(
    shards, chunk,
    normed, turned_from, w_gate_up, cotangent, down_near,
    w_down, hidden, grad_gate_up, grad_weight,
    weight_in, cotangent_in, gates, ups, hn, turned, acts, grads, weight_out,
    load_sem, save_sem, tile_sem, near_sem, *line_sems,
):
    size = gates.shape[1]
    rows, model = normed.shape
    tile = 2 * w_down.shape[0] // shards
    loads = [
        pltpu.make_async_copy(a, b, load_sem.at[n])
        for n, (a, b) in enumerate(
            ((normed, hn), (w_gate_up, weight_in), (cotangent, cotangent_in), (turned_from, turned))
        )
    ]
    saves = [
        pltpu.make_async_copy(a, b, save_sem.at[n])
        for n, (a, b) in enumerate(
            ((acts, hidden), (weight_out.at[:, pl.ds(2 * size, size)], grad_weight.at[:, pl.ds(2 * size, size)]))
        )
    ]
    line = Line(shards, None, w_down, line_sems)
    line.near_start(down_near, near_sem)
    for copy in loads:
        copy.start()
    greet([], line)
    line.resume(down_near, near_sem)
    loads[0].wait()
    loads[1].wait()

    def span(turn, start=0):
        return pl.ds(pl.multiple_of(start + turn * tile, LANES), tile)

    def activate(turn):
        gate = dot(hn[...], weight_in[:, span(turn)])
        up = dot(hn[...], weight_in[:, span(turn, size)])
        gates[:, span(turn)] = gate
        ups[:, span(turn)] = up
        acts[:, span(turn)] = (jax.nn.silu(gate) * up).astype(BF16)

    tiles, high, wide, _ = fold_tiles(tile // 2, model, model // shards)

    def down_grad(turn):
        product = left_product(acts[:, span(turn)], cotangent_in[...]).astype(BF16)
        for half in range(2):
            base = (2 * turn + half) * (model // shards)
            for row, col, new_row, new_col in tiles:
                row = row + half * (tile // 2)
                weight_out[
                    pl.ds(pl.multiple_of(base + new_row, high), high), 2 * size + new_col : 2 * size + new_col + wide
                ] = product[row : row + high, col : col + wide]

    count = size // tile
    pl.loop(0, count)(activate)
    saves[0].start()
    loads[2].wait()
    loads[3].wait()
    line.near_load(down_near, near_sem, 0).wait()

    def consume(turn):
        grad = right_product(cotangent_in[...], w_down[span(turn), :])
        gate, up = gates[:, span(turn)], ups[:, span(turn)]
        sig = jax.nn.sigmoid(gate)
        grads[:, span(turn)] = (grad * up * sig * (1.0 + gate * (1.0 - sig))).astype(BF16)
        grads[:, span(turn, size)] = (grad * gate * sig).astype(BF16)

        for start in (0, size):
            here = span(turn, start)

            @turns(model, 3 * chunk if model % (3 * chunk) == 0 else chunk)
            def _(part):
                weight_out[part, here] = dot(turned[part, :], grads[:, here]).astype(BF16)

        for copy in tile_saves(turn):
            copy.start()

    def tile_saves(turn):
        for n, start in enumerate((0, size)):
            here = span(turn, start)
            yield pltpu.make_async_copy(grads.at[:, here], grad_gate_up.at[:, here], tile_sem.at[turn, 2 * n])
            yield pltpu.make_async_copy(weight_out.at[:, here], grad_weight.at[:, here], tile_sem.at[turn, 2 * n + 1])

    def consume_at(distance):
        lower, upper = line.layer - distance, line.layer + distance

        @pl.when(lower >= 0)
        def _():
            line.from_side(lower)
            consume(lower)

        @pl.when(upper < line.layers)
        def _():
            line.from_side(upper)
            consume(upper)

    line.step(2)
    consume(line.layer)
    consume_at(1)
    pl.loop(0, count)(down_grad)
    saves[1].start()
    for distance in range(3, line.layers):
        line.step(distance)
    for distance in range(2, line.layers):
        consume_at(distance)
    line.resumed_sent()
    for copy in saves:
        copy.wait()

    @pl.loop(0, count)
    def _(turn):
        for copy in tile_saves(turn):
            copy.wait()


def ffn(collective_id, shards, normed, turned, w_gate_up, cotangent, down_near):
    rows, model = normed.shape
    size = w_gate_up.shape[1] // 2
    shape, vmem = jax.ShapeDtypeStruct, pltpu.VMEM
    return pl.pallas_call(
        functools.partial(ffn_kernel, shards, pick_chunk(rows)),
        in_specs=[ANY] * 5,
        out_specs=[VMEM_WHOLE] + [ANY] * 3,
        out_shape=[
            shape((size, model), BF16),
            shape((rows, size), BF16),
            shape((rows, 2 * size), BF16),
            shape((model, 3 * size), BF16),
        ],
        scratch_shapes=[
            vmem(w_gate_up.shape, BF16),
            vmem((rows, model), BF16),
            vmem((rows, size), F32),
            vmem((rows, size), F32),
            vmem((rows, model), BF16),
            vmem((model, rows), BF16),
            vmem((rows, size), BF16),
            vmem((rows, 2 * size), BF16),
            vmem((model, 3 * size), BF16),
            pltpu.SemaphoreType.DMA((4,)),
            pltpu.SemaphoreType.DMA((2,)),
            pltpu.SemaphoreType.DMA((shards // 2, 4)),
            pltpu.SemaphoreType.DMA((3,)),
        ]
        + line_scratch(shards),
        compiler_params=pltpu.CompilerParams(
            collective_id=collective_id, has_side_effects=True, vmem_limit_bytes=VMEM_LIMIT
        ),
        cost_estimate=pl.CostEstimate(flops=0, bytes_accessed=100 << 20, transcendentals=0),
        name="ffn",
    )(normed, turned, w_gate_up, cotangent, down_near)


class Fold:
    def __init__(self, rank, piece, first, between, second, send_sem, recv_sem):
        self.rank, self.piece, self.first, self.between, self.second = rank, piece, first, between, second
        self.send_sem, self.recv_sem = send_sem, recv_sem

    def copy(self, number):
        me = self.rank
        source, target, distance = (
            lambda: (self.piece(me ^ 1, 0), self.first(0, 0), 1),
            lambda: (self.piece(me ^ 3, 0), self.first(1, 0), 1),
            lambda: (self.piece(me ^ 2, 1), self.first(0, 1), 2),
            lambda: (self.piece(me ^ 3, 1), self.first(1, 1), 2),
            lambda: (self.between(0), self.second(0), 2),
            lambda: (self.between(1), self.second(1), 1),
        )[number]()
        return to_rank(source, target, self.send_sem.at[number], self.recv_sem.at[number], me ^ distance)

    def start(self):
        for number in range(4):
            self.copy(number).start()

    def pass_on(self):
        for h, distance in ((0, 2), (1, 1)):
            self.copy(2 * h).wait_recv()
            self.copy(2 * h + 1).wait_recv()
            own = self.piece(self.rank ^ distance, h)[...].astype(F32)
            self.between(h)[...] = (own + self.first(1, h)[...].astype(F32)).astype(BF16)
            self.copy(4 + h).start()

    def total(self, h):
        self.copy(4 + h).wait_recv()
        own = self.piece(self.rank, h)[...].astype(F32)
        return own + self.first(0, h)[...].astype(F32) + self.second(h)[...].astype(F32)

    def sent(self):
        for number in range(6):
            self.copy(number).wait_send()


def middle_kernel(
    ranks,
    grad_gate_up, w_gate_up, mixed, cotangent, w_out, hidden, w_down, gated, gain,
    mixed_grad, gated_grad, gain_grad, down_part, out_grad,
    grad_in, weight_in, mixed_in, cotangent_in, out_in, hidden_in, down_in, gated_in, low_grad, down_all, out_all,
    wide, first_out, first_in, first_between, first_end, second_out, second_in, second_between, second_end,
    load_sem, save_sem, first_send, first_recv, second_send, second_recv,
):
    rank = lax.axis_index("ctx")
    rows = mixed.shape[0] // ranks
    model, width = w_out.shape
    tile = 256
    loads = [
        pltpu.make_async_copy(a, b, load_sem.at[n])
        for n, (a, b) in enumerate(
            (
                (w_gate_up, weight_in), (grad_gate_up, grad_in), (mixed, mixed_in), (cotangent, cotangent_in),
                (w_out, out_in), (hidden, hidden_in), (w_down, down_in), (gated, gated_in),
            )
        )
    ]
    saves = [
        pltpu.make_async_copy(down_all, down_part, save_sem.at[0]),
        pltpu.make_async_copy(out_all, out_grad, save_sem.at[1]),
    ]
    for copy in loads:
        copy.start()
    greet([{"ctx": rank ^ distance} for distance in range(1, ranks)])
    gain_grad[...] = jnp.zeros_like(gain_grad)
    for copy in loads[:2]:
        copy.wait()

    def part(turn):
        return pl.ds(pl.multiple_of(turn * rows, 16), rows)

    half = rows // 2

    def fold(out, into, between, end, send_sem, recv_sem):
        def make(turn):
            def at(h):
                return pl.ds(pl.multiple_of(turn * rows + h * half, 16), half)

            return Fold(
                rank,
                lambda index, h: out.at[index, at(h), :],
                lambda slot, h: into.at[slot, at(h), :],
                lambda h: between.at[at(h), :],
                lambda h: end.at[at(h), :],
                send_sem.at[turn],
                recv_sem.at[turn],
            )

        return make

    first = fold(first_out, first_in, first_between, first_end, first_send, first_recv)
    second = fold(second_out, second_in, second_between, second_end, second_send, second_recv)

    def compute(turn):
        here = part(turn)

        @pl.loop(0, model // tile)
        def _(step):
            cols = pl.ds(pl.multiple_of(step * tile, tile), tile)
            wide[:, cols] = right_product(grad_in[here, :], weight_in[cols, :])

        @pl.when(turn == 0)
        def _():
            for copy in loads[2:5]:
                copy.wait()

        values = mixed_in[here, :].astype(F32)
        scale = rms_scale(values)
        grad = wide[...]
        gain_grad[0:1, :] += jnp.sum(grad * values * scale, axis=0, keepdims=True)
        back = norm_back(grad, values, scale, gain[0:1, :]).astype(BF16)
        for index in range(ranks):
            first_out[index, here, :] = back[:, index * width : (index + 1) * width]
        first(turn).start()

    def project(turn):
        here = part(turn)
        for h in range(2):
            at = pl.ds(pl.multiple_of(turn * rows + h * half, 16), half)
            total = cotangent_in[at, pl.ds(pl.multiple_of(rank * width, LANES), width)].astype(F32)
            total = total + first(turn).total(h)
            mixed_grad[at, :] = total
            low_grad[at, :] = total.astype(BF16)
        for index in range(ranks):
            second_out[index, here, :] = right_product(
                low_grad[here, :], out_in[index * width : (index + 1) * width, :]
            ).astype(BF16)
        second(turn).start()

    def collect(turn):
        for h in range(2):
            at = pl.ds(pl.multiple_of(turn * rows + h * half, 16), half)
            gated_grad[at, :] = second(turn).total(h)

    def aside(turn):
        @pl.when(turn == ranks)
        def _():
            for copy in loads[5:]:
                copy.wait()

            @pl.loop(0, model // tile)
            def _(step):
                cols = pl.ds(pl.multiple_of(step * tile, tile), tile)
                down_all[:, cols] = dot(hidden_in[...], down_in[:, cols]).astype(BF16)

            saves[0].start()

        @pl.when(turn == ranks + 2)
        def _():
            @pl.loop(0, gated_in.shape[0])
            def _(block):
                out_all[pl.ds(pl.multiple_of(block * LANES, LANES), LANES), :] = left_product(
                    gated_in[block], low_grad[...]
                ).astype(BF16)

            saves[1].start()

    @pl.loop(0, ranks + 4)
    def _(turn):
        stages = (
            compute, lambda t: first(t).pass_on(), project, lambda t: second(t).pass_on(), collect,
        )
        for lag, stage in enumerate(stages):
            if lag == 4:
                aside(turn)

            @pl.when((turn >= lag) & (turn < ranks + lag))
            def _():
                stage(turn - lag)

    @pl.loop(0, ranks)
    def _(turn):
        first(turn).sent()
        second(turn).sent()

    for copy in saves:
        copy.wait()


def middle(collective_id, ranks, grad_gate_up, w_gate_up, mixed, cotangent, w_out, hidden, w_down, gated, gain):
    rows, model = mixed.shape
    width = w_out.shape[1]
    flat = pltpu.VMEM((rows, width), BF16)
    blocks = [pltpu.VMEM((ranks, rows, width), BF16), pltpu.VMEM((2, rows, width), BF16), flat, flat]
    sems = pltpu.SemaphoreType.DMA((ranks, 6))
    return pl.pallas_call(
        functools.partial(middle_kernel, ranks),
        in_specs=[ANY] * 8 + [VMEM_WHOLE],
        out_specs=[VMEM_WHOLE] * 3 + [ANY] * 2,
        out_shape=[
            jax.ShapeDtypeStruct((rows, width), F32),
            jax.ShapeDtypeStruct((rows, width), F32),
            jax.ShapeDtypeStruct((8, model), F32),
            jax.ShapeDtypeStruct((rows, model), BF16),
            jax.ShapeDtypeStruct((model, width), BF16),
        ],
        scratch_shapes=[
            pltpu.VMEM(grad_gate_up.shape, BF16),
            pltpu.VMEM(w_gate_up.shape, BF16),
            pltpu.VMEM(mixed.shape, BF16),
            pltpu.VMEM(cotangent.shape, BF16),
            pltpu.VMEM(w_out.shape, BF16),
            pltpu.VMEM(hidden.shape, BF16),
            pltpu.VMEM(w_down.shape, BF16),
            pltpu.VMEM(gated.shape, BF16),
            pltpu.VMEM((rows, width), BF16),
            pltpu.VMEM((rows, model), BF16),
            pltpu.VMEM((model, width), BF16),
            pltpu.VMEM((rows // ranks, model), F32),
            *blocks, *blocks,
            pltpu.SemaphoreType.DMA((8,)),
            pltpu.SemaphoreType.DMA((2,)),
            sems, sems, sems, sems,
        ],
        compiler_params=pltpu.CompilerParams(
            collective_id=collective_id, has_side_effects=True, vmem_limit_bytes=VMEM_LIMIT
        ),
        cost_estimate=pl.CostEstimate(flops=0, bytes_accessed=150 << 20, transcendentals=0),
        name="middle",
    )(grad_gate_up, w_gate_up, mixed, cotangent, w_out, hidden, w_down, gated, gain)


def last_kernel(
    ranks, shards,
    grad_project, w_in, inputs, aside, pieces, mixed, mixed_grad, gain, gain_two_grad, small, segments,
    tokens_grad, block_out, total_sums, parts, aside_all,
    grad_in, weight_in, inputs_in, aside_in, pieces_in, mixed_in, wide, out, into, between, end, sums_out, sums_in,
    load_sem, send_sem, recv_sem, sums_send, sums_recv, aside_send, aside_recv, aside_own,
):
    rank = lax.axis_index("ctx")
    rows = inputs.shape[0] // ranks
    model, width = inputs.shape[1], mixed_grad.shape[1]
    tile = 256
    loads = [
        pltpu.make_async_copy(a, b, load_sem.at[n])
        for n, (a, b) in enumerate(
            (
                (aside, aside_in), (w_in, weight_in), (grad_project, grad_in), (inputs, inputs_in),
                (pieces, pieces_in), (rows_of(mixed, rank, rows), mixed_in),
            )
        )
    ]
    for copy in loads:
        copy.start()
    greet([{"ctx": rank ^ distance} for distance in range(1, ranks)])
    relay = relay_ops("stack", rank, aside_in, aside_all, (aside_send, aside_recv, aside_own))
    loads[0].wait()
    relay.start()
    sums_out[...] = jnp.zeros_like(sums_out)
    sums_out[1:2, :] = gain_two_grad[0:1, :]
    sums_out[2:3, 0:LANES] = small[0:1, :]
    sums_out[2:3, LANES : 2 * LANES] = small[1:2, :]
    for index in range(ranks):
        sums_out[3 + index : 4 + index, 0:LANES] = jnp.where(rank == index, small[2:3, :], 0.0)
    for copy in loads[1:4]:
        copy.wait()

    half = rows // 2

    def at(h):
        return pl.ds(h * half, half)

    fold = Fold(
        rank,
        lambda index, h: out.at[index, at(h), :],
        lambda slot, h: into.at[slot, at(h), :],
        lambda h: between.at[at(h), :],
        lambda h: end.at[at(h), :],
        send_sem,
        recv_sem,
    )

    def send_sums(distance):
        return to_rank(
            sums_out, sums_in.at[distance], sums_send.at[distance - 1], sums_recv.at[distance - 1], rank ^ distance
        )

    def compute(other):
        here = pl.ds(pl.multiple_of(other * rows, 16), rows)

        @pl.loop(0, model // tile)
        def _(step):
            cols = pl.ds(pl.multiple_of(step * tile, tile), tile)
            wide[:, cols] = right_product(grad_in[here, :], weight_in[cols, :])

        values = inputs_in[here, :].astype(F32)
        scale = rms_scale(values)
        grad = wide[...]
        sums_out[0:1, :] += jnp.sum(grad * values * scale, axis=0, keepdims=True)
        wide[...] = norm_back(grad, values, scale, gain[0:1, :])
        own = pl.ds(pl.multiple_of(rank * width, LANES), width)
        wide[:, own] += mixed_grad[here, :]
        out[other] = wide[...].astype(BF16)

    @pl.loop(1, ranks)
    def _(turn):
        compute(rank ^ (ranks - turn))

        @pl.when(turn == 2)
        def _():
            for number in (2, 3):
                fold.copy(number).start()

        @pl.when(turn == 3)
        def _():
            for number in (0, 1):
                fold.copy(number).start()

    for copy in loads[4:]:
        copy.wait()
    own = pl.ds(pl.multiple_of(rank * rows, 16), rows)
    result = mixed_in[...].astype(F32)
    for index in range(ranks):
        result = result + pieces_in[index].astype(F32)
    block_out[...] = result.astype(BF16)
    branch = result - inputs_in[own, :].astype(F32)
    valid = jnp.where(segments[own, :] >= 0.0, 1.0, 0.0)
    lane = lax.broadcasted_iota(jnp.int32, (1, LANES), 1)
    stats = jnp.zeros((1, LANES), F32)
    for index, values in enumerate((result, branch)):
        total = jnp.sum(valid * jnp.sum(values * values, axis=-1, keepdims=True), axis=0, keepdims=True)
        stats = jnp.where(lane == index, total, stats)
    sums_out[7:8, 0:LANES] = stats
    compute(rank)
    for distance in range(1, ranks):
        send_sums(distance).start()
    relay.forward()
    fold.pass_on()
    for h in range(2):
        tokens_grad[at(h), :] = fold.total(h).astype(BF16)
    total = sums_out[...]
    for distance in range(1, ranks):
        send_sums(distance).wait_recv()
        total = total + sums_in[distance]
    total_sums[...] = total
    share = model // shards
    parts[...] = jnp.zeros_like(parts)
    for index in range(shards):
        parts[index, 0:2, 0:share] = total[0:2, index * share : (index + 1) * share]
        parts[index, 2:8, :] = total[2:8, 0 : parts.shape[2]]
    fold.sent()
    for distance in range(1, ranks):
        send_sums(distance).wait_send()
    relay.finish()


def last_moves(
    collective_id, ranks, shards,
    grad_project, w_in, inputs, aside, pieces, mixed, mixed_grad, gain, gain_two_grad, small, segments,
):
    rows, model = inputs.shape
    own = (rows // ranks, model)
    flat = pltpu.VMEM(own, BF16)
    blocks = [pltpu.VMEM((ranks,) + own, BF16), pltpu.VMEM((2,) + own, BF16), flat, flat]
    sems = pltpu.SemaphoreType.DMA((ranks - 1,))
    return pl.pallas_call(
        functools.partial(last_kernel, ranks, shards),
        in_specs=[ANY] * 6 + [VMEM_WHOLE] * 5,
        out_specs=[VMEM_WHOLE] * 4 + [ANY],
        out_shape=[
            jax.ShapeDtypeStruct(own, BF16),
            jax.ShapeDtypeStruct(own, BF16),
            jax.ShapeDtypeStruct((8, model), F32),
            jax.ShapeDtypeStruct((shards, 8, max(2 * LANES, -(-model // shards // LANES) * LANES)), F32),
            jax.ShapeDtypeStruct((ranks,) + aside.shape, BF16),
        ],
        scratch_shapes=[
            pltpu.VMEM(grad_project.shape, BF16),
            pltpu.VMEM(w_in.shape, BF16),
            pltpu.VMEM(inputs.shape, BF16),
            pltpu.VMEM(aside.shape, BF16),
            pltpu.VMEM(pieces.shape, BF16),
            pltpu.VMEM(own, BF16),
            pltpu.VMEM(own, F32),
            *blocks,
            pltpu.VMEM((8, model), F32),
            pltpu.VMEM((ranks, 8, model), F32),
            pltpu.SemaphoreType.DMA((6,)),
            pltpu.SemaphoreType.DMA((6,)),
            pltpu.SemaphoreType.DMA((6,)),
            sems, sems,
            pltpu.SemaphoreType.DMA((6,)),
            pltpu.SemaphoreType.DMA((6,)),
            pltpu.SemaphoreType.DMA((2,)),
        ],
        compiler_params=pltpu.CompilerParams(
            collective_id=collective_id, has_side_effects=True, vmem_limit_bytes=VMEM_LIMIT
        ),
        cost_estimate=pl.CostEstimate(flops=0, bytes_accessed=150 << 20, transcendentals=0),
        name="last_moves",
    )(grad_project, w_in, inputs, aside, pieces, mixed, mixed_grad, gain, gain_two_grad, small, segments)


def finish_kernel(ranks, shards, late, parts, late_all, part_sum, late_in, into, load_sem, send_sem, recv_sem, own_sem,
                  part_send, part_recv):
    rank = lax.axis_index("ctx")
    shard = lax.axis_index("fsdp")
    load = pltpu.make_async_copy(late, late_in, load_sem.at[0])
    load.start()
    relay = relay_ops("stack", rank, late_in, late_all, (send_sem, recv_sem, own_sem))
    greet([{"ctx": rank ^ 1}, {"ctx": rank ^ 2}] + [{"fsdp": shard ^ distance} for distance in range(1, shards)])
    load.wait()
    relay.start()

    def send(distance):
        other = shard ^ distance
        return pltpu.make_async_remote_copy(
            parts.at[other], into.at[distance], part_send.at[distance - 1], part_recv.at[distance - 1],
            device_id={"fsdp": other}, device_id_type=MESH,
        )

    for distance in range(1, shards):
        send(distance).start()
    relay.forward()
    total = parts[shard]
    for distance in range(1, shards):
        send(distance).wait_recv()
        total = total + into[distance]
    part_sum[...] = total
    for distance in range(1, shards):
        send(distance).wait_send()
    relay.finish()


def finish_moves(collective_id, ranks, shards, late, parts):
    sems = pltpu.SemaphoreType.DMA((shards - 1,))
    return pl.pallas_call(
        functools.partial(finish_kernel, ranks, shards),
        in_specs=[ANY, VMEM_WHOLE],
        out_specs=[ANY, VMEM_WHOLE],
        out_shape=[
            jax.ShapeDtypeStruct((ranks,) + late.shape, BF16),
            jax.ShapeDtypeStruct(parts.shape[1:], F32),
        ],
        scratch_shapes=[
            pltpu.VMEM(late.shape, BF16),
            pltpu.VMEM(parts.shape, F32),
            pltpu.SemaphoreType.DMA((1,)),
            pltpu.SemaphoreType.DMA((6,)),
            pltpu.SemaphoreType.DMA((6,)),
            pltpu.SemaphoreType.DMA((2,)),
            sems, sems,
        ],
        compiler_params=pltpu.CompilerParams(
            collective_id=collective_id, has_side_effects=True, vmem_limit_bytes=VMEM_LIMIT
        ),
        cost_estimate=pl.CostEstimate(flops=0, bytes_accessed=50 << 20, transcendentals=0),
        name="finish_moves",
    )(late, parts)


def spread_kernel(pieces, *refs):
    source, targets = refs[0], refs[1:]
    ranks = source.shape[0]
    for target, (piece, first, count) in zip(targets, pieces):
        for block in range(count):
            for index in range(ranks):
                target[:, pl.ds((block * ranks + index) * piece, piece)] = source[
                    index, :, pl.ds(first + block * piece, piece)
                ].astype(F32)


def spread_cols(source, *pieces):
    ranks, rows, cols = source.shape
    if any(piece % LANES or first % LANES for piece, first, _ in pieces):
        return [
            jnp.concatenate(
                [
                    source[c, :, first + i * piece : first + (i + 1) * piece]
                    for i in range(count)
                    for c in range(ranks)
                ],
                axis=1,
            ).astype(F32)
            for piece, first, count in pieces
        ]
    part = rows // 4 if rows % 64 == 0 else rows
    widths = [count * ranks * piece for piece, _, count in pieces]
    return pl.pallas_call(
        functools.partial(spread_kernel, pieces),
        grid=(rows // part,),
        in_specs=[pl.BlockSpec((ranks, part, cols), lambda step: (0, step, 0))],
        out_specs=[pl.BlockSpec((part, w), lambda step: (step, 0)) for w in widths],
        out_shape=[jax.ShapeDtypeStruct((rows, w), F32) for w in widths],
        compiler_params=pltpu.CompilerParams(vmem_limit_bytes=VMEM_LIMIT),
        cost_estimate=pl.CostEstimate(flops=0, bytes_accessed=rows * sum(widths) * 6, transcendentals=0),
        name="spread_cols",
    )(source)


def unfold_kernel(tiles, high, wide, source, target):
    for row, col, new_row, new_col in tiles:
        target[row : row + high, col : col + wide] = source[
            0, new_row : new_row + high, new_col : new_col + wide
        ].astype(F32)


def unfold_rows(source, rows, cols, first):
    ranks, share_rows, _ = source.shape
    tiles, high, wide, extra = fold_tiles(rows, cols, share_rows)
    return pl.pallas_call(
        functools.partial(unfold_kernel, tiles, high, wide),
        grid=(ranks,),
        in_specs=[pl.BlockSpec((1, share_rows, extra), lambda step: (step, 0, first // extra))],
        out_specs=pl.BlockSpec((rows, cols), lambda step: (step, 0)),
        out_shape=jax.ShapeDtypeStruct((ranks * rows, cols), F32),
        compiler_params=pltpu.CompilerParams(vmem_limit_bytes=VMEM_LIMIT),
        cost_estimate=pl.CostEstimate(flops=0, bytes_accessed=ranks * rows * cols * 6, transcendentals=0),
        name="unfold_rows",
    )(source)


def unpack_kernel(
    width, heads, head, late, late_tail, sums, totals, segments, first_rows, second_rows,
    in_out, out_out, first_out, second_out, forget_out, gains, bias, qk, rms,
):
    ranks = late.shape[0]
    first = 4 * width
    for block in range(4):
        for index in range(ranks):
            in_out[:, (block * ranks + index) * width : (block * ranks + index + 1) * width] = late[
                index, :, block * width : (block + 1) * width
            ].astype(F32)
    first_out[...] = first_rows[...]
    second_out[...] = second_rows[...]
    lane = lax.broadcasted_iota(jnp.int32, (LANES, ranks * heads), 0)
    place = lax.broadcasted_iota(jnp.int32, (LANES, ranks * heads), 1)
    lane_t = lax.broadcasted_iota(jnp.int32, (ranks * heads, LANES), 1)
    place_t = lax.broadcasted_iota(jnp.int32, (ranks * heads, LANES), 0)
    forget = jnp.zeros(forget_out.shape, F32)
    biases = jnp.zeros((8, ranks * heads), F32)
    for index in range(ranks):
        chosen = (lane < heads) & (place == index * heads + lane)
        out_out[:, index * width : (index + 1) * width] = late[index, :, first : first + width].astype(F32)
        chosen_t = (lane_t < heads) & (place_t == index * heads + lane_t)
        forget = forget + right_product(jnp.where(chosen_t, 1.0, 0.0).astype(BF16), late_tail[index])
        row = jnp.broadcast_to(sums[3 + index : 4 + index, 0:LANES], (8, LANES))
        for part in split_three(row):
            biases = biases + dot(part.astype(BF16), jnp.where(chosen, 1.0, 0.0).astype(BF16))
    forget_out[...] = forget
    gains[...] = sums[0:2, 0 : gains.shape[1]]
    bias[...] = biases[0:1, :]
    for row in range(2):
        qk[row : row + 1, :] = sum(
            sums[2:3, row * LANES + side * head : row * LANES + (side + 1) * head] for side in range(LANES // head)
        )
    count = jnp.sum(jnp.where(segments[...] >= 0, 1.0, 0.0), axis=-1, keepdims=True)
    rms[...] = jnp.sqrt(totals[7:8, 0:2] / (count * totals.shape[1]))


def unpack(late, sums, totals, segments, first_rows, second_rows, width, heads, head):
    ranks, rows, cols = late.shape
    part = rows // 4

    def block(lanes):
        return pl.BlockSpec((part, lanes), lambda step: (step, 0))

    share = rows
    shape = jax.ShapeDtypeStruct
    return pl.pallas_call(
        functools.partial(unpack_kernel, width, heads, head),
        grid=(rows // part,),
        in_specs=[
            pl.BlockSpec((ranks, part, cols), lambda step: (0, step, 0)),
            pl.BlockSpec((ranks, rows, LANES), lambda step: (0, 0, 5 * width // LANES)),
        ]
        + [whole(a.shape) for a in (sums, totals, segments)]
        + [block(first_rows.shape[1])] * 2,
        out_specs=[block(4 * ranks * width), block(ranks * width)] + [block(first_rows.shape[1])] * 2
        + [whole(a) for a in ((ranks * heads, rows), (2, share), (1, ranks * heads), (2, head), (1, 2))],
        out_shape=[
            shape((rows, 4 * ranks * width), F32),
            shape((rows, ranks * width), F32),
            shape(first_rows.shape, BF16),
            shape(second_rows.shape, BF16),
            shape((ranks * heads, rows), F32),
            shape((2, share), F32),
            shape((1, ranks * heads), F32),
            shape((2, head), F32),
            shape((1, 2), F32),
        ],
        compiler_params=pltpu.CompilerParams(vmem_limit_bytes=VMEM_LIMIT),
        cost_estimate=pl.CostEstimate(flops=0, bytes_accessed=ranks * rows * cols * 6, transcendentals=0),
        name="unpack",
    )(late, late, sums, totals, segments, first_rows, second_rows)


class Native:
    def __init__(self, ranks):
        self.ranks = ranks

    def begin(self, tokens, cotangent, weight, tail, other, piece, width, padded):
        rank, model = lax.axis_index("ctx"), tokens.shape[1]
        parts = [lax.dynamic_slice_in_dim(weight, i * model + rank * width, width, 1) for i in range(4)]
        parts = [jnp.pad(part, ((0, 0), (0, padded - width))) for part in parts]
        cols = other.shape[1] // self.ranks
        picks = [
            lax.dynamic_slice_in_dim(other, (i * self.ranks + rank) * piece, piece, 1) for i in range(cols // piece)
        ]
        return (
            lax.all_gather(tokens, "ctx", axis=0, tiled=True),
            lax.all_gather(cotangent, "ctx", axis=0, tiled=True),
            lax.all_gather(jnp.concatenate(parts + [tail], axis=1), "fsdp", axis=0, tiled=True),
            jnp.concatenate(picks, axis=1),
        )

    def gather_cols(self, array, piece):
        return lax.all_gather(array, "ctx", axis=1, tiled=True), lax.all_gather(piece, "fsdp", axis=0, tiled=True)


def body(
    tokens, block_order, segment_ids, norm_gains, attn_in_weight, forget_weight, forget_bias,
    qk_gains, out_weight, gate_up_weight, down_weight, out_grad,
):
    ranks = lax.axis_size("ctx")
    shards = lax.axis_size("fsdp")
    rank = lax.axis_index("ctx")
    row_count, model_width = tokens.shape[1], tokens.shape[2]
    head_count, head_dim = forget_bias.shape[0], qk_gains.shape[1]
    local_heads = head_count // ranks
    width = local_heads * head_dim
    padded = -(-width // LANES) * LANES
    seq_order = block_order[0]
    seq_len = segment_ids.shape[1]
    block_len = seq_len // seq_order.shape[0]
    hidden_piece = down_weight.shape[0] // ranks
    hidden = hidden_piece * shards
    plain = ranks == 4 and shards & (shards - 1) == 0 and width == padded
    comm = Native(ranks)

    def slab(array, start, size, axis):
        return lax.dynamic_slice_in_dim(array, start, size, axis)

    def widen(array):
        return jnp.pad(array, ((0, 0), (0, padded - width))) if padded > width else array

    if plain:
        (
            inputs, grad_low, w_in, w_out, w_gate_up, normed, project, gated_all, attended,
            wide_query, wide_key, wide_value, mixed_low, down_near, normed_two, turned, gain_rows, *places_all,
            bias, head_gains,
        ) = front(
            0, ranks, shards, head_dim, local_heads, width, hidden_piece,
            tokens[0], out_grad[0], attn_in_weight, out_weight, gate_up_weight, down_weight, forget_weight.T,
            norm_gains, qk_gains, segment_ids, block_order, forget_bias[None],
        )
        gain_one, gain_two = gain_rows[0], gain_rows[1]
        w_down, hidden_act, grad_gate_up, early_grad = ffn(
            1, shards, normed_two, turned, w_gate_up, grad_low, down_near
        )
    else:
        tail = jnp.concatenate(
            [
                slab(forget_weight, rank * local_heads, local_heads, 1),
                norm_gains.T,
                jnp.zeros((attn_in_weight.shape[0], LANES - local_heads - 2), BF16),
            ],
            axis=1,
        )
        offsets = jnp.arange(block_len, dtype=jnp.int32)
        blocks = jnp.arange(seq_order.shape[0], dtype=jnp.int32)
        places = (seq_order[:, None] * block_len + offsets[None]).reshape(-1)
        by_block = segment_ids[0].reshape(-1, block_len)
        chosen = seq_order[:, None, None] == blocks[None, :, None]
        segments = jnp.sum(jnp.where(chosen, by_block[None], 0), axis=1).reshape(-1)
        places, segments = places.astype(F32), segments.astype(F32)
        places_all = (places[None, :], places[:, None], segments[None, :], segments[:, None])
        bias = jnp.pad(slab(forget_bias, rank * local_heads, local_heads, 0), (0, LANES - local_heads))[None]
        head_gains = jnp.tile(qk_gains, (1, LANES // head_dim))
        down_piece = slab(down_weight, rank * hidden_piece, hidden_piece, 0)
        inputs, grad_low, w_in, gate_up_piece = comm.begin(
            tokens[0], out_grad[0], attn_in_weight, tail, gate_up_weight, hidden_piece, width, padded
        )
        w_gate_up = lax.all_gather(gate_up_piece, "fsdp", axis=0, tiled=True)
        gain_cols = w_in[:, 4 * padded : 4 * padded + LANES].astype(F32).T
        gain_one = gain_cols[local_heads]
        gain_two = gain_cols[local_heads + 1]
        wide_inputs = inputs.astype(F32)
        scale_one = rms_scale(wide_inputs)
        normed = (wide_inputs * scale_one * gain_one).astype(BF16)
        project = dot(normed, w_in)
        gated, attended, wide_query, wide_key, wide_value = attend(
            project, places_all, bias, head_gains, head_dim, padded, local_heads
        )
        gated_all, w_out = comm.gather_cols(gated[:, :width], slab(out_weight, rank * width, width, 1))
        mixed_cols = slab(inputs, rank * width, width, 1).astype(F32) + dot(gated_all, w_out)
        mixed_low, w_down = comm.gather_cols(mixed_cols.astype(BF16), down_piece)
        mixed = mixed_low.astype(F32)
        scale_two = rms_scale(mixed)
        normed_two = (mixed * scale_two * gain_two).astype(BF16)
        gate_up = dot(normed_two, w_gate_up)
        gate_part, up_part = gate_up[:, :hidden], gate_up[:, hidden:]
        gate_sigmoid = jax.nn.sigmoid(gate_part)
        silu = gate_part * gate_sigmoid
        hidden_act = (silu * up_part).astype(BF16)
        grad_hidden = right_product(grad_low, w_down)
        grad_gate = grad_hidden * up_part * gate_sigmoid * (1.0 + gate_part * (1.0 - gate_sigmoid))
        grad_gate_up = jnp.concatenate([grad_gate, grad_hidden * silu], axis=1).astype(BF16)
        down_part_grad = left_product(hidden_act, grad_low).astype(BF16)
        gate_up_grad = left_product(normed_two, grad_gate_up).astype(BF16)
        down_part = dot(hidden_act, w_down).astype(BF16)

    def own_rows(array):
        return slab(array, rank * row_count, row_count, 0)

    def reduce_shards(array):
        return lax.psum_scatter(array.astype(BF16), "fsdp", scatter_dimension=0, tiled=True)

    if plain:
        early_share = (reduce_shards(early_grad),)
    else:
        early_share = (reduce_shards(down_part_grad), reduce_shards(gate_up_grad))
    if plain:
        grad_mixed_cols, grad_gated, gain_two_grad, down_part, out_part = middle(
            3, ranks, grad_gate_up, w_gate_up, mixed_low, grad_low, w_out, hidden_act, w_down, gated_all, gain_two[None]
        )
    else:
        grad_normed_two = right_product(grad_gate_up, w_gate_up)
        gain_two_grad = jnp.sum(grad_normed_two * mixed * scale_two, axis=0)
        grad_mixed_part = norm_back(grad_normed_two, mixed, scale_two, gain_two).astype(BF16)
        grad_mixed_cols = slab(grad_low, rank * width, width, 1).astype(F32) + lax.psum_scatter(
            grad_mixed_part, "ctx", scatter_dimension=1, tiled=True
        ).astype(F32)
        grad_branch = grad_mixed_cols.astype(BF16)
        grad_gated = widen(
            lax.psum_scatter(
                right_product(grad_branch, w_out).astype(BF16), "ctx", scatter_dimension=1, tiled=True
            ).astype(F32)
        )
    grad_project, small, *rest = attend_back(
        project, places_all, bias, head_gains, attended, (wide_query, wide_key, wide_value),
        grad_gated, (down_part, normed, out_part) if plain else (), ranks if plain else 0, head_dim, padded, local_heads,
    )
    if plain:
        down_pieces, late = rest
    else:
        in_part = left_product(normed, grad_project).astype(BF16)
        out_part = left_product(gated_all, grad_branch).astype(BF16)
        late = jnp.concatenate([in_part[:, : 4 * padded], out_part, in_part[:, 4 * padded :]], axis=1)
    late, early_share = lax.optimization_barrier((late, early_share))
    late_share = reduce_shards(late)

    if plain:
        tokens_grad, block_out, sums, parts, early_own = last_moves(
            4, ranks, shards, grad_project, w_in, inputs, early_share[0], down_pieces, mixed_low, grad_mixed_cols,
            gain_one[None], gain_two_grad, small, places_all[3],
        )
        late_own, piece_sum = finish_moves(6, ranks, shards, late_share, parts)
        gate_up_out = spread_cols(early_own, (hidden_piece, 0, 2 * shards))[0]
        down_out = unfold_rows(early_own, hidden_piece, model_width, 2 * hidden)
    else:
        grad_normed = right_product(grad_project, w_in)
        gain_one_grad = jnp.sum(grad_normed * wide_inputs * scale_one, axis=0)
        in_own = jnp.arange(model_width, dtype=jnp.int32) // width == rank
        grad_inputs = norm_back(grad_normed, wide_inputs, scale_one, gain_one) + jnp.where(
            in_own[None], jnp.tile(grad_mixed_cols, (1, ranks)), 0.0
        )
        down_sum = lax.psum_scatter(down_part, "ctx", scatter_dimension=0, tiled=True).astype(F32)
        tokens_grad = lax.psum_scatter(grad_inputs.astype(BF16), "ctx", scatter_dimension=0, tiled=True)[None]
        own_bias = jnp.where(jnp.arange(ranks, dtype=jnp.int32)[:, None] == rank, small[2:3], 0.0)
        small_rows = jnp.concatenate([small[0:2].reshape(1, -1), jnp.pad(own_bias, ((0, 0), (0, LANES)))], axis=0)
        sums = jnp.concatenate(
            [
                jnp.stack([gain_one_grad, gain_two_grad]),
                jnp.pad(small_rows, ((0, 0), (0, model_width - 2 * LANES))),
            ],
            axis=0,
        )
        sums = lax.psum(sums, "ctx")
        down_own, gate_up_own = [lax.all_gather(a, "ctx", axis=0, tiled=False) for a in early_share]
        down_out = down_own.astype(F32).reshape(down_weight.shape)
        gate_up_out = spread_cols(gate_up_own, (hidden_piece, 0, 2 * shards))[0]
        result = own_rows(mixed_low).astype(F32) + down_sum
        block_out = result.astype(BF16)[None]
        branch = result - own_rows(inputs).astype(F32)
        own_valid = own_rows(places_all[3][:, 0] >= 0).astype(F32)
        totals = lax.psum(
            jnp.stack(
                [
                    jnp.sum(own_valid * jnp.sum(result * result, axis=-1)),
                    jnp.sum(own_valid * jnp.sum(branch * branch, axis=-1)),
                ]
            ),
            "ctx",
        )
        share = model_width // shards
        room = 2 * LANES
        gain_pieces = sums[0:2].reshape(2, shards, share).transpose(1, 0, 2)
        gain_pieces = jnp.pad(gain_pieces, ((0, 0), (0, 0), (0, room - share)))
        others = jnp.broadcast_to(sums[None, 2 : 3 + ranks, :room], (shards, 1 + ranks, room))
        piece_sum = lax.psum_scatter(
            jnp.concatenate([gain_pieces, others], axis=1), "fsdp", scatter_dimension=0, tiled=False
        )
        late_own = lax.all_gather(late_share, "ctx", axis=0, tiled=False)
    if plain:
        in_out, out_out, tokens_grad, block_out, forget_out, gains_sum, bias_sum, qk_sum, rms = unpack(
            late_own, piece_sum, sums, segment_ids, tokens_grad, block_out, width, local_heads, head_dim
        )
        tokens_grad, block_out = tokens_grad[None], block_out[None]
        bias_sum, forget_out = bias_sum[0], forget_out.T
    else:
        share = model_width // shards
        valid_count = jnp.sum((segment_ids[0] >= 0).astype(F32)) * model_width
        in_out = jnp.concatenate(
            [late_own[c, :, i * padded : i * padded + width] for i in range(4) for c in range(ranks)], axis=1
        ).astype(F32)
        out_out = jnp.concatenate(
            [late_own[c, :, 4 * padded : 4 * padded + width] for c in range(ranks)], axis=1
        ).astype(F32)
        last = 4 * padded + width
        forget_out = jnp.concatenate(
            [late_own[c, :, last : last + local_heads] for c in range(ranks)], axis=1
        ).astype(F32)
        gains_sum = piece_sum[0:2, :share]
        bias_sum = piece_sum[3 : 3 + ranks, :local_heads].reshape(-1)
        qk_sum = piece_sum[2, : 2 * LANES].reshape(2, LANES // head_dim, head_dim).sum(axis=1)
        rms = jnp.sqrt(totals / valid_count)[None]
    return (
        block_out, tokens_grad, gains_sum, in_out, forget_out, bias_sum, qk_sum,
        out_out, gate_up_out, down_out, rms,
    )


def solution(mesh):
    rows = P("fsdp", "ctx", None)
    return jax.shard_map(
        body,
        mesh=mesh,
        in_specs=(
            rows, P("fsdp", None), P("fsdp", None), P(None, "fsdp"), P("fsdp", None), P("fsdp", None),
            P(), P(), P("fsdp", None), P("fsdp", None), P("fsdp", None), rows,
        ),
        out_specs=(
            rows, rows, P(None, "fsdp"), P("fsdp", None), P("fsdp", None), P(), P(),
            P("fsdp", None), P("fsdp", None), P("fsdp", None), P("fsdp", None),
        ),
        check_vma=False,
    )
```

```python
import functools

import jax
import jax.numpy as jnp
from jax import lax
from jax.experimental import pallas as pl
from jax.experimental.pallas import tpu as pltpu
from jax.sharding import PartitionSpec as P

EPS = 1e-06
SCALE = 0.125
LANES = 128
VMEM_LIMIT = 60 << 20
F32 = jnp.float32
BF16 = jnp.bfloat16


MESH = pl.DeviceIdType.MESH
ANY = pl.BlockSpec(memory_space=pltpu.HBM)


def rms_scale(values):
    return lax.rsqrt(jnp.mean(values * values, axis=-1, keepdims=True) + EPS)


def norm_back(grad_normed, values, scale_values, gain_values):
    scaled = grad_normed * gain_values
    cubed = scale_values * scale_values * scale_values
    return scale_values * scaled - values * cubed * jnp.mean(
        scaled * values, axis=-1, keepdims=True
    )


def dot(left, right):
    return lax.dot_general(
        left, right, (((1,), (0,)), ((), ())), preferred_element_type=F32
    )


def left_product(left, right):
    return lax.dot_general(
        left, right, (((0,), (0,)), ((), ())), preferred_element_type=F32
    )


def right_product(left, right):
    return lax.dot_general(
        left, right, (((1,), (1,)), ((), ())), preferred_element_type=F32
    )


def split_three(values):
    high = values.astype(BF16).astype(F32)
    rest = values - high
    middle = rest.astype(BF16).astype(F32)
    return high, middle, rest - middle


def lane_ids(rows, lanes=LANES):
    return lax.broadcasted_iota(jnp.int32, (rows, lanes), 1)


def pick_lane(values, lanes, index):
    return jnp.sum(jnp.where(lanes == index, values, 0.0), axis=-1, keepdims=True)


def turns(rows, chunk, unroll=False):
    def decorate(body):
        @pl.loop(0, rows // chunk, unroll=rows // chunk if unroll else None)
        def _(turn):
            body(pl.ds(pl.multiple_of(turn * chunk, chunk), chunk))

    return decorate


def fill_mask(chunk, pos_row, pos_col, seg_row, seg_col, mask):
    @turns(mask.shape[0], chunk)
    def _(part):
        allowed = (pos_row[0:1, :] <= pos_col[part, :]) & (seg_row[0:1, :] == seg_col[part, :])
        mask[part, :] = jnp.where(allowed, 0.0, -jnp.inf)


def fill_prefix(chunk, heads, pos_row, pos_col, logits, prefix):
    rows = prefix.shape[0]
    log_forget = jax.nn.log_sigmoid(jnp.where(lane_ids(rows) < heads, logits, 0.0))
    high, middle, low = split_three(log_forget)

    @turns(rows, chunk)
    def _(part):
        before = jnp.where(pos_row[0:1, :] <= pos_col[part, :], 1.0, 0.0).astype(BF16)
        prefix[part, :] = (
            dot(before, high.astype(BF16)) + dot(before, middle.astype(BF16)) + dot(before, low.astype(BF16))
        )


def attend_block(
    head, chunk, index, query, key, value, gate, gains, mask, prefix,
    gated, attended, wide_query, wide_key, wide_value,
):
    rows = mask.shape[0]
    lanes = lane_ids(rows)
    half = lane_ids(rows, head)
    short = lane_ids(chunk, head)
    for side in range(LANES // head):
        here = slice(side * head, (side + 1) * head)
        column = pick_lane(prefix[...], lanes, (LANES // head) * index + side)
        high, middle, low = split_three(column)
        wide = jnp.where(half == 1, high, 0.0)
        wide = jnp.where(half == 2, middle, wide)
        wide = jnp.where(half == 3, low, wide)
        query_rest = jnp.where((half >= 4) & (half < 7), 1.0, wide)
        wide = jnp.where(half == 4, -high, 0.0)
        wide = jnp.where(half == 5, -middle, wide)
        wide = jnp.where(half == 6, -low, wide)
        ones = ((half >= 1) & (half < 4)) | ((half >= 7) & (half < 10))
        key_rest = jnp.where(ones, 1.0, wide)
        raw = query[:, here]
        normed = (raw * rms_scale(raw) * gains[0:1, here]).astype(BF16)
        wide_query[side, :, 0:head] = (normed.astype(F32) * SCALE).astype(BF16)
        wide_query[side, :, head:LANES] = query_rest.astype(BF16)
        raw = key[:, here]
        wide_key[side, :, 0:head] = (raw * rms_scale(raw) * gains[1:2, here]).astype(BF16)
        wide_key[side, :, head:LANES] = key_rest.astype(BF16)
        wide_value[side, :, 0:head] = value[:, here].astype(BF16)
        wide_value[side, :, head:LANES] = jnp.where(half < 3, 1.0, 0.0).astype(BF16)

        @turns(rows, chunk, unroll=True)
        def _(part):
            scores = right_product(wide_query[side, part, :], wide_key[side]) + mask[part, :]
            expos = jnp.exp(scores)
            total = jnp.sum(expos, axis=-1, keepdims=True)
            result = dot(expos.astype(BF16), wide_value[side])[:, 0:head] / total
            attended[part, here] = result
            gated[part, here] = (result * jax.nn.sigmoid(gate(part)[:, here])).astype(BF16)
            high, middle, low = split_three(-jnp.log(total))
            rest = wide_query[side, part, head:LANES].astype(F32)
            rest = jnp.where(short == 7, high, rest)
            rest = jnp.where(short == 8, middle, rest)
            rest = jnp.where(short == 9, low, rest)
            wide_query[side, part, head:LANES] = rest.astype(BF16)


def attend_kernel(
    head, chunk, heads,
    pos_row, pos_col, seg_row, seg_col, bias, gains, query, key, value, gate, forget,
    gated, attended, wide_query, wide_key, wide_value,
    mask, prefix,
):
    @pl.when(pl.program_id(0) == 0)
    def _():
        fill_mask(chunk, pos_row, pos_col, seg_row, seg_col, mask)
        fill_prefix(chunk, heads, pos_row, pos_col, forget[...] + bias[0:1, :], prefix)

    attend_block(
        head, chunk, pl.program_id(0), query, key, value, lambda part: gate[part, :], gains, mask, prefix,
        gated, attended.at[0], wide_query, wide_key, wide_value,
    )


def attend_back_kernel(
    head, chunk, width, heads, ranks, shards,
    pos_row, pos_col, seg_row, seg_col, bias, gains, query, key, gate, forget,
    attended, wide_query, wide_key, wide_value, grad_gated, *rest,
):
    if ranks:
        aside, normed, out_grad, blocks, grad_project, small, aside_in, late, share, forget_grad = rest[:10]
        mask, wide_grad, grad_query, grad_key, grad_value, grad_prefix = rest[10:16]
        normed_in, out_in, aside_own, blocks_in, side_in, kept, from_below, from_above = rest[16:24]
        late_all, load_sem, save_sem = rest[24:27]
        sems = rest[27:29]
        over_shards = ShardSum(shards, blocks_in, side_in, kept, from_below, from_above, rest[29:])

        def loads():
            own = rows_of(aside, lax.axis_index("ctx"), aside_in.shape[1])
            for n, pair in enumerate(((normed, normed_in), (out_grad, out_in), (own, aside_own))):
                yield pltpu.make_async_copy(*pair, load_sem.at[n])

    else:
        grad_project, small, mask, wide_grad, grad_query, grad_key, grad_value, grad_prefix = rest
    step = pl.program_id(0)
    steps = pl.num_programs(0)

    def aside_copies():
        send_sem, recv_sem = sems
        rank = lax.axis_index("ctx")
        size = aside_in.shape[1]
        for distance in range(1, ranks):
            other = rank ^ distance
            yield to_rank(
                rows_of(aside, other, size), aside_in.at[rank],
                send_sem.at[distance - 1], recv_sem.at[distance - 1], other,
            )

    def sum_stage(hook):
        if not ranks:
            return
        now = (LANES // head) * step + hook
        for stage in range(over_shards.layers - 1):

            @pl.when(now == 2 + 2 * stage)
            def _():
                if stage == 0:
                    over_shards.presum()
                else:
                    over_shards.receive(stage - 1)
                over_shards.send(stage)

    if ranks:

        @pl.when(step == 0)
        def _():
            rank = lax.axis_index("ctx")
            greet([{"ctx": rank ^ distance} for distance in range(1, ranks)], over_shards)
            early = pltpu.make_async_copy(blocks, blocks_in, load_sem.at[4])
            early.start()
            for copy in aside_copies():
                copy.start()
            for copy in loads():
                copy.start()
            early.wait()
            over_shards.start()

    rows = query.shape[0]
    lanes = lane_ids(rows)
    half = lane_ids(rows, head)

    @pl.when(step == 0)
    def _():
        @pl.loop(0, rows // chunk)
        def _(turn):
            part = pl.ds(pl.multiple_of(turn * chunk, chunk), chunk)
            after = pos_row[0:1, :] >= pos_col[part, :]
            same = seg_row[0:1, :] == seg_col[part, :]
            mask[part, :] = jnp.where(after & same, 0.0, -jnp.inf)
        grad_prefix[...] = jnp.zeros_like(grad_prefix)
        small[...] = jnp.zeros_like(small)

    for side in range(LANES // head):
        sum_stage(side)
        here = pl.ds(side * head, head)

        def column(part):
            return pl.ds(pl.multiple_of(part * width + step * LANES, LANES), LANES)

        sig = jax.nn.sigmoid(gate[:, here])
        grad_in = grad_gated[:, here]
        result = attended[0, :, here]
        grad_result = (grad_in * sig).astype(BF16)
        grad_gate = (grad_in * result * sig * (1.0 - sig)).astype(BF16)
        inner = -jnp.sum(grad_result.astype(F32) * result, axis=-1, keepdims=True)
        high, middle, low = split_three(inner)
        rest = jnp.where(half == 0, high, 0.0)
        rest = jnp.where(half == 1, middle, rest)
        rest = jnp.where(half == 2, low, rest)
        wide_grad[:, 0:head] = grad_result
        wide_grad[:, head:LANES] = rest.astype(BF16)
        grad_query[...] = jnp.zeros_like(grad_query)
        @turns(rows, chunk, unroll=True)
        def _(part):
            scores = right_product(wide_key[side, part, :], wide_query[side]) + mask[part, :]
            probs = jnp.exp(scores)
            outer = right_product(wide_value[side, part, :], wide_grad[...])
            grad_scores = (probs * outer).astype(BF16)
            grad_key[part, :] = dot(grad_scores, wide_query[side])
            grad_value[part, :] = dot(probs.astype(BF16), wide_grad[...])
            grad_query[...] += left_product(wide_key[side, part, :], grad_scores)
        from_query = grad_query[...].T
        from_key = grad_key[...]
        change = pick_lane(from_query, lanes, head + 1) - pick_lane(from_key, lanes, head + 4)
        grad_prefix[...] += jnp.where(lanes == (LANES // head) * step + side, change, 0.0)

        raw = query[:, here]
        scale_raw = rms_scale(raw)
        grad_normed = from_query[:, 0:head] * SCALE
        grad_raw_query = norm_back(grad_normed, raw, scale_raw, gains[0:1, here])
        small[0:1, here] += jnp.sum(grad_normed * raw * scale_raw, axis=0, keepdims=True)
        raw = key[:, here]
        scale_raw = rms_scale(raw)
        grad_normed = from_key[:, 0:head]
        grad_raw_key = norm_back(grad_normed, raw, scale_raw, gains[1:2, here])
        small[1:2, here] += jnp.sum(grad_normed * raw * scale_raw, axis=0, keepdims=True)
        wide_grad[:, here] = grad_gate
        for part_id, piece in enumerate(
            (grad_raw_query.astype(BF16), grad_raw_key.astype(BF16), grad_value[:, 0:head].astype(BF16), grad_gate)
        ):
            if side == 0:
                grad_project[:, column(part_id)] = jnp.concatenate([piece, piece], axis=1)
            else:
                keep = grad_project[:, column(part_id)]
                both = jnp.concatenate([piece, piece], axis=1)
                grad_project[:, column(part_id)] = jnp.where(lanes < head, keep, both)

    @pl.when(step == steps - 1)
    def _():
        high, middle, low = split_three(grad_prefix[...])
        short = lane_ids(chunk)

        @pl.loop(0, rows // chunk)
        def _(turn):
            part = pl.ds(pl.multiple_of(turn * chunk, chunk), chunk)
            after = jnp.where(pos_row[0:1, :] >= pos_col[part, :], 1.0, 0.0).astype(BF16)
            total = dot(after, high.astype(BF16)) + dot(after, middle.astype(BF16)) + dot(after, low.astype(BF16))
            grad_logit = total * jax.nn.sigmoid(-(forget[part, :] + bias[0:1, :]))
            grad_logit = jnp.where(short < heads, grad_logit, 0.0).astype(BF16)
            grad_project[part, 4 * width : 4 * width + LANES] = grad_logit
            small[2:3, :] += jnp.sum(grad_logit.astype(F32), axis=0, keepdims=True)

        if ranks:
            for copy in loads():
                copy.wait()
            keep = pltpu.make_async_copy(aside_own, aside_in.at[lax.axis_index("ctx")], load_sem.at[3])
            keep.start()
            late_stages = [n for n in range(over_shards.layers - 1) if 2 + 2 * n >= heads]
            for stage in late_stages:
                over_shards.receive(stage - 1)
                over_shards.send(stage)
            ends = 4 * width, 4 * width + out_grad.shape[1]
            late_all[:, ends[0] : ends[1]] = out_in[...]
            piece = 2 * LANES

            def save(turn, size=piece):
                cols = pl.ds(pl.multiple_of(turn * piece, LANES), size)
                return pltpu.make_async_copy(late_all.at[:, cols], late.at[:, cols], save_sem.at[turn])

            count = 4 * width // piece
            rest_save = pltpu.make_async_copy(
                late_all.at[:, pl.ds(ends[0], late.shape[1] - ends[0])],
                late.at[:, pl.ds(ends[0], late.shape[1] - ends[0])],
                save_sem.at[count],
            )

            def product(into, cols):
                @turns(late.shape[0], 3 * chunk if late.shape[0] % (3 * chunk) == 0 else chunk)
                def _(part):
                    late_all[part, into] = dot(normed_in[part, :], grad_project[:, cols]).astype(BF16)

            rest_save.start()
            turned = grad_project[:, ends[0] : ends[0] + LANES].astype(F32).T[0:8, :]
            forget_grad[...] = right_product(turned.astype(BF16), normed_in[...])

            @pl.loop(0, count)
            def _(turn):
                cols = pl.ds(pl.multiple_of(turn * piece, LANES), piece)
                product(cols, cols)
                save(turn).start()

            for copy in aside_copies():
                copy.wait()
            keep.wait()
            over_shards.receive(over_shards.layers - 2)
            share[...] = kept[over_shards.layer]
            over_shards.sent()
            rest_save.wait()

            @pl.loop(0, count)
            def _(turn):
                save(turn).wait()


def pick_chunk(rows):
    return 256 if rows % 256 == 0 else 128


def whole(shape):
    return pl.BlockSpec(shape, lambda step: tuple(0 for _ in shape))


def attend(project, places, bias, gains, head, width, heads):
    rows = project.shape[0]
    steps = width // LANES
    per = LANES // head
    chunk = pick_chunk(rows)

    def part(index):
        return pl.BlockSpec((rows, LANES), lambda step: (0, index * steps + step))

    own = pl.BlockSpec((rows, LANES), lambda step: (0, step))
    wide = pl.BlockSpec((per, rows, LANES), lambda step: (step, 0, 0))
    forget = pl.BlockSpec((rows, LANES), lambda step: (0, 4 * steps))
    wide_shape = jax.ShapeDtypeStruct((per * steps, rows, LANES), BF16)
    return pl.pallas_call(
        functools.partial(attend_kernel, head, chunk, heads),
        grid=(steps,),
        in_specs=[whole(p.shape) for p in places] + [whole(bias.shape), whole(gains.shape)]
        + [part(0), part(1), part(2), part(3), forget],
        out_specs=[own, pl.BlockSpec((1, rows, LANES), lambda step: (step, 0, 0)), wide, wide, wide],
        out_shape=[
            jax.ShapeDtypeStruct((rows, width), BF16),
            jax.ShapeDtypeStruct((steps, rows, LANES), F32),
            wide_shape, wide_shape, wide_shape,
        ],
        scratch_shapes=[pltpu.VMEM((rows, rows), F32), pltpu.VMEM((rows, LANES), F32)],
        compiler_params=pltpu.CompilerParams(vmem_limit_bytes=VMEM_LIMIT),
        name="attend",
    )(*places, bias, gains, project, project, project, project, project)


def attend_back(project, places, bias, gains, attended, wides, grad_gated, beside, ranks, shards, head, width, heads):
    rows = project.shape[0]
    steps = width // LANES
    per = LANES // head
    chunk = pick_chunk(rows)

    def part(index):
        return pl.BlockSpec((rows, LANES), lambda step: (0, index * steps + step))

    own = pl.BlockSpec((rows, LANES), lambda step: (0, step))
    block = pl.BlockSpec((1, rows, LANES), lambda step: (step, 0, 0))
    wide = pl.BlockSpec((per, rows, LANES), lambda step: (step, 0, 0))
    forget = pl.BlockSpec((rows, LANES), lambda step: (0, 4 * steps))
    total = 4 * width + LANES
    out_specs = [whole((rows, total)), whole((8, LANES))]
    out_shape = [jax.ShapeDtypeStruct((rows, total), BF16), jax.ShapeDtypeStruct((8, LANES), F32)]
    scratch = [
        pltpu.VMEM((rows, rows), F32),
        pltpu.VMEM((rows, LANES), BF16),
        pltpu.VMEM((LANES, rows), F32),
        pltpu.VMEM((rows, LANES), F32),
        pltpu.VMEM((rows, LANES), F32),
        pltpu.VMEM((rows, LANES), F32),
    ]
    if ranks:
        aside, normed, out_grad, blocks = beside
        share = (blocks.shape[0] // shards, blocks.shape[1])
        sum_blocks, sum_sems = shard_sum_scratch(shards, *share)
        model, late_cols = normed.shape[0], 4 * width + out_grad.shape[1]
        out_specs += [ANY, ANY, whole(share), whole((8, model))]
        out_shape += [
            jax.ShapeDtypeStruct((ranks, aside.shape[0] // ranks, aside.shape[1]), BF16),
            jax.ShapeDtypeStruct((model, late_cols), BF16),
            jax.ShapeDtypeStruct(share, BF16),
            jax.ShapeDtypeStruct((8, model), F32),
        ]
        scratch += [
            pltpu.VMEM(normed.shape, BF16),
            pltpu.VMEM(out_grad.shape, BF16),
            pltpu.VMEM((aside.shape[0] // ranks, aside.shape[1]), BF16),
            pltpu.VMEM(blocks.shape, BF16),
            *sum_blocks,
            pltpu.VMEM((model, late_cols), BF16),
            pltpu.SemaphoreType.DMA((5,)),
            pltpu.SemaphoreType.DMA((4 * width // (2 * LANES) + 1,)),
            pltpu.SemaphoreType.DMA((ranks - 1,)),
            pltpu.SemaphoreType.DMA((ranks - 1,)),
            *sum_sems,
        ]
    return pl.pallas_call(
        functools.partial(attend_back_kernel, head, chunk, width, heads, ranks, shards),
        grid=(steps,),
        in_specs=[whole(p.shape) for p in places] + [whole(bias.shape), whole(gains.shape)]
        + [part(0), part(1), part(3), forget, block, wide, wide, wide, own] + [ANY] * len(beside),
        out_specs=out_specs,
        out_shape=out_shape,
        scratch_shapes=scratch,
        compiler_params=pltpu.CompilerParams(
            collective_id=5 if ranks else None, has_side_effects=ranks > 0, vmem_limit_bytes=VMEM_LIMIT
        ),
        name="attend_back",
    )(*places, bias, gains, project, project, project, project, attended, *wides, grad_gated, *beside)


def greet(peers, line=None):
    barrier = pltpu.get_barrier_semaphore()
    if line is not None:
        peers = peers + [line.sibling]
    for peer in peers:
        pl.semaphore_signal(barrier, inc=1, device_id=peer, device_id_type=MESH)
    if line is not None:
        for there, peer in ((line.has_above, line.above), (line.has_below, line.below)):

            @pl.when(there)
            def _():
                pl.semaphore_signal(barrier, inc=1, device_id=peer, device_id_type=MESH)

    count = len(peers)
    if line is not None:
        last = line.layers - 1
        count = count + (1 - line.layer // last) + (line.layer + last) // line.layers
    pl.semaphore_wait(barrier, count)


class Line:
    def __init__(self, shards, source, target, sems):
        self.shard = lax.axis_index("fsdp")
        self.layers = shards // 2
        self.layer, self.core = self.shard // 2, self.shard % 2
        self.sibling = {"fsdp": self.shard ^ 1}
        self.above, self.below = {"fsdp": self.shard + 2}, {"fsdp": self.shard - 2}
        self.has_above, self.has_below = self.layer < self.layers - 1, self.layer > 0
        self.source, self.target = source, target
        self.rows = target.shape[0] // shards
        self.line_send, self.line_recv, self.side_send, self.side_recv, self.own_sem = sems

    def block(self, owner):
        return rows_of(self.target, owner, self.rows)

    def line(self, owner_layer, peer, way, own=False):
        here = self.block(owner_layer * 2 + self.core)
        return pltpu.make_async_remote_copy(
            self.source if own else here, here, self.line_send.at[way, owner_layer], self.line_recv.at[owner_layer],
            device_id=peer, device_id_type=MESH,
        )

    def side(self, owner_layer, owner_core, own=False):
        here = self.block(owner_layer * 2 + owner_core)
        return pltpu.make_async_remote_copy(
            self.source if own else here, here, self.side_send.at[owner_layer], self.side_recv.at[owner_layer],
            device_id=self.sibling, device_id_type=MESH,
        )

    def start(self):
        own = self.source is not None

        @pl.when(self.has_above)
        def _():
            self.line(self.layer, self.above, 0, own).start()

        @pl.when(self.has_below)
        def _():
            self.line(self.layer, self.below, 1, own).start()

        self.side(self.layer, self.core, own).start()
        if own:
            self.keep = pltpu.make_async_copy(self.source, self.block(self.shard), self.own_sem)
            self.keep.start()

    def step(self, distance):
        lower, upper = self.layer - distance, self.layer + distance

        @pl.when(lower >= 0)
        def _():
            self.line(lower, self.below, 1).wait_recv()

            @pl.when(self.has_above)
            def _():
                self.line(lower, self.above, 0).start()

            self.side(lower, self.core).start()

        @pl.when(upper < self.layers)
        def _():
            self.line(upper, self.above, 0).wait_recv()

            @pl.when(self.has_below)
            def _():
                self.line(upper, self.below, 1).start()

            self.side(upper, self.core).start()

    def from_side(self, owner_layer):
        self.side(owner_layer, 1 - self.core).wait_recv()

    def finish(self):
        self.keep.wait()
        for owner_layer in range(self.layers):
            self.from_side(owner_layer)
        self.sent()

    def sent(self):
        for owner_layer in range(self.layers):
            self.side(owner_layer, self.core).wait_send()

            @pl.when(self.has_above & (owner_layer <= self.layer))
            def _():
                self.line(owner_layer, self.above, 0).wait_send()

            @pl.when(self.has_below & (owner_layer >= self.layer))
            def _():
                self.line(owner_layer, self.below, 1).wait_send()

    def near_finish(self):
        self.keep.wait()
        self.from_side(self.layer)
        self.side(self.layer, self.core).wait_send()

        @pl.when(self.has_below)
        def _():
            self.line(self.layer - 1, self.below, 1).wait_recv()
            self.line(self.layer, self.below, 1).wait_send()

        @pl.when(self.has_above)
        def _():
            self.line(self.layer + 1, self.above, 0).wait_recv()
            self.line(self.layer, self.above, 0).wait_send()

    def near_load(self, near, sems, number):
        if number == 0:
            chip = 2 * self.rows
            source, target = rows_of(near, self.layer, chip), rows_of(self.target, self.layer, chip)
        else:
            owner = self.shard + (-2, 2)[number - 1]
            source, target = rows_of(near, owner, self.rows), self.block(owner)
        return pltpu.make_async_copy(source, target, sems.at[number])

    def near_start(self, near, sems):
        self.near_load(near, sems, 0).start()

        @pl.when(self.has_below)
        def _():
            self.near_load(near, sems, 1).start()

        @pl.when(self.has_above)
        def _():
            self.near_load(near, sems, 2).start()

    def resume(self, near, sems):
        @pl.when(self.has_below)
        def _():
            self.near_load(near, sems, 1).wait()

            @pl.when(self.has_above)
            def _():
                self.line(self.layer - 1, self.above, 0).start()

            self.side(self.layer - 1, self.core).start()

        @pl.when(self.has_above)
        def _():
            self.near_load(near, sems, 2).wait()

            @pl.when(self.has_below)
            def _():
                self.line(self.layer + 1, self.below, 1).start()

            self.side(self.layer + 1, self.core).start()

    def resumed_sent(self):
        for owner_layer in range(self.layers):

            @pl.when(owner_layer != self.layer)
            def _():
                self.side(owner_layer, self.core).wait_send()

            @pl.when(self.has_above & (owner_layer < self.layer))
            def _():
                self.line(owner_layer, self.above, 0).wait_send()

            @pl.when(self.has_below & (owner_layer > self.layer))
            def _():
                self.line(owner_layer, self.below, 1).wait_send()


def line_scratch(shards):
    layers = shards // 2
    return [
        pltpu.SemaphoreType.DMA((2, layers)),
        pltpu.SemaphoreType.DMA((layers,)),
        pltpu.SemaphoreType.DMA((layers,)),
        pltpu.SemaphoreType.DMA((layers,)),
        pltpu.SemaphoreType.DMA,
    ]


class Relay:
    def __init__(self, rank, source, place, send_sem, recv_sem, own_sem):
        self.rank, self.source, self.place = rank, source, place
        self.send_sem, self.recv_sem, self.own_sem = send_sem, recv_sem, own_sem

    def copy(self, number):
        me = self.rank
        source, place, distance = (
            lambda: (self.source(0), self.place(me, 0), 1),
            lambda: (self.source(1), self.place(me, 1), 2),
            lambda: (self.source(1), self.place(me, 1), 1),
            lambda: (self.source(0), self.place(me, 0), 2),
            lambda: (self.place(me ^ 1, 0), self.place(me ^ 1, 0), 2),
            lambda: (self.place(me ^ 2, 1), self.place(me ^ 2, 1), 1),
        )[number]()
        return pltpu.make_async_remote_copy(
            source, place, self.send_sem.at[number], self.recv_sem.at[number],
            device_id={"ctx": me ^ distance}, device_id_type=MESH,
        )

    def own(self, h):
        return pltpu.make_async_copy(self.source(h), self.place(self.rank, h), self.own_sem.at[h])

    def start(self, keep=True):
        for number in range(4):
            self.copy(number).start()
        if keep:
            for h in range(2):
                self.own(h).start()

    def forward(self):
        for number in range(2):
            self.copy(number).wait_recv()
            self.copy(number + 4).start()

    def arrive(self):
        for number in range(2, 6):
            self.copy(number).wait_recv()

    def finish(self, arrive=True, keep=True):
        if keep:
            for h in range(2):
                self.own(h).wait()
        if arrive:
            self.arrive()
        for number in range(6):
            self.copy(number).wait_send()


def rows_of(ref, index, size):
    return ref.at[pl.ds(pl.multiple_of(index * size, 16), size), :]


def cols_of(ref, index, size):
    return ref.at[:, pl.ds(pl.multiple_of(index * size, LANES), size)]


def relay_ops(mode, rank, source, target, sems):
    rows, cols = source.shape
    half = rows // 2

    def part(h):
        return source.at[pl.ds(h * half, half), :]

    def place(block, h):
        if mode == "gather_rows":
            return target.at[pl.ds(pl.multiple_of(block * rows + h * half, 16), half), :]
        if mode == "gather_cols":
            return target.at[pl.ds(h * half, half), pl.ds(pl.multiple_of(block * cols, LANES), cols)]
        return target.at[block, pl.ds(h * half, half), :]

    return Relay(rank, part, place, *sems)


VMEM_WHOLE = pl.BlockSpec(memory_space=pltpu.VMEM)


def to_rank(source, target, send, recv, other):
    return pltpu.make_async_remote_copy(
        source, target, send, recv, device_id={"ctx": other}, device_id_type=MESH
    )


FRONT_LOADS = 6
FRONT_SAVES = 12


def front_kernel(
    shards, head, heads, width, piece, chunk,
    tokens, cotangent, weight, weight_out, other, down, forget_weight, norm_gains, qk_gains, segments, order, forget_bias,
    inputs, grad_low, w_in, w_out, w_gate_up, normed, project, gated, attended, wide_query, wide_key, wide_value,
    mixed, down_near, normed_two, turned, gain_rows, pos_row, pos_col, seg_row, seg_col, bias, gains,
    weight_all, other_all, out_all, own_x, own_g, own_in, own_pick, own_out, x_all, in_all, hn_all, proj_all, mask, prefix,
    gated_all, attended_all, query_all, key_all, value_all, out_cols, scale_one, y_own, own_down,
    mixed_all, h2_all, turned_all,
    send_sem, recv_sem, own_sem, load_sem, save_sem, *line_sems,
):
    rank = lax.axis_index("ctx")
    ranks = lax.axis_size("ctx")
    model = weight.shape[1] // 4
    rows = x_all.shape[0]
    steps = width // LANES
    tail_at = 4 * width
    loads = [
        pltpu.make_async_copy(a, b, load_sem.at[n])
        for n, (a, b) in enumerate(
            (
                (weight, weight_all), (other, other_all), (weight_out, out_all), (tokens, own_x), (cotangent, own_g),
                (rows_of(down, rank, own_down.shape[0]), own_down),
            )
        )
    ]
    saves = [
        pltpu.make_async_copy(a, b, save_sem.at[n])
        for n, (a, b) in enumerate(
            (
                (x_all, inputs), (in_all, w_in), (hn_all, normed), (proj_all, project), (query_all, wide_query),
                (key_all, wide_key), (value_all, wide_value), (attended_all, attended), (gated_all, gated),
                (mixed_all, mixed), (h2_all, normed_two), (turned_all, turned),
            )
        )
    ]
    for copy in loads:
        copy.start()
    per = len(line_sems) // 4
    in_line = Line(shards, own_in, in_all, line_sems[:per])
    out_line = Line(shards, own_out, out_cols, line_sems[per : 2 * per])
    up_line = Line(shards, own_pick, w_gate_up, line_sems[2 * per : 3 * per])
    down_line = Line(shards, own_down, down_near, line_sems[3 * per :])
    greet([{"ctx": rank ^ 1}, {"ctx": rank ^ 2}], in_line)

    def sems(n):
        return send_sem.at[n], recv_sem.at[n], own_sem.at[n]

    first = relay_ops("gather_rows", rank, own_x, x_all, sems(0))
    second = relay_ops("gather_rows", rank, own_g, grad_low, sems(1))

    def cols(start, size):
        return pl.ds(pl.multiple_of(start, LANES), size)

    loads[0].wait()
    for i in range(4):
        own_in[:, i * width : (i + 1) * width] = weight_all[:, cols(i * model + rank * width, width)]
    total_heads = forget_weight.shape[0]
    from_head = lax.broadcasted_iota(jnp.int32, (total_heads, LANES), 0)
    to_lane = lax.broadcasted_iota(jnp.int32, (total_heads, LANES), 1)
    chosen = jnp.where((to_lane < heads) & (from_head == rank * heads + to_lane), 1.0, 0.0).astype(BF16)
    from_gain = lax.broadcasted_iota(jnp.int32, (2, LANES), 0)
    to_lane = lax.broadcasted_iota(jnp.int32, (2, LANES), 1)
    chosen_gain = jnp.where(to_lane == heads + from_gain, 1.0, 0.0).astype(BF16)
    tail = left_product(forget_weight[...], chosen) + left_product(norm_gains[...], chosen_gain)
    own_in[:, tail_at : tail_at + LANES] = tail.astype(BF16)
    in_line.start()
    loads[3].wait()
    first.start()
    loads[1].wait()
    for i in range(own_pick.shape[1] // piece):
        own_pick[:, i * piece : (i + 1) * piece] = other_all[:, cols((i * ranks + rank) * piece, piece)]
    loads[2].wait()
    own_out[...] = out_all[:, cols(rank * width, width)]
    count = order.shape[1]
    length = rows // count
    row_ids = lax.broadcasted_iota(jnp.int32, (rows, LANES), 0)
    lane_id = lax.broadcasted_iota(jnp.int32, (8, rows), 1)
    tall = jnp.zeros((rows, LANES), jnp.int32)
    flat = jnp.zeros((8, rows), jnp.int32)
    for block in range(count):
        start = order[0, block] * length - block * length
        tall = jnp.where((row_ids >= block * length) & (row_ids < (block + 1) * length), row_ids + start, tall)
        flat = jnp.where((lane_id >= block * length) & (lane_id < (block + 1) * length), lane_id + start, flat)
    pos_col[...] = tall[:, 0:1].astype(F32)
    pos_row[...] = flat[0:1, :].astype(F32)
    true_segments = segments[0:1, :].astype(F32)

    @turns(rows, chunk)
    def _(part):
        true_place = lax.broadcasted_iota(jnp.int32, (chunk, rows), 1).astype(F32)
        own_place = true_place == pos_col[part, :]
        seg_col[part, :] = jnp.sum(jnp.where(own_place, true_segments, 0.0), axis=-1, keepdims=True)

    seg_row[...] = jnp.broadcast_to(seg_col[...], (rows, LANES)).T[0:1, :]
    lane = lax.broadcasted_iota(jnp.int32, (1, LANES), 1)
    bias_row = jnp.zeros((1, LANES), F32)
    for index in range(heads):
        bias_row = jnp.where(lane == index, forget_bias[0, rank * heads + index], bias_row)
    bias[...] = bias_row
    for side in range(LANES // head):
        gains[:, side * head : (side + 1) * head] = qk_gains[...]
    fill_mask(chunk, pos_row, pos_col, seg_row, seg_col, mask)
    proj_all[...] = jnp.zeros_like(proj_all)
    gain_rows[...] = jnp.zeros_like(gain_rows)
    first.forward()
    loads[4].wait()
    second.start()
    in_line.step(1)
    first.finish()
    saves[0].start()

    @turns(rows, chunk)
    def _(part):
        values = x_all[part, :].astype(F32)
        scale_one[part, :] = jnp.broadcast_to(rms_scale(values), (chunk, LANES))

    def consume(layer):
        in_line.from_side(layer)
        size = 2 * in_line.rows
        here = cols(layer * size, size)
        tail_block = in_all[here, tail_at : tail_at + LANES].astype(F32).T
        gain_rows[0:1, here] = tail_block[heads : heads + 1, :]
        gain_rows[1:2, here] = tail_block[heads + 1 : heads + 2, :]

        @turns(rows, chunk)
        def _(part):
            values = x_all[part, here].astype(F32) * scale_one[part, 0:1] * gain_rows[0:1, here]
            hn_all[here, part] = values.T.astype(BF16)
            proj_all[part, :] += dot(values.astype(BF16), in_all[here, :])

    def consume_at(distance):
        lower, upper = in_line.layer - distance, in_line.layer + distance

        @pl.when(lower >= 0)
        def _():
            consume(lower)

        @pl.when(upper < in_line.layers)
        def _():
            consume(upper)

    in_line.keep.wait()
    consume(in_line.layer)
    consume_at(1)
    second.forward()
    for distance in range(2, in_line.layers):
        in_line.step(distance)
        if distance == in_line.layers - 1:
            out_line.start()
            up_line.start()
        consume_at(distance)

    for n in (1, 2, 3):
        saves[n].start()
    out_line.step(1)
    fill_prefix(chunk, heads, pos_row, pos_col, proj_all[:, tail_at : tail_at + LANES] + bias[0:1, :], prefix)

    def share(index):
        block = rank * steps + index
        half = rows // 2

        def source(h):
            return gated_all.at[block, pl.ds(h * half, half), :]

        def place(owner, h):
            return gated_all.at[owner * steps + index, pl.ds(h * half, half), :]

        return Relay(rank, source, place, send_sem.at[2 + index], recv_sem.at[2 + index], None)

    per_block = LANES // head

    @pl.loop(0, steps)
    def _(index):
        def lanes_of(part_id):
            return proj_all[:, cols(part_id * width + index * LANES, LANES)]

        def gate(part):
            return proj_all[part, cols(3 * width + index * LANES, LANES)]

        group = pl.ds(index * per_block, per_block)
        attend_block(
            head, chunk, index, lanes_of(0), lanes_of(1), lanes_of(2), gate, gains, mask, prefix,
            gated_all.at[rank * steps + index], attended_all.at[index],
            query_all.at[group], key_all.at[group], value_all.at[group],
        )
        share(index).start(keep=False)

        @pl.when(index == 0)
        def _():
            out_line.step(2)

        @pl.when(index > 0)
        def _():
            share(index - 1).forward()

    up_line.step(1)
    out_line.step(3)
    share(steps - 1).forward()
    for n in (4, 5, 6, 7):
        saves[n].start()
    for index in range(steps):
        share(index).arrive()
    saves[8].start()
    out_line.keep.wait()
    for layer in range(out_line.layers):
        out_line.from_side(layer)
    save_out = pltpu.make_async_copy(out_cols, w_out, save_sem.at[len(saves)])
    save_out.start()

    third = relay_ops("gather_cols", rank, y_own, mixed_all, sems(2 + steps))

    @turns(rows, chunk)
    def _(part):
        total = x_all[part, cols(rank * width, width)].astype(F32)
        for block in range(gated_all.shape[0]):
            total = total + dot(gated_all[block, part, :], out_cols[block * LANES : (block + 1) * LANES, :])
        y_own[part, :] = total.astype(BF16)

    third.start()
    third.forward()
    up_line.step(2)
    loads[5].wait()
    down_line.start()
    third.finish()
    saves[9].start()

    @turns(rows, chunk)
    def _(part):
        values = mixed_all[part, :].astype(F32)
        low = values * rms_scale(values) * gain_rows[1:2, :]
        h2_all[part, :] = low.astype(BF16)
        turned_all[:, part] = low.T.astype(BF16)

    saves[10].start()
    saves[11].start()
    for distance in range(3, up_line.layers):
        up_line.step(distance)
    up_line.finish()
    down_line.near_finish()
    out_line.sent()
    in_line.sent()
    second.finish()
    for index in range(steps):
        share(index).finish(arrive=False, keep=False)
    for copy in saves:
        copy.wait()
    save_out.wait()


def front(
    collective_id, ranks, shards, head, heads, width, piece,
    tokens, cotangent, weight, weight_out, other, down, forget_weight, norm_gains, qk_gains, segments, order, forget_bias,
):
    own_rows, model = tokens.shape
    rows = ranks * own_rows
    chunk = pick_chunk(rows)
    steps, shard_rows = width // LANES, weight.shape[0]
    wide_in = 4 * width + LANES
    other_cols = other.shape[1] // ranks
    wide = (heads, rows, LANES)
    shape, vmem = jax.ShapeDtypeStruct, pltpu.VMEM
    return pl.pallas_call(
        functools.partial(front_kernel, shards, head, heads, width, piece, chunk),
        in_specs=[ANY] * 6 + [VMEM_WHOLE] * 4 + [pl.BlockSpec(memory_space=pltpu.SMEM)] * 2,
        out_specs=[ANY] * 16 + [VMEM_WHOLE] * 7,
        out_shape=[
            shape((rows, model), BF16),
            shape((rows, model), BF16),
            shape((model, wide_in), BF16),
            shape((model, width), BF16),
            shape((model, other_cols), BF16),
            shape((model, rows), BF16),
            shape((rows, wide_in), F32),
            shape((ranks * steps, rows, LANES), BF16),
            shape((steps, rows, LANES), F32),
            shape(wide, BF16), shape(wide, BF16), shape(wide, BF16),
            shape((rows, model), BF16),
            shape((shards * (down.shape[0] // ranks), model), BF16),
            shape((rows, model), BF16),
            shape((model, rows), BF16),
            shape((8, model), F32),
            shape((1, rows), F32), shape((rows, 1), F32), shape((1, rows), F32), shape((rows, 1), F32),
            shape((1, LANES), F32),
            shape((2, LANES), F32),
        ],
        scratch_shapes=[
            vmem(weight.shape, BF16),
            vmem(other.shape, BF16),
            vmem(weight_out.shape, BF16),
            vmem(tokens.shape, BF16),
            vmem(cotangent.shape, BF16),
            vmem((shard_rows, wide_in), BF16),
            vmem((shard_rows, other_cols), BF16),
            vmem((shard_rows, width), BF16),
            vmem((rows, model), BF16),
            vmem((model, wide_in), BF16),
            vmem((model, rows), BF16),
            vmem((rows, wide_in), F32),
            vmem((rows, rows), F32),
            vmem((rows, LANES), F32),
            vmem((ranks * steps, rows, LANES), BF16),
            vmem((steps, rows, LANES), F32),
            vmem(wide, BF16), vmem(wide, BF16), vmem(wide, BF16),
            vmem((model, width), BF16),
            vmem((rows, LANES), F32),
            vmem((rows, width), BF16),
            vmem((down.shape[0] // ranks, model), BF16),
            vmem((rows, model), BF16),
            vmem((rows, model), BF16),
            vmem((model, rows), BF16),
            pltpu.SemaphoreType.DMA((3 + steps, 6)),
            pltpu.SemaphoreType.DMA((3 + steps, 6)),
            pltpu.SemaphoreType.DMA((3 + steps, 2)),
            pltpu.SemaphoreType.DMA((FRONT_LOADS,)),
            pltpu.SemaphoreType.DMA((FRONT_SAVES + 1,)),
        ]
        + 4 * line_scratch(shards),
        compiler_params=pltpu.CompilerParams(
            collective_id=collective_id, has_side_effects=True, vmem_limit_bytes=VMEM_LIMIT
        ),
        cost_estimate=pl.CostEstimate(flops=0, bytes_accessed=300 << 20, transcendentals=0),
        name="front",
    )(
        tokens, cotangent, weight, weight_out, other, down, forget_weight, norm_gains, qk_gains, segments, order, forget_bias
    )


def ffn_kernel(
    shards, chunk,
    normed, turned_from, w_gate_up, cotangent, down_near,
    w_down, hidden, grad_gate_up, grad_weight, grad_down,
    weight_in, cotangent_in, gates, ups, hn, turned, acts, grads, weight_out, down_out,
    load_sem, save_sem, tile_sem, near_sem, *line_sems,
):
    size = gates.shape[1]
    rows, model = normed.shape
    tile = 2 * w_down.shape[0] // shards
    loads = [
        pltpu.make_async_copy(a, b, load_sem.at[n])
        for n, (a, b) in enumerate(
            ((normed, hn), (w_gate_up, weight_in), (cotangent, cotangent_in), (turned_from, turned))
        )
    ]
    saves = [
        pltpu.make_async_copy(a, b, save_sem.at[n])
        for n, (a, b) in enumerate(
            ((acts, hidden), (down_out, grad_down))
        )
    ]
    line = Line(shards, None, w_down, line_sems)
    line.near_start(down_near, near_sem)
    for copy in loads:
        copy.start()
    greet([], line)
    line.resume(down_near, near_sem)
    loads[0].wait()
    loads[1].wait()

    def span(turn, start=0):
        return pl.ds(pl.multiple_of(start + turn * tile, LANES), tile)

    def activate(turn):
        gate = dot(hn[...], weight_in[:, span(turn)])
        up = dot(hn[...], weight_in[:, span(turn, size)])
        gates[:, span(turn)] = gate
        ups[:, span(turn)] = up
        acts[:, span(turn)] = (jax.nn.silu(gate) * up).astype(BF16)

    def down_grad(turn):
        down_out[span(turn), :] = left_product(acts[:, span(turn)], cotangent_in[...]).astype(BF16)

    count = size // tile
    pl.loop(0, count)(activate)
    saves[0].start()
    loads[2].wait()
    loads[3].wait()
    line.near_load(down_near, near_sem, 0).wait()

    def consume(turn):
        grad = right_product(cotangent_in[...], w_down[span(turn), :])
        gate, up = gates[:, span(turn)], ups[:, span(turn)]
        sig = jax.nn.sigmoid(gate)
        grads[:, span(turn)] = (grad * up * sig * (1.0 + gate * (1.0 - sig))).astype(BF16)
        grads[:, span(turn, size)] = (grad * gate * sig).astype(BF16)

        for start in (0, size):
            here = span(turn, start)

            @turns(model, 3 * chunk if model % (3 * chunk) == 0 else chunk)
            def _(part):
                weight_out[part, here] = dot(turned[part, :], grads[:, here]).astype(BF16)

        for copy in tile_saves(turn):
            copy.start()

    def tile_saves(turn):
        for n, start in enumerate((0, size)):
            here = span(turn, start)
            yield pltpu.make_async_copy(grads.at[:, here], grad_gate_up.at[:, here], tile_sem.at[turn, 2 * n])
            yield pltpu.make_async_copy(weight_out.at[:, here], grad_weight.at[:, here], tile_sem.at[turn, 2 * n + 1])

    def consume_at(distance):
        lower, upper = line.layer - distance, line.layer + distance

        @pl.when(lower >= 0)
        def _():
            line.from_side(lower)
            consume(lower)

        @pl.when(upper < line.layers)
        def _():
            line.from_side(upper)
            consume(upper)

    line.step(2)
    consume(line.layer)
    consume_at(1)
    pl.loop(0, count)(down_grad)
    saves[1].start()
    for distance in range(3, line.layers):
        line.step(distance)
    for distance in range(2, line.layers):
        consume_at(distance)
    line.resumed_sent()
    for copy in saves:
        copy.wait()

    @pl.loop(0, count)
    def _(turn):
        for copy in tile_saves(turn):
            copy.wait()


def ffn(collective_id, shards, normed, turned, w_gate_up, cotangent, down_near):
    rows, model = normed.shape
    size = w_gate_up.shape[1] // 2
    shape, vmem = jax.ShapeDtypeStruct, pltpu.VMEM
    return pl.pallas_call(
        functools.partial(ffn_kernel, shards, pick_chunk(rows)),
        in_specs=[ANY] * 5,
        out_specs=[VMEM_WHOLE] + [ANY] * 4,
        out_shape=[
            shape((size, model), BF16),
            shape((rows, size), BF16),
            shape((rows, 2 * size), BF16),
            shape((model, 2 * size), BF16),
            shape((size, model), BF16),
        ],
        scratch_shapes=[
            vmem(w_gate_up.shape, BF16),
            vmem((rows, model), BF16),
            vmem((rows, size), F32),
            vmem((rows, size), F32),
            vmem((rows, model), BF16),
            vmem((model, rows), BF16),
            vmem((rows, size), BF16),
            vmem((rows, 2 * size), BF16),
            vmem((model, 2 * size), BF16),
            vmem((size, model), BF16),
            pltpu.SemaphoreType.DMA((4,)),
            pltpu.SemaphoreType.DMA((2,)),
            pltpu.SemaphoreType.DMA((shards // 2, 4)),
            pltpu.SemaphoreType.DMA((3,)),
        ]
        + line_scratch(shards),
        compiler_params=pltpu.CompilerParams(
            collective_id=collective_id, has_side_effects=True, vmem_limit_bytes=VMEM_LIMIT
        ),
        cost_estimate=pl.CostEstimate(flops=0, bytes_accessed=100 << 20, transcendentals=0),
        name="ffn",
    )(normed, turned, w_gate_up, cotangent, down_near)


class ShardSum:
    def __init__(self, shards, blocks, side_in, kept, from_below, from_above, sems):
        self.shard = lax.axis_index("fsdp")
        self.layers = shards // 2
        self.layer, self.core = self.shard // 2, self.shard % 2
        self.sibling = {"fsdp": self.shard ^ 1}
        self.above, self.below = {"fsdp": self.shard + 2}, {"fsdp": self.shard - 2}
        self.has_above, self.has_below = self.layer < self.layers - 1, self.layer > 0
        self.blocks, self.side_in, self.kept = blocks, side_in, kept
        self.from_below, self.from_above = from_below, from_above
        self.rows = kept.shape[1]
        self.side_send, self.side_recv, self.up_send, self.up_recv, self.down_send, self.down_recv = sems

    def side(self, layer):
        return pltpu.make_async_remote_copy(
            rows_of(self.blocks, 2 * layer + 1 - self.core, self.rows), self.side_in.at[layer],
            self.side_send.at[layer], self.side_recv.at[layer], device_id=self.sibling, device_id_type=MESH,
        )

    def start(self):
        for layer in range(self.layers):
            self.side(layer).start()

    def presum(self):
        for layer in range(self.layers):
            self.side(layer).wait_recv()
            own = rows_of(self.blocks, 2 * layer + self.core, self.rows)[...].astype(F32)
            self.kept[layer] = (own + self.side_in[layer].astype(F32)).astype(BF16)

    def up(self, stage):
        return pltpu.make_async_remote_copy(
            self.kept.at[self.layers - 1 - stage + self.layer], self.from_below.at[stage],
            self.up_send.at[stage], self.up_recv.at[stage], device_id=self.above, device_id_type=MESH,
        )

    def down(self, stage):
        return pltpu.make_async_remote_copy(
            self.kept.at[stage - self.layers + 1 + self.layer], self.from_above.at[stage],
            self.down_send.at[stage], self.down_recv.at[stage], device_id=self.below, device_id_type=MESH,
        )

    def each_sent(self, stage, what):
        @pl.when(self.has_above & (self.layer <= stage))
        def _():
            what(self.up(stage))

        @pl.when(self.has_below & (self.layers - 1 - self.layer <= stage))
        def _():
            what(self.down(stage))

    def send(self, stage):
        self.each_sent(stage, lambda copy: copy.start())

    def receive(self, stage):
        def add(target, arrived):
            self.kept[target] = (self.kept[target].astype(F32) + arrived[stage].astype(F32)).astype(BF16)

        @pl.when(self.has_below & (self.layer - 1 <= stage))
        def _():
            pltpu.make_async_remote_copy(
                self.from_below.at[stage], self.from_below.at[stage], self.up_send.at[stage], self.up_recv.at[stage],
                device_id=self.below, device_id_type=MESH,
            ).wait_recv()
            add(self.layers - 2 - stage + self.layer, self.from_below)

        @pl.when(self.has_above & (self.layers - 2 - self.layer <= stage))
        def _():
            pltpu.make_async_remote_copy(
                self.from_above.at[stage], self.from_above.at[stage], self.down_send.at[stage],
                self.down_recv.at[stage], device_id=self.above, device_id_type=MESH,
            ).wait_recv()
            add(stage - self.layers + 2 + self.layer, self.from_above)

    def sent(self):
        for layer in range(self.layers):
            self.side(layer).wait_send()
        for stage in range(self.layers - 1):
            self.each_sent(stage, lambda copy: copy.wait_send())


def shard_sum_scratch(shards, rows, cols):
    layers = shards // 2
    few, all_layers = pltpu.SemaphoreType.DMA((layers - 1,)), pltpu.SemaphoreType.DMA((layers,))
    block = pltpu.VMEM((layers, rows, cols), BF16)
    part = pltpu.VMEM((layers - 1, rows, cols), BF16)
    return [block, block, part, part], [all_layers, all_layers, few, few, few, few]


class Fold:
    def __init__(self, rank, piece, first, between, second, send_sem, recv_sem):
        self.rank, self.piece, self.first, self.between, self.second = rank, piece, first, between, second
        self.send_sem, self.recv_sem = send_sem, recv_sem

    def copy(self, number):
        me = self.rank
        source, target, distance = (
            lambda: (self.piece(me ^ 1, 0), self.first(0, 0), 1),
            lambda: (self.piece(me ^ 3, 0), self.first(1, 0), 1),
            lambda: (self.piece(me ^ 2, 1), self.first(0, 1), 2),
            lambda: (self.piece(me ^ 3, 1), self.first(1, 1), 2),
            lambda: (self.between(0), self.second(0), 2),
            lambda: (self.between(1), self.second(1), 1),
        )[number]()
        return to_rank(source, target, self.send_sem.at[number], self.recv_sem.at[number], me ^ distance)

    def start(self):
        for number in range(4):
            self.copy(number).start()

    def pass_on(self):
        for h, distance in ((0, 2), (1, 1)):
            self.copy(2 * h).wait_recv()
            self.copy(2 * h + 1).wait_recv()
            own = self.piece(self.rank ^ distance, h)[...].astype(F32)
            self.between(h)[...] = (own + self.first(1, h)[...].astype(F32)).astype(BF16)
            self.copy(4 + h).start()

    def total(self, h):
        self.copy(4 + h).wait_recv()
        own = self.piece(self.rank, h)[...].astype(F32)
        return own + self.first(0, h)[...].astype(F32) + self.second(h)[...].astype(F32)

    def sent(self):
        for number in range(6):
            self.copy(number).wait_send()


def middle_kernel(
    ranks,
    grad_gate_up, w_gate_up, mixed, cotangent, w_out, hidden, w_down, gated, gain,
    mixed_grad, gated_grad, gain_grad, down_part, out_grad,
    grad_in, weight_in, mixed_in, cotangent_in, out_in, hidden_in, down_in, gated_in, low_grad, down_all, out_all,
    wide, first_out, first_in, first_between, first_end, second_out, second_in, second_between, second_end,
    load_sem, save_sem, first_send, first_recv, second_send, second_recv,
):
    rank = lax.axis_index("ctx")
    rows = mixed.shape[0] // ranks
    model, width = w_out.shape
    tile = 256
    loads = [
        pltpu.make_async_copy(a, b, load_sem.at[n])
        for n, (a, b) in enumerate(
            (
                (w_gate_up, weight_in), (grad_gate_up, grad_in), (mixed, mixed_in), (cotangent, cotangent_in),
                (w_out, out_in), (hidden, hidden_in), (w_down, down_in), (gated, gated_in),
            )
        )
    ]
    saves = [
        pltpu.make_async_copy(down_all, down_part, save_sem.at[0]),
        pltpu.make_async_copy(out_all, out_grad, save_sem.at[1]),
    ]
    for copy in loads:
        copy.start()
    greet([{"ctx": rank ^ distance} for distance in range(1, ranks)])
    gain_grad[...] = jnp.zeros_like(gain_grad)
    for copy in loads[:2]:
        copy.wait()

    def part(turn):
        return pl.ds(pl.multiple_of(turn * rows, 16), rows)

    half = rows // 2

    def fold(out, into, between, end, send_sem, recv_sem):
        def make(turn):
            def at(h):
                return pl.ds(pl.multiple_of(turn * rows + h * half, 16), half)

            return Fold(
                rank,
                lambda index, h: out.at[index, at(h), :],
                lambda slot, h: into.at[slot, at(h), :],
                lambda h: between.at[at(h), :],
                lambda h: end.at[at(h), :],
                send_sem.at[turn],
                recv_sem.at[turn],
            )

        return make

    first = fold(first_out, first_in, first_between, first_end, first_send, first_recv)
    second = fold(second_out, second_in, second_between, second_end, second_send, second_recv)

    def compute(turn):
        here = part(turn)

        @pl.loop(0, model // tile)
        def _(step):
            cols = pl.ds(pl.multiple_of(step * tile, tile), tile)
            wide[:, cols] = right_product(grad_in[here, :], weight_in[cols, :])

        @pl.when(turn == 0)
        def _():
            for copy in loads[2:5]:
                copy.wait()

        values = mixed_in[here, :].astype(F32)
        scale = rms_scale(values)
        grad = wide[...]
        gain_grad[0:1, :] += jnp.sum(grad * values * scale, axis=0, keepdims=True)
        back = norm_back(grad, values, scale, gain[1:2, :]).astype(BF16)
        for index in range(ranks):
            first_out[index, here, :] = back[:, index * width : (index + 1) * width]
        first(turn).start()

    def project(turn):
        here = part(turn)
        for h in range(2):
            at = pl.ds(pl.multiple_of(turn * rows + h * half, 16), half)
            total = cotangent_in[at, pl.ds(pl.multiple_of(rank * width, LANES), width)].astype(F32)
            total = total + first(turn).total(h)
            mixed_grad[at, :] = total
            low_grad[at, :] = total.astype(BF16)
        for index in range(ranks):
            second_out[index, here, :] = right_product(
                low_grad[here, :], out_in[index * width : (index + 1) * width, :]
            ).astype(BF16)
        second(turn).start()

    def collect(turn):
        for h in range(2):
            at = pl.ds(pl.multiple_of(turn * rows + h * half, 16), half)
            gated_grad[at, :] = second(turn).total(h)

    def aside(turn):
        @pl.when(turn == ranks)
        def _():
            for copy in loads[5:8]:
                copy.wait()

            @pl.loop(0, model // tile)
            def _(step):
                cols = pl.ds(pl.multiple_of(step * tile, tile), tile)
                down_all[:, cols] = dot(hidden_in[...], down_in[:, cols]).astype(BF16)

            saves[0].start()

        @pl.when(turn == ranks + 2)
        def _():
            @pl.loop(0, gated_in.shape[0])
            def _(block):
                out_all[pl.ds(pl.multiple_of(block * LANES, LANES), LANES), :] = left_product(
                    gated_in[block], low_grad[...]
                ).astype(BF16)

            saves[1].start()

    @pl.loop(0, ranks + 4)
    def _(turn):
        stages = (
            compute, lambda t: first(t).pass_on(), project, lambda t: second(t).pass_on(), collect,
        )
        for lag, stage in enumerate(stages):
            if lag == 4:
                aside(turn)

            @pl.when((turn >= lag) & (turn < ranks + lag))
            def _():
                stage(turn - lag)

    @pl.loop(0, ranks)
    def _(turn):
        first(turn).sent()
        second(turn).sent()

    for copy in saves:
        copy.wait()


def middle(
    collective_id, ranks, grad_gate_up, w_gate_up, mixed, cotangent, w_out, hidden, w_down, gated, gain
):
    rows, model = mixed.shape
    width = w_out.shape[1]
    flat = pltpu.VMEM((rows, width), BF16)
    blocks = [pltpu.VMEM((ranks, rows, width), BF16), pltpu.VMEM((2, rows, width), BF16), flat, flat]
    sems = pltpu.SemaphoreType.DMA((ranks, 6))
    return pl.pallas_call(
        functools.partial(middle_kernel, ranks),
        in_specs=[ANY] * 8 + [VMEM_WHOLE],
        out_specs=[VMEM_WHOLE] * 3 + [ANY] * 2,
        out_shape=[
            jax.ShapeDtypeStruct((rows, width), F32),
            jax.ShapeDtypeStruct((rows, width), F32),
            jax.ShapeDtypeStruct((8, model), F32),
            jax.ShapeDtypeStruct((rows, model), BF16),
            jax.ShapeDtypeStruct((model, width), BF16),
        ],
        scratch_shapes=[
            pltpu.VMEM(grad_gate_up.shape, BF16),
            pltpu.VMEM(w_gate_up.shape, BF16),
            pltpu.VMEM(mixed.shape, BF16),
            pltpu.VMEM(cotangent.shape, BF16),
            pltpu.VMEM(w_out.shape, BF16),
            pltpu.VMEM(hidden.shape, BF16),
            pltpu.VMEM(w_down.shape, BF16),
            pltpu.VMEM(gated.shape, BF16),
            pltpu.VMEM((rows, width), BF16),
            pltpu.VMEM((rows, model), BF16),
            pltpu.VMEM((model, width), BF16),
            pltpu.VMEM((rows // ranks, model), F32),
            *blocks, *blocks,
            pltpu.SemaphoreType.DMA((8,)),
            pltpu.SemaphoreType.DMA((2,)),
            sems, sems, sems, sems,
        ],
        compiler_params=pltpu.CompilerParams(
            collective_id=collective_id, has_side_effects=True, vmem_limit_bytes=VMEM_LIMIT
        ),
        cost_estimate=pl.CostEstimate(flops=0, bytes_accessed=150 << 20, transcendentals=0),
        name="middle",
    )(grad_gate_up, w_gate_up, mixed, cotangent, w_out, hidden, w_down, gated, gain)


def last_kernel(
    ranks, shards,
    grad_project, w_in, inputs, aside, pieces, mixed, share, mixed_grad, gain, gain_two_grad, small, segments, forget_grad,
    tokens_grad, block_out, total_sums, parts, aside_all, share_all,
    grad_in, weight_in, inputs_in, aside_in, pieces_in, mixed_in, wide, out, into, between, end, sums_out, sums_in,
    share_in, load_sem, send_sem, recv_sem, sums_send, sums_recv, aside_send, aside_recv, aside_own,
):
    rank = lax.axis_index("ctx")
    rows = inputs.shape[0] // ranks
    model, width = inputs.shape[1], mixed_grad.shape[1]
    tile = 256
    loads = [
        pltpu.make_async_copy(a, b, load_sem.at[n])
        for n, (a, b) in enumerate(
            (
                (aside, aside_in), (w_in, weight_in), (grad_project, grad_in), (inputs, inputs_in),
                (pieces, pieces_in), (rows_of(mixed, rank, rows), mixed_in), (share, share_in),
            )
        )
    ]
    for copy in loads:
        copy.start()
    greet([{"ctx": rank ^ distance} for distance in range(1, ranks)])
    relay, share_relay = [
        relay_ops("stack", rank, a, b, (aside_send.at[n], aside_recv.at[n], aside_own.at[n]))
        for n, (a, b) in enumerate(((aside_in, aside_all), (share_in, share_all)))
    ]
    loads[6].wait()
    share_relay.start()
    loads[0].wait()
    relay.start()
    sums_out[...] = jnp.zeros_like(sums_out)
    sums_out[1:2, :] = gain_two_grad[0:1, :]
    sums_out[2:3, 0:LANES] = small[0:1, :]
    sums_out[2:3, LANES : 2 * LANES] = small[1:2, :]
    for index in range(ranks):
        sums_out[3 + index : 4 + index, 0:LANES] = jnp.where(rank == index, small[2:3, :], 0.0)
    for copy in loads[1:4]:
        copy.wait()

    half = rows // 2

    def at(h):
        return pl.ds(h * half, half)

    fold = Fold(
        rank,
        lambda index, h: out.at[index, at(h), :],
        lambda slot, h: into.at[slot, at(h), :],
        lambda h: between.at[at(h), :],
        lambda h: end.at[at(h), :],
        send_sem,
        recv_sem,
    )

    def send_sums(distance):
        return to_rank(
            sums_out, sums_in.at[distance], sums_send.at[distance - 1], sums_recv.at[distance - 1], rank ^ distance
        )

    def compute(other):
        here = pl.ds(pl.multiple_of(other * rows, 16), rows)

        @pl.loop(0, model // tile)
        def _(step):
            cols = pl.ds(pl.multiple_of(step * tile, tile), tile)
            wide[:, cols] = right_product(grad_in[here, :], weight_in[cols, :])

        values = inputs_in[here, :].astype(F32)
        scale = rms_scale(values)
        grad = wide[...]
        sums_out[0:1, :] += jnp.sum(grad * values * scale, axis=0, keepdims=True)
        wide[...] = norm_back(grad, values, scale, gain[0:1, :])
        own = pl.ds(pl.multiple_of(rank * width, LANES), width)
        wide[:, own] += mixed_grad[here, :]
        out[other] = wide[...].astype(BF16)

    @pl.loop(1, ranks)
    def _(turn):
        compute(rank ^ (ranks - turn))

        @pl.when(turn == 2)
        def _():
            for number in (2, 3):
                fold.copy(number).start()

        @pl.when(turn == 3)
        def _():
            for number in (0, 1):
                fold.copy(number).start()

    share_relay.forward()
    for copy in loads[4:6]:
        copy.wait()
    own = pl.ds(pl.multiple_of(rank * rows, 16), rows)
    result = mixed_in[...].astype(F32)
    for index in range(ranks):
        result = result + pieces_in[index].astype(F32)
    block_out[...] = result.astype(BF16)
    branch = result - inputs_in[own, :].astype(F32)
    valid = jnp.where(segments[own, :] >= 0.0, 1.0, 0.0)
    lane = lax.broadcasted_iota(jnp.int32, (1, LANES), 1)
    stats = jnp.zeros((1, LANES), F32)
    for index, values in enumerate((result, branch)):
        total = jnp.sum(valid * jnp.sum(values * values, axis=-1, keepdims=True), axis=0, keepdims=True)
        stats = jnp.where(lane == index, total, stats)
    sums_out[7:8, 0:LANES] = stats
    compute(rank)
    for distance in range(1, ranks):
        send_sums(distance).start()
    relay.forward()
    fold.pass_on()
    for h in range(2):
        tokens_grad[at(h), :] = fold.total(h).astype(BF16)
    total = sums_out[...]
    for distance in range(1, ranks):
        send_sums(distance).wait_recv()
        total = total + sums_in[distance]
    total_sums[...] = total
    share = model // shards
    parts[...] = jnp.zeros_like(parts)
    for index in range(shards):
        parts[index, 0:2, 0:share] = total[0:2, index * share : (index + 1) * share]
        parts[index, 2:8, :] = total[2:8, 0 : parts.shape[2]]
        parts[index, 8:16, 0:share] = forget_grad[:, index * share : (index + 1) * share]
    fold.sent()
    for distance in range(1, ranks):
        send_sums(distance).wait_send()
    relay.finish()
    share_relay.finish()


def last_moves(
    collective_id, ranks, shards,
    grad_project, w_in, inputs, aside, pieces, mixed, share, mixed_grad, gain, gain_two_grad, small, segments,
    forget_grad,
):
    rows, model = inputs.shape
    own = (rows // ranks, model)
    flat = pltpu.VMEM(own, BF16)
    blocks = [pltpu.VMEM((ranks,) + own, BF16), pltpu.VMEM((2,) + own, BF16), flat, flat]
    sems = pltpu.SemaphoreType.DMA((ranks - 1,))
    return pl.pallas_call(
        functools.partial(last_kernel, ranks, shards),
        in_specs=[ANY] * 7 + [VMEM_WHOLE] * 6,
        out_specs=[VMEM_WHOLE] * 4 + [ANY] * 2,
        out_shape=[
            jax.ShapeDtypeStruct(own, BF16),
            jax.ShapeDtypeStruct(own, BF16),
            jax.ShapeDtypeStruct((8, model), F32),
            jax.ShapeDtypeStruct((shards, 16, max(2 * LANES, -(-model // shards // LANES) * LANES)), F32),
            jax.ShapeDtypeStruct((ranks,) + aside.shape, BF16),
            jax.ShapeDtypeStruct((ranks,) + share.shape, BF16),
        ],
        scratch_shapes=[
            pltpu.VMEM(grad_project.shape, BF16),
            pltpu.VMEM(w_in.shape, BF16),
            pltpu.VMEM(inputs.shape, BF16),
            pltpu.VMEM(aside.shape, BF16),
            pltpu.VMEM(pieces.shape, BF16),
            pltpu.VMEM(own, BF16),
            pltpu.VMEM(own, F32),
            *blocks,
            pltpu.VMEM((8, model), F32),
            pltpu.VMEM((ranks, 8, model), F32),
            pltpu.VMEM(share.shape, BF16),
            pltpu.SemaphoreType.DMA((7,)),
            pltpu.SemaphoreType.DMA((6,)),
            pltpu.SemaphoreType.DMA((6,)),
            sems, sems,
            pltpu.SemaphoreType.DMA((2, 6)),
            pltpu.SemaphoreType.DMA((2, 6)),
            pltpu.SemaphoreType.DMA((2, 2)),
        ],
        compiler_params=pltpu.CompilerParams(
            collective_id=collective_id, has_side_effects=True, vmem_limit_bytes=VMEM_LIMIT
        ),
        cost_estimate=pl.CostEstimate(flops=0, bytes_accessed=150 << 20, transcendentals=0),
        name="last_moves",
    )(grad_project, w_in, inputs, aside, pieces, mixed, share, mixed_grad, gain, gain_two_grad, small, segments, forget_grad)


def finish_kernel(
    ranks, shards, late, parts, late_all, part_sum, forget_all,
    late_in, into, load_sem, send_sem, recv_sem, own_sem, part_send, part_recv, forget_send, forget_recv,
):
    rank = lax.axis_index("ctx")
    shard = lax.axis_index("fsdp")
    load = pltpu.make_async_copy(late, late_in, load_sem.at[0])
    load.start()
    relay = relay_ops("stack", rank, late_in, late_all, (send_sem, recv_sem, own_sem))
    greet(
        [{"ctx": rank ^ distance} for distance in range(1, ranks)]
        + [{"fsdp": shard ^ distance} for distance in range(1, shards)]
    )
    load.wait()
    relay.start()

    def send(distance):
        other = shard ^ distance
        return pltpu.make_async_remote_copy(
            parts.at[other], into.at[distance], part_send.at[distance - 1], part_recv.at[distance - 1],
            device_id={"fsdp": other}, device_id_type=MESH,
        )

    def send_forget(distance):
        return to_rank(
            forget_all.at[rank], forget_all.at[rank], forget_send.at[distance - 1], forget_recv.at[distance - 1],
            rank ^ distance,
        )

    for distance in range(1, shards):
        send(distance).start()
    total = parts[shard]
    for distance in range(1, shards):
        send(distance).wait_recv()
        total = total + into[distance]
    part_sum[...] = total
    forget_all[rank] = total[8:16, :]
    for distance in range(1, ranks):
        send_forget(distance).start()
    relay.forward()
    for distance in range(1, ranks):
        send_forget(distance).wait()
    for distance in range(1, shards):
        send(distance).wait_send()
    relay.finish()


def finish_moves(collective_id, ranks, shards, late, parts):
    sems = pltpu.SemaphoreType.DMA((shards - 1,))
    return pl.pallas_call(
        functools.partial(finish_kernel, ranks, shards),
        in_specs=[ANY, VMEM_WHOLE],
        out_specs=[ANY, VMEM_WHOLE, VMEM_WHOLE],
        out_shape=[
            jax.ShapeDtypeStruct((ranks,) + late.shape, BF16),
            jax.ShapeDtypeStruct(parts.shape[1:], F32),
            jax.ShapeDtypeStruct((ranks, 8, parts.shape[2]), F32),
        ],
        scratch_shapes=[
            pltpu.VMEM(late.shape, BF16),
            pltpu.VMEM(parts.shape, F32),
            pltpu.SemaphoreType.DMA((1,)),
            pltpu.SemaphoreType.DMA((6,)),
            pltpu.SemaphoreType.DMA((6,)),
            pltpu.SemaphoreType.DMA((2,)),
            sems, sems,
            pltpu.SemaphoreType.DMA((ranks - 1,)),
            pltpu.SemaphoreType.DMA((ranks - 1,)),
        ],
        compiler_params=pltpu.CompilerParams(
            collective_id=collective_id, has_side_effects=True, vmem_limit_bytes=VMEM_LIMIT
        ),
        cost_estimate=pl.CostEstimate(flops=0, bytes_accessed=50 << 20, transcendentals=0),
        name="finish_moves",
    )(late, parts)


def spread_kernel(pieces, *refs):
    source, targets = refs[0], refs[1:]
    ranks = source.shape[0]
    for target, (piece, first, count) in zip(targets, pieces):
        for block in range(count):
            for index in range(ranks):
                target[:, pl.ds((block * ranks + index) * piece, piece)] = source[
                    index, :, pl.ds(first + block * piece, piece)
                ].astype(F32)


def spread_cols(source, *pieces):
    ranks, rows, cols = source.shape
    if any(piece % LANES or first % LANES for piece, first, _ in pieces):
        return [
            jnp.concatenate(
                [
                    source[c, :, first + i * piece : first + (i + 1) * piece]
                    for i in range(count)
                    for c in range(ranks)
                ],
                axis=1,
            ).astype(F32)
            for piece, first, count in pieces
        ]
    part = rows // 4 if rows % 64 == 0 else rows
    widths = [count * ranks * piece for piece, _, count in pieces]
    return pl.pallas_call(
        functools.partial(spread_kernel, pieces),
        grid=(rows // part,),
        in_specs=[pl.BlockSpec((ranks, part, cols), lambda step: (0, step, 0))],
        out_specs=[pl.BlockSpec((part, w), lambda step: (step, 0)) for w in widths],
        out_shape=[jax.ShapeDtypeStruct((rows, w), F32) for w in widths],
        compiler_params=pltpu.CompilerParams(vmem_limit_bytes=VMEM_LIMIT),
        cost_estimate=pl.CostEstimate(flops=0, bytes_accessed=rows * sum(widths) * 6, transcendentals=0),
        name="spread_cols",
    )(source)


def unpack_kernel(
    width, heads, head, late, forget_all, sums, totals, segments, first_rows, second_rows,
    in_out, out_out, first_out, second_out, forget_out, gains, bias, qk, rms,
):
    ranks = late.shape[0]
    first = 4 * width
    for block in range(4):
        for index in range(ranks):
            in_out[:, (block * ranks + index) * width : (block * ranks + index + 1) * width] = late[
                index, :, block * width : (block + 1) * width
            ].astype(F32)
    first_out[...] = first_rows[...]
    second_out[...] = second_rows[...]
    lane = lax.broadcasted_iota(jnp.int32, (LANES, ranks * heads), 0)
    place = lax.broadcasted_iota(jnp.int32, (LANES, ranks * heads), 1)
    biases = jnp.zeros((8, ranks * heads), F32)
    for index in range(ranks):
        chosen = (lane < heads) & (place == index * heads + lane)
        out_out[:, index * width : (index + 1) * width] = late[index, :, first : first + width].astype(F32)
        forget_out[index * heads : (index + 1) * heads, :] = forget_all[index, 0:heads, 0 : forget_out.shape[1]]
        row = jnp.broadcast_to(sums[3 + index : 4 + index, 0:LANES], (8, LANES))
        for part in split_three(row):
            biases = biases + dot(part.astype(BF16), jnp.where(chosen, 1.0, 0.0).astype(BF16))
    gains[...] = sums[0:2, 0 : gains.shape[1]]
    bias[...] = biases[0:1, :]
    for row in range(2):
        qk[row : row + 1, :] = sum(
            sums[2:3, row * LANES + side * head : row * LANES + (side + 1) * head] for side in range(LANES // head)
        )
    count = jnp.sum(jnp.where(segments[...] >= 0, 1.0, 0.0), axis=-1, keepdims=True)
    rms[...] = jnp.sqrt(totals[7:8, 0:2] / (count * totals.shape[1]))


def unpack(late, forget_all, sums, totals, segments, first_rows, second_rows, width, heads, head):
    ranks, rows, cols = late.shape
    part = rows // 4

    def block(lanes):
        return pl.BlockSpec((part, lanes), lambda step: (step, 0))

    share = rows
    shape = jax.ShapeDtypeStruct
    return pl.pallas_call(
        functools.partial(unpack_kernel, width, heads, head),
        grid=(rows // part,),
        in_specs=[
            pl.BlockSpec((ranks, part, cols), lambda step: (0, step, 0)),
        ]
        + [whole(a.shape) for a in (forget_all, sums, totals, segments)]
        + [block(first_rows.shape[1])] * 2,
        out_specs=[block(4 * ranks * width), block(ranks * width)] + [block(first_rows.shape[1])] * 2
        + [whole(a) for a in ((ranks * heads, rows), (2, share), (1, ranks * heads), (2, head), (1, 2))],
        out_shape=[
            shape((rows, 4 * ranks * width), F32),
            shape((rows, ranks * width), F32),
            shape(first_rows.shape, BF16),
            shape(second_rows.shape, BF16),
            shape((ranks * heads, rows), F32),
            shape((2, share), F32),
            shape((1, ranks * heads), F32),
            shape((2, head), F32),
            shape((1, 2), F32),
        ],
        compiler_params=pltpu.CompilerParams(vmem_limit_bytes=VMEM_LIMIT),
        cost_estimate=pl.CostEstimate(flops=0, bytes_accessed=ranks * rows * cols * 6, transcendentals=0),
        name="unpack",
    )(late, forget_all, sums, totals, segments, first_rows, second_rows)


class Native:
    def __init__(self, ranks):
        self.ranks = ranks

    def begin(self, tokens, cotangent, weight, tail, other, piece, width, padded):
        rank, model = lax.axis_index("ctx"), tokens.shape[1]
        parts = [lax.dynamic_slice_in_dim(weight, i * model + rank * width, width, 1) for i in range(4)]
        parts = [jnp.pad(part, ((0, 0), (0, padded - width))) for part in parts]
        cols = other.shape[1] // self.ranks
        picks = [
            lax.dynamic_slice_in_dim(other, (i * self.ranks + rank) * piece, piece, 1) for i in range(cols // piece)
        ]
        return (
            lax.all_gather(tokens, "ctx", axis=0, tiled=True),
            lax.all_gather(cotangent, "ctx", axis=0, tiled=True),
            lax.all_gather(jnp.concatenate(parts + [tail], axis=1), "fsdp", axis=0, tiled=True),
            jnp.concatenate(picks, axis=1),
        )

    def gather_cols(self, array, piece):
        return lax.all_gather(array, "ctx", axis=1, tiled=True), lax.all_gather(piece, "fsdp", axis=0, tiled=True)


def body(
    tokens, block_order, segment_ids, norm_gains, attn_in_weight, forget_weight, forget_bias,
    qk_gains, out_weight, gate_up_weight, down_weight, out_grad,
):
    ranks = lax.axis_size("ctx")
    shards = lax.axis_size("fsdp")
    rank = lax.axis_index("ctx")
    row_count, model_width = tokens.shape[1], tokens.shape[2]
    head_count, head_dim = forget_bias.shape[0], qk_gains.shape[1]
    local_heads = head_count // ranks
    width = local_heads * head_dim
    padded = -(-width // LANES) * LANES
    seq_order = block_order[0]
    seq_len = segment_ids.shape[1]
    block_len = seq_len // seq_order.shape[0]
    hidden_piece = down_weight.shape[0] // ranks
    hidden = hidden_piece * shards
    plain = ranks == 4 and shards & (shards - 1) == 0 and width == padded
    comm = Native(ranks)

    def slab(array, start, size, axis):
        return lax.dynamic_slice_in_dim(array, start, size, axis)

    def widen(array):
        return jnp.pad(array, ((0, 0), (0, padded - width))) if padded > width else array

    if plain:
        (
            inputs, grad_low, w_in, w_out, w_gate_up, normed, project, gated_all, attended,
            wide_query, wide_key, wide_value, mixed_low, down_near, normed_two, turned, gain_rows, *places_all,
            bias, head_gains,
        ) = front(
            0, ranks, shards, head_dim, local_heads, width, hidden_piece,
            tokens[0], out_grad[0], attn_in_weight, out_weight, gate_up_weight, down_weight, forget_weight.T,
            norm_gains, qk_gains, segment_ids, block_order, forget_bias[None],
        )
        w_down, hidden_act, grad_gate_up, early_grad, down_part_grad = ffn(
            1, shards, normed_two, turned, w_gate_up, grad_low, down_near
        )
    else:
        tail = jnp.concatenate(
            [
                slab(forget_weight, rank * local_heads, local_heads, 1),
                norm_gains.T,
                jnp.zeros((attn_in_weight.shape[0], LANES - local_heads - 2), BF16),
            ],
            axis=1,
        )
        offsets = jnp.arange(block_len, dtype=jnp.int32)
        blocks = jnp.arange(seq_order.shape[0], dtype=jnp.int32)
        places = (seq_order[:, None] * block_len + offsets[None]).reshape(-1)
        by_block = segment_ids[0].reshape(-1, block_len)
        chosen = seq_order[:, None, None] == blocks[None, :, None]
        segments = jnp.sum(jnp.where(chosen, by_block[None], 0), axis=1).reshape(-1)
        places, segments = places.astype(F32), segments.astype(F32)
        places_all = (places[None, :], places[:, None], segments[None, :], segments[:, None])
        bias = jnp.pad(slab(forget_bias, rank * local_heads, local_heads, 0), (0, LANES - local_heads))[None]
        head_gains = jnp.tile(qk_gains, (1, LANES // head_dim))
        down_piece = slab(down_weight, rank * hidden_piece, hidden_piece, 0)
        inputs, grad_low, w_in, gate_up_piece = comm.begin(
            tokens[0], out_grad[0], attn_in_weight, tail, gate_up_weight, hidden_piece, width, padded
        )
        w_gate_up = lax.all_gather(gate_up_piece, "fsdp", axis=0, tiled=True)
        gain_cols = w_in[:, 4 * padded : 4 * padded + LANES].astype(F32).T
        gain_one = gain_cols[local_heads]
        gain_two = gain_cols[local_heads + 1]
        wide_inputs = inputs.astype(F32)
        scale_one = rms_scale(wide_inputs)
        normed = (wide_inputs * scale_one * gain_one).astype(BF16)
        project = dot(normed, w_in)
        gated, attended, wide_query, wide_key, wide_value = attend(
            project, places_all, bias, head_gains, head_dim, padded, local_heads
        )
        gated_all, w_out = comm.gather_cols(gated[:, :width], slab(out_weight, rank * width, width, 1))
        mixed_cols = slab(inputs, rank * width, width, 1).astype(F32) + dot(gated_all, w_out)
        mixed_low, w_down = comm.gather_cols(mixed_cols.astype(BF16), down_piece)
        mixed = mixed_low.astype(F32)
        scale_two = rms_scale(mixed)
        normed_two = (mixed * scale_two * gain_two).astype(BF16)
        gate_up = dot(normed_two, w_gate_up)
        gate_part, up_part = gate_up[:, :hidden], gate_up[:, hidden:]
        gate_sigmoid = jax.nn.sigmoid(gate_part)
        silu = gate_part * gate_sigmoid
        hidden_act = (silu * up_part).astype(BF16)
        grad_hidden = right_product(grad_low, w_down)
        grad_gate = grad_hidden * up_part * gate_sigmoid * (1.0 + gate_part * (1.0 - gate_sigmoid))
        grad_gate_up = jnp.concatenate([grad_gate, grad_hidden * silu], axis=1).astype(BF16)
        down_part_grad = left_product(hidden_act, grad_low).astype(BF16)
        gate_up_grad = left_product(normed_two, grad_gate_up).astype(BF16)
        down_part = dot(hidden_act, w_down).astype(BF16)

    def own_rows(array):
        return slab(array, rank * row_count, row_count, 0)

    def reduce_shards(array):
        return lax.psum_scatter(array.astype(BF16), "fsdp", scatter_dimension=0, tiled=True)

    if plain:
        early_share = (reduce_shards(early_grad),)
    else:
        early_share = (reduce_shards(down_part_grad), reduce_shards(gate_up_grad))
    if plain:
        grad_mixed_cols, grad_gated, gain_two_grad, down_part, out_part = middle(
            3, ranks, grad_gate_up, w_gate_up, mixed_low, grad_low, w_out, hidden_act, w_down, gated_all,
            gain_rows,
        )
    else:
        grad_normed_two = right_product(grad_gate_up, w_gate_up)
        gain_two_grad = jnp.sum(grad_normed_two * mixed * scale_two, axis=0)
        grad_mixed_part = norm_back(grad_normed_two, mixed, scale_two, gain_two).astype(BF16)
        grad_mixed_cols = slab(grad_low, rank * width, width, 1).astype(F32) + lax.psum_scatter(
            grad_mixed_part, "ctx", scatter_dimension=1, tiled=True
        ).astype(F32)
        grad_branch = grad_mixed_cols.astype(BF16)
        grad_gated = widen(
            lax.psum_scatter(
                right_product(grad_branch, w_out).astype(BF16), "ctx", scatter_dimension=1, tiled=True
            ).astype(F32)
        )
    grad_project, small, *rest = attend_back(
        project, places_all, bias, head_gains, attended, (wide_query, wide_key, wide_value),
        grad_gated, (down_part, normed, out_part, down_part_grad) if plain else (), ranks if plain else 0, shards, head_dim, padded, local_heads,
    )
    if plain:
        down_pieces, late, down_share, forget_grad = rest
    else:
        in_part = left_product(normed, grad_project).astype(BF16)
        out_part = left_product(gated_all, grad_branch).astype(BF16)
        late = jnp.concatenate([in_part[:, : 4 * padded], out_part, in_part[:, 4 * padded :]], axis=1)
    late, early_share = lax.optimization_barrier((late, early_share))
    late_share = reduce_shards(late)

    if plain:
        tokens_grad, block_out, sums, parts, early_own, down_own = last_moves(
            4, ranks, shards, grad_project, w_in, inputs, early_share[0], down_pieces, mixed_low, down_share,
            grad_mixed_cols,             gain_rows, gain_two_grad, small, places_all[3], forget_grad,
        )
        late_own, piece_sum, forget_all = finish_moves(6, ranks, shards, late_share, parts)
        gate_up_out = spread_cols(early_own, (hidden_piece, 0, 2 * shards))[0]
        down_out = down_own.astype(F32).reshape(down_weight.shape)
    else:
        grad_normed = right_product(grad_project, w_in)
        gain_one_grad = jnp.sum(grad_normed * wide_inputs * scale_one, axis=0)
        in_own = jnp.arange(model_width, dtype=jnp.int32) // width == rank
        grad_inputs = norm_back(grad_normed, wide_inputs, scale_one, gain_one) + jnp.where(
            in_own[None], jnp.tile(grad_mixed_cols, (1, ranks)), 0.0
        )
        down_sum = lax.psum_scatter(down_part, "ctx", scatter_dimension=0, tiled=True).astype(F32)
        tokens_grad = lax.psum_scatter(grad_inputs.astype(BF16), "ctx", scatter_dimension=0, tiled=True)[None]
        own_bias = jnp.where(jnp.arange(ranks, dtype=jnp.int32)[:, None] == rank, small[2:3], 0.0)
        small_rows = jnp.concatenate([small[0:2].reshape(1, -1), jnp.pad(own_bias, ((0, 0), (0, LANES)))], axis=0)
        sums = jnp.concatenate(
            [
                jnp.stack([gain_one_grad, gain_two_grad]),
                jnp.pad(small_rows, ((0, 0), (0, model_width - 2 * LANES))),
            ],
            axis=0,
        )
        sums = lax.psum(sums, "ctx")
        down_own, gate_up_own = [lax.all_gather(a, "ctx", axis=0, tiled=False) for a in early_share]
        down_out = down_own.astype(F32).reshape(down_weight.shape)
        gate_up_out = spread_cols(gate_up_own, (hidden_piece, 0, 2 * shards))[0]
        result = own_rows(mixed_low).astype(F32) + down_sum
        block_out = result.astype(BF16)[None]
        branch = result - own_rows(inputs).astype(F32)
        own_valid = own_rows(places_all[3][:, 0] >= 0).astype(F32)
        totals = lax.psum(
            jnp.stack(
                [
                    jnp.sum(own_valid * jnp.sum(result * result, axis=-1)),
                    jnp.sum(own_valid * jnp.sum(branch * branch, axis=-1)),
                ]
            ),
            "ctx",
        )
        share = model_width // shards
        room = 2 * LANES
        gain_pieces = sums[0:2].reshape(2, shards, share).transpose(1, 0, 2)
        gain_pieces = jnp.pad(gain_pieces, ((0, 0), (0, 0), (0, room - share)))
        others = jnp.broadcast_to(sums[None, 2 : 3 + ranks, :room], (shards, 1 + ranks, room))
        piece_sum = lax.psum_scatter(
            jnp.concatenate([gain_pieces, others], axis=1), "fsdp", scatter_dimension=0, tiled=False
        )
        late_own = lax.all_gather(late_share, "ctx", axis=0, tiled=False)
    if plain:
        in_out, out_out, tokens_grad, block_out, forget_out, gains_sum, bias_sum, qk_sum, rms = unpack(
            late_own, forget_all, piece_sum, sums, segment_ids, tokens_grad, block_out, width, local_heads, head_dim
        )
        tokens_grad, block_out = tokens_grad[None], block_out[None]
        bias_sum, forget_out = bias_sum[0], forget_out.T
    else:
        share = model_width // shards
        valid_count = jnp.sum((segment_ids[0] >= 0).astype(F32)) * model_width
        in_out = jnp.concatenate(
            [late_own[c, :, i * padded : i * padded + width] for i in range(4) for c in range(ranks)], axis=1
        ).astype(F32)
        out_out = jnp.concatenate(
            [late_own[c, :, 4 * padded : 4 * padded + width] for c in range(ranks)], axis=1
        ).astype(F32)
        last = 4 * padded + width
        forget_out = jnp.concatenate(
            [late_own[c, :, last : last + local_heads] for c in range(ranks)], axis=1
        ).astype(F32)
        gains_sum = piece_sum[0:2, :share]
        bias_sum = piece_sum[3 : 3 + ranks, :local_heads].reshape(-1)
        qk_sum = piece_sum[2, : 2 * LANES].reshape(2, LANES // head_dim, head_dim).sum(axis=1)
        rms = jnp.sqrt(totals / valid_count)[None]
    return (
        block_out, tokens_grad, gains_sum, in_out, forget_out, bias_sum, qk_sum,
        out_out, gate_up_out, down_out, rms,
    )


def solution(mesh):
    rows = P("fsdp", "ctx", None)
    return jax.shard_map(
        body,
        mesh=mesh,
        in_specs=(
            rows, P("fsdp", None), P("fsdp", None), P(None, "fsdp"), P("fsdp", None), P("fsdp", None),
            P(), P(), P("fsdp", None), P("fsdp", None), P("fsdp", None), rows,
        ),
        out_specs=(
            rows, rows, P(None, "fsdp"), P("fsdp", None), P("fsdp", None), P(), P(),
            P("fsdp", None), P("fsdp", None), P("fsdp", None), P("fsdp", None),
        ),
        check_vma=False,
    )
```

```python
import functools

import jax
import jax.numpy as jnp
from jax import lax
from jax.experimental import pallas as pl
from jax.experimental.pallas import tpu as pltpu
from jax.sharding import PartitionSpec as P

EPS = 1e-06
SCALE = 0.125
LANES = 128
VMEM_LIMIT = 60 << 20
F32 = jnp.float32
BF16 = jnp.bfloat16


MESH = pl.DeviceIdType.MESH
ANY = pl.BlockSpec(memory_space=pltpu.HBM)


def rms_scale(values):
    return lax.rsqrt(jnp.mean(values * values, axis=-1, keepdims=True) + EPS)


def norm_back(grad_normed, values, scale_values, gain_values):
    scaled = grad_normed * gain_values
    cubed = scale_values * scale_values * scale_values
    return scale_values * scaled - values * cubed * jnp.mean(
        scaled * values, axis=-1, keepdims=True
    )


def dot(left, right):
    return lax.dot_general(
        left, right, (((1,), (0,)), ((), ())), preferred_element_type=F32
    )


def left_product(left, right):
    return lax.dot_general(
        left, right, (((0,), (0,)), ((), ())), preferred_element_type=F32
    )


def right_product(left, right):
    return lax.dot_general(
        left, right, (((1,), (1,)), ((), ())), preferred_element_type=F32
    )


def split_three(values):
    high = values.astype(BF16).astype(F32)
    rest = values - high
    middle = rest.astype(BF16).astype(F32)
    return high, middle, rest - middle


def lane_ids(rows, lanes=LANES):
    return lax.broadcasted_iota(jnp.int32, (rows, lanes), 1)


def pick_lane(values, lanes, index):
    return jnp.sum(jnp.where(lanes == index, values, 0.0), axis=-1, keepdims=True)


def turns(rows, chunk, unroll=False):
    def decorate(body):
        @pl.loop(0, rows // chunk, unroll=rows // chunk if unroll else None)
        def _(turn):
            body(pl.ds(pl.multiple_of(turn * chunk, chunk), chunk))

    return decorate


def fill_mask(chunk, pos_row, pos_col, seg_row, seg_col, mask):
    @turns(mask.shape[0], chunk)
    def _(part):
        allowed = (pos_row[0:1, :] <= pos_col[part, :]) & (seg_row[0:1, :] == seg_col[part, :])
        mask[part, :] = jnp.where(allowed, 0.0, -jnp.inf)


def fill_prefix(chunk, heads, pos_row, pos_col, logits, prefix):
    rows = prefix.shape[0]
    log_forget = jax.nn.log_sigmoid(jnp.where(lane_ids(rows) < heads, logits, 0.0))
    high, middle, low = split_three(log_forget)

    @turns(rows, chunk)
    def _(part):
        before = jnp.where(pos_row[0:1, :] <= pos_col[part, :], 1.0, 0.0).astype(BF16)
        prefix[part, :] = (
            dot(before, high.astype(BF16)) + dot(before, middle.astype(BF16)) + dot(before, low.astype(BF16))
        )


def attend_block(
    head, chunk, index, query, key, value, gate, gains, mask, prefix,
    gated, attended, wide_query, wide_key, wide_value,
):
    rows = mask.shape[0]
    lanes = lane_ids(rows)
    half = lane_ids(rows, head)
    short = lane_ids(chunk, head)
    for side in range(LANES // head):
        here = slice(side * head, (side + 1) * head)
        column = pick_lane(prefix[...], lanes, (LANES // head) * index + side)
        high, middle, low = split_three(column)
        wide = jnp.where(half == 1, high, 0.0)
        wide = jnp.where(half == 2, middle, wide)
        wide = jnp.where(half == 3, low, wide)
        query_rest = jnp.where((half >= 4) & (half < 7), 1.0, wide)
        wide = jnp.where(half == 4, -high, 0.0)
        wide = jnp.where(half == 5, -middle, wide)
        wide = jnp.where(half == 6, -low, wide)
        ones = ((half >= 1) & (half < 4)) | ((half >= 7) & (half < 10))
        key_rest = jnp.where(ones, 1.0, wide)
        raw = query[:, here]
        normed = (raw * rms_scale(raw) * gains[0:1, here]).astype(BF16)
        wide_query[side, :, 0:head] = (normed.astype(F32) * SCALE).astype(BF16)
        wide_query[side, :, head:LANES] = query_rest.astype(BF16)
        raw = key[:, here]
        wide_key[side, :, 0:head] = (raw * rms_scale(raw) * gains[1:2, here]).astype(BF16)
        wide_key[side, :, head:LANES] = key_rest.astype(BF16)
        wide_value[side, :, 0:head] = value[:, here].astype(BF16)
        wide_value[side, :, head:LANES] = jnp.where(half < 3, 1.0, 0.0).astype(BF16)

        @turns(rows, chunk, unroll=True)
        def _(part):
            scores = right_product(wide_query[side, part, :], wide_key[side]) + mask[part, :]
            expos = jnp.exp(scores)
            total = jnp.sum(expos, axis=-1, keepdims=True)
            result = dot(expos.astype(BF16), wide_value[side])[:, 0:head] / total
            attended[part, here] = result
            gated[part, here] = (result * jax.nn.sigmoid(gate(part)[:, here])).astype(BF16)
            high, middle, low = split_three(-jnp.log(total))
            rest = wide_query[side, part, head:LANES].astype(F32)
            rest = jnp.where(short == 7, high, rest)
            rest = jnp.where(short == 8, middle, rest)
            rest = jnp.where(short == 9, low, rest)
            wide_query[side, part, head:LANES] = rest.astype(BF16)


def attend_kernel(
    head, chunk, heads,
    pos_row, pos_col, seg_row, seg_col, bias, gains, query, key, value, gate, forget,
    gated, attended, wide_query, wide_key, wide_value,
    mask, prefix,
):
    @pl.when(pl.program_id(0) == 0)
    def _():
        fill_mask(chunk, pos_row, pos_col, seg_row, seg_col, mask)
        fill_prefix(chunk, heads, pos_row, pos_col, forget[...] + bias[0:1, :], prefix)

    attend_block(
        head, chunk, pl.program_id(0), query, key, value, lambda part: gate[part, :], gains, mask, prefix,
        gated, attended.at[0], wide_query, wide_key, wide_value,
    )


def attend_back_kernel(
    head, chunk, width, heads, ranks, shards,
    pos_row, pos_col, seg_row, seg_col, bias, gains, query, key, gate, forget,
    attended, wide_query, wide_key, wide_value, grad_gated, *rest,
):
    if ranks:
        aside, normed, out_grad, blocks, grad_project, small, aside_in, late, share, forget_grad = rest[:10]
        mask, wide_grad, grad_query, grad_key, grad_value, grad_prefix = rest[10:16]
        normed_in, out_in, aside_own, blocks_in, side_in, kept, from_below, from_above = rest[16:24]
        late_all, load_sem, save_sem = rest[24:27]
        sems = rest[27:29]
        over_shards = ShardSum(shards, blocks_in, side_in, kept, from_below, from_above, rest[29:])

        def loads():
            own = rows_of(aside, lax.axis_index("ctx"), aside_in.shape[1])
            for n, pair in enumerate(((normed, normed_in), (out_grad, out_in), (own, aside_own))):
                yield pltpu.make_async_copy(*pair, load_sem.at[n])

    else:
        grad_project, small, mask, wide_grad, grad_query, grad_key, grad_value, grad_prefix = rest
    step = pl.program_id(0)
    steps = pl.num_programs(0)

    def aside_copies():
        send_sem, recv_sem = sems
        rank = lax.axis_index("ctx")
        size = aside_in.shape[1]
        for distance in range(1, ranks):
            other = rank ^ distance
            yield to_rank(
                rows_of(aside, other, size), aside_in.at[rank],
                send_sem.at[distance - 1], recv_sem.at[distance - 1], other,
            )

    def sum_stage(hook):
        if not ranks:
            return
        now = (LANES // head) * step + hook
        for stage in range(over_shards.layers - 1):

            @pl.when(now == 2 + 2 * stage)
            def _():
                if stage == 0:
                    over_shards.presum()
                else:
                    over_shards.receive(stage - 1)
                over_shards.send(stage)

    if ranks:

        @pl.when(step == 0)
        def _():
            rank = lax.axis_index("ctx")
            greet([{"ctx": rank ^ distance} for distance in range(1, ranks)], over_shards)
            early = pltpu.make_async_copy(blocks, blocks_in, load_sem.at[4])
            early.start()
            for copy in aside_copies():
                copy.start()
            for copy in loads():
                copy.start()
            early.wait()
            over_shards.start()

    rows = query.shape[0]
    lanes = lane_ids(rows)
    half = lane_ids(rows, head)

    @pl.when(step == 0)
    def _():
        @pl.loop(0, rows // chunk)
        def _(turn):
            part = pl.ds(pl.multiple_of(turn * chunk, chunk), chunk)
            after = pos_row[0:1, :] >= pos_col[part, :]
            same = seg_row[0:1, :] == seg_col[part, :]
            mask[part, :] = jnp.where(after & same, 0.0, -jnp.inf)
        grad_prefix[...] = jnp.zeros_like(grad_prefix)
        small[...] = jnp.zeros_like(small)

    for side in range(LANES // head):
        sum_stage(side)
        here = pl.ds(side * head, head)

        def column(part):
            return pl.ds(pl.multiple_of(part * width + step * LANES, LANES), LANES)

        sig = jax.nn.sigmoid(gate[:, here])
        grad_in = grad_gated[:, here]
        result = attended[0, :, here]
        grad_result = (grad_in * sig).astype(BF16)
        grad_gate = (grad_in * result * sig * (1.0 - sig)).astype(BF16)
        inner = -jnp.sum(grad_result.astype(F32) * result, axis=-1, keepdims=True)
        high, middle, low = split_three(inner)
        rest = jnp.where(half == 0, high, 0.0)
        rest = jnp.where(half == 1, middle, rest)
        rest = jnp.where(half == 2, low, rest)
        wide_grad[:, 0:head] = grad_result
        wide_grad[:, head:LANES] = rest.astype(BF16)
        grad_query[...] = jnp.zeros_like(grad_query)
        @turns(rows, chunk, unroll=True)
        def _(part):
            scores = right_product(wide_key[side, part, :], wide_query[side]) + mask[part, :]
            probs = jnp.exp(scores)
            outer = right_product(wide_value[side, part, :], wide_grad[...])
            grad_scores = (probs * outer).astype(BF16)
            grad_key[part, :] = dot(grad_scores, wide_query[side])
            grad_value[part, :] = dot(probs.astype(BF16), wide_grad[...])
            grad_query[...] += left_product(wide_key[side, part, :], grad_scores)
        from_query = grad_query[...].T
        from_key = grad_key[...]
        change = pick_lane(from_query, lanes, head + 1) - pick_lane(from_key, lanes, head + 4)
        grad_prefix[...] += jnp.where(lanes == (LANES // head) * step + side, change, 0.0)

        raw = query[:, here]
        scale_raw = rms_scale(raw)
        grad_normed = from_query[:, 0:head] * SCALE
        grad_raw_query = norm_back(grad_normed, raw, scale_raw, gains[0:1, here])
        small[0:1, here] += jnp.sum(grad_normed * raw * scale_raw, axis=0, keepdims=True)
        raw = key[:, here]
        scale_raw = rms_scale(raw)
        grad_normed = from_key[:, 0:head]
        grad_raw_key = norm_back(grad_normed, raw, scale_raw, gains[1:2, here])
        small[1:2, here] += jnp.sum(grad_normed * raw * scale_raw, axis=0, keepdims=True)
        wide_grad[:, here] = grad_gate
        for part_id, piece in enumerate(
            (grad_raw_query.astype(BF16), grad_raw_key.astype(BF16), grad_value[:, 0:head].astype(BF16), grad_gate)
        ):
            if side == 0:
                grad_project[:, column(part_id)] = jnp.concatenate([piece, piece], axis=1)
            else:
                keep = grad_project[:, column(part_id)]
                both = jnp.concatenate([piece, piece], axis=1)
                grad_project[:, column(part_id)] = jnp.where(lanes < head, keep, both)

    @pl.when(step == steps - 1)
    def _():
        high, middle, low = split_three(grad_prefix[...])
        short = lane_ids(chunk)

        @pl.loop(0, rows // chunk)
        def _(turn):
            part = pl.ds(pl.multiple_of(turn * chunk, chunk), chunk)
            after = jnp.where(pos_row[0:1, :] >= pos_col[part, :], 1.0, 0.0).astype(BF16)
            total = dot(after, high.astype(BF16)) + dot(after, middle.astype(BF16)) + dot(after, low.astype(BF16))
            grad_logit = total * jax.nn.sigmoid(-(forget[part, :] + bias[0:1, :]))
            grad_logit = jnp.where(short < heads, grad_logit, 0.0).astype(BF16)
            grad_project[part, 4 * width : 4 * width + LANES] = grad_logit
            small[2:3, :] += jnp.sum(grad_logit.astype(F32), axis=0, keepdims=True)

        if ranks:
            for copy in loads():
                copy.wait()
            keep = pltpu.make_async_copy(aside_own, aside_in.at[lax.axis_index("ctx")], load_sem.at[3])
            keep.start()
            late_stages = [n for n in range(over_shards.layers - 1) if 2 + 2 * n >= heads]
            for stage in late_stages:
                over_shards.receive(stage - 1)
                over_shards.send(stage)
            ends = 4 * width, 4 * width + out_grad.shape[1]
            late_all[:, ends[0] : ends[1]] = out_in[...]
            piece = 2 * LANES

            def save(turn, size=piece):
                cols = pl.ds(pl.multiple_of(turn * piece, LANES), size)
                return pltpu.make_async_copy(late_all.at[:, cols], late.at[:, cols], save_sem.at[turn])

            count = 4 * width // piece
            rest_save = pltpu.make_async_copy(
                late_all.at[:, pl.ds(ends[0], late.shape[1] - ends[0])],
                late.at[:, pl.ds(ends[0], late.shape[1] - ends[0])],
                save_sem.at[count],
            )

            def product(into, cols):
                @turns(late.shape[0], 3 * chunk if late.shape[0] % (3 * chunk) == 0 else chunk)
                def _(part):
                    late_all[part, into] = dot(normed_in[part, :], grad_project[:, cols]).astype(BF16)

            rest_save.start()
            turned = grad_project[:, ends[0] : ends[0] + LANES].astype(F32).T[0:8, :]
            forget_grad[...] = right_product(turned.astype(BF16), normed_in[...])

            @pl.loop(0, count)
            def _(turn):
                cols = pl.ds(pl.multiple_of(turn * piece, LANES), piece)
                product(cols, cols)
                save(turn).start()

            for copy in aside_copies():
                copy.wait()
            keep.wait()
            over_shards.receive(over_shards.layers - 2)
            share[...] = kept[over_shards.layer]
            over_shards.sent()
            rest_save.wait()

            @pl.loop(0, count)
            def _(turn):
                save(turn).wait()


def pick_chunk(rows):
    return 256 if rows % 256 == 0 else 128


def whole(shape):
    return pl.BlockSpec(shape, lambda step: tuple(0 for _ in shape))


def attend(project, places, bias, gains, head, width, heads):
    rows = project.shape[0]
    steps = width // LANES
    per = LANES // head
    chunk = pick_chunk(rows)

    def part(index):
        return pl.BlockSpec((rows, LANES), lambda step: (0, index * steps + step))

    own = pl.BlockSpec((rows, LANES), lambda step: (0, step))
    wide = pl.BlockSpec((per, rows, LANES), lambda step: (step, 0, 0))
    forget = pl.BlockSpec((rows, LANES), lambda step: (0, 4 * steps))
    wide_shape = jax.ShapeDtypeStruct((per * steps, rows, LANES), BF16)
    return pl.pallas_call(
        functools.partial(attend_kernel, head, chunk, heads),
        grid=(steps,),
        in_specs=[whole(p.shape) for p in places] + [whole(bias.shape), whole(gains.shape)]
        + [part(0), part(1), part(2), part(3), forget],
        out_specs=[own, pl.BlockSpec((1, rows, LANES), lambda step: (step, 0, 0)), wide, wide, wide],
        out_shape=[
            jax.ShapeDtypeStruct((rows, width), BF16),
            jax.ShapeDtypeStruct((steps, rows, LANES), F32),
            wide_shape, wide_shape, wide_shape,
        ],
        scratch_shapes=[pltpu.VMEM((rows, rows), F32), pltpu.VMEM((rows, LANES), F32)],
        compiler_params=pltpu.CompilerParams(vmem_limit_bytes=VMEM_LIMIT),
        name="attend",
    )(*places, bias, gains, project, project, project, project, project)


def attend_back(project, places, bias, gains, attended, wides, grad_gated, beside, ranks, shards, head, width, heads):
    rows = project.shape[0]
    steps = width // LANES
    per = LANES // head
    chunk = pick_chunk(rows)

    def part(index):
        return pl.BlockSpec((rows, LANES), lambda step: (0, index * steps + step))

    own = pl.BlockSpec((rows, LANES), lambda step: (0, step))
    block = pl.BlockSpec((1, rows, LANES), lambda step: (step, 0, 0))
    wide = pl.BlockSpec((per, rows, LANES), lambda step: (step, 0, 0))
    forget = pl.BlockSpec((rows, LANES), lambda step: (0, 4 * steps))
    total = 4 * width + LANES
    out_specs = [whole((rows, total)), whole((8, LANES))]
    out_shape = [jax.ShapeDtypeStruct((rows, total), BF16), jax.ShapeDtypeStruct((8, LANES), F32)]
    scratch = [
        pltpu.VMEM((rows, rows), F32),
        pltpu.VMEM((rows, LANES), BF16),
        pltpu.VMEM((LANES, rows), F32),
        pltpu.VMEM((rows, LANES), F32),
        pltpu.VMEM((rows, LANES), F32),
        pltpu.VMEM((rows, LANES), F32),
    ]
    if ranks:
        aside, normed, out_grad, blocks = beside
        share = (blocks.shape[0] // shards, blocks.shape[1])
        sum_blocks, sum_sems = shard_sum_scratch(shards, *share)
        model, late_cols = normed.shape[0], 4 * width + out_grad.shape[1]
        out_specs += [ANY, ANY, whole(share), whole((8, model))]
        out_shape += [
            jax.ShapeDtypeStruct((ranks, aside.shape[0] // ranks, aside.shape[1]), BF16),
            jax.ShapeDtypeStruct((model, late_cols), BF16),
            jax.ShapeDtypeStruct(share, BF16),
            jax.ShapeDtypeStruct((8, model), F32),
        ]
        scratch += [
            pltpu.VMEM(normed.shape, BF16),
            pltpu.VMEM(out_grad.shape, BF16),
            pltpu.VMEM((aside.shape[0] // ranks, aside.shape[1]), BF16),
            pltpu.VMEM(blocks.shape, BF16),
            *sum_blocks,
            pltpu.VMEM((model, late_cols), BF16),
            pltpu.SemaphoreType.DMA((5,)),
            pltpu.SemaphoreType.DMA((4 * width // (2 * LANES) + 1,)),
            pltpu.SemaphoreType.DMA((ranks - 1,)),
            pltpu.SemaphoreType.DMA((ranks - 1,)),
            *sum_sems,
        ]
    return pl.pallas_call(
        functools.partial(attend_back_kernel, head, chunk, width, heads, ranks, shards),
        grid=(steps,),
        in_specs=[whole(p.shape) for p in places] + [whole(bias.shape), whole(gains.shape)]
        + [part(0), part(1), part(3), forget, block, wide, wide, wide, own] + [ANY] * len(beside),
        out_specs=out_specs,
        out_shape=out_shape,
        scratch_shapes=scratch,
        compiler_params=pltpu.CompilerParams(
            collective_id=5 if ranks else None, has_side_effects=ranks > 0, vmem_limit_bytes=VMEM_LIMIT
        ),
        name="attend_back",
    )(*places, bias, gains, project, project, project, project, attended, *wides, grad_gated, *beside)


def greet(peers, line=None):
    barrier = pltpu.get_barrier_semaphore()
    if line is not None:
        peers = peers + [line.sibling]
    for peer in peers:
        pl.semaphore_signal(barrier, inc=1, device_id=peer, device_id_type=MESH)
    if line is not None:
        for there, peer in ((line.has_above, line.above), (line.has_below, line.below)):

            @pl.when(there)
            def _():
                pl.semaphore_signal(barrier, inc=1, device_id=peer, device_id_type=MESH)

    count = len(peers)
    if line is not None:
        last = line.layers - 1
        count = count + (1 - line.layer // last) + (line.layer + last) // line.layers
    pl.semaphore_wait(barrier, count)


class Line:
    def __init__(self, shards, source, target, sems):
        self.shard = lax.axis_index("fsdp")
        self.layers = shards // 2
        self.layer, self.core = self.shard // 2, self.shard % 2
        self.sibling = {"fsdp": self.shard ^ 1}
        self.above, self.below = {"fsdp": self.shard + 2}, {"fsdp": self.shard - 2}
        self.has_above, self.has_below = self.layer < self.layers - 1, self.layer > 0
        self.source, self.target = source, target
        self.rows = target.shape[0] // shards
        self.line_send, self.line_recv, self.side_send, self.side_recv, self.own_sem = sems

    def block(self, owner):
        return rows_of(self.target, owner, self.rows)

    def line(self, owner_layer, peer, way, own=False):
        here = self.block(owner_layer * 2 + self.core)
        return pltpu.make_async_remote_copy(
            self.source if own else here, here, self.line_send.at[way, owner_layer], self.line_recv.at[owner_layer],
            device_id=peer, device_id_type=MESH,
        )

    def side(self, owner_layer, owner_core, own=False):
        here = self.block(owner_layer * 2 + owner_core)
        return pltpu.make_async_remote_copy(
            self.source if own else here, here, self.side_send.at[owner_layer], self.side_recv.at[owner_layer],
            device_id=self.sibling, device_id_type=MESH,
        )

    def start(self):
        own = self.source is not None

        @pl.when(self.has_above)
        def _():
            self.line(self.layer, self.above, 0, own).start()

        @pl.when(self.has_below)
        def _():
            self.line(self.layer, self.below, 1, own).start()

        self.side(self.layer, self.core, own).start()
        if own:
            self.keep = pltpu.make_async_copy(self.source, self.block(self.shard), self.own_sem)
            self.keep.start()

    def step(self, distance):
        lower, upper = self.layer - distance, self.layer + distance

        @pl.when(lower >= 0)
        def _():
            self.line(lower, self.below, 1).wait_recv()

            @pl.when(self.has_above)
            def _():
                self.line(lower, self.above, 0).start()

            self.side(lower, self.core).start()

        @pl.when(upper < self.layers)
        def _():
            self.line(upper, self.above, 0).wait_recv()

            @pl.when(self.has_below)
            def _():
                self.line(upper, self.below, 1).start()

            self.side(upper, self.core).start()

    def from_side(self, owner_layer):
        self.side(owner_layer, 1 - self.core).wait_recv()

    def finish(self):
        self.keep.wait()
        for owner_layer in range(self.layers):
            self.from_side(owner_layer)
        self.sent()

    def sent(self):
        for owner_layer in range(self.layers):
            self.side(owner_layer, self.core).wait_send()

            @pl.when(self.has_above & (owner_layer <= self.layer))
            def _():
                self.line(owner_layer, self.above, 0).wait_send()

            @pl.when(self.has_below & (owner_layer >= self.layer))
            def _():
                self.line(owner_layer, self.below, 1).wait_send()

    def near_finish(self):
        self.keep.wait()
        self.from_side(self.layer)
        self.side(self.layer, self.core).wait_send()

        @pl.when(self.has_below)
        def _():
            self.line(self.layer - 1, self.below, 1).wait_recv()
            self.line(self.layer, self.below, 1).wait_send()

        @pl.when(self.has_above)
        def _():
            self.line(self.layer + 1, self.above, 0).wait_recv()
            self.line(self.layer, self.above, 0).wait_send()

    def near_load(self, near, sems, number):
        if number == 0:
            chip = 2 * self.rows
            source, target = rows_of(near, self.layer, chip), rows_of(self.target, self.layer, chip)
        else:
            owner = self.shard + (-2, 2)[number - 1]
            source, target = rows_of(near, owner, self.rows), self.block(owner)
        return pltpu.make_async_copy(source, target, sems.at[number])

    def near_start(self, near, sems):
        self.near_load(near, sems, 0).start()

        @pl.when(self.has_below)
        def _():
            self.near_load(near, sems, 1).start()

        @pl.when(self.has_above)
        def _():
            self.near_load(near, sems, 2).start()

    def resume(self, near, sems):
        @pl.when(self.has_below)
        def _():
            self.near_load(near, sems, 1).wait()

            @pl.when(self.has_above)
            def _():
                self.line(self.layer - 1, self.above, 0).start()

            self.side(self.layer - 1, self.core).start()

        @pl.when(self.has_above)
        def _():
            self.near_load(near, sems, 2).wait()

            @pl.when(self.has_below)
            def _():
                self.line(self.layer + 1, self.below, 1).start()

            self.side(self.layer + 1, self.core).start()

    def resumed_sent(self):
        for owner_layer in range(self.layers):

            @pl.when(owner_layer != self.layer)
            def _():
                self.side(owner_layer, self.core).wait_send()

            @pl.when(self.has_above & (owner_layer < self.layer))
            def _():
                self.line(owner_layer, self.above, 0).wait_send()

            @pl.when(self.has_below & (owner_layer > self.layer))
            def _():
                self.line(owner_layer, self.below, 1).wait_send()


def line_scratch(shards):
    layers = shards // 2
    return [
        pltpu.SemaphoreType.DMA((2, layers)),
        pltpu.SemaphoreType.DMA((layers,)),
        pltpu.SemaphoreType.DMA((layers,)),
        pltpu.SemaphoreType.DMA((layers,)),
        pltpu.SemaphoreType.DMA,
    ]


class Relay:
    def __init__(self, rank, source, place, send_sem, recv_sem, own_sem):
        self.rank, self.source, self.place = rank, source, place
        self.send_sem, self.recv_sem, self.own_sem = send_sem, recv_sem, own_sem

    def copy(self, number):
        me = self.rank
        source, place, distance = (
            lambda: (self.source(0), self.place(me, 0), 1),
            lambda: (self.source(1), self.place(me, 1), 2),
            lambda: (self.source(1), self.place(me, 1), 1),
            lambda: (self.source(0), self.place(me, 0), 2),
            lambda: (self.place(me ^ 1, 0), self.place(me ^ 1, 0), 2),
            lambda: (self.place(me ^ 2, 1), self.place(me ^ 2, 1), 1),
        )[number]()
        return pltpu.make_async_remote_copy(
            source, place, self.send_sem.at[number], self.recv_sem.at[number],
            device_id={"ctx": me ^ distance}, device_id_type=MESH,
        )

    def own(self, h):
        return pltpu.make_async_copy(self.source(h), self.place(self.rank, h), self.own_sem.at[h])

    def start(self, keep=True):
        for number in range(4):
            self.copy(number).start()
        if keep:
            for h in range(2):
                self.own(h).start()

    def forward(self):
        for number in range(2):
            self.copy(number).wait_recv()
            self.copy(number + 4).start()

    def arrive(self):
        for number in range(2, 6):
            self.copy(number).wait_recv()

    def finish(self, arrive=True, keep=True):
        if keep:
            for h in range(2):
                self.own(h).wait()
        if arrive:
            self.arrive()
        for number in range(6):
            self.copy(number).wait_send()


def rows_of(ref, index, size):
    return ref.at[pl.ds(pl.multiple_of(index * size, 16), size), :]


def cols_of(ref, index, size):
    return ref.at[:, pl.ds(pl.multiple_of(index * size, LANES), size)]


def relay_ops(mode, rank, source, target, sems):
    rows, cols = source.shape
    half = rows // 2

    def part(h):
        return source.at[pl.ds(h * half, half), :]

    def place(block, h):
        if mode == "gather_rows":
            return target.at[pl.ds(pl.multiple_of(block * rows + h * half, 16), half), :]
        if mode == "gather_cols":
            return target.at[pl.ds(h * half, half), pl.ds(pl.multiple_of(block * cols, LANES), cols)]
        return target.at[block, pl.ds(h * half, half), :]

    return Relay(rank, part, place, *sems)


VMEM_WHOLE = pl.BlockSpec(memory_space=pltpu.VMEM)


def to_rank(source, target, send, recv, other):
    return pltpu.make_async_remote_copy(
        source, target, send, recv, device_id={"ctx": other}, device_id_type=MESH
    )


FRONT_LOADS = 6
FRONT_SAVES = 12


def front_kernel(
    shards, head, heads, width, piece, chunk,
    tokens, cotangent, weight, weight_out, other, down, forget_weight, norm_gains, qk_gains, segments, order, forget_bias,
    inputs, grad_low, w_in, w_out, w_gate_up, normed, project, gated, attended, wide_query, wide_key, wide_value,
    mixed, down_near, normed_two, turned, gain_rows, pos_row, pos_col, seg_row, seg_col, bias, gains,
    weight_all, other_all, out_all, own_x, own_g, own_in, own_pick, own_out, x_all, in_all, hn_all, proj_all, mask, prefix,
    gated_all, attended_all, query_all, key_all, value_all, out_cols, scale_one, y_own, own_down,
    mixed_all, h2_all, turned_all,
    send_sem, recv_sem, own_sem, load_sem, save_sem, *line_sems,
):
    rank = lax.axis_index("ctx")
    ranks = lax.axis_size("ctx")
    model = weight.shape[1] // 4
    rows = x_all.shape[0]
    steps = width // LANES
    tail_at = 4 * width
    loads = [
        pltpu.make_async_copy(a, b, load_sem.at[n])
        for n, (a, b) in enumerate(
            (
                (weight, weight_all), (other, other_all), (weight_out, out_all), (tokens, own_x), (cotangent, own_g),
                (rows_of(down, rank, own_down.shape[0]), own_down),
            )
        )
    ]
    saves = [
        pltpu.make_async_copy(a, b, save_sem.at[n])
        for n, (a, b) in enumerate(
            (
                (x_all, inputs), (in_all, w_in), (hn_all, normed), (proj_all, project), (query_all, wide_query),
                (key_all, wide_key), (value_all, wide_value), (attended_all, attended), (gated_all, gated),
                (mixed_all, mixed), (h2_all, normed_two), (turned_all, turned),
            )
        )
    ]
    for copy in loads:
        copy.start()
    per = len(line_sems) // 4
    in_line = Line(shards, own_in, in_all, line_sems[:per])
    out_line = Line(shards, own_out, out_cols, line_sems[per : 2 * per])
    up_line = Line(shards, own_pick, w_gate_up, line_sems[2 * per : 3 * per])
    down_line = Line(shards, own_down, down_near, line_sems[3 * per :])
    greet([{"ctx": rank ^ 1}, {"ctx": rank ^ 2}], in_line)

    def sems(n):
        return send_sem.at[n], recv_sem.at[n], own_sem.at[n]

    first = relay_ops("gather_rows", rank, own_x, x_all, sems(0))
    second = relay_ops("gather_rows", rank, own_g, grad_low, sems(1))

    def cols(start, size):
        return pl.ds(pl.multiple_of(start, LANES), size)

    loads[0].wait()
    for i in range(4):
        own_in[:, i * width : (i + 1) * width] = weight_all[:, cols(i * model + rank * width, width)]
    total_heads = forget_weight.shape[0]
    from_head = lax.broadcasted_iota(jnp.int32, (total_heads, LANES), 0)
    to_lane = lax.broadcasted_iota(jnp.int32, (total_heads, LANES), 1)
    chosen = jnp.where((to_lane < heads) & (from_head == rank * heads + to_lane), 1.0, 0.0).astype(BF16)
    from_gain = lax.broadcasted_iota(jnp.int32, (2, LANES), 0)
    to_lane = lax.broadcasted_iota(jnp.int32, (2, LANES), 1)
    chosen_gain = jnp.where(to_lane == heads + from_gain, 1.0, 0.0).astype(BF16)
    tail = left_product(forget_weight[...], chosen) + left_product(norm_gains[...], chosen_gain)
    own_in[:, tail_at : tail_at + LANES] = tail.astype(BF16)
    in_line.start()
    loads[3].wait()
    first.start()
    loads[1].wait()
    for i in range(own_pick.shape[1] // piece):
        own_pick[:, i * piece : (i + 1) * piece] = other_all[:, cols((i * ranks + rank) * piece, piece)]
    loads[2].wait()
    own_out[...] = out_all[:, cols(rank * width, width)]
    count = order.shape[1]
    length = rows // count
    row_ids = lax.broadcasted_iota(jnp.int32, (rows, LANES), 0)
    lane_id = lax.broadcasted_iota(jnp.int32, (8, rows), 1)
    tall = jnp.zeros((rows, LANES), jnp.int32)
    flat = jnp.zeros((8, rows), jnp.int32)
    for block in range(count):
        start = order[0, block] * length - block * length
        tall = jnp.where((row_ids >= block * length) & (row_ids < (block + 1) * length), row_ids + start, tall)
        flat = jnp.where((lane_id >= block * length) & (lane_id < (block + 1) * length), lane_id + start, flat)
    pos_col[...] = tall[:, 0:1].astype(F32)
    pos_row[...] = flat[0:1, :].astype(F32)
    true_segments = segments[0:1, :].astype(F32)

    @turns(rows, chunk)
    def _(part):
        true_place = lax.broadcasted_iota(jnp.int32, (chunk, rows), 1).astype(F32)
        own_place = true_place == pos_col[part, :]
        seg_col[part, :] = jnp.sum(jnp.where(own_place, true_segments, 0.0), axis=-1, keepdims=True)

    seg_row[...] = jnp.broadcast_to(seg_col[...], (rows, LANES)).T[0:1, :]
    lane = lax.broadcasted_iota(jnp.int32, (1, LANES), 1)
    bias_row = jnp.zeros((1, LANES), F32)
    for index in range(heads):
        bias_row = jnp.where(lane == index, forget_bias[0, rank * heads + index], bias_row)
    bias[...] = bias_row
    for side in range(LANES // head):
        gains[:, side * head : (side + 1) * head] = qk_gains[...]
    fill_mask(chunk, pos_row, pos_col, seg_row, seg_col, mask)
    proj_all[...] = jnp.zeros_like(proj_all)
    gain_rows[...] = jnp.zeros_like(gain_rows)
    first.forward()
    loads[4].wait()
    second.start()
    in_line.step(1)
    first.finish()
    saves[0].start()

    @turns(rows, chunk)
    def _(part):
        values = x_all[part, :].astype(F32)
        scale_one[part, :] = jnp.broadcast_to(rms_scale(values), (chunk, LANES))

    def consume(layer):
        in_line.from_side(layer)
        size = 2 * in_line.rows
        here = cols(layer * size, size)
        tail_block = in_all[here, tail_at : tail_at + LANES].astype(F32).T
        gain_rows[0:1, here] = tail_block[heads : heads + 1, :]
        gain_rows[1:2, here] = tail_block[heads + 1 : heads + 2, :]

        @turns(rows, chunk)
        def _(part):
            values = x_all[part, here].astype(F32) * scale_one[part, 0:1] * gain_rows[0:1, here]
            hn_all[here, part] = values.T.astype(BF16)
            proj_all[part, :] += dot(values.astype(BF16), in_all[here, :])

    def consume_at(distance):
        lower, upper = in_line.layer - distance, in_line.layer + distance

        @pl.when(lower >= 0)
        def _():
            consume(lower)

        @pl.when(upper < in_line.layers)
        def _():
            consume(upper)

    in_line.keep.wait()
    consume(in_line.layer)
    consume_at(1)
    second.forward()
    for distance in range(2, in_line.layers):
        in_line.step(distance)
        if distance == in_line.layers - 1:
            out_line.start()
            up_line.start()
        consume_at(distance)

    for n in (1, 2, 3):
        saves[n].start()
    out_line.step(1)
    fill_prefix(chunk, heads, pos_row, pos_col, proj_all[:, tail_at : tail_at + LANES] + bias[0:1, :], prefix)

    def share(index):
        block = rank * steps + index
        half = rows // 2

        def source(h):
            return gated_all.at[block, pl.ds(h * half, half), :]

        def place(owner, h):
            return gated_all.at[owner * steps + index, pl.ds(h * half, half), :]

        return Relay(rank, source, place, send_sem.at[2 + index], recv_sem.at[2 + index], None)

    per_block = LANES // head

    @pl.loop(0, steps)
    def _(index):
        def lanes_of(part_id):
            return proj_all[:, cols(part_id * width + index * LANES, LANES)]

        def gate(part):
            return proj_all[part, cols(3 * width + index * LANES, LANES)]

        group = pl.ds(index * per_block, per_block)
        attend_block(
            head, chunk, index, lanes_of(0), lanes_of(1), lanes_of(2), gate, gains, mask, prefix,
            gated_all.at[rank * steps + index], attended_all.at[index],
            query_all.at[group], key_all.at[group], value_all.at[group],
        )
        share(index).start(keep=False)

        @pl.when(index == 0)
        def _():
            out_line.step(2)

        @pl.when(index > 0)
        def _():
            share(index - 1).forward()

    up_line.step(1)
    out_line.step(3)
    share(steps - 1).forward()
    for n in (4, 5, 6, 7):
        saves[n].start()
    for index in range(steps):
        share(index).arrive()
    saves[8].start()
    out_line.keep.wait()
    for layer in range(out_line.layers):
        out_line.from_side(layer)
    save_out = pltpu.make_async_copy(out_cols, w_out, save_sem.at[len(saves)])
    save_out.start()

    third = relay_ops("gather_cols", rank, y_own, mixed_all, sems(2 + steps))

    @turns(rows, chunk)
    def _(part):
        total = x_all[part, cols(rank * width, width)].astype(F32)
        for block in range(gated_all.shape[0]):
            total = total + dot(gated_all[block, part, :], out_cols[block * LANES : (block + 1) * LANES, :])
        y_own[part, :] = total.astype(BF16)

    third.start()
    third.forward()
    up_line.step(2)
    loads[5].wait()
    down_line.start()
    third.finish()
    saves[9].start()

    @turns(rows, chunk)
    def _(part):
        values = mixed_all[part, :].astype(F32)
        low = values * rms_scale(values) * gain_rows[1:2, :]
        h2_all[part, :] = low.astype(BF16)
        turned_all[:, part] = low.T.astype(BF16)

    saves[10].start()
    saves[11].start()
    for distance in range(3, up_line.layers):
        up_line.step(distance)
    up_line.finish()
    down_line.near_finish()
    out_line.sent()
    in_line.sent()
    second.finish()
    for index in range(steps):
        share(index).finish(arrive=False, keep=False)
    for copy in saves:
        copy.wait()
    save_out.wait()


def front(
    collective_id, ranks, shards, head, heads, width, piece,
    tokens, cotangent, weight, weight_out, other, down, forget_weight, norm_gains, qk_gains, segments, order, forget_bias,
):
    own_rows, model = tokens.shape
    rows = ranks * own_rows
    chunk = pick_chunk(rows)
    steps, shard_rows = width // LANES, weight.shape[0]
    wide_in = 4 * width + LANES
    other_cols = other.shape[1] // ranks
    wide = (heads, rows, LANES)
    shape, vmem = jax.ShapeDtypeStruct, pltpu.VMEM
    return pl.pallas_call(
        functools.partial(front_kernel, shards, head, heads, width, piece, chunk),
        in_specs=[ANY] * 6 + [VMEM_WHOLE] * 4 + [pl.BlockSpec(memory_space=pltpu.SMEM)] * 2,
        out_specs=[ANY] * 16 + [VMEM_WHOLE] * 7,
        out_shape=[
            shape((rows, model), BF16),
            shape((rows, model), BF16),
            shape((model, wide_in), BF16),
            shape((model, width), BF16),
            shape((model, other_cols), BF16),
            shape((model, rows), BF16),
            shape((rows, wide_in), F32),
            shape((ranks * steps, rows, LANES), BF16),
            shape((steps, rows, LANES), F32),
            shape(wide, BF16), shape(wide, BF16), shape(wide, BF16),
            shape((rows, model), BF16),
            shape((shards * (down.shape[0] // ranks), model), BF16),
            shape((rows, model), BF16),
            shape((model, rows), BF16),
            shape((8, model), F32),
            shape((1, rows), F32), shape((rows, 1), F32), shape((1, rows), F32), shape((rows, 1), F32),
            shape((1, LANES), F32),
            shape((2, LANES), F32),
        ],
        scratch_shapes=[
            vmem(weight.shape, BF16),
            vmem(other.shape, BF16),
            vmem(weight_out.shape, BF16),
            vmem(tokens.shape, BF16),
            vmem(cotangent.shape, BF16),
            vmem((shard_rows, wide_in), BF16),
            vmem((shard_rows, other_cols), BF16),
            vmem((shard_rows, width), BF16),
            vmem((rows, model), BF16),
            vmem((model, wide_in), BF16),
            vmem((model, rows), BF16),
            vmem((rows, wide_in), F32),
            vmem((rows, rows), F32),
            vmem((rows, LANES), F32),
            vmem((ranks * steps, rows, LANES), BF16),
            vmem((steps, rows, LANES), F32),
            vmem(wide, BF16), vmem(wide, BF16), vmem(wide, BF16),
            vmem((model, width), BF16),
            vmem((rows, LANES), F32),
            vmem((rows, width), BF16),
            vmem((down.shape[0] // ranks, model), BF16),
            vmem((rows, model), BF16),
            vmem((rows, model), BF16),
            vmem((model, rows), BF16),
            pltpu.SemaphoreType.DMA((3 + steps, 6)),
            pltpu.SemaphoreType.DMA((3 + steps, 6)),
            pltpu.SemaphoreType.DMA((3 + steps, 2)),
            pltpu.SemaphoreType.DMA((FRONT_LOADS,)),
            pltpu.SemaphoreType.DMA((FRONT_SAVES + 1,)),
        ]
        + 4 * line_scratch(shards),
        compiler_params=pltpu.CompilerParams(
            collective_id=collective_id, has_side_effects=True, vmem_limit_bytes=VMEM_LIMIT
        ),
        cost_estimate=pl.CostEstimate(flops=0, bytes_accessed=300 << 20, transcendentals=0),
        name="front",
    )(
        tokens, cotangent, weight, weight_out, other, down, forget_weight, norm_gains, qk_gains, segments, order, forget_bias
    )


def ffn_kernel(
    shards, chunk,
    normed, turned_from, w_gate_up, cotangent, down_near,
    w_down, hidden, grad_gate_up, grad_weight, grad_down,
    weight_in, cotangent_in, gates, ups, hn, turned, acts, grads, weight_out, down_out,
    load_sem, save_sem, tile_sem, near_sem, *line_sems,
):
    size = gates.shape[1]
    rows, model = normed.shape
    tile = 2 * w_down.shape[0] // shards
    loads = [
        pltpu.make_async_copy(a, b, load_sem.at[n])
        for n, (a, b) in enumerate(
            ((normed, hn), (w_gate_up, weight_in), (cotangent, cotangent_in), (turned_from, turned))
        )
    ]
    saves = [
        pltpu.make_async_copy(a, b, save_sem.at[n])
        for n, (a, b) in enumerate(
            ((acts, hidden), (down_out, grad_down))
        )
    ]
    line = Line(shards, None, w_down, line_sems)
    line.near_start(down_near, near_sem)
    for copy in loads:
        copy.start()
    greet([], line)
    line.resume(down_near, near_sem)
    loads[0].wait()
    loads[1].wait()

    def span(turn, start=0):
        return pl.ds(pl.multiple_of(start + turn * tile, LANES), tile)

    def activate(turn):
        gate = dot(hn[...], weight_in[:, span(turn)])
        up = dot(hn[...], weight_in[:, span(turn, size)])
        gates[:, span(turn)] = gate
        ups[:, span(turn)] = up
        acts[:, span(turn)] = (jax.nn.silu(gate) * up).astype(BF16)

    def down_grad(turn):
        down_out[span(turn), :] = left_product(acts[:, span(turn)], cotangent_in[...]).astype(BF16)

    count = size // tile
    pl.loop(0, count)(activate)
    saves[0].start()
    loads[2].wait()
    loads[3].wait()
    line.near_load(down_near, near_sem, 0).wait()

    def consume(turn):
        grad = right_product(cotangent_in[...], w_down[span(turn), :])
        gate, up = gates[:, span(turn)], ups[:, span(turn)]
        sig = jax.nn.sigmoid(gate)
        grads[:, span(turn)] = (grad * up * sig * (1.0 + gate * (1.0 - sig))).astype(BF16)
        grads[:, span(turn, size)] = (grad * gate * sig).astype(BF16)

        for start in (0, size):
            here = span(turn, start)

            @turns(model, 3 * chunk if model % (3 * chunk) == 0 else chunk)
            def _(part):
                weight_out[part, here] = dot(turned[part, :], grads[:, here]).astype(BF16)

        for copy in tile_saves(turn):
            copy.start()

    def tile_saves(turn):
        for n, start in enumerate((0, size)):
            here = span(turn, start)
            yield pltpu.make_async_copy(grads.at[:, here], grad_gate_up.at[:, here], tile_sem.at[turn, 2 * n])
            yield pltpu.make_async_copy(weight_out.at[:, here], grad_weight.at[:, here], tile_sem.at[turn, 2 * n + 1])

    def consume_at(distance):
        lower, upper = line.layer - distance, line.layer + distance

        @pl.when(lower >= 0)
        def _():
            line.from_side(lower)
            consume(lower)

        @pl.when(upper < line.layers)
        def _():
            line.from_side(upper)
            consume(upper)

    line.step(2)
    consume(line.layer)
    consume_at(1)
    pl.loop(0, count)(down_grad)
    saves[1].start()
    for distance in range(3, line.layers):
        line.step(distance)
    for distance in range(2, line.layers):
        consume_at(distance)
    line.resumed_sent()
    for copy in saves:
        copy.wait()

    @pl.loop(0, count)
    def _(turn):
        for copy in tile_saves(turn):
            copy.wait()


def ffn(collective_id, shards, normed, turned, w_gate_up, cotangent, down_near):
    rows, model = normed.shape
    size = w_gate_up.shape[1] // 2
    shape, vmem = jax.ShapeDtypeStruct, pltpu.VMEM
    return pl.pallas_call(
        functools.partial(ffn_kernel, shards, pick_chunk(rows)),
        in_specs=[ANY] * 5,
        out_specs=[VMEM_WHOLE] + [ANY] * 4,
        out_shape=[
            shape((size, model), BF16),
            shape((rows, size), BF16),
            shape((rows, 2 * size), BF16),
            shape((model, 2 * size), BF16),
            shape((size, model), BF16),
        ],
        scratch_shapes=[
            vmem(w_gate_up.shape, BF16),
            vmem((rows, model), BF16),
            vmem((rows, size), F32),
            vmem((rows, size), F32),
            vmem((rows, model), BF16),
            vmem((model, rows), BF16),
            vmem((rows, size), BF16),
            vmem((rows, 2 * size), BF16),
            vmem((model, 2 * size), BF16),
            vmem((size, model), BF16),
            pltpu.SemaphoreType.DMA((4,)),
            pltpu.SemaphoreType.DMA((2,)),
            pltpu.SemaphoreType.DMA((shards // 2, 4)),
            pltpu.SemaphoreType.DMA((3,)),
        ]
        + line_scratch(shards),
        compiler_params=pltpu.CompilerParams(
            collective_id=collective_id, has_side_effects=True, vmem_limit_bytes=VMEM_LIMIT
        ),
        cost_estimate=pl.CostEstimate(flops=0, bytes_accessed=100 << 20, transcendentals=0),
        name="ffn",
    )(normed, turned, w_gate_up, cotangent, down_near)


class ShardSum:
    def __init__(self, shards, blocks, side_in, kept, from_below, from_above, sems):
        self.shard = lax.axis_index("fsdp")
        self.layers = shards // 2
        self.layer, self.core = self.shard // 2, self.shard % 2
        self.sibling = {"fsdp": self.shard ^ 1}
        self.above, self.below = {"fsdp": self.shard + 2}, {"fsdp": self.shard - 2}
        self.has_above, self.has_below = self.layer < self.layers - 1, self.layer > 0
        self.blocks, self.side_in, self.kept = blocks, side_in, kept
        self.from_below, self.from_above = from_below, from_above
        self.rows = kept.shape[1]
        self.side_send, self.side_recv, self.up_send, self.up_recv, self.down_send, self.down_recv = sems

    def side(self, layer):
        return pltpu.make_async_remote_copy(
            rows_of(self.blocks, 2 * layer + 1 - self.core, self.rows), self.side_in.at[layer],
            self.side_send.at[layer], self.side_recv.at[layer], device_id=self.sibling, device_id_type=MESH,
        )

    def start(self):
        for layer in range(self.layers):
            self.side(layer).start()

    def presum(self):
        for layer in range(self.layers):
            self.side(layer).wait_recv()
            own = rows_of(self.blocks, 2 * layer + self.core, self.rows)[...].astype(F32)
            self.kept[layer] = (own + self.side_in[layer].astype(F32)).astype(BF16)

    def up(self, stage):
        return pltpu.make_async_remote_copy(
            self.kept.at[self.layers - 1 - stage + self.layer], self.from_below.at[stage],
            self.up_send.at[stage], self.up_recv.at[stage], device_id=self.above, device_id_type=MESH,
        )

    def down(self, stage):
        return pltpu.make_async_remote_copy(
            self.kept.at[stage - self.layers + 1 + self.layer], self.from_above.at[stage],
            self.down_send.at[stage], self.down_recv.at[stage], device_id=self.below, device_id_type=MESH,
        )

    def each_sent(self, stage, what):
        @pl.when(self.has_above & (self.layer <= stage))
        def _():
            what(self.up(stage))

        @pl.when(self.has_below & (self.layers - 1 - self.layer <= stage))
        def _():
            what(self.down(stage))

    def send(self, stage):
        self.each_sent(stage, lambda copy: copy.start())

    def receive(self, stage):
        def add(target, arrived):
            self.kept[target] = (self.kept[target].astype(F32) + arrived[stage].astype(F32)).astype(BF16)

        @pl.when(self.has_below & (self.layer - 1 <= stage))
        def _():
            pltpu.make_async_remote_copy(
                self.from_below.at[stage], self.from_below.at[stage], self.up_send.at[stage], self.up_recv.at[stage],
                device_id=self.below, device_id_type=MESH,
            ).wait_recv()
            add(self.layers - 2 - stage + self.layer, self.from_below)

        @pl.when(self.has_above & (self.layers - 2 - self.layer <= stage))
        def _():
            pltpu.make_async_remote_copy(
                self.from_above.at[stage], self.from_above.at[stage], self.down_send.at[stage],
                self.down_recv.at[stage], device_id=self.above, device_id_type=MESH,
            ).wait_recv()
            add(stage - self.layers + 2 + self.layer, self.from_above)

    def sent(self):
        for layer in range(self.layers):
            self.side(layer).wait_send()
        for stage in range(self.layers - 1):
            self.each_sent(stage, lambda copy: copy.wait_send())


def shard_sum_scratch(shards, rows, cols):
    layers = shards // 2
    few, all_layers = pltpu.SemaphoreType.DMA((layers - 1,)), pltpu.SemaphoreType.DMA((layers,))
    block = pltpu.VMEM((layers, rows, cols), BF16)
    part = pltpu.VMEM((layers - 1, rows, cols), BF16)
    return [block, block, part, part], [all_layers, all_layers, few, few, few, few]


class Fold:
    def __init__(self, rank, piece, first, between, second, send_sem, recv_sem):
        self.rank, self.piece, self.first, self.between, self.second = rank, piece, first, between, second
        self.send_sem, self.recv_sem = send_sem, recv_sem

    def copy(self, number):
        me = self.rank
        source, target, distance = (
            lambda: (self.piece(me ^ 1, 0), self.first(0, 0), 1),
            lambda: (self.piece(me ^ 3, 0), self.first(1, 0), 1),
            lambda: (self.piece(me ^ 2, 1), self.first(0, 1), 2),
            lambda: (self.piece(me ^ 3, 1), self.first(1, 1), 2),
            lambda: (self.between(0), self.second(0), 2),
            lambda: (self.between(1), self.second(1), 1),
        )[number]()
        return to_rank(source, target, self.send_sem.at[number], self.recv_sem.at[number], me ^ distance)

    def start(self):
        for number in range(4):
            self.copy(number).start()

    def pass_on(self):
        for h, distance in ((0, 2), (1, 1)):
            self.copy(2 * h).wait_recv()
            self.copy(2 * h + 1).wait_recv()
            own = self.piece(self.rank ^ distance, h)[...].astype(F32)
            self.between(h)[...] = (own + self.first(1, h)[...].astype(F32)).astype(BF16)
            self.copy(4 + h).start()

    def total(self, h):
        self.copy(4 + h).wait_recv()
        own = self.piece(self.rank, h)[...].astype(F32)
        return own + self.first(0, h)[...].astype(F32) + self.second(h)[...].astype(F32)

    def sent(self):
        for number in range(6):
            self.copy(number).wait_send()


def middle_kernel(
    ranks,
    grad_gate_up, w_gate_up, mixed, cotangent, w_out, hidden, w_down, gated, gain,
    mixed_grad, gated_grad, gain_grad, down_part, out_grad,
    grad_in, weight_in, mixed_in, cotangent_in, out_in, hidden_in, down_in, gated_in, low_grad, down_all, out_all,
    wide, first_out, first_in, first_between, first_end, second_out, second_in, second_between, second_end,
    load_sem, save_sem, first_send, first_recv, second_send, second_recv,
):
    rank = lax.axis_index("ctx")
    rows = mixed.shape[0] // ranks
    model, width = w_out.shape
    tile = 256
    loads = [
        pltpu.make_async_copy(a, b, load_sem.at[n])
        for n, (a, b) in enumerate(
            (
                (w_gate_up, weight_in), (grad_gate_up, grad_in), (mixed, mixed_in), (cotangent, cotangent_in),
                (w_out, out_in), (hidden, hidden_in), (w_down, down_in), (gated, gated_in),
            )
        )
    ]
    saves = [
        pltpu.make_async_copy(down_all, down_part, save_sem.at[0]),
        pltpu.make_async_copy(out_all, out_grad, save_sem.at[1]),
    ]
    for copy in loads:
        copy.start()
    greet([{"ctx": rank ^ distance} for distance in range(1, ranks)])
    gain_grad[...] = jnp.zeros_like(gain_grad)
    for copy in loads[:2]:
        copy.wait()

    def part(turn):
        return pl.ds(pl.multiple_of(turn * rows, 16), rows)

    half = rows // 2

    def fold(out, into, between, end, send_sem, recv_sem):
        def make(turn):
            def at(h):
                return pl.ds(pl.multiple_of(turn * rows + h * half, 16), half)

            return Fold(
                rank,
                lambda index, h: out.at[index, at(h), :],
                lambda slot, h: into.at[slot, at(h), :],
                lambda h: between.at[at(h), :],
                lambda h: end.at[at(h), :],
                send_sem.at[turn],
                recv_sem.at[turn],
            )

        return make

    first = fold(first_out, first_in, first_between, first_end, first_send, first_recv)
    second = fold(second_out, second_in, second_between, second_end, second_send, second_recv)

    def compute(turn):
        here = part(turn)

        @pl.loop(0, model // tile)
        def _(step):
            cols = pl.ds(pl.multiple_of(step * tile, tile), tile)
            wide[:, cols] = right_product(grad_in[here, :], weight_in[cols, :])

        @pl.when(turn == 0)
        def _():
            for copy in loads[2:5]:
                copy.wait()

        values = mixed_in[here, :].astype(F32)
        scale = rms_scale(values)
        grad = wide[...]
        gain_grad[0:1, :] += jnp.sum(grad * values * scale, axis=0, keepdims=True)
        back = norm_back(grad, values, scale, gain[1:2, :]).astype(BF16)
        for index in range(ranks):
            first_out[index, here, :] = back[:, index * width : (index + 1) * width]
        first(turn).start()

    def project(turn):
        here = part(turn)
        for h in range(2):
            at = pl.ds(pl.multiple_of(turn * rows + h * half, 16), half)
            total = cotangent_in[at, pl.ds(pl.multiple_of(rank * width, LANES), width)].astype(F32)
            total = total + first(turn).total(h)
            mixed_grad[at, :] = total
            low_grad[at, :] = total.astype(BF16)
        for index in range(ranks):
            second_out[index, here, :] = right_product(
                low_grad[here, :], out_in[index * width : (index + 1) * width, :]
            ).astype(BF16)
        second(turn).start()

    def collect(turn):
        for h in range(2):
            at = pl.ds(pl.multiple_of(turn * rows + h * half, 16), half)
            gated_grad[at, :] = second(turn).total(h)

    def aside(turn):
        @pl.when(turn == ranks)
        def _():
            for copy in loads[5:8]:
                copy.wait()

            @pl.loop(0, model // tile)
            def _(step):
                cols = pl.ds(pl.multiple_of(step * tile, tile), tile)
                down_all[:, cols] = dot(hidden_in[...], down_in[:, cols]).astype(BF16)

            saves[0].start()

        @pl.when(turn == ranks + 2)
        def _():
            @pl.loop(0, gated_in.shape[0])
            def _(block):
                out_all[pl.ds(pl.multiple_of(block * LANES, LANES), LANES), :] = left_product(
                    gated_in[block], low_grad[...]
                ).astype(BF16)

            saves[1].start()

    @pl.loop(0, ranks + 4)
    def _(turn):
        stages = (
            compute, lambda t: first(t).pass_on(), project, lambda t: second(t).pass_on(), collect,
        )
        for lag, stage in enumerate(stages):
            if lag == 4:
                aside(turn)

            @pl.when((turn >= lag) & (turn < ranks + lag))
            def _():
                stage(turn - lag)

    @pl.loop(0, ranks)
    def _(turn):
        first(turn).sent()
        second(turn).sent()

    for copy in saves:
        copy.wait()


def middle(
    collective_id, ranks, grad_gate_up, w_gate_up, mixed, cotangent, w_out, hidden, w_down, gated, gain
):
    rows, model = mixed.shape
    width = w_out.shape[1]
    flat = pltpu.VMEM((rows, width), BF16)
    blocks = [pltpu.VMEM((ranks, rows, width), BF16), pltpu.VMEM((2, rows, width), BF16), flat, flat]
    sems = pltpu.SemaphoreType.DMA((ranks, 6))
    return pl.pallas_call(
        functools.partial(middle_kernel, ranks),
        in_specs=[ANY] * 8 + [VMEM_WHOLE],
        out_specs=[VMEM_WHOLE] * 3 + [ANY] * 2,
        out_shape=[
            jax.ShapeDtypeStruct((rows, width), F32),
            jax.ShapeDtypeStruct((rows, width), F32),
            jax.ShapeDtypeStruct((8, model), F32),
            jax.ShapeDtypeStruct((rows, model), BF16),
            jax.ShapeDtypeStruct((model, width), BF16),
        ],
        scratch_shapes=[
            pltpu.VMEM(grad_gate_up.shape, BF16),
            pltpu.VMEM(w_gate_up.shape, BF16),
            pltpu.VMEM(mixed.shape, BF16),
            pltpu.VMEM(cotangent.shape, BF16),
            pltpu.VMEM(w_out.shape, BF16),
            pltpu.VMEM(hidden.shape, BF16),
            pltpu.VMEM(w_down.shape, BF16),
            pltpu.VMEM(gated.shape, BF16),
            pltpu.VMEM((rows, width), BF16),
            pltpu.VMEM((rows, model), BF16),
            pltpu.VMEM((model, width), BF16),
            pltpu.VMEM((rows // ranks, model), F32),
            *blocks, *blocks,
            pltpu.SemaphoreType.DMA((8,)),
            pltpu.SemaphoreType.DMA((2,)),
            sems, sems, sems, sems,
        ],
        compiler_params=pltpu.CompilerParams(
            collective_id=collective_id, has_side_effects=True, vmem_limit_bytes=VMEM_LIMIT
        ),
        cost_estimate=pl.CostEstimate(flops=0, bytes_accessed=150 << 20, transcendentals=0),
        name="middle",
    )(grad_gate_up, w_gate_up, mixed, cotangent, w_out, hidden, w_down, gated, gain)


def last_kernel(
    ranks, shards,
    grad_project, w_in, inputs, aside, pieces, mixed, share, mixed_grad, gain, gain_two_grad, small, segments, forget_grad,
    tokens_grad, block_out, total_sums, parts, aside_all, share_all,
    grad_in, weight_in, inputs_in, aside_in, pieces_in, mixed_in, wide, out, into, between, end, sums_out, sums_in,
    share_in, load_sem, send_sem, recv_sem, sums_send, sums_recv, aside_send, aside_recv, aside_own,
):
    rank = lax.axis_index("ctx")
    rows = inputs.shape[0] // ranks
    model, width = inputs.shape[1], mixed_grad.shape[1]
    tile = 256
    loads = [
        pltpu.make_async_copy(a, b, load_sem.at[n])
        for n, (a, b) in enumerate(
            (
                (aside, aside_in), (w_in, weight_in), (grad_project, grad_in), (inputs, inputs_in),
                (pieces, pieces_in), (rows_of(mixed, rank, rows), mixed_in), (share, share_in),
            )
        )
    ]
    for copy in loads:
        copy.start()
    greet([{"ctx": rank ^ distance} for distance in range(1, ranks)])
    relay, share_relay = [
        relay_ops("stack", rank, a, b, (aside_send.at[n], aside_recv.at[n], aside_own.at[n]))
        for n, (a, b) in enumerate(((aside_in, aside_all), (share_in, share_all)))
    ]
    loads[6].wait()
    share_relay.start()
    loads[0].wait()
    relay.start()
    sums_out[...] = jnp.zeros_like(sums_out)
    sums_out[1:2, :] = gain_two_grad[0:1, :]
    sums_out[2:3, 0:LANES] = small[0:1, :]
    sums_out[2:3, LANES : 2 * LANES] = small[1:2, :]
    for index in range(ranks):
        sums_out[3 + index : 4 + index, 0:LANES] = jnp.where(rank == index, small[2:3, :], 0.0)
    for copy in loads[1:4]:
        copy.wait()

    half = rows // 2

    def at(h):
        return pl.ds(h * half, half)

    fold = Fold(
        rank,
        lambda index, h: out.at[index, at(h), :],
        lambda slot, h: into.at[slot, at(h), :],
        lambda h: between.at[at(h), :],
        lambda h: end.at[at(h), :],
        send_sem,
        recv_sem,
    )

    def send_sums(distance):
        return to_rank(
            sums_out, sums_in.at[distance], sums_send.at[distance - 1], sums_recv.at[distance - 1], rank ^ distance
        )

    def compute(other):
        here = pl.ds(pl.multiple_of(other * rows, 16), rows)

        @pl.loop(0, model // tile)
        def _(step):
            cols = pl.ds(pl.multiple_of(step * tile, tile), tile)
            wide[:, cols] = right_product(grad_in[here, :], weight_in[cols, :])

        values = inputs_in[here, :].astype(F32)
        scale = rms_scale(values)
        grad = wide[...]
        sums_out[0:1, :] += jnp.sum(grad * values * scale, axis=0, keepdims=True)
        wide[...] = norm_back(grad, values, scale, gain[0:1, :])
        own = pl.ds(pl.multiple_of(rank * width, LANES), width)
        wide[:, own] += mixed_grad[here, :]
        out[other] = wide[...].astype(BF16)

    @pl.loop(1, ranks)
    def _(turn):
        compute(rank ^ (ranks - turn))

        @pl.when(turn == 2)
        def _():
            for number in (2, 3):
                fold.copy(number).start()

        @pl.when(turn == 3)
        def _():
            for number in (0, 1):
                fold.copy(number).start()

    share_relay.forward()
    for copy in loads[4:6]:
        copy.wait()
    own = pl.ds(pl.multiple_of(rank * rows, 16), rows)
    result = mixed_in[...].astype(F32)
    for index in range(ranks):
        result = result + pieces_in[index].astype(F32)
    block_out[...] = result.astype(BF16)
    branch = result - inputs_in[own, :].astype(F32)
    valid = jnp.where(segments[own, :] >= 0.0, 1.0, 0.0)
    lane = lax.broadcasted_iota(jnp.int32, (1, LANES), 1)
    stats = jnp.zeros((1, LANES), F32)
    for index, values in enumerate((result, branch)):
        total = jnp.sum(valid * jnp.sum(values * values, axis=-1, keepdims=True), axis=0, keepdims=True)
        stats = jnp.where(lane == index, total, stats)
    sums_out[7:8, 0:LANES] = stats
    compute(rank)
    for distance in range(1, ranks):
        send_sums(distance).start()
    relay.forward()
    fold.pass_on()
    for h in range(2):
        tokens_grad[at(h), :] = fold.total(h).astype(BF16)
    total = sums_out[...]
    for distance in range(1, ranks):
        send_sums(distance).wait_recv()
        total = total + sums_in[distance]
    total_sums[...] = total
    share = model // shards
    parts[...] = jnp.zeros_like(parts)
    for index in range(shards):
        parts[index, 0:2, 0:share] = total[0:2, index * share : (index + 1) * share]
        parts[index, 2:8, :] = total[2:8, 0 : parts.shape[2]]
        parts[index, 8:16, 0:share] = forget_grad[:, index * share : (index + 1) * share]
    fold.sent()
    for distance in range(1, ranks):
        send_sums(distance).wait_send()
    relay.finish()
    share_relay.finish()


def last_moves(
    collective_id, ranks, shards,
    grad_project, w_in, inputs, aside, pieces, mixed, share, mixed_grad, gain, gain_two_grad, small, segments,
    forget_grad,
):
    rows, model = inputs.shape
    own = (rows // ranks, model)
    flat = pltpu.VMEM(own, BF16)
    blocks = [pltpu.VMEM((ranks,) + own, BF16), pltpu.VMEM((2,) + own, BF16), flat, flat]
    sems = pltpu.SemaphoreType.DMA((ranks - 1,))
    return pl.pallas_call(
        functools.partial(last_kernel, ranks, shards),
        in_specs=[ANY] * 7 + [VMEM_WHOLE] * 6,
        out_specs=[VMEM_WHOLE] * 4 + [ANY] * 2,
        out_shape=[
            jax.ShapeDtypeStruct(own, BF16),
            jax.ShapeDtypeStruct(own, BF16),
            jax.ShapeDtypeStruct((8, model), F32),
            jax.ShapeDtypeStruct((shards, 16, max(2 * LANES, -(-model // shards // LANES) * LANES)), F32),
            jax.ShapeDtypeStruct((ranks,) + aside.shape, BF16),
            jax.ShapeDtypeStruct((ranks,) + share.shape, BF16),
        ],
        scratch_shapes=[
            pltpu.VMEM(grad_project.shape, BF16),
            pltpu.VMEM(w_in.shape, BF16),
            pltpu.VMEM(inputs.shape, BF16),
            pltpu.VMEM(aside.shape, BF16),
            pltpu.VMEM(pieces.shape, BF16),
            pltpu.VMEM(own, BF16),
            pltpu.VMEM(own, F32),
            *blocks,
            pltpu.VMEM((8, model), F32),
            pltpu.VMEM((ranks, 8, model), F32),
            pltpu.VMEM(share.shape, BF16),
            pltpu.SemaphoreType.DMA((7,)),
            pltpu.SemaphoreType.DMA((6,)),
            pltpu.SemaphoreType.DMA((6,)),
            sems, sems,
            pltpu.SemaphoreType.DMA((2, 6)),
            pltpu.SemaphoreType.DMA((2, 6)),
            pltpu.SemaphoreType.DMA((2, 2)),
        ],
        compiler_params=pltpu.CompilerParams(
            collective_id=collective_id, has_side_effects=True, vmem_limit_bytes=VMEM_LIMIT
        ),
        cost_estimate=pl.CostEstimate(flops=0, bytes_accessed=150 << 20, transcendentals=0),
        name="last_moves",
    )(grad_project, w_in, inputs, aside, pieces, mixed, share, mixed_grad, gain, gain_two_grad, small, segments, forget_grad)


def finish_kernel(
    ranks, shards, late, parts, late_all, part_sum, forget_all,
    late_in, into, load_sem, send_sem, recv_sem, own_sem, part_send, part_recv, forget_send, forget_recv,
):
    rank = lax.axis_index("ctx")
    shard = lax.axis_index("fsdp")
    load = pltpu.make_async_copy(late, late_in, load_sem.at[0])
    load.start()
    relay = relay_ops("stack", rank, late_in, late_all, (send_sem, recv_sem, own_sem))
    greet(
        [{"ctx": rank ^ distance} for distance in range(1, ranks)]
        + [{"fsdp": shard ^ distance} for distance in range(1, shards)]
    )
    load.wait()
    relay.start()

    def send(distance):
        other = shard ^ distance
        return pltpu.make_async_remote_copy(
            parts.at[other], into.at[distance], part_send.at[distance - 1], part_recv.at[distance - 1],
            device_id={"fsdp": other}, device_id_type=MESH,
        )

    def send_forget(distance):
        return to_rank(
            forget_all.at[rank], forget_all.at[rank], forget_send.at[distance - 1], forget_recv.at[distance - 1],
            rank ^ distance,
        )

    for distance in range(1, shards):
        send(distance).start()
    total = parts[shard]
    for distance in range(1, shards):
        send(distance).wait_recv()
        total = total + into[distance]
    part_sum[...] = total
    forget_all[rank] = total[8:16, :]
    for distance in range(1, ranks):
        send_forget(distance).start()
    relay.forward()
    for distance in range(1, ranks):
        send_forget(distance).wait()
    for distance in range(1, shards):
        send(distance).wait_send()
    relay.finish()


def finish_moves(collective_id, ranks, shards, late, parts):
    sems = pltpu.SemaphoreType.DMA((shards - 1,))
    return pl.pallas_call(
        functools.partial(finish_kernel, ranks, shards),
        in_specs=[ANY, VMEM_WHOLE],
        out_specs=[ANY, VMEM_WHOLE, VMEM_WHOLE],
        out_shape=[
            jax.ShapeDtypeStruct((ranks,) + late.shape, BF16),
            jax.ShapeDtypeStruct(parts.shape[1:], F32),
            jax.ShapeDtypeStruct((ranks, 8, parts.shape[2]), F32),
        ],
        scratch_shapes=[
            pltpu.VMEM(late.shape, BF16),
            pltpu.VMEM(parts.shape, F32),
            pltpu.SemaphoreType.DMA((1,)),
            pltpu.SemaphoreType.DMA((6,)),
            pltpu.SemaphoreType.DMA((6,)),
            pltpu.SemaphoreType.DMA((2,)),
            sems, sems,
            pltpu.SemaphoreType.DMA((ranks - 1,)),
            pltpu.SemaphoreType.DMA((ranks - 1,)),
        ],
        compiler_params=pltpu.CompilerParams(
            collective_id=collective_id, has_side_effects=True, vmem_limit_bytes=VMEM_LIMIT
        ),
        cost_estimate=pl.CostEstimate(flops=0, bytes_accessed=50 << 20, transcendentals=0),
        name="finish_moves",
    )(late, parts)


def spread_kernel(pieces, *refs):
    source, targets = refs[0], refs[1:]
    ranks = source.shape[0]
    for target, (piece, first, count) in zip(targets, pieces):
        for block in range(count):
            for index in range(ranks):
                target[:, pl.ds((block * ranks + index) * piece, piece)] = source[
                    index, :, pl.ds(first + block * piece, piece)
                ].astype(F32)


def spread_cols(source, *pieces):
    ranks, rows, cols = source.shape
    if any(piece % LANES or first % LANES for piece, first, _ in pieces):
        return [
            jnp.concatenate(
                [
                    source[c, :, first + i * piece : first + (i + 1) * piece]
                    for i in range(count)
                    for c in range(ranks)
                ],
                axis=1,
            ).astype(F32)
            for piece, first, count in pieces
        ]
    part = rows // 4 if rows % 64 == 0 else rows
    widths = [count * ranks * piece for piece, _, count in pieces]
    return pl.pallas_call(
        functools.partial(spread_kernel, pieces),
        grid=(rows // part,),
        in_specs=[pl.BlockSpec((ranks, part, cols), lambda step: (0, step, 0))],
        out_specs=[pl.BlockSpec((part, w), lambda step: (step, 0)) for w in widths],
        out_shape=[jax.ShapeDtypeStruct((rows, w), F32) for w in widths],
        compiler_params=pltpu.CompilerParams(vmem_limit_bytes=VMEM_LIMIT),
        cost_estimate=pl.CostEstimate(flops=0, bytes_accessed=rows * sum(widths) * 6, transcendentals=0),
        name="spread_cols",
    )(source)


def spread_early_kernel(piece, gate_up, down, gate_up_out, down_out):
    ranks = gate_up.shape[0]
    for block in range(gate_up.shape[2] // piece):
        for index in range(ranks):
            gate_up_out[:, (block * ranks + index) * piece : (block * ranks + index + 1) * piece] = gate_up[
                index, :, block * piece : (block + 1) * piece
            ].astype(F32)
    size = down.shape[1]
    for index in range(down.shape[0]):
        down_out[index * size : (index + 1) * size, :] = down[index].astype(F32)


def spread_early(gate_up, down, piece):
    ranks, rows, cols = gate_up.shape
    _, down_rows, model = down.shape
    steps = 2
    part, each = rows // steps, ranks // steps
    return pl.pallas_call(
        functools.partial(spread_early_kernel, piece),
        grid=(steps,),
        in_specs=[
            pl.BlockSpec((ranks, part, cols), lambda step: (0, step, 0)),
            pl.BlockSpec((each, down_rows, model), lambda step: (step, 0, 0)),
        ],
        out_specs=[
            pl.BlockSpec((part, ranks * cols), lambda step: (step, 0)),
            pl.BlockSpec((each * down_rows, model), lambda step: (step, 0)),
        ],
        out_shape=[
            jax.ShapeDtypeStruct((rows, ranks * cols), F32),
            jax.ShapeDtypeStruct((ranks * down_rows, model), F32),
        ],
        compiler_params=pltpu.CompilerParams(vmem_limit_bytes=VMEM_LIMIT),
        cost_estimate=pl.CostEstimate(
            flops=0, bytes_accessed=6 * ranks * (rows * cols + down_rows * model), transcendentals=0
        ),
        name="spread_early",
    )(gate_up, down)


def unpack_kernel(
    width, heads, head, late, forget_all, sums, totals, segments, first_rows, second_rows,
    in_out, out_out, first_out, second_out, forget_out, gains, bias, qk, rms,
):
    ranks = late.shape[0]
    first = 4 * width
    for block in range(4):
        for index in range(ranks):
            in_out[:, (block * ranks + index) * width : (block * ranks + index + 1) * width] = late[
                index, :, block * width : (block + 1) * width
            ].astype(F32)
    first_out[...] = first_rows[...]
    second_out[...] = second_rows[...]
    lane = lax.broadcasted_iota(jnp.int32, (LANES, ranks * heads), 0)
    place = lax.broadcasted_iota(jnp.int32, (LANES, ranks * heads), 1)
    biases = jnp.zeros((8, ranks * heads), F32)
    for index in range(ranks):
        chosen = (lane < heads) & (place == index * heads + lane)
        out_out[:, index * width : (index + 1) * width] = late[index, :, first : first + width].astype(F32)
        forget_out[index * heads : (index + 1) * heads, :] = forget_all[index, 0:heads, 0 : forget_out.shape[1]]
        row = jnp.broadcast_to(sums[3 + index : 4 + index, 0:LANES], (8, LANES))
        for part in split_three(row):
            biases = biases + dot(part.astype(BF16), jnp.where(chosen, 1.0, 0.0).astype(BF16))
    gains[...] = sums[0:2, 0 : gains.shape[1]]
    bias[...] = biases[0:1, :]
    for row in range(2):
        qk[row : row + 1, :] = sum(
            sums[2:3, row * LANES + side * head : row * LANES + (side + 1) * head] for side in range(LANES // head)
        )
    count = jnp.sum(jnp.where(segments[...] >= 0, 1.0, 0.0), axis=-1, keepdims=True)
    rms[...] = jnp.sqrt(totals[7:8, 0:2] / (count * totals.shape[1]))


def unpack(late, forget_all, sums, totals, segments, first_rows, second_rows, width, heads, head):
    ranks, rows, cols = late.shape
    part = rows // 2

    def block(lanes):
        return pl.BlockSpec((part, lanes), lambda step: (step, 0))

    share = rows
    shape = jax.ShapeDtypeStruct
    return pl.pallas_call(
        functools.partial(unpack_kernel, width, heads, head),
        grid=(rows // part,),
        in_specs=[
            pl.BlockSpec((ranks, part, cols), lambda step: (0, step, 0)),
        ]
        + [whole(a.shape) for a in (forget_all, sums, totals, segments)]
        + [block(first_rows.shape[1])] * 2,
        out_specs=[block(4 * ranks * width), block(ranks * width)] + [block(first_rows.shape[1])] * 2
        + [whole(a) for a in ((ranks * heads, rows), (2, share), (1, ranks * heads), (2, head), (1, 2))],
        out_shape=[
            shape((rows, 4 * ranks * width), F32),
            shape((rows, ranks * width), F32),
            shape(first_rows.shape, BF16),
            shape(second_rows.shape, BF16),
            shape((ranks * heads, rows), F32),
            shape((2, share), F32),
            shape((1, ranks * heads), F32),
            shape((2, head), F32),
            shape((1, 2), F32),
        ],
        compiler_params=pltpu.CompilerParams(vmem_limit_bytes=VMEM_LIMIT),
        cost_estimate=pl.CostEstimate(flops=0, bytes_accessed=ranks * rows * cols * 6, transcendentals=0),
        name="unpack",
    )(late, forget_all, sums, totals, segments, first_rows, second_rows)


class Native:
    def __init__(self, ranks):
        self.ranks = ranks

    def begin(self, tokens, cotangent, weight, tail, other, piece, width, padded):
        rank, model = lax.axis_index("ctx"), tokens.shape[1]
        parts = [lax.dynamic_slice_in_dim(weight, i * model + rank * width, width, 1) for i in range(4)]
        parts = [jnp.pad(part, ((0, 0), (0, padded - width))) for part in parts]
        cols = other.shape[1] // self.ranks
        picks = [
            lax.dynamic_slice_in_dim(other, (i * self.ranks + rank) * piece, piece, 1) for i in range(cols // piece)
        ]
        return (
            lax.all_gather(tokens, "ctx", axis=0, tiled=True),
            lax.all_gather(cotangent, "ctx", axis=0, tiled=True),
            lax.all_gather(jnp.concatenate(parts + [tail], axis=1), "fsdp", axis=0, tiled=True),
            jnp.concatenate(picks, axis=1),
        )

    def gather_cols(self, array, piece):
        return lax.all_gather(array, "ctx", axis=1, tiled=True), lax.all_gather(piece, "fsdp", axis=0, tiled=True)


def body(
    tokens, block_order, segment_ids, norm_gains, attn_in_weight, forget_weight, forget_bias,
    qk_gains, out_weight, gate_up_weight, down_weight, out_grad,
):
    ranks = lax.axis_size("ctx")
    shards = lax.axis_size("fsdp")
    rank = lax.axis_index("ctx")
    row_count, model_width = tokens.shape[1], tokens.shape[2]
    head_count, head_dim = forget_bias.shape[0], qk_gains.shape[1]
    local_heads = head_count // ranks
    width = local_heads * head_dim
    padded = -(-width // LANES) * LANES
    seq_order = block_order[0]
    seq_len = segment_ids.shape[1]
    block_len = seq_len // seq_order.shape[0]
    hidden_piece = down_weight.shape[0] // ranks
    hidden = hidden_piece * shards
    plain = ranks == 4 and shards & (shards - 1) == 0 and width == padded
    comm = Native(ranks)

    def slab(array, start, size, axis):
        return lax.dynamic_slice_in_dim(array, start, size, axis)

    def widen(array):
        return jnp.pad(array, ((0, 0), (0, padded - width))) if padded > width else array

    if plain:
        (
            inputs, grad_low, w_in, w_out, w_gate_up, normed, project, gated_all, attended,
            wide_query, wide_key, wide_value, mixed_low, down_near, normed_two, turned, gain_rows, *places_all,
            bias, head_gains,
        ) = front(
            0, ranks, shards, head_dim, local_heads, width, hidden_piece,
            tokens[0], out_grad[0], attn_in_weight, out_weight, gate_up_weight, down_weight, forget_weight.T,
            norm_gains, qk_gains, segment_ids, block_order, forget_bias[None],
        )
        w_down, hidden_act, grad_gate_up, early_grad, down_part_grad = ffn(
            1, shards, normed_two, turned, w_gate_up, grad_low, down_near
        )
    else:
        tail = jnp.concatenate(
            [
                slab(forget_weight, rank * local_heads, local_heads, 1),
                norm_gains.T,
                jnp.zeros((attn_in_weight.shape[0], LANES - local_heads - 2), BF16),
            ],
            axis=1,
        )
        offsets = jnp.arange(block_len, dtype=jnp.int32)
        blocks = jnp.arange(seq_order.shape[0], dtype=jnp.int32)
        places = (seq_order[:, None] * block_len + offsets[None]).reshape(-1)
        by_block = segment_ids[0].reshape(-1, block_len)
        chosen = seq_order[:, None, None] == blocks[None, :, None]
        segments = jnp.sum(jnp.where(chosen, by_block[None], 0), axis=1).reshape(-1)
        places, segments = places.astype(F32), segments.astype(F32)
        places_all = (places[None, :], places[:, None], segments[None, :], segments[:, None])
        bias = jnp.pad(slab(forget_bias, rank * local_heads, local_heads, 0), (0, LANES - local_heads))[None]
        head_gains = jnp.tile(qk_gains, (1, LANES // head_dim))
        down_piece = slab(down_weight, rank * hidden_piece, hidden_piece, 0)
        inputs, grad_low, w_in, gate_up_piece = comm.begin(
            tokens[0], out_grad[0], attn_in_weight, tail, gate_up_weight, hidden_piece, width, padded
        )
        w_gate_up = lax.all_gather(gate_up_piece, "fsdp", axis=0, tiled=True)
        gain_cols = w_in[:, 4 * padded : 4 * padded + LANES].astype(F32).T
        gain_one = gain_cols[local_heads]
        gain_two = gain_cols[local_heads + 1]
        wide_inputs = inputs.astype(F32)
        scale_one = rms_scale(wide_inputs)
        normed = (wide_inputs * scale_one * gain_one).astype(BF16)
        project = dot(normed, w_in)
        gated, attended, wide_query, wide_key, wide_value = attend(
            project, places_all, bias, head_gains, head_dim, padded, local_heads
        )
        gated_all, w_out = comm.gather_cols(gated[:, :width], slab(out_weight, rank * width, width, 1))
        mixed_cols = slab(inputs, rank * width, width, 1).astype(F32) + dot(gated_all, w_out)
        mixed_low, w_down = comm.gather_cols(mixed_cols.astype(BF16), down_piece)
        mixed = mixed_low.astype(F32)
        scale_two = rms_scale(mixed)
        normed_two = (mixed * scale_two * gain_two).astype(BF16)
        gate_up = dot(normed_two, w_gate_up)
        gate_part, up_part = gate_up[:, :hidden], gate_up[:, hidden:]
        gate_sigmoid = jax.nn.sigmoid(gate_part)
        silu = gate_part * gate_sigmoid
        hidden_act = (silu * up_part).astype(BF16)
        grad_hidden = right_product(grad_low, w_down)
        grad_gate = grad_hidden * up_part * gate_sigmoid * (1.0 + gate_part * (1.0 - gate_sigmoid))
        grad_gate_up = jnp.concatenate([grad_gate, grad_hidden * silu], axis=1).astype(BF16)
        down_part_grad = left_product(hidden_act, grad_low).astype(BF16)
        gate_up_grad = left_product(normed_two, grad_gate_up).astype(BF16)
        down_part = dot(hidden_act, w_down).astype(BF16)

    def own_rows(array):
        return slab(array, rank * row_count, row_count, 0)

    def reduce_shards(array):
        return lax.psum_scatter(array.astype(BF16), "fsdp", scatter_dimension=0, tiled=True)

    if plain:
        early_share = (reduce_shards(early_grad),)
    else:
        early_share = (reduce_shards(down_part_grad), reduce_shards(gate_up_grad))
    if plain:
        grad_mixed_cols, grad_gated, gain_two_grad, down_part, out_part = middle(
            3, ranks, grad_gate_up, w_gate_up, mixed_low, grad_low, w_out, hidden_act, w_down, gated_all,
            gain_rows,
        )
    else:
        grad_normed_two = right_product(grad_gate_up, w_gate_up)
        gain_two_grad = jnp.sum(grad_normed_two * mixed * scale_two, axis=0)
        grad_mixed_part = norm_back(grad_normed_two, mixed, scale_two, gain_two).astype(BF16)
        grad_mixed_cols = slab(grad_low, rank * width, width, 1).astype(F32) + lax.psum_scatter(
            grad_mixed_part, "ctx", scatter_dimension=1, tiled=True
        ).astype(F32)
        grad_branch = grad_mixed_cols.astype(BF16)
        grad_gated = widen(
            lax.psum_scatter(
                right_product(grad_branch, w_out).astype(BF16), "ctx", scatter_dimension=1, tiled=True
            ).astype(F32)
        )
    grad_project, small, *rest = attend_back(
        project, places_all, bias, head_gains, attended, (wide_query, wide_key, wide_value),
        grad_gated, (down_part, normed, out_part, down_part_grad) if plain else (), ranks if plain else 0, shards, head_dim, padded, local_heads,
    )
    if plain:
        down_pieces, late, down_share, forget_grad = rest
    else:
        in_part = left_product(normed, grad_project).astype(BF16)
        out_part = left_product(gated_all, grad_branch).astype(BF16)
        late = jnp.concatenate([in_part[:, : 4 * padded], out_part, in_part[:, 4 * padded :]], axis=1)
    late, early_share = lax.optimization_barrier((late, early_share))
    late_share = reduce_shards(late)

    if plain:
        tokens_grad, block_out, sums, parts, early_own, down_own = last_moves(
            4, ranks, shards, grad_project, w_in, inputs, early_share[0], down_pieces, mixed_low, down_share,
            grad_mixed_cols,             gain_rows, gain_two_grad, small, places_all[3], forget_grad,
        )
        late_own, piece_sum, forget_all = finish_moves(6, ranks, shards, late_share, parts)
        gate_up_out, down_out = spread_early(early_own, down_own, hidden_piece)
    else:
        grad_normed = right_product(grad_project, w_in)
        gain_one_grad = jnp.sum(grad_normed * wide_inputs * scale_one, axis=0)
        in_own = jnp.arange(model_width, dtype=jnp.int32) // width == rank
        grad_inputs = norm_back(grad_normed, wide_inputs, scale_one, gain_one) + jnp.where(
            in_own[None], jnp.tile(grad_mixed_cols, (1, ranks)), 0.0
        )
        down_sum = lax.psum_scatter(down_part, "ctx", scatter_dimension=0, tiled=True).astype(F32)
        tokens_grad = lax.psum_scatter(grad_inputs.astype(BF16), "ctx", scatter_dimension=0, tiled=True)[None]
        own_bias = jnp.where(jnp.arange(ranks, dtype=jnp.int32)[:, None] == rank, small[2:3], 0.0)
        small_rows = jnp.concatenate([small[0:2].reshape(1, -1), jnp.pad(own_bias, ((0, 0), (0, LANES)))], axis=0)
        sums = jnp.concatenate(
            [
                jnp.stack([gain_one_grad, gain_two_grad]),
                jnp.pad(small_rows, ((0, 0), (0, model_width - 2 * LANES))),
            ],
            axis=0,
        )
        sums = lax.psum(sums, "ctx")
        down_own, gate_up_own = [lax.all_gather(a, "ctx", axis=0, tiled=False) for a in early_share]
        down_out = down_own.astype(F32).reshape(down_weight.shape)
        gate_up_out = spread_cols(gate_up_own, (hidden_piece, 0, 2 * shards))[0]
        result = own_rows(mixed_low).astype(F32) + down_sum
        block_out = result.astype(BF16)[None]
        branch = result - own_rows(inputs).astype(F32)
        own_valid = own_rows(places_all[3][:, 0] >= 0).astype(F32)
        totals = lax.psum(
            jnp.stack(
                [
                    jnp.sum(own_valid * jnp.sum(result * result, axis=-1)),
                    jnp.sum(own_valid * jnp.sum(branch * branch, axis=-1)),
                ]
            ),
            "ctx",
        )
        share = model_width // shards
        room = 2 * LANES
        gain_pieces = sums[0:2].reshape(2, shards, share).transpose(1, 0, 2)
        gain_pieces = jnp.pad(gain_pieces, ((0, 0), (0, 0), (0, room - share)))
        others = jnp.broadcast_to(sums[None, 2 : 3 + ranks, :room], (shards, 1 + ranks, room))
        piece_sum = lax.psum_scatter(
            jnp.concatenate([gain_pieces, others], axis=1), "fsdp", scatter_dimension=0, tiled=False
        )
        late_own = lax.all_gather(late_share, "ctx", axis=0, tiled=False)
    if plain:
        in_out, out_out, tokens_grad, block_out, forget_out, gains_sum, bias_sum, qk_sum, rms = unpack(
            late_own, forget_all, piece_sum, sums, segment_ids, tokens_grad, block_out, width, local_heads, head_dim
        )
        tokens_grad, block_out = tokens_grad[None], block_out[None]
        bias_sum, forget_out = bias_sum[0], forget_out.T
    else:
        share = model_width // shards
        valid_count = jnp.sum((segment_ids[0] >= 0).astype(F32)) * model_width
        in_out = jnp.concatenate(
            [late_own[c, :, i * padded : i * padded + width] for i in range(4) for c in range(ranks)], axis=1
        ).astype(F32)
        out_out = jnp.concatenate(
            [late_own[c, :, 4 * padded : 4 * padded + width] for c in range(ranks)], axis=1
        ).astype(F32)
        last = 4 * padded + width
        forget_out = jnp.concatenate(
            [late_own[c, :, last : last + local_heads] for c in range(ranks)], axis=1
        ).astype(F32)
        gains_sum = piece_sum[0:2, :share]
        bias_sum = piece_sum[3 : 3 + ranks, :local_heads].reshape(-1)
        qk_sum = piece_sum[2, : 2 * LANES].reshape(2, LANES // head_dim, head_dim).sum(axis=1)
        rms = jnp.sqrt(totals / valid_count)[None]
    return (
        block_out, tokens_grad, gains_sum, in_out, forget_out, bias_sum, qk_sum,
        out_out, gate_up_out, down_out, rms,
    )


def solution(mesh):
    rows = P("fsdp", "ctx", None)
    return jax.shard_map(
        body,
        mesh=mesh,
        in_specs=(
            rows, P("fsdp", None), P("fsdp", None), P(None, "fsdp"), P("fsdp", None), P("fsdp", None),
            P(), P(), P("fsdp", None), P("fsdp", None), P("fsdp", None), rows,
        ),
        out_specs=(
            rows, rows, P(None, "fsdp"), P("fsdp", None), P("fsdp", None), P(), P(),
            P("fsdp", None), P("fsdp", None), P("fsdp", None), P("fsdp", None),
        ),
        check_vma=False,
    )
```

```python
import functools

import jax
import jax.numpy as jnp
from jax import lax
from jax.experimental import pallas as pl
from jax.experimental.pallas import tpu as pltpu
from jax.sharding import PartitionSpec as P

EPS = 1e-06
SCALE = 0.125
LANES = 128
VMEM_LIMIT = 60 << 20
F32 = jnp.float32
BF16 = jnp.bfloat16


MESH = pl.DeviceIdType.MESH
ANY = pl.BlockSpec(memory_space=pltpu.HBM)


def rms_scale(values):
    return lax.rsqrt(jnp.mean(values * values, axis=-1, keepdims=True) + EPS)


def norm_back(grad_normed, values, scale_values, gain_values):
    scaled = grad_normed * gain_values
    cubed = scale_values * scale_values * scale_values
    return scale_values * scaled - values * cubed * jnp.mean(
        scaled * values, axis=-1, keepdims=True
    )


def dot(left, right):
    return lax.dot_general(
        left, right, (((1,), (0,)), ((), ())), preferred_element_type=F32
    )


def left_product(left, right):
    return lax.dot_general(
        left, right, (((0,), (0,)), ((), ())), preferred_element_type=F32
    )


def right_product(left, right):
    return lax.dot_general(
        left, right, (((1,), (1,)), ((), ())), preferred_element_type=F32
    )


def split_three(values):
    high = values.astype(BF16).astype(F32)
    rest = values - high
    middle = rest.astype(BF16).astype(F32)
    return high, middle, rest - middle


def lane_ids(rows, lanes=LANES):
    return lax.broadcasted_iota(jnp.int32, (rows, lanes), 1)


def pick_lane(values, lanes, index):
    return jnp.sum(jnp.where(lanes == index, values, 0.0), axis=-1, keepdims=True)


def turns(rows, chunk, unroll=False):
    def decorate(body):
        @pl.loop(0, rows // chunk, unroll=rows // chunk if unroll else None)
        def _(turn):
            body(pl.ds(pl.multiple_of(turn * chunk, chunk), chunk))

    return decorate


def fill_mask(chunk, pos_row, pos_col, seg_row, seg_col, mask):
    @turns(mask.shape[0], chunk)
    def _(part):
        allowed = (pos_row[0:1, :] <= pos_col[part, :]) & (seg_row[0:1, :] == seg_col[part, :])
        mask[part, :] = jnp.where(allowed, 0.0, -jnp.inf)


def fill_prefix(chunk, heads, pos_row, pos_col, logits, prefix):
    rows = prefix.shape[0]
    log_forget = jax.nn.log_sigmoid(jnp.where(lane_ids(rows) < heads, logits, 0.0))
    high, middle, low = split_three(log_forget)

    @turns(rows, chunk)
    def _(part):
        before = jnp.where(pos_row[0:1, :] <= pos_col[part, :], 1.0, 0.0).astype(BF16)
        prefix[part, :] = (
            dot(before, high.astype(BF16)) + dot(before, middle.astype(BF16)) + dot(before, low.astype(BF16))
        )


def attend_block(
    head, chunk, index, query, key, value, gate, gains, mask, prefix,
    gated, attended, wide_query, wide_key, wide_value,
):
    rows = mask.shape[0]
    lanes = lane_ids(rows)
    half = lane_ids(rows, head)
    short = lane_ids(chunk, head)
    for side in range(LANES // head):
        here = slice(side * head, (side + 1) * head)
        column = pick_lane(prefix[...], lanes, (LANES // head) * index + side)
        high, middle, low = split_three(column)
        wide = jnp.where(half == 1, high, 0.0)
        wide = jnp.where(half == 2, middle, wide)
        wide = jnp.where(half == 3, low, wide)
        query_rest = jnp.where((half >= 4) & (half < 7), 1.0, wide)
        wide = jnp.where(half == 4, -high, 0.0)
        wide = jnp.where(half == 5, -middle, wide)
        wide = jnp.where(half == 6, -low, wide)
        ones = ((half >= 1) & (half < 4)) | ((half >= 7) & (half < 10))
        key_rest = jnp.where(ones, 1.0, wide)
        raw = query[:, here]
        normed = (raw * rms_scale(raw) * gains[0:1, here]).astype(BF16)
        wide_query[side, :, 0:head] = (normed.astype(F32) * SCALE).astype(BF16)
        wide_query[side, :, head:LANES] = query_rest.astype(BF16)
        raw = key[:, here]
        wide_key[side, :, 0:head] = (raw * rms_scale(raw) * gains[1:2, here]).astype(BF16)
        wide_key[side, :, head:LANES] = key_rest.astype(BF16)
        wide_value[side, :, 0:head] = value[:, here].astype(BF16)
        wide_value[side, :, head:LANES] = jnp.where(half < 3, 1.0, 0.0).astype(BF16)

        @turns(rows, chunk, unroll=True)
        def _(part):
            scores = right_product(wide_query[side, part, :], wide_key[side]) + mask[part, :]
            expos = jnp.exp(scores)
            total = jnp.sum(expos, axis=-1, keepdims=True)
            result = dot(expos.astype(BF16), wide_value[side])[:, 0:head] / total
            attended[part, here] = result
            gated[part, here] = (result * jax.nn.sigmoid(gate(part)[:, here])).astype(BF16)
            high, middle, low = split_three(-jnp.log(total))
            rest = wide_query[side, part, head:LANES].astype(F32)
            rest = jnp.where(short == 7, high, rest)
            rest = jnp.where(short == 8, middle, rest)
            rest = jnp.where(short == 9, low, rest)
            wide_query[side, part, head:LANES] = rest.astype(BF16)


def attend_kernel(
    head, chunk, heads,
    pos_row, pos_col, seg_row, seg_col, bias, gains, query, key, value, gate, forget,
    gated, attended, wide_query, wide_key, wide_value,
    mask, prefix,
):
    @pl.when(pl.program_id(0) == 0)
    def _():
        fill_mask(chunk, pos_row, pos_col, seg_row, seg_col, mask)
        fill_prefix(chunk, heads, pos_row, pos_col, forget[...] + bias[0:1, :], prefix)

    attend_block(
        head, chunk, pl.program_id(0), query, key, value, lambda part: gate[part, :], gains, mask, prefix,
        gated, attended.at[0], wide_query, wide_key, wide_value,
    )


def attend_back_kernel(
    head, chunk, width, heads, ranks, shards,
    pos_row, pos_col, seg_row, seg_col, bias, gains, query, key, gate, forget,
    attended, wide_query, wide_key, wide_value, grad_gated, *rest,
):
    if ranks:
        aside, normed, out_grad, blocks, grad_project, small, aside_in, late, share = rest[:9]
        mask, wide_grad, grad_query, grad_key, grad_value, grad_prefix = rest[9:15]
        normed_in, out_in, aside_own, blocks_in, side_in, kept, from_below, from_above = rest[15:23]
        late_all, load_sem, save_sem = rest[23:26]
        sems = rest[26:28]
        over_shards = ShardSum(shards, blocks_in, side_in, kept, from_below, from_above, rest[28:])

        def loads():
            own = rows_of(aside, lax.axis_index("ctx"), aside_in.shape[1])
            for n, pair in enumerate(((normed, normed_in), (out_grad, out_in), (own, aside_own))):
                yield pltpu.make_async_copy(*pair, load_sem.at[n])

    else:
        grad_project, small, mask, wide_grad, grad_query, grad_key, grad_value, grad_prefix = rest
    step = pl.program_id(0)
    steps = pl.num_programs(0)

    def aside_copies():
        send_sem, recv_sem = sems
        rank = lax.axis_index("ctx")
        size = aside_in.shape[1]
        for distance in range(1, ranks):
            other = rank ^ distance
            yield to_rank(
                rows_of(aside, other, size), aside_in.at[rank],
                send_sem.at[distance - 1], recv_sem.at[distance - 1], other,
            )

    def sum_stage(hook):
        if not ranks:
            return
        now = (LANES // head) * step + hook

        @pl.when(now == 1)
        def _():
            pltpu.make_async_copy(blocks, blocks_in, load_sem.at[4]).wait()
            over_shards.start()

        for stage in range(over_shards.layers - 1):

            @pl.when(now == 2 + 2 * stage)
            def _():
                if stage == 0:
                    over_shards.presum()
                else:
                    over_shards.receive(stage - 1)
                over_shards.send(stage)

    if ranks:

        @pl.when(step == 0)
        def _():
            rank = lax.axis_index("ctx")
            greet([{"ctx": rank ^ distance} for distance in range(1, ranks)], over_shards)
            early = pltpu.make_async_copy(blocks, blocks_in, load_sem.at[4])
            early.start()
            for copy in aside_copies():
                copy.start()
            for copy in loads():
                copy.start()

    rows = query.shape[0]
    lanes = lane_ids(rows)
    half = lane_ids(rows, head)

    @pl.when(step == 0)
    def _():
        @pl.loop(0, rows // chunk)
        def _(turn):
            part = pl.ds(pl.multiple_of(turn * chunk, chunk), chunk)
            after = pos_row[0:1, :] >= pos_col[part, :]
            same = seg_row[0:1, :] == seg_col[part, :]
            mask[part, :] = jnp.where(after & same, 0.0, -jnp.inf)
        grad_prefix[...] = jnp.zeros_like(grad_prefix)
        small[...] = jnp.zeros_like(small)

    for side in range(LANES // head):
        sum_stage(side)
        here = pl.ds(side * head, head)

        def column(part):
            return pl.ds(pl.multiple_of(part * width + step * LANES, LANES), LANES)

        sig = jax.nn.sigmoid(gate[:, here])
        grad_in = grad_gated[:, here]
        result = attended[0, :, here]
        grad_result = (grad_in * sig).astype(BF16)
        grad_gate = (grad_in * result * sig * (1.0 - sig)).astype(BF16)
        inner = -jnp.sum(grad_result.astype(F32) * result, axis=-1, keepdims=True)
        high, middle, low = split_three(inner)
        rest = jnp.where(half == 0, high, 0.0)
        rest = jnp.where(half == 1, middle, rest)
        rest = jnp.where(half == 2, low, rest)
        wide_grad[:, 0:head] = grad_result
        wide_grad[:, head:LANES] = rest.astype(BF16)
        grad_query[...] = jnp.zeros_like(grad_query)
        @turns(rows, chunk, unroll=True)
        def _(part):
            scores = right_product(wide_key[side, part, :], wide_query[side]) + mask[part, :]
            probs = jnp.exp(scores)
            outer = right_product(wide_value[side, part, :], wide_grad[...])
            grad_scores = (probs * outer).astype(BF16)
            grad_key[part, :] = dot(grad_scores, wide_query[side])
            grad_value[part, :] = dot(probs.astype(BF16), wide_grad[...])
            grad_query[...] += left_product(wide_key[side, part, :], grad_scores)
        from_query = grad_query[...].T
        from_key = grad_key[...]
        change = pick_lane(from_query, lanes, head + 1) - pick_lane(from_key, lanes, head + 4)
        grad_prefix[...] += jnp.where(lanes == (LANES // head) * step + side, change, 0.0)

        raw = query[:, here]
        scale_raw = rms_scale(raw)
        grad_normed = from_query[:, 0:head] * SCALE
        grad_raw_query = norm_back(grad_normed, raw, scale_raw, gains[0:1, here])
        small[0:1, here] += jnp.sum(grad_normed * raw * scale_raw, axis=0, keepdims=True)
        raw = key[:, here]
        scale_raw = rms_scale(raw)
        grad_normed = from_key[:, 0:head]
        grad_raw_key = norm_back(grad_normed, raw, scale_raw, gains[1:2, here])
        small[1:2, here] += jnp.sum(grad_normed * raw * scale_raw, axis=0, keepdims=True)
        wide_grad[:, here] = grad_gate
        for part_id, piece in enumerate(
            (grad_raw_query.astype(BF16), grad_raw_key.astype(BF16), grad_value[:, 0:head].astype(BF16), grad_gate)
        ):
            if side == 0:
                grad_project[:, column(part_id)] = jnp.concatenate([piece, piece], axis=1)
            else:
                keep = grad_project[:, column(part_id)]
                both = jnp.concatenate([piece, piece], axis=1)
                grad_project[:, column(part_id)] = jnp.where(lanes < head, keep, both)

    @pl.when(step == steps - 1)
    def _():
        high, middle, low = split_three(grad_prefix[...])
        short = lane_ids(chunk)

        @pl.loop(0, rows // chunk)
        def _(turn):
            part = pl.ds(pl.multiple_of(turn * chunk, chunk), chunk)
            after = jnp.where(pos_row[0:1, :] >= pos_col[part, :], 1.0, 0.0).astype(BF16)
            total = dot(after, high.astype(BF16)) + dot(after, middle.astype(BF16)) + dot(after, low.astype(BF16))
            grad_logit = total * jax.nn.sigmoid(-(forget[part, :] + bias[0:1, :]))
            grad_logit = jnp.where(short < heads, grad_logit, 0.0).astype(BF16)
            grad_project[part, 4 * width : 4 * width + LANES] = grad_logit
            small[2:3, :] += jnp.sum(grad_logit.astype(F32), axis=0, keepdims=True)

        if ranks:
            for copy in loads():
                copy.wait()
            keep = pltpu.make_async_copy(aside_own, aside_in.at[lax.axis_index("ctx")], load_sem.at[3])
            keep.start()
            late_stages = [n for n in range(over_shards.layers - 1) if 2 + 2 * n >= heads]
            for stage in late_stages:
                over_shards.receive(stage - 1)
                over_shards.send(stage)
            ends = 4 * width, 4 * width + out_grad.shape[1]
            late_all[:, ends[0] : ends[1]] = out_in[...]
            piece = 2 * LANES

            def save(turn, size=piece):
                cols = pl.ds(pl.multiple_of(turn * piece, LANES), size)
                return pltpu.make_async_copy(late_all.at[:, cols], late.at[:, cols], save_sem.at[turn])

            count = 4 * width // piece
            rest_save = pltpu.make_async_copy(
                late_all.at[:, pl.ds(ends[0], late.shape[1] - ends[0])],
                late.at[:, pl.ds(ends[0], late.shape[1] - ends[0])],
                save_sem.at[count],
            )

            def product(into, cols):
                @turns(late.shape[0], 3 * chunk if late.shape[0] % (3 * chunk) == 0 else chunk)
                def _(part):
                    late_all[part, into] = dot(normed_in[part, :], grad_project[:, cols]).astype(BF16)

            rest_save.start()

            @pl.loop(0, count)
            def _(turn):
                cols = pl.ds(pl.multiple_of(turn * piece, LANES), piece)
                product(cols, cols)
                save(turn).start()

            for copy in aside_copies():
                copy.wait()
            keep.wait()
            over_shards.receive(over_shards.layers - 2)
            share[...] = kept[over_shards.layer]
            over_shards.sent()
            rest_save.wait()

            @pl.loop(0, count)
            def _(turn):
                save(turn).wait()


def pick_chunk(rows):
    return 256 if rows % 256 == 0 else 128


def whole(shape):
    return pl.BlockSpec(shape, lambda step: tuple(0 for _ in shape))


def attend(project, places, bias, gains, head, width, heads):
    rows = project.shape[0]
    steps = width // LANES
    per = LANES // head
    chunk = pick_chunk(rows)

    def part(index):
        return pl.BlockSpec((rows, LANES), lambda step: (0, index * steps + step))

    own = pl.BlockSpec((rows, LANES), lambda step: (0, step))
    wide = pl.BlockSpec((per, rows, LANES), lambda step: (step, 0, 0))
    forget = pl.BlockSpec((rows, LANES), lambda step: (0, 4 * steps))
    wide_shape = jax.ShapeDtypeStruct((per * steps, rows, LANES), BF16)
    return pl.pallas_call(
        functools.partial(attend_kernel, head, chunk, heads),
        grid=(steps,),
        in_specs=[whole(p.shape) for p in places] + [whole(bias.shape), whole(gains.shape)]
        + [part(0), part(1), part(2), part(3), forget],
        out_specs=[own, pl.BlockSpec((1, rows, LANES), lambda step: (step, 0, 0)), wide, wide, wide],
        out_shape=[
            jax.ShapeDtypeStruct((rows, width), BF16),
            jax.ShapeDtypeStruct((steps, rows, LANES), F32),
            wide_shape, wide_shape, wide_shape,
        ],
        scratch_shapes=[pltpu.VMEM((rows, rows), F32), pltpu.VMEM((rows, LANES), F32)],
        compiler_params=pltpu.CompilerParams(vmem_limit_bytes=VMEM_LIMIT),
        name="attend",
    )(*places, bias, gains, project, project, project, project, project)


def attend_back(project, places, bias, gains, attended, wides, grad_gated, beside, ranks, shards, head, width, heads):
    rows = project.shape[0]
    steps = width // LANES
    per = LANES // head
    chunk = pick_chunk(rows)

    def part(index):
        return pl.BlockSpec((rows, LANES), lambda step: (0, index * steps + step))

    own = pl.BlockSpec((rows, LANES), lambda step: (0, step))
    block = pl.BlockSpec((1, rows, LANES), lambda step: (step, 0, 0))
    wide = pl.BlockSpec((per, rows, LANES), lambda step: (step, 0, 0))
    forget = pl.BlockSpec((rows, LANES), lambda step: (0, 4 * steps))
    total = 4 * width + LANES
    out_specs = [whole((rows, total)), whole((8, LANES))]
    out_shape = [jax.ShapeDtypeStruct((rows, total), BF16), jax.ShapeDtypeStruct((8, LANES), F32)]
    scratch = [
        pltpu.VMEM((rows, rows), F32),
        pltpu.VMEM((rows, LANES), BF16),
        pltpu.VMEM((LANES, rows), F32),
        pltpu.VMEM((rows, LANES), F32),
        pltpu.VMEM((rows, LANES), F32),
        pltpu.VMEM((rows, LANES), F32),
    ]
    if ranks:
        aside, normed, out_grad, blocks = beside
        share = (blocks.shape[0] // shards, blocks.shape[1])
        sum_blocks, sum_sems = shard_sum_scratch(shards, *share)
        model, late_cols = normed.shape[0], 4 * width + out_grad.shape[1]
        out_specs += [ANY, ANY, whole(share)]
        out_shape += [
            jax.ShapeDtypeStruct((ranks, aside.shape[0] // ranks, aside.shape[1]), BF16),
            jax.ShapeDtypeStruct((model, late_cols), BF16),
            jax.ShapeDtypeStruct(share, BF16),
        ]
        scratch += [
            pltpu.VMEM(normed.shape, BF16),
            pltpu.VMEM(out_grad.shape, BF16),
            pltpu.VMEM((aside.shape[0] // ranks, aside.shape[1]), BF16),
            pltpu.VMEM(blocks.shape, BF16),
            *sum_blocks,
            pltpu.VMEM((model, late_cols), BF16),
            pltpu.SemaphoreType.DMA((5,)),
            pltpu.SemaphoreType.DMA((4 * width // (2 * LANES) + 1,)),
            pltpu.SemaphoreType.DMA((ranks - 1,)),
            pltpu.SemaphoreType.DMA((ranks - 1,)),
            *sum_sems,
        ]
    return pl.pallas_call(
        functools.partial(attend_back_kernel, head, chunk, width, heads, ranks, shards),
        grid=(steps,),
        in_specs=[whole(p.shape) for p in places] + [whole(bias.shape), whole(gains.shape)]
        + [part(0), part(1), part(3), forget, block, wide, wide, wide, own] + [ANY] * len(beside),
        out_specs=out_specs,
        out_shape=out_shape,
        scratch_shapes=scratch,
        compiler_params=pltpu.CompilerParams(
            collective_id=5 if ranks else None, has_side_effects=ranks > 0, vmem_limit_bytes=VMEM_LIMIT
        ),
        name="attend_back",
    )(*places, bias, gains, project, project, project, project, attended, *wides, grad_gated, *beside)


def greet(peers, line=None):
    barrier = pltpu.get_barrier_semaphore()
    if line is not None:
        peers = peers + [line.sibling]
    for peer in peers:
        pl.semaphore_signal(barrier, inc=1, device_id=peer, device_id_type=MESH)
    if line is not None:
        for there, peer in ((line.has_above, line.above), (line.has_below, line.below)):

            @pl.when(there)
            def _():
                pl.semaphore_signal(barrier, inc=1, device_id=peer, device_id_type=MESH)

    count = len(peers)
    if line is not None:
        last = line.layers - 1
        count = count + (1 - line.layer // last) + (line.layer + last) // line.layers
    pl.semaphore_wait(barrier, count)


class Line:
    def __init__(self, shards, source, target, sems):
        self.shard = lax.axis_index("fsdp")
        self.layers = shards // 2
        self.layer, self.core = self.shard // 2, self.shard % 2
        self.sibling = {"fsdp": self.shard ^ 1}
        self.above, self.below = {"fsdp": self.shard + 2}, {"fsdp": self.shard - 2}
        self.has_above, self.has_below = self.layer < self.layers - 1, self.layer > 0
        self.source, self.target = source, target
        self.rows = target.shape[0] // shards
        self.line_send, self.line_recv, self.side_send, self.side_recv, self.own_sem = sems

    def block(self, owner):
        return rows_of(self.target, owner, self.rows)

    def line(self, owner_layer, peer, way, own=False):
        here = self.block(owner_layer * 2 + self.core)
        return pltpu.make_async_remote_copy(
            self.source if own else here, here, self.line_send.at[way, owner_layer], self.line_recv.at[owner_layer],
            device_id=peer, device_id_type=MESH,
        )

    def side(self, owner_layer, owner_core, own=False):
        here = self.block(owner_layer * 2 + owner_core)
        return pltpu.make_async_remote_copy(
            self.source if own else here, here, self.side_send.at[owner_layer], self.side_recv.at[owner_layer],
            device_id=self.sibling, device_id_type=MESH,
        )

    def start(self):
        own = self.source is not None

        @pl.when(self.has_above)
        def _():
            self.line(self.layer, self.above, 0, own).start()

        @pl.when(self.has_below)
        def _():
            self.line(self.layer, self.below, 1, own).start()

        self.side(self.layer, self.core, own).start()
        if own:
            self.keep = pltpu.make_async_copy(self.source, self.block(self.shard), self.own_sem)
            self.keep.start()

    def step(self, distance):
        lower, upper = self.layer - distance, self.layer + distance

        @pl.when(lower >= 0)
        def _():
            self.line(lower, self.below, 1).wait_recv()

            @pl.when(self.has_above)
            def _():
                self.line(lower, self.above, 0).start()

            self.side(lower, self.core).start()

        @pl.when(upper < self.layers)
        def _():
            self.line(upper, self.above, 0).wait_recv()

            @pl.when(self.has_below)
            def _():
                self.line(upper, self.below, 1).start()

            self.side(upper, self.core).start()

    def from_side(self, owner_layer):
        self.side(owner_layer, 1 - self.core).wait_recv()

    def finish(self):
        self.keep.wait()
        for owner_layer in range(self.layers):
            self.from_side(owner_layer)
        self.sent()

    def sent(self):
        for owner_layer in range(self.layers):
            self.side(owner_layer, self.core).wait_send()

            @pl.when(self.has_above & (owner_layer <= self.layer))
            def _():
                self.line(owner_layer, self.above, 0).wait_send()

            @pl.when(self.has_below & (owner_layer >= self.layer))
            def _():
                self.line(owner_layer, self.below, 1).wait_send()

    def near_finish(self):
        self.keep.wait()
        self.from_side(self.layer)
        self.side(self.layer, self.core).wait_send()

        @pl.when(self.has_below)
        def _():
            self.line(self.layer - 1, self.below, 1).wait_recv()
            self.line(self.layer, self.below, 1).wait_send()

        @pl.when(self.has_above)
        def _():
            self.line(self.layer + 1, self.above, 0).wait_recv()
            self.line(self.layer, self.above, 0).wait_send()

    def near_load(self, near, sems, number):
        if number == 0:
            chip = 2 * self.rows
            source, target = rows_of(near, self.layer, chip), rows_of(self.target, self.layer, chip)
        else:
            owner = self.shard + (-2, 2)[number - 1]
            source, target = rows_of(near, owner, self.rows), self.block(owner)
        return pltpu.make_async_copy(source, target, sems.at[number])

    def near_start(self, near, sems):
        self.near_load(near, sems, 0).start()

        @pl.when(self.has_below)
        def _():
            self.near_load(near, sems, 1).start()

        @pl.when(self.has_above)
        def _():
            self.near_load(near, sems, 2).start()

    def resume(self, near, sems):
        @pl.when(self.has_below)
        def _():
            self.near_load(near, sems, 1).wait()

            @pl.when(self.has_above)
            def _():
                self.line(self.layer - 1, self.above, 0).start()

            self.side(self.layer - 1, self.core).start()

        @pl.when(self.has_above)
        def _():
            self.near_load(near, sems, 2).wait()

            @pl.when(self.has_below)
            def _():
                self.line(self.layer + 1, self.below, 1).start()

            self.side(self.layer + 1, self.core).start()

    def resumed_sent(self):
        for owner_layer in range(self.layers):

            @pl.when(owner_layer != self.layer)
            def _():
                self.side(owner_layer, self.core).wait_send()

            @pl.when(self.has_above & (owner_layer < self.layer))
            def _():
                self.line(owner_layer, self.above, 0).wait_send()

            @pl.when(self.has_below & (owner_layer > self.layer))
            def _():
                self.line(owner_layer, self.below, 1).wait_send()


def line_scratch(shards):
    layers = shards // 2
    return [
        pltpu.SemaphoreType.DMA((2, layers)),
        pltpu.SemaphoreType.DMA((layers,)),
        pltpu.SemaphoreType.DMA((layers,)),
        pltpu.SemaphoreType.DMA((layers,)),
        pltpu.SemaphoreType.DMA,
    ]


class Relay:
    def __init__(self, rank, source, place, send_sem, recv_sem, own_sem):
        self.rank, self.source, self.place = rank, source, place
        self.send_sem, self.recv_sem, self.own_sem = send_sem, recv_sem, own_sem

    def copy(self, number):
        me = self.rank
        source, place, distance = (
            lambda: (self.source(0), self.place(me, 0), 1),
            lambda: (self.source(1), self.place(me, 1), 2),
            lambda: (self.source(1), self.place(me, 1), 1),
            lambda: (self.source(0), self.place(me, 0), 2),
            lambda: (self.place(me ^ 1, 0), self.place(me ^ 1, 0), 2),
            lambda: (self.place(me ^ 2, 1), self.place(me ^ 2, 1), 1),
        )[number]()
        return pltpu.make_async_remote_copy(
            source, place, self.send_sem.at[number], self.recv_sem.at[number],
            device_id={"ctx": me ^ distance}, device_id_type=MESH,
        )

    def own(self, h):
        return pltpu.make_async_copy(self.source(h), self.place(self.rank, h), self.own_sem.at[h])

    def start(self, keep=True):
        for number in range(4):
            self.copy(number).start()
        if keep:
            for h in range(2):
                self.own(h).start()

    def forward(self):
        for number in range(2):
            self.copy(number).wait_recv()
            self.copy(number + 4).start()

    def arrive(self):
        for number in range(2, 6):
            self.copy(number).wait_recv()

    def finish(self, arrive=True, keep=True):
        if keep:
            for h in range(2):
                self.own(h).wait()
        if arrive:
            self.arrive()
        for number in range(6):
            self.copy(number).wait_send()


def rows_of(ref, index, size):
    return ref.at[pl.ds(pl.multiple_of(index * size, 16), size), :]


def cols_of(ref, index, size):
    return ref.at[:, pl.ds(pl.multiple_of(index * size, LANES), size)]


def relay_ops(mode, rank, source, target, sems):
    rows, cols = source.shape
    half = rows // 2

    def part(h):
        return source.at[pl.ds(h * half, half), :]

    def place(block, h):
        if mode == "gather_rows":
            return target.at[pl.ds(pl.multiple_of(block * rows + h * half, 16), half), :]
        if mode == "gather_cols":
            return target.at[pl.ds(h * half, half), pl.ds(pl.multiple_of(block * cols, LANES), cols)]
        return target.at[block, pl.ds(h * half, half), :]

    return Relay(rank, part, place, *sems)


VMEM_WHOLE = pl.BlockSpec(memory_space=pltpu.VMEM)


def to_rank(source, target, send, recv, other):
    return pltpu.make_async_remote_copy(
        source, target, send, recv, device_id={"ctx": other}, device_id_type=MESH
    )


FRONT_LOADS = 6
FRONT_SAVES = 12


def front_kernel(
    shards, head, heads, width, piece, chunk,
    tokens, cotangent, weight, weight_out, other, down, forget_weight, norm_gains, qk_gains, segments, order, forget_bias,
    inputs, grad_low, w_in, w_out, w_gate_up, normed, project, gated, attended, wide_query, wide_key, wide_value,
    mixed, down_near, normed_two, turned, gain_rows, pos_row, pos_col, seg_row, seg_col, bias, gains,
    weight_all, other_all, out_all, own_x, own_g, own_in, own_pick, own_out, x_all, in_all, hn_all, proj_all, mask, prefix,
    gated_all, attended_all, query_all, key_all, value_all, out_cols, scale_one, y_own, own_down,
    mixed_all, h2_all, turned_all,
    send_sem, recv_sem, own_sem, load_sem, save_sem, *line_sems,
):
    rank = lax.axis_index("ctx")
    ranks = lax.axis_size("ctx")
    model = weight.shape[1] // 4
    rows = x_all.shape[0]
    steps = width // LANES
    tail_at = 4 * width
    loads = [
        pltpu.make_async_copy(a, b, load_sem.at[n])
        for n, (a, b) in enumerate(
            (
                (weight, weight_all), (other, other_all), (weight_out, out_all), (tokens, own_x), (cotangent, own_g),
                (rows_of(down, rank, own_down.shape[0]), own_down),
            )
        )
    ]
    saves = [
        pltpu.make_async_copy(a, b, save_sem.at[n])
        for n, (a, b) in enumerate(
            (
                (x_all, inputs), (in_all, w_in), (hn_all, normed), (proj_all, project), (query_all, wide_query),
                (key_all, wide_key), (value_all, wide_value), (attended_all, attended), (gated_all, gated),
                (mixed_all, mixed), (h2_all, normed_two), (turned_all, turned),
            )
        )
    ]
    for copy in loads:
        copy.start()
    per = len(line_sems) // 4
    in_line = Line(shards, own_in, in_all, line_sems[:per])
    out_line = Line(shards, own_out, out_cols, line_sems[per : 2 * per])
    up_line = Line(shards, own_pick, w_gate_up, line_sems[2 * per : 3 * per])
    down_line = Line(shards, own_down, down_near, line_sems[3 * per :])
    greet([{"ctx": rank ^ 1}, {"ctx": rank ^ 2}], in_line)

    def sems(n):
        return send_sem.at[n], recv_sem.at[n], own_sem.at[n]

    first = relay_ops("gather_rows", rank, own_x, x_all, sems(0))
    second = relay_ops("gather_rows", rank, own_g, grad_low, sems(1))

    def cols(start, size):
        return pl.ds(pl.multiple_of(start, LANES), size)

    loads[0].wait()
    for i in range(4):
        own_in[:, i * width : (i + 1) * width] = weight_all[:, cols(i * model + rank * width, width)]
    total_heads = forget_weight.shape[0]
    from_head = lax.broadcasted_iota(jnp.int32, (total_heads, LANES), 0)
    to_lane = lax.broadcasted_iota(jnp.int32, (total_heads, LANES), 1)
    chosen = jnp.where((to_lane < heads) & (from_head == rank * heads + to_lane), 1.0, 0.0).astype(BF16)
    from_gain = lax.broadcasted_iota(jnp.int32, (2, LANES), 0)
    to_lane = lax.broadcasted_iota(jnp.int32, (2, LANES), 1)
    chosen_gain = jnp.where(to_lane == heads + from_gain, 1.0, 0.0).astype(BF16)
    tail = left_product(forget_weight[...], chosen) + left_product(norm_gains[...], chosen_gain)
    own_in[:, tail_at : tail_at + LANES] = tail.astype(BF16)
    in_line.start()
    loads[3].wait()
    first.start()
    loads[1].wait()
    for i in range(own_pick.shape[1] // piece):
        own_pick[:, i * piece : (i + 1) * piece] = other_all[:, cols((i * ranks + rank) * piece, piece)]
    loads[2].wait()
    own_out[...] = out_all[:, cols(rank * width, width)]
    count = order.shape[1]
    length = rows // count
    row_ids = lax.broadcasted_iota(jnp.int32, (rows, LANES), 0)
    lane_id = lax.broadcasted_iota(jnp.int32, (8, rows), 1)
    tall = jnp.zeros((rows, LANES), jnp.int32)
    flat = jnp.zeros((8, rows), jnp.int32)
    for block in range(count):
        start = order[0, block] * length - block * length
        tall = jnp.where((row_ids >= block * length) & (row_ids < (block + 1) * length), row_ids + start, tall)
        flat = jnp.where((lane_id >= block * length) & (lane_id < (block + 1) * length), lane_id + start, flat)
    pos_col[...] = tall[:, 0:1].astype(F32)
    pos_row[...] = flat[0:1, :].astype(F32)
    true_segments = segments[0:1, :].astype(F32)

    @turns(rows, chunk)
    def _(part):
        true_place = lax.broadcasted_iota(jnp.int32, (chunk, rows), 1).astype(F32)
        own_place = true_place == pos_col[part, :]
        seg_col[part, :] = jnp.sum(jnp.where(own_place, true_segments, 0.0), axis=-1, keepdims=True)

    seg_row[...] = jnp.broadcast_to(seg_col[...], (rows, LANES)).T[0:1, :]
    lane = lax.broadcasted_iota(jnp.int32, (1, LANES), 1)
    bias_row = jnp.zeros((1, LANES), F32)
    for index in range(heads):
        bias_row = jnp.where(lane == index, forget_bias[0, rank * heads + index], bias_row)
    bias[...] = bias_row
    for side in range(LANES // head):
        gains[:, side * head : (side + 1) * head] = qk_gains[...]
    fill_mask(chunk, pos_row, pos_col, seg_row, seg_col, mask)
    proj_all[...] = jnp.zeros_like(proj_all)
    gain_rows[...] = jnp.zeros_like(gain_rows)
    first.forward()
    loads[4].wait()
    second.start()
    in_line.step(1)
    first.finish()
    saves[0].start()

    @turns(rows, chunk)
    def _(part):
        values = x_all[part, :].astype(F32)
        scale_one[part, :] = jnp.broadcast_to(rms_scale(values), (chunk, LANES))

    def consume(layer):
        in_line.from_side(layer)
        size = 2 * in_line.rows
        here = cols(layer * size, size)
        tail_block = in_all[here, tail_at : tail_at + LANES].astype(F32).T
        gain_rows[0:1, here] = tail_block[heads : heads + 1, :]
        gain_rows[1:2, here] = tail_block[heads + 1 : heads + 2, :]

        @turns(rows, chunk)
        def _(part):
            values = x_all[part, here].astype(F32) * scale_one[part, 0:1] * gain_rows[0:1, here]
            hn_all[here, part] = values.T.astype(BF16)
            proj_all[part, :] += dot(values.astype(BF16), in_all[here, :])

    def consume_at(distance):
        lower, upper = in_line.layer - distance, in_line.layer + distance

        @pl.when(lower >= 0)
        def _():
            consume(lower)

        @pl.when(upper < in_line.layers)
        def _():
            consume(upper)

    in_line.keep.wait()
    consume(in_line.layer)
    consume_at(1)
    second.forward()
    for distance in range(2, in_line.layers):
        in_line.step(distance)
        if distance == in_line.layers - 1:
            out_line.start()
            up_line.start()
        consume_at(distance)

    for n in (1, 2, 3):
        saves[n].start()
    out_line.step(1)
    fill_prefix(chunk, heads, pos_row, pos_col, proj_all[:, tail_at : tail_at + LANES] + bias[0:1, :], prefix)

    def share(index):
        block = rank * steps + index
        half = rows // 2

        def source(h):
            return gated_all.at[block, pl.ds(h * half, half), :]

        def place(owner, h):
            return gated_all.at[owner * steps + index, pl.ds(h * half, half), :]

        return Relay(rank, source, place, send_sem.at[2 + index], recv_sem.at[2 + index], None)

    per_block = LANES // head

    @pl.loop(0, steps)
    def _(index):
        def lanes_of(part_id):
            return proj_all[:, cols(part_id * width + index * LANES, LANES)]

        def gate(part):
            return proj_all[part, cols(3 * width + index * LANES, LANES)]

        group = pl.ds(index * per_block, per_block)
        attend_block(
            head, chunk, index, lanes_of(0), lanes_of(1), lanes_of(2), gate, gains, mask, prefix,
            gated_all.at[rank * steps + index], attended_all.at[index],
            query_all.at[group], key_all.at[group], value_all.at[group],
        )
        share(index).start(keep=False)

        @pl.when(index == 0)
        def _():
            out_line.step(2)

        @pl.when(index > 0)
        def _():
            share(index - 1).forward()

    up_line.step(1)
    out_line.step(3)
    share(steps - 1).forward()
    for n in (4, 5, 6, 7):
        saves[n].start()
    for index in range(steps):
        share(index).arrive()
    saves[8].start()
    out_line.keep.wait()
    for layer in range(out_line.layers):
        out_line.from_side(layer)
    save_out = pltpu.make_async_copy(out_cols, w_out, save_sem.at[len(saves)])
    save_out.start()

    third = relay_ops("gather_cols", rank, y_own, mixed_all, sems(2 + steps))

    @turns(rows, chunk)
    def _(part):
        total = x_all[part, cols(rank * width, width)].astype(F32)
        for block in range(gated_all.shape[0]):
            total = total + dot(gated_all[block, part, :], out_cols[block * LANES : (block + 1) * LANES, :])
        y_own[part, :] = total.astype(BF16)

    third.start()
    third.forward()
    up_line.step(2)
    loads[5].wait()
    down_line.start()
    third.finish()
    saves[9].start()

    @turns(rows, chunk)
    def _(part):
        values = mixed_all[part, :].astype(F32)
        low = values * rms_scale(values) * gain_rows[1:2, :]
        h2_all[part, :] = low.astype(BF16)
        turned_all[:, part] = low.T.astype(BF16)

    saves[10].start()
    saves[11].start()
    for distance in range(3, up_line.layers):
        up_line.step(distance)
    up_line.finish()
    down_line.near_finish()
    out_line.sent()
    in_line.sent()
    second.finish()
    for index in range(steps):
        share(index).finish(arrive=False, keep=False)
    for copy in saves:
        copy.wait()
    save_out.wait()


def front(
    collective_id, ranks, shards, head, heads, width, piece,
    tokens, cotangent, weight, weight_out, other, down, forget_weight, norm_gains, qk_gains, segments, order, forget_bias,
):
    own_rows, model = tokens.shape
    rows = ranks * own_rows
    chunk = pick_chunk(rows)
    steps, shard_rows = width // LANES, weight.shape[0]
    wide_in = 4 * width + LANES
    other_cols = other.shape[1] // ranks
    wide = (heads, rows, LANES)
    shape, vmem = jax.ShapeDtypeStruct, pltpu.VMEM
    return pl.pallas_call(
        functools.partial(front_kernel, shards, head, heads, width, piece, chunk),
        in_specs=[ANY] * 6 + [VMEM_WHOLE] * 4 + [pl.BlockSpec(memory_space=pltpu.SMEM)] * 2,
        out_specs=[ANY] * 16 + [VMEM_WHOLE] * 7,
        out_shape=[
            shape((rows, model), BF16),
            shape((rows, model), BF16),
            shape((model, wide_in), BF16),
            shape((model, width), BF16),
            shape((model, other_cols), BF16),
            shape((model, rows), BF16),
            shape((rows, wide_in), F32),
            shape((ranks * steps, rows, LANES), BF16),
            shape((steps, rows, LANES), F32),
            shape(wide, BF16), shape(wide, BF16), shape(wide, BF16),
            shape((rows, model), BF16),
            shape((shards * (down.shape[0] // ranks), model), BF16),
            shape((rows, model), BF16),
            shape((model, rows), BF16),
            shape((8, model), F32),
            shape((1, rows), F32), shape((rows, 1), F32), shape((1, rows), F32), shape((rows, 1), F32),
            shape((1, LANES), F32),
            shape((2, LANES), F32),
        ],
        scratch_shapes=[
            vmem(weight.shape, BF16),
            vmem(other.shape, BF16),
            vmem(weight_out.shape, BF16),
            vmem(tokens.shape, BF16),
            vmem(cotangent.shape, BF16),
            vmem((shard_rows, wide_in), BF16),
            vmem((shard_rows, other_cols), BF16),
            vmem((shard_rows, width), BF16),
            vmem((rows, model), BF16),
            vmem((model, wide_in), BF16),
            vmem((model, rows), BF16),
            vmem((rows, wide_in), F32),
            vmem((rows, rows), F32),
            vmem((rows, LANES), F32),
            vmem((ranks * steps, rows, LANES), BF16),
            vmem((steps, rows, LANES), F32),
            vmem(wide, BF16), vmem(wide, BF16), vmem(wide, BF16),
            vmem((model, width), BF16),
            vmem((rows, LANES), F32),
            vmem((rows, width), BF16),
            vmem((down.shape[0] // ranks, model), BF16),
            vmem((rows, model), BF16),
            vmem((rows, model), BF16),
            vmem((model, rows), BF16),
            pltpu.SemaphoreType.DMA((3 + steps, 6)),
            pltpu.SemaphoreType.DMA((3 + steps, 6)),
            pltpu.SemaphoreType.DMA((3 + steps, 2)),
            pltpu.SemaphoreType.DMA((FRONT_LOADS,)),
            pltpu.SemaphoreType.DMA((FRONT_SAVES + 1,)),
        ]
        + 4 * line_scratch(shards),
        compiler_params=pltpu.CompilerParams(
            collective_id=collective_id, has_side_effects=True, vmem_limit_bytes=VMEM_LIMIT
        ),
        cost_estimate=pl.CostEstimate(flops=0, bytes_accessed=300 << 20, transcendentals=0),
        name="front",
    )(
        tokens, cotangent, weight, weight_out, other, down, forget_weight, norm_gains, qk_gains, segments, order, forget_bias
    )


def ffn_kernel(
    shards, chunk,
    normed, turned_from, w_gate_up, cotangent, down_near,
    w_down, hidden, grad_gate_up, grad_weight, grad_down,
    weight_in, cotangent_in, gates, ups, hn, turned, acts, grads, weight_out, down_out,
    load_sem, save_sem, tile_sem, near_sem, *line_sems,
):
    size = gates.shape[1]
    rows, model = normed.shape
    tile = 2 * w_down.shape[0] // shards
    loads = [
        pltpu.make_async_copy(a, b, load_sem.at[n])
        for n, (a, b) in enumerate(
            ((normed, hn), (w_gate_up, weight_in), (cotangent, cotangent_in), (turned_from, turned))
        )
    ]
    saves = [
        pltpu.make_async_copy(a, b, save_sem.at[n])
        for n, (a, b) in enumerate(
            ((acts, hidden), (down_out, grad_down))
        )
    ]
    line = Line(shards, None, w_down, line_sems)
    line.near_start(down_near, near_sem)
    for copy in loads:
        copy.start()
    greet([], line)
    line.resume(down_near, near_sem)
    loads[0].wait()
    loads[1].wait()

    def span(turn, start=0):
        return pl.ds(pl.multiple_of(start + turn * tile, LANES), tile)

    def activate(turn):
        gate = dot(hn[...], weight_in[:, span(turn)])
        up = dot(hn[...], weight_in[:, span(turn, size)])
        gates[:, span(turn)] = gate
        ups[:, span(turn)] = up
        acts[:, span(turn)] = (jax.nn.silu(gate) * up).astype(BF16)

    def down_grad(turn):
        down_out[span(turn), :] = left_product(acts[:, span(turn)], cotangent_in[...]).astype(BF16)

    count = size // tile
    pl.loop(0, count)(activate)
    saves[0].start()
    loads[2].wait()
    loads[3].wait()
    line.near_load(down_near, near_sem, 0).wait()

    def consume(turn):
        grad = right_product(cotangent_in[...], w_down[span(turn), :])
        gate, up = gates[:, span(turn)], ups[:, span(turn)]
        sig = jax.nn.sigmoid(gate)
        grads[:, span(turn)] = (grad * up * sig * (1.0 + gate * (1.0 - sig))).astype(BF16)
        grads[:, span(turn, size)] = (grad * gate * sig).astype(BF16)

        for start in (0, size):
            here = span(turn, start)

            @turns(model, 3 * chunk if model % (3 * chunk) == 0 else chunk)
            def _(part):
                weight_out[part, here] = dot(turned[part, :], grads[:, here]).astype(BF16)

        for copy in tile_saves(turn):
            copy.start()

    def tile_saves(turn):
        for n, start in enumerate((0, size)):
            here = span(turn, start)
            yield pltpu.make_async_copy(grads.at[:, here], grad_gate_up.at[:, here], tile_sem.at[turn, 2 * n])
            yield pltpu.make_async_copy(weight_out.at[:, here], grad_weight.at[:, here], tile_sem.at[turn, 2 * n + 1])

    def consume_at(distance):
        lower, upper = line.layer - distance, line.layer + distance

        @pl.when(lower >= 0)
        def _():
            line.from_side(lower)
            consume(lower)

        @pl.when(upper < line.layers)
        def _():
            line.from_side(upper)
            consume(upper)

    line.step(2)
    consume(line.layer)
    consume_at(1)
    pl.loop(0, count)(down_grad)
    saves[1].start()
    for distance in range(3, line.layers):
        line.step(distance)
    for distance in range(2, line.layers):
        consume_at(distance)
    line.resumed_sent()
    for copy in saves:
        copy.wait()

    @pl.loop(0, count)
    def _(turn):
        for copy in tile_saves(turn):
            copy.wait()


def ffn(collective_id, shards, normed, turned, w_gate_up, cotangent, down_near):
    rows, model = normed.shape
    size = w_gate_up.shape[1] // 2
    shape, vmem = jax.ShapeDtypeStruct, pltpu.VMEM
    return pl.pallas_call(
        functools.partial(ffn_kernel, shards, pick_chunk(rows)),
        in_specs=[ANY] * 5,
        out_specs=[VMEM_WHOLE] + [ANY] * 4,
        out_shape=[
            shape((size, model), BF16),
            shape((rows, size), BF16),
            shape((rows, 2 * size), BF16),
            shape((model, 2 * size), BF16),
            shape((size, model), BF16),
        ],
        scratch_shapes=[
            vmem(w_gate_up.shape, BF16),
            vmem((rows, model), BF16),
            vmem((rows, size), F32),
            vmem((rows, size), F32),
            vmem((rows, model), BF16),
            vmem((model, rows), BF16),
            vmem((rows, size), BF16),
            vmem((rows, 2 * size), BF16),
            vmem((model, 2 * size), BF16),
            vmem((size, model), BF16),
            pltpu.SemaphoreType.DMA((4,)),
            pltpu.SemaphoreType.DMA((2,)),
            pltpu.SemaphoreType.DMA((shards // 2, 4)),
            pltpu.SemaphoreType.DMA((3,)),
        ]
        + line_scratch(shards),
        compiler_params=pltpu.CompilerParams(
            collective_id=collective_id, has_side_effects=True, vmem_limit_bytes=VMEM_LIMIT
        ),
        cost_estimate=pl.CostEstimate(flops=0, bytes_accessed=100 << 20, transcendentals=0),
        name="ffn",
    )(normed, turned, w_gate_up, cotangent, down_near)


class ShardSum:
    def __init__(self, shards, blocks, side_in, kept, from_below, from_above, sems):
        self.shard = lax.axis_index("fsdp")
        self.layers = shards // 2
        self.layer, self.core = self.shard // 2, self.shard % 2
        self.sibling = {"fsdp": self.shard ^ 1}
        self.above, self.below = {"fsdp": self.shard + 2}, {"fsdp": self.shard - 2}
        self.has_above, self.has_below = self.layer < self.layers - 1, self.layer > 0
        self.blocks, self.side_in, self.kept = blocks, side_in, kept
        self.from_below, self.from_above = from_below, from_above
        self.rows = kept.shape[1]
        self.side_send, self.side_recv, self.up_send, self.up_recv, self.down_send, self.down_recv = sems

    def side(self, layer):
        return pltpu.make_async_remote_copy(
            rows_of(self.blocks, 2 * layer + 1 - self.core, self.rows), self.side_in.at[layer],
            self.side_send.at[layer], self.side_recv.at[layer], device_id=self.sibling, device_id_type=MESH,
        )

    def start(self):
        for layer in range(self.layers):
            self.side(layer).start()

    def presum(self):
        for layer in range(self.layers):
            self.side(layer).wait_recv()
            own = rows_of(self.blocks, 2 * layer + self.core, self.rows)[...].astype(F32)
            self.kept[layer] = (own + self.side_in[layer].astype(F32)).astype(BF16)

    def up(self, stage):
        return pltpu.make_async_remote_copy(
            self.kept.at[self.layers - 1 - stage + self.layer], self.from_below.at[stage],
            self.up_send.at[stage], self.up_recv.at[stage], device_id=self.above, device_id_type=MESH,
        )

    def down(self, stage):
        return pltpu.make_async_remote_copy(
            self.kept.at[stage - self.layers + 1 + self.layer], self.from_above.at[stage],
            self.down_send.at[stage], self.down_recv.at[stage], device_id=self.below, device_id_type=MESH,
        )

    def each_sent(self, stage, what):
        @pl.when(self.has_above & (self.layer <= stage))
        def _():
            what(self.up(stage))

        @pl.when(self.has_below & (self.layers - 1 - self.layer <= stage))
        def _():
            what(self.down(stage))

    def send(self, stage):
        self.each_sent(stage, lambda copy: copy.start())

    def receive(self, stage):
        def add(target, arrived):
            self.kept[target] = (self.kept[target].astype(F32) + arrived[stage].astype(F32)).astype(BF16)

        @pl.when(self.has_below & (self.layer - 1 <= stage))
        def _():
            pltpu.make_async_remote_copy(
                self.from_below.at[stage], self.from_below.at[stage], self.up_send.at[stage], self.up_recv.at[stage],
                device_id=self.below, device_id_type=MESH,
            ).wait_recv()
            add(self.layers - 2 - stage + self.layer, self.from_below)

        @pl.when(self.has_above & (self.layers - 2 - self.layer <= stage))
        def _():
            pltpu.make_async_remote_copy(
                self.from_above.at[stage], self.from_above.at[stage], self.down_send.at[stage],
                self.down_recv.at[stage], device_id=self.above, device_id_type=MESH,
            ).wait_recv()
            add(stage - self.layers + 2 + self.layer, self.from_above)

    def sent(self):
        for layer in range(self.layers):
            self.side(layer).wait_send()
        for stage in range(self.layers - 1):
            self.each_sent(stage, lambda copy: copy.wait_send())


def shard_sum_scratch(shards, rows, cols):
    layers = shards // 2
    few, all_layers = pltpu.SemaphoreType.DMA((layers - 1,)), pltpu.SemaphoreType.DMA((layers,))
    block = pltpu.VMEM((layers, rows, cols), BF16)
    part = pltpu.VMEM((layers - 1, rows, cols), BF16)
    return [block, block, part, part], [all_layers, all_layers, few, few, few, few]


class Fold:
    def __init__(self, rank, piece, first, between, second, send_sem, recv_sem):
        self.rank, self.piece, self.first, self.between, self.second = rank, piece, first, between, second
        self.send_sem, self.recv_sem = send_sem, recv_sem

    def copy(self, number):
        me = self.rank
        source, target, distance = (
            lambda: (self.piece(me ^ 1, 0), self.first(0, 0), 1),
            lambda: (self.piece(me ^ 3, 0), self.first(1, 0), 1),
            lambda: (self.piece(me ^ 2, 1), self.first(0, 1), 2),
            lambda: (self.piece(me ^ 3, 1), self.first(1, 1), 2),
            lambda: (self.between(0), self.second(0), 2),
            lambda: (self.between(1), self.second(1), 1),
        )[number]()
        return to_rank(source, target, self.send_sem.at[number], self.recv_sem.at[number], me ^ distance)

    def start(self):
        for number in range(4):
            self.copy(number).start()

    def pass_on(self):
        for h, distance in ((0, 2), (1, 1)):
            self.copy(2 * h).wait_recv()
            self.copy(2 * h + 1).wait_recv()
            own = self.piece(self.rank ^ distance, h)[...].astype(F32)
            self.between(h)[...] = (own + self.first(1, h)[...].astype(F32)).astype(BF16)
            self.copy(4 + h).start()

    def total(self, h):
        self.copy(4 + h).wait_recv()
        own = self.piece(self.rank, h)[...].astype(F32)
        return own + self.first(0, h)[...].astype(F32) + self.second(h)[...].astype(F32)

    def sent(self):
        for number in range(6):
            self.copy(number).wait_send()


def middle_kernel(
    ranks,
    grad_gate_up, w_gate_up, mixed, cotangent, w_out, hidden, w_down, gated, gain,
    mixed_grad, gated_grad, gain_grad, down_part, out_grad,
    grad_in, weight_in, mixed_in, cotangent_in, out_in, hidden_in, down_in, gated_in, low_grad, down_all, out_all,
    wide, first_out, first_in, first_between, first_end, second_out, second_in, second_between, second_end,
    load_sem, save_sem, first_send, first_recv, second_send, second_recv,
):
    rank = lax.axis_index("ctx")
    rows = mixed.shape[0] // ranks
    model, width = w_out.shape
    tile = 256
    loads = [
        pltpu.make_async_copy(a, b, load_sem.at[n])
        for n, (a, b) in enumerate(
            (
                (w_gate_up, weight_in), (grad_gate_up, grad_in), (mixed, mixed_in), (cotangent, cotangent_in),
                (w_out, out_in), (hidden, hidden_in), (w_down, down_in), (gated, gated_in),
            )
        )
    ]
    saves = [
        pltpu.make_async_copy(down_all, down_part, save_sem.at[0]),
        pltpu.make_async_copy(out_all, out_grad, save_sem.at[1]),
    ]
    for copy in loads:
        copy.start()
    greet([{"ctx": rank ^ distance} for distance in range(1, ranks)])
    gain_grad[...] = jnp.zeros_like(gain_grad)
    for copy in loads[:2]:
        copy.wait()

    def part(turn):
        return pl.ds(pl.multiple_of(turn * rows, 16), rows)

    half = rows // 2

    def fold(out, into, between, end, send_sem, recv_sem):
        def make(turn):
            def at(h):
                return pl.ds(pl.multiple_of(turn * rows + h * half, 16), half)

            return Fold(
                rank,
                lambda index, h: out.at[index, at(h), :],
                lambda slot, h: into.at[slot, at(h), :],
                lambda h: between.at[at(h), :],
                lambda h: end.at[at(h), :],
                send_sem.at[turn],
                recv_sem.at[turn],
            )

        return make

    first = fold(first_out, first_in, first_between, first_end, first_send, first_recv)
    second = fold(second_out, second_in, second_between, second_end, second_send, second_recv)

    def compute(turn):
        here = part(turn)

        @pl.loop(0, model // tile)
        def _(step):
            cols = pl.ds(pl.multiple_of(step * tile, tile), tile)
            wide[:, cols] = right_product(grad_in[here, :], weight_in[cols, :])

        @pl.when(turn == 0)
        def _():
            for copy in loads[2:5]:
                copy.wait()

        values = mixed_in[here, :].astype(F32)
        scale = rms_scale(values)
        grad = wide[...]
        gain_grad[0:1, :] += jnp.sum(grad * values * scale, axis=0, keepdims=True)
        back = norm_back(grad, values, scale, gain[1:2, :]).astype(BF16)
        for index in range(ranks):
            first_out[index, here, :] = back[:, index * width : (index + 1) * width]
        first(turn).start()

    def project(turn):
        here = part(turn)
        for h in range(2):
            at = pl.ds(pl.multiple_of(turn * rows + h * half, 16), half)
            total = cotangent_in[at, pl.ds(pl.multiple_of(rank * width, LANES), width)].astype(F32)
            total = total + first(turn).total(h)
            mixed_grad[at, :] = total
            low_grad[at, :] = total.astype(BF16)
        for index in range(ranks):
            second_out[index, here, :] = right_product(
                low_grad[here, :], out_in[index * width : (index + 1) * width, :]
            ).astype(BF16)
        second(turn).start()

    def collect(turn):
        for h in range(2):
            at = pl.ds(pl.multiple_of(turn * rows + h * half, 16), half)
            gated_grad[at, :] = second(turn).total(h)

    def aside(turn):
        @pl.when(turn == ranks)
        def _():
            for copy in loads[5:8]:
                copy.wait()

            @pl.loop(0, model // tile)
            def _(step):
                cols = pl.ds(pl.multiple_of(step * tile, tile), tile)
                down_all[:, cols] = dot(hidden_in[...], down_in[:, cols]).astype(BF16)

            saves[0].start()

        @pl.when(turn == ranks + 2)
        def _():
            @pl.loop(0, gated_in.shape[0])
            def _(block):
                out_all[pl.ds(pl.multiple_of(block * LANES, LANES), LANES), :] = left_product(
                    gated_in[block], low_grad[...]
                ).astype(BF16)

            saves[1].start()

    @pl.loop(0, ranks + 4)
    def _(turn):
        stages = (
            compute, lambda t: first(t).pass_on(), project, lambda t: second(t).pass_on(), collect,
        )
        for lag, stage in enumerate(stages):
            if lag == 4:
                aside(turn)

            @pl.when((turn >= lag) & (turn < ranks + lag))
            def _():
                stage(turn - lag)

    @pl.loop(0, ranks)
    def _(turn):
        first(turn).sent()
        second(turn).sent()

    for copy in saves:
        copy.wait()


def middle(
    collective_id, ranks, grad_gate_up, w_gate_up, mixed, cotangent, w_out, hidden, w_down, gated, gain
):
    rows, model = mixed.shape
    width = w_out.shape[1]
    flat = pltpu.VMEM((rows, width), BF16)
    blocks = [pltpu.VMEM((ranks, rows, width), BF16), pltpu.VMEM((2, rows, width), BF16), flat, flat]
    sems = pltpu.SemaphoreType.DMA((ranks, 6))
    return pl.pallas_call(
        functools.partial(middle_kernel, ranks),
        in_specs=[ANY] * 8 + [VMEM_WHOLE],
        out_specs=[VMEM_WHOLE] * 3 + [ANY] * 2,
        out_shape=[
            jax.ShapeDtypeStruct((rows, width), F32),
            jax.ShapeDtypeStruct((rows, width), F32),
            jax.ShapeDtypeStruct((8, model), F32),
            jax.ShapeDtypeStruct((rows, model), BF16),
            jax.ShapeDtypeStruct((model, width), BF16),
        ],
        scratch_shapes=[
            pltpu.VMEM(grad_gate_up.shape, BF16),
            pltpu.VMEM(w_gate_up.shape, BF16),
            pltpu.VMEM(mixed.shape, BF16),
            pltpu.VMEM(cotangent.shape, BF16),
            pltpu.VMEM(w_out.shape, BF16),
            pltpu.VMEM(hidden.shape, BF16),
            pltpu.VMEM(w_down.shape, BF16),
            pltpu.VMEM(gated.shape, BF16),
            pltpu.VMEM((rows, width), BF16),
            pltpu.VMEM((rows, model), BF16),
            pltpu.VMEM((model, width), BF16),
            pltpu.VMEM((rows // ranks, model), F32),
            *blocks, *blocks,
            pltpu.SemaphoreType.DMA((8,)),
            pltpu.SemaphoreType.DMA((2,)),
            sems, sems, sems, sems,
        ],
        compiler_params=pltpu.CompilerParams(
            collective_id=collective_id, has_side_effects=True, vmem_limit_bytes=VMEM_LIMIT
        ),
        cost_estimate=pl.CostEstimate(flops=0, bytes_accessed=150 << 20, transcendentals=0),
        name="middle",
    )(grad_gate_up, w_gate_up, mixed, cotangent, w_out, hidden, w_down, gated, gain)


def last_kernel(
    ranks, shards,
    grad_project, w_in, inputs, aside, pieces, mixed, share, normed, mixed_grad, gain, gain_two_grad, small, segments,
    tokens_grad, block_out, total_sums, parts, aside_all, share_all,
    grad_in, weight_in, inputs_in, aside_in, pieces_in, mixed_in, wide, out, into, between, end, sums_out, sums_in,
    share_in, normed_in, load_sem, send_sem, recv_sem, sums_send, sums_recv, aside_send, aside_recv, aside_own,
):
    rank = lax.axis_index("ctx")
    rows = inputs.shape[0] // ranks
    model, width = inputs.shape[1], mixed_grad.shape[1]
    tile = 256
    loads = [
        pltpu.make_async_copy(a, b, load_sem.at[n])
        for n, (a, b) in enumerate(
            (
                (aside, aside_in), (w_in, weight_in), (grad_project, grad_in), (inputs, inputs_in),
                (pieces, pieces_in), (rows_of(mixed, rank, rows), mixed_in), (share, share_in),
                (normed, normed_in),
            )
        )
    ]
    for copy in loads:
        copy.start()
    greet([{"ctx": rank ^ distance} for distance in range(1, ranks)])
    relay, share_relay = [
        relay_ops("stack", rank, a, b, (aside_send.at[n], aside_recv.at[n], aside_own.at[n]))
        for n, (a, b) in enumerate(((aside_in, aside_all), (share_in, share_all)))
    ]
    loads[6].wait()
    share_relay.start()
    loads[0].wait()
    relay.start()
    sums_out[...] = jnp.zeros_like(sums_out)
    sums_out[1:2, :] = gain_two_grad[0:1, :]
    sums_out[2:3, 0:LANES] = small[0:1, :]
    sums_out[2:3, LANES : 2 * LANES] = small[1:2, :]
    for index in range(ranks):
        sums_out[3 + index : 4 + index, 0:LANES] = jnp.where(rank == index, small[2:3, :], 0.0)
    for copy in loads[1:4]:
        copy.wait()

    half = rows // 2

    def at(h):
        return pl.ds(h * half, half)

    fold = Fold(
        rank,
        lambda index, h: out.at[index, at(h), :],
        lambda slot, h: into.at[slot, at(h), :],
        lambda h: between.at[at(h), :],
        lambda h: end.at[at(h), :],
        send_sem,
        recv_sem,
    )

    def send_sums(distance):
        return to_rank(
            sums_out, sums_in.at[distance], sums_send.at[distance - 1], sums_recv.at[distance - 1], rank ^ distance
        )

    def compute(other):
        here = pl.ds(pl.multiple_of(other * rows, 16), rows)

        @pl.loop(0, model // tile)
        def _(step):
            cols = pl.ds(pl.multiple_of(step * tile, tile), tile)
            wide[:, cols] = right_product(grad_in[here, :], weight_in[cols, :])

        values = inputs_in[here, :].astype(F32)
        scale = rms_scale(values)
        grad = wide[...]
        sums_out[0:1, :] += jnp.sum(grad * values * scale, axis=0, keepdims=True)
        wide[...] = norm_back(grad, values, scale, gain[0:1, :])
        own = pl.ds(pl.multiple_of(rank * width, LANES), width)
        wide[:, own] += mixed_grad[here, :]
        out[other] = wide[...].astype(BF16)

    @pl.loop(1, ranks)
    def _(turn):
        compute(rank ^ (ranks - turn))

        @pl.when(turn == 2)
        def _():
            for number in (2, 3):
                fold.copy(number).start()

        @pl.when(turn == 3)
        def _():
            for number in (0, 1):
                fold.copy(number).start()

    share_relay.forward()
    for copy in loads[4:6]:
        copy.wait()
    own = pl.ds(pl.multiple_of(rank * rows, 16), rows)
    result = mixed_in[...].astype(F32)
    for index in range(ranks):
        result = result + pieces_in[index].astype(F32)
    block_out[...] = result.astype(BF16)
    branch = result - inputs_in[own, :].astype(F32)
    valid = jnp.where(segments[own, :] >= 0.0, 1.0, 0.0)
    lane = lax.broadcasted_iota(jnp.int32, (1, LANES), 1)
    stats = jnp.zeros((1, LANES), F32)
    for index, values in enumerate((result, branch)):
        total = jnp.sum(valid * jnp.sum(values * values, axis=-1, keepdims=True), axis=0, keepdims=True)
        stats = jnp.where(lane == index, total, stats)
    sums_out[7:8, 0:LANES] = stats
    compute(rank)
    loads[7].wait()
    turned = grad_in[:, 4 * width : 4 * width + LANES].astype(F32).T[0:8, :]
    forget_grad = right_product(turned.astype(BF16), normed_in[...])
    for distance in range(1, ranks):
        send_sums(distance).start()
    relay.forward()
    fold.pass_on()
    for h in range(2):
        tokens_grad[at(h), :] = fold.total(h).astype(BF16)
    total = sums_out[...]
    for distance in range(1, ranks):
        send_sums(distance).wait_recv()
        total = total + sums_in[distance]
    total_sums[...] = total
    share = model // shards
    parts[...] = jnp.zeros_like(parts)
    for index in range(shards):
        parts[index, 0:2, 0:share] = total[0:2, index * share : (index + 1) * share]
        parts[index, 2:8, :] = total[2:8, 0 : parts.shape[2]]
        parts[index, 8:16, 0:share] = forget_grad[:, index * share : (index + 1) * share]
    fold.sent()
    for distance in range(1, ranks):
        send_sums(distance).wait_send()
    relay.finish()
    share_relay.finish()


def last_moves(
    collective_id, ranks, shards,
    grad_project, w_in, inputs, aside, pieces, mixed, share, normed, mixed_grad, gain, gain_two_grad, small,
    segments,
):
    rows, model = inputs.shape
    own = (rows // ranks, model)
    flat = pltpu.VMEM(own, BF16)
    blocks = [pltpu.VMEM((ranks,) + own, BF16), pltpu.VMEM((2,) + own, BF16), flat, flat]
    sems = pltpu.SemaphoreType.DMA((ranks - 1,))
    return pl.pallas_call(
        functools.partial(last_kernel, ranks, shards),
        in_specs=[ANY] * 8 + [VMEM_WHOLE] * 5,
        out_specs=[VMEM_WHOLE] * 4 + [ANY] * 2,
        out_shape=[
            jax.ShapeDtypeStruct(own, BF16),
            jax.ShapeDtypeStruct(own, BF16),
            jax.ShapeDtypeStruct((8, model), F32),
            jax.ShapeDtypeStruct((shards, 16, max(2 * LANES, -(-model // shards // LANES) * LANES)), F32),
            jax.ShapeDtypeStruct((ranks,) + aside.shape, BF16),
            jax.ShapeDtypeStruct((ranks,) + share.shape, BF16),
        ],
        scratch_shapes=[
            pltpu.VMEM(grad_project.shape, BF16),
            pltpu.VMEM(w_in.shape, BF16),
            pltpu.VMEM(inputs.shape, BF16),
            pltpu.VMEM(aside.shape, BF16),
            pltpu.VMEM(pieces.shape, BF16),
            pltpu.VMEM(own, BF16),
            pltpu.VMEM(own, F32),
            *blocks,
            pltpu.VMEM((8, model), F32),
            pltpu.VMEM((ranks, 8, model), F32),
            pltpu.VMEM(share.shape, BF16),
            pltpu.VMEM(normed.shape, BF16),
            pltpu.SemaphoreType.DMA((8,)),
            pltpu.SemaphoreType.DMA((6,)),
            pltpu.SemaphoreType.DMA((6,)),
            sems, sems,
            pltpu.SemaphoreType.DMA((2, 6)),
            pltpu.SemaphoreType.DMA((2, 6)),
            pltpu.SemaphoreType.DMA((2, 2)),
        ],
        compiler_params=pltpu.CompilerParams(
            collective_id=collective_id, has_side_effects=True, vmem_limit_bytes=VMEM_LIMIT
        ),
        cost_estimate=pl.CostEstimate(flops=0, bytes_accessed=150 << 20, transcendentals=0),
        name="last_moves",
    )(grad_project, w_in, inputs, aside, pieces, mixed, share, normed, mixed_grad, gain, gain_two_grad, small, segments)


def finish_kernel(
    ranks, shards, late, parts, late_all, part_sum, forget_all,
    late_in, into, load_sem, send_sem, recv_sem, own_sem, part_send, part_recv, forget_send, forget_recv,
):
    rank = lax.axis_index("ctx")
    shard = lax.axis_index("fsdp")
    load = pltpu.make_async_copy(late, late_in, load_sem.at[0])
    load.start()
    relay = relay_ops("stack", rank, late_in, late_all, (send_sem, recv_sem, own_sem))
    greet(
        [{"ctx": rank ^ distance} for distance in range(1, ranks)]
        + [{"fsdp": shard ^ distance} for distance in range(1, shards)]
    )
    load.wait()
    relay.start()

    def send(distance):
        other = shard ^ distance
        return pltpu.make_async_remote_copy(
            parts.at[other], into.at[distance], part_send.at[distance - 1], part_recv.at[distance - 1],
            device_id={"fsdp": other}, device_id_type=MESH,
        )

    def send_forget(distance):
        return to_rank(
            forget_all.at[rank], forget_all.at[rank], forget_send.at[distance - 1], forget_recv.at[distance - 1],
            rank ^ distance,
        )

    for distance in range(1, shards):
        send(distance).start()
    total = parts[shard]
    for distance in range(1, shards):
        send(distance).wait_recv()
        total = total + into[distance]
    part_sum[...] = total
    forget_all[rank] = total[8:16, :]
    for distance in range(1, ranks):
        send_forget(distance).start()
    relay.forward()
    for distance in range(1, ranks):
        send_forget(distance).wait()
    for distance in range(1, shards):
        send(distance).wait_send()
    relay.finish()


def finish_moves(collective_id, ranks, shards, late, parts):
    sems = pltpu.SemaphoreType.DMA((shards - 1,))
    return pl.pallas_call(
        functools.partial(finish_kernel, ranks, shards),
        in_specs=[ANY, VMEM_WHOLE],
        out_specs=[ANY, VMEM_WHOLE, VMEM_WHOLE],
        out_shape=[
            jax.ShapeDtypeStruct((ranks,) + late.shape, BF16),
            jax.ShapeDtypeStruct(parts.shape[1:], F32),
            jax.ShapeDtypeStruct((ranks, 8, parts.shape[2]), F32),
        ],
        scratch_shapes=[
            pltpu.VMEM(late.shape, BF16),
            pltpu.VMEM(parts.shape, F32),
            pltpu.SemaphoreType.DMA((1,)),
            pltpu.SemaphoreType.DMA((6,)),
            pltpu.SemaphoreType.DMA((6,)),
            pltpu.SemaphoreType.DMA((2,)),
            sems, sems,
            pltpu.SemaphoreType.DMA((ranks - 1,)),
            pltpu.SemaphoreType.DMA((ranks - 1,)),
        ],
        compiler_params=pltpu.CompilerParams(
            collective_id=collective_id, has_side_effects=True, vmem_limit_bytes=VMEM_LIMIT
        ),
        cost_estimate=pl.CostEstimate(flops=0, bytes_accessed=50 << 20, transcendentals=0),
        name="finish_moves",
    )(late, parts)


def spread_kernel(pieces, *refs):
    source, targets = refs[0], refs[1:]
    ranks = source.shape[0]
    for target, (piece, first, count) in zip(targets, pieces):
        for block in range(count):
            for index in range(ranks):
                target[:, pl.ds((block * ranks + index) * piece, piece)] = source[
                    index, :, pl.ds(first + block * piece, piece)
                ].astype(F32)


def spread_cols(source, *pieces):
    ranks, rows, cols = source.shape
    if any(piece % LANES or first % LANES for piece, first, _ in pieces):
        return [
            jnp.concatenate(
                [
                    source[c, :, first + i * piece : first + (i + 1) * piece]
                    for i in range(count)
                    for c in range(ranks)
                ],
                axis=1,
            ).astype(F32)
            for piece, first, count in pieces
        ]
    part = rows // 4 if rows % 64 == 0 else rows
    widths = [count * ranks * piece for piece, _, count in pieces]
    return pl.pallas_call(
        functools.partial(spread_kernel, pieces),
        grid=(rows // part,),
        in_specs=[pl.BlockSpec((ranks, part, cols), lambda step: (0, step, 0))],
        out_specs=[pl.BlockSpec((part, w), lambda step: (step, 0)) for w in widths],
        out_shape=[jax.ShapeDtypeStruct((rows, w), F32) for w in widths],
        compiler_params=pltpu.CompilerParams(vmem_limit_bytes=VMEM_LIMIT),
        cost_estimate=pl.CostEstimate(flops=0, bytes_accessed=rows * sum(widths) * 6, transcendentals=0),
        name="spread_cols",
    )(source)


def spread_early_kernel(piece, gate_up, down, gate_up_out, down_out):
    ranks = gate_up.shape[0]
    for block in range(gate_up.shape[2] // piece):
        for index in range(ranks):
            gate_up_out[:, (block * ranks + index) * piece : (block * ranks + index + 1) * piece] = gate_up[
                index, :, block * piece : (block + 1) * piece
            ].astype(F32)
    size = down.shape[1]
    for index in range(down.shape[0]):
        down_out[index * size : (index + 1) * size, :] = down[index].astype(F32)


def spread_early(gate_up, down, piece):
    ranks, rows, cols = gate_up.shape
    _, down_rows, model = down.shape
    steps = 2
    part, each = rows // steps, ranks // steps
    return pl.pallas_call(
        functools.partial(spread_early_kernel, piece),
        grid=(steps,),
        in_specs=[
            pl.BlockSpec((ranks, part, cols), lambda step: (0, step, 0)),
            pl.BlockSpec((each, down_rows, model), lambda step: (step, 0, 0)),
        ],
        out_specs=[
            pl.BlockSpec((part, ranks * cols), lambda step: (step, 0)),
            pl.BlockSpec((each * down_rows, model), lambda step: (step, 0)),
        ],
        out_shape=[
            jax.ShapeDtypeStruct((rows, ranks * cols), F32),
            jax.ShapeDtypeStruct((ranks * down_rows, model), F32),
        ],
        compiler_params=pltpu.CompilerParams(vmem_limit_bytes=VMEM_LIMIT),
        cost_estimate=pl.CostEstimate(
            flops=0, bytes_accessed=6 * ranks * (rows * cols + down_rows * model), transcendentals=0
        ),
        name="spread_early",
    )(gate_up, down)


def unpack_kernel(
    width, heads, head, late, forget_all, sums, totals, segments, first_rows, second_rows,
    in_out, out_out, first_out, second_out, forget_out, gains, bias, qk, rms,
):
    ranks = late.shape[0]
    first = 4 * width
    for block in range(4):
        for index in range(ranks):
            in_out[:, (block * ranks + index) * width : (block * ranks + index + 1) * width] = late[
                index, :, block * width : (block + 1) * width
            ].astype(F32)
    first_out[...] = first_rows[...]
    second_out[...] = second_rows[...]
    lane = lax.broadcasted_iota(jnp.int32, (LANES, ranks * heads), 0)
    place = lax.broadcasted_iota(jnp.int32, (LANES, ranks * heads), 1)
    biases = jnp.zeros((8, ranks * heads), F32)
    for index in range(ranks):
        chosen = (lane < heads) & (place == index * heads + lane)
        out_out[:, index * width : (index + 1) * width] = late[index, :, first : first + width].astype(F32)
        forget_out[index * heads : (index + 1) * heads, :] = forget_all[index, 0:heads, 0 : forget_out.shape[1]]
        row = jnp.broadcast_to(sums[3 + index : 4 + index, 0:LANES], (8, LANES))
        for part in split_three(row):
            biases = biases + dot(part.astype(BF16), jnp.where(chosen, 1.0, 0.0).astype(BF16))
    gains[...] = sums[0:2, 0 : gains.shape[1]]
    bias[...] = biases[0:1, :]
    for row in range(2):
        qk[row : row + 1, :] = sum(
            sums[2:3, row * LANES + side * head : row * LANES + (side + 1) * head] for side in range(LANES // head)
        )
    count = jnp.sum(jnp.where(segments[...] >= 0, 1.0, 0.0), axis=-1, keepdims=True)
    rms[...] = jnp.sqrt(totals[7:8, 0:2] / (count * totals.shape[1]))


def unpack(late, forget_all, sums, totals, segments, first_rows, second_rows, width, heads, head):
    ranks, rows, cols = late.shape
    part = rows // 2

    def block(lanes):
        return pl.BlockSpec((part, lanes), lambda step: (step, 0))

    share = rows
    shape = jax.ShapeDtypeStruct
    return pl.pallas_call(
        functools.partial(unpack_kernel, width, heads, head),
        grid=(rows // part,),
        in_specs=[
            pl.BlockSpec((ranks, part, cols), lambda step: (0, step, 0)),
        ]
        + [whole(a.shape) for a in (forget_all, sums, totals, segments)]
        + [block(first_rows.shape[1])] * 2,
        out_specs=[block(4 * ranks * width), block(ranks * width)] + [block(first_rows.shape[1])] * 2
        + [whole(a) for a in ((ranks * heads, rows), (2, share), (1, ranks * heads), (2, head), (1, 2))],
        out_shape=[
            shape((rows, 4 * ranks * width), F32),
            shape((rows, ranks * width), F32),
            shape(first_rows.shape, BF16),
            shape(second_rows.shape, BF16),
            shape((ranks * heads, rows), F32),
            shape((2, share), F32),
            shape((1, ranks * heads), F32),
            shape((2, head), F32),
            shape((1, 2), F32),
        ],
        compiler_params=pltpu.CompilerParams(vmem_limit_bytes=VMEM_LIMIT),
        cost_estimate=pl.CostEstimate(flops=0, bytes_accessed=ranks * rows * cols * 6, transcendentals=0),
        name="unpack",
    )(late, forget_all, sums, totals, segments, first_rows, second_rows)


class Native:
    def __init__(self, ranks):
        self.ranks = ranks

    def begin(self, tokens, cotangent, weight, tail, other, piece, width, padded):
        rank, model = lax.axis_index("ctx"), tokens.shape[1]
        parts = [lax.dynamic_slice_in_dim(weight, i * model + rank * width, width, 1) for i in range(4)]
        parts = [jnp.pad(part, ((0, 0), (0, padded - width))) for part in parts]
        cols = other.shape[1] // self.ranks
        picks = [
            lax.dynamic_slice_in_dim(other, (i * self.ranks + rank) * piece, piece, 1) for i in range(cols // piece)
        ]
        return (
            lax.all_gather(tokens, "ctx", axis=0, tiled=True),
            lax.all_gather(cotangent, "ctx", axis=0, tiled=True),
            lax.all_gather(jnp.concatenate(parts + [tail], axis=1), "fsdp", axis=0, tiled=True),
            jnp.concatenate(picks, axis=1),
        )

    def gather_cols(self, array, piece):
        return lax.all_gather(array, "ctx", axis=1, tiled=True), lax.all_gather(piece, "fsdp", axis=0, tiled=True)


def body(
    tokens, block_order, segment_ids, norm_gains, attn_in_weight, forget_weight, forget_bias,
    qk_gains, out_weight, gate_up_weight, down_weight, out_grad,
):
    ranks = lax.axis_size("ctx")
    shards = lax.axis_size("fsdp")
    rank = lax.axis_index("ctx")
    row_count, model_width = tokens.shape[1], tokens.shape[2]
    head_count, head_dim = forget_bias.shape[0], qk_gains.shape[1]
    local_heads = head_count // ranks
    width = local_heads * head_dim
    padded = -(-width // LANES) * LANES
    seq_order = block_order[0]
    seq_len = segment_ids.shape[1]
    block_len = seq_len // seq_order.shape[0]
    hidden_piece = down_weight.shape[0] // ranks
    hidden = hidden_piece * shards
    plain = ranks == 4 and shards & (shards - 1) == 0 and width == padded
    comm = Native(ranks)

    def slab(array, start, size, axis):
        return lax.dynamic_slice_in_dim(array, start, size, axis)

    def widen(array):
        return jnp.pad(array, ((0, 0), (0, padded - width))) if padded > width else array

    if plain:
        (
            inputs, grad_low, w_in, w_out, w_gate_up, normed, project, gated_all, attended,
            wide_query, wide_key, wide_value, mixed_low, down_near, normed_two, turned, gain_rows, *places_all,
            bias, head_gains,
        ) = front(
            0, ranks, shards, head_dim, local_heads, width, hidden_piece,
            tokens[0], out_grad[0], attn_in_weight, out_weight, gate_up_weight, down_weight, forget_weight.T,
            norm_gains, qk_gains, segment_ids, block_order, forget_bias[None],
        )
        w_down, hidden_act, grad_gate_up, early_grad, down_part_grad = ffn(
            1, shards, normed_two, turned, w_gate_up, grad_low, down_near
        )
    else:
        tail = jnp.concatenate(
            [
                slab(forget_weight, rank * local_heads, local_heads, 1),
                norm_gains.T,
                jnp.zeros((attn_in_weight.shape[0], LANES - local_heads - 2), BF16),
            ],
            axis=1,
        )
        offsets = jnp.arange(block_len, dtype=jnp.int32)
        blocks = jnp.arange(seq_order.shape[0], dtype=jnp.int32)
        places = (seq_order[:, None] * block_len + offsets[None]).reshape(-1)
        by_block = segment_ids[0].reshape(-1, block_len)
        chosen = seq_order[:, None, None] == blocks[None, :, None]
        segments = jnp.sum(jnp.where(chosen, by_block[None], 0), axis=1).reshape(-1)
        places, segments = places.astype(F32), segments.astype(F32)
        places_all = (places[None, :], places[:, None], segments[None, :], segments[:, None])
        bias = jnp.pad(slab(forget_bias, rank * local_heads, local_heads, 0), (0, LANES - local_heads))[None]
        head_gains = jnp.tile(qk_gains, (1, LANES // head_dim))
        down_piece = slab(down_weight, rank * hidden_piece, hidden_piece, 0)
        inputs, grad_low, w_in, gate_up_piece = comm.begin(
            tokens[0], out_grad[0], attn_in_weight, tail, gate_up_weight, hidden_piece, width, padded
        )
        w_gate_up = lax.all_gather(gate_up_piece, "fsdp", axis=0, tiled=True)
        gain_cols = w_in[:, 4 * padded : 4 * padded + LANES].astype(F32).T
        gain_one = gain_cols[local_heads]
        gain_two = gain_cols[local_heads + 1]
        wide_inputs = inputs.astype(F32)
        scale_one = rms_scale(wide_inputs)
        normed = (wide_inputs * scale_one * gain_one).astype(BF16)
        project = dot(normed, w_in)
        gated, attended, wide_query, wide_key, wide_value = attend(
            project, places_all, bias, head_gains, head_dim, padded, local_heads
        )
        gated_all, w_out = comm.gather_cols(gated[:, :width], slab(out_weight, rank * width, width, 1))
        mixed_cols = slab(inputs, rank * width, width, 1).astype(F32) + dot(gated_all, w_out)
        mixed_low, w_down = comm.gather_cols(mixed_cols.astype(BF16), down_piece)
        mixed = mixed_low.astype(F32)
        scale_two = rms_scale(mixed)
        normed_two = (mixed * scale_two * gain_two).astype(BF16)
        gate_up = dot(normed_two, w_gate_up)
        gate_part, up_part = gate_up[:, :hidden], gate_up[:, hidden:]
        gate_sigmoid = jax.nn.sigmoid(gate_part)
        silu = gate_part * gate_sigmoid
        hidden_act = (silu * up_part).astype(BF16)
        grad_hidden = right_product(grad_low, w_down)
        grad_gate = grad_hidden * up_part * gate_sigmoid * (1.0 + gate_part * (1.0 - gate_sigmoid))
        grad_gate_up = jnp.concatenate([grad_gate, grad_hidden * silu], axis=1).astype(BF16)
        down_part_grad = left_product(hidden_act, grad_low).astype(BF16)
        gate_up_grad = left_product(normed_two, grad_gate_up).astype(BF16)
        down_part = dot(hidden_act, w_down).astype(BF16)

    def own_rows(array):
        return slab(array, rank * row_count, row_count, 0)

    def reduce_shards(array):
        return lax.psum_scatter(array.astype(BF16), "fsdp", scatter_dimension=0, tiled=True)

    if plain:
        early_share = (reduce_shards(early_grad),)
    else:
        early_share = (reduce_shards(down_part_grad), reduce_shards(gate_up_grad))
    if plain:
        grad_mixed_cols, grad_gated, gain_two_grad, down_part, out_part = middle(
            3, ranks, grad_gate_up, w_gate_up, mixed_low, grad_low, w_out, hidden_act, w_down, gated_all,
            gain_rows,
        )
    else:
        grad_normed_two = right_product(grad_gate_up, w_gate_up)
        gain_two_grad = jnp.sum(grad_normed_two * mixed * scale_two, axis=0)
        grad_mixed_part = norm_back(grad_normed_two, mixed, scale_two, gain_two).astype(BF16)
        grad_mixed_cols = slab(grad_low, rank * width, width, 1).astype(F32) + lax.psum_scatter(
            grad_mixed_part, "ctx", scatter_dimension=1, tiled=True
        ).astype(F32)
        grad_branch = grad_mixed_cols.astype(BF16)
        grad_gated = widen(
            lax.psum_scatter(
                right_product(grad_branch, w_out).astype(BF16), "ctx", scatter_dimension=1, tiled=True
            ).astype(F32)
        )
    grad_project, small, *rest = attend_back(
        project, places_all, bias, head_gains, attended, (wide_query, wide_key, wide_value),
        grad_gated, (down_part, normed, out_part, down_part_grad) if plain else (), ranks if plain else 0, shards, head_dim, padded, local_heads,
    )
    if plain:
        down_pieces, late, down_share = rest
    else:
        in_part = left_product(normed, grad_project).astype(BF16)
        out_part = left_product(gated_all, grad_branch).astype(BF16)
        late = jnp.concatenate([in_part[:, : 4 * padded], out_part, in_part[:, 4 * padded :]], axis=1)
    late, early_share = lax.optimization_barrier((late, early_share))
    late_share = reduce_shards(late)

    if plain:
        tokens_grad, block_out, sums, parts, early_own, down_own = last_moves(
            4, ranks, shards, grad_project, w_in, inputs, early_share[0], down_pieces, mixed_low, down_share,
            normed, grad_mixed_cols,             gain_rows, gain_two_grad, small, places_all[3],
        )
        late_own, piece_sum, forget_all = finish_moves(6, ranks, shards, late_share, parts)
        gate_up_out, down_out = spread_early(early_own, down_own, hidden_piece)
    else:
        grad_normed = right_product(grad_project, w_in)
        gain_one_grad = jnp.sum(grad_normed * wide_inputs * scale_one, axis=0)
        in_own = jnp.arange(model_width, dtype=jnp.int32) // width == rank
        grad_inputs = norm_back(grad_normed, wide_inputs, scale_one, gain_one) + jnp.where(
            in_own[None], jnp.tile(grad_mixed_cols, (1, ranks)), 0.0
        )
        down_sum = lax.psum_scatter(down_part, "ctx", scatter_dimension=0, tiled=True).astype(F32)
        tokens_grad = lax.psum_scatter(grad_inputs.astype(BF16), "ctx", scatter_dimension=0, tiled=True)[None]
        own_bias = jnp.where(jnp.arange(ranks, dtype=jnp.int32)[:, None] == rank, small[2:3], 0.0)
        small_rows = jnp.concatenate([small[0:2].reshape(1, -1), jnp.pad(own_bias, ((0, 0), (0, LANES)))], axis=0)
        sums = jnp.concatenate(
            [
                jnp.stack([gain_one_grad, gain_two_grad]),
                jnp.pad(small_rows, ((0, 0), (0, model_width - 2 * LANES))),
            ],
            axis=0,
        )
        sums = lax.psum(sums, "ctx")
        down_own, gate_up_own = [lax.all_gather(a, "ctx", axis=0, tiled=False) for a in early_share]
        down_out = down_own.astype(F32).reshape(down_weight.shape)
        gate_up_out = spread_cols(gate_up_own, (hidden_piece, 0, 2 * shards))[0]
        result = own_rows(mixed_low).astype(F32) + down_sum
        block_out = result.astype(BF16)[None]
        branch = result - own_rows(inputs).astype(F32)
        own_valid = own_rows(places_all[3][:, 0] >= 0).astype(F32)
        totals = lax.psum(
            jnp.stack(
                [
                    jnp.sum(own_valid * jnp.sum(result * result, axis=-1)),
                    jnp.sum(own_valid * jnp.sum(branch * branch, axis=-1)),
                ]
            ),
            "ctx",
        )
        share = model_width // shards
        room = 2 * LANES
        gain_pieces = sums[0:2].reshape(2, shards, share).transpose(1, 0, 2)
        gain_pieces = jnp.pad(gain_pieces, ((0, 0), (0, 0), (0, room - share)))
        others = jnp.broadcast_to(sums[None, 2 : 3 + ranks, :room], (shards, 1 + ranks, room))
        piece_sum = lax.psum_scatter(
            jnp.concatenate([gain_pieces, others], axis=1), "fsdp", scatter_dimension=0, tiled=False
        )
        late_own = lax.all_gather(late_share, "ctx", axis=0, tiled=False)
    if plain:
        in_out, out_out, tokens_grad, block_out, forget_out, gains_sum, bias_sum, qk_sum, rms = unpack(
            late_own, forget_all, piece_sum, sums, segment_ids, tokens_grad, block_out, width, local_heads, head_dim
        )
        tokens_grad, block_out = tokens_grad[None], block_out[None]
        bias_sum, forget_out = bias_sum[0], forget_out.T
    else:
        share = model_width // shards
        valid_count = jnp.sum((segment_ids[0] >= 0).astype(F32)) * model_width
        in_out = jnp.concatenate(
            [late_own[c, :, i * padded : i * padded + width] for i in range(4) for c in range(ranks)], axis=1
        ).astype(F32)
        out_out = jnp.concatenate(
            [late_own[c, :, 4 * padded : 4 * padded + width] for c in range(ranks)], axis=1
        ).astype(F32)
        last = 4 * padded + width
        forget_out = jnp.concatenate(
            [late_own[c, :, last : last + local_heads] for c in range(ranks)], axis=1
        ).astype(F32)
        gains_sum = piece_sum[0:2, :share]
        bias_sum = piece_sum[3 : 3 + ranks, :local_heads].reshape(-1)
        qk_sum = piece_sum[2, : 2 * LANES].reshape(2, LANES // head_dim, head_dim).sum(axis=1)
        rms = jnp.sqrt(totals / valid_count)[None]
    return (
        block_out, tokens_grad, gains_sum, in_out, forget_out, bias_sum, qk_sum,
        out_out, gate_up_out, down_out, rms,
    )


def solution(mesh):
    rows = P("fsdp", "ctx", None)
    return jax.shard_map(
        body,
        mesh=mesh,
        in_specs=(
            rows, P("fsdp", None), P("fsdp", None), P(None, "fsdp"), P("fsdp", None), P("fsdp", None),
            P(), P(), P("fsdp", None), P("fsdp", None), P("fsdp", None), rows,
        ),
        out_specs=(
            rows, rows, P(None, "fsdp"), P("fsdp", None), P("fsdp", None), P(), P(),
            P("fsdp", None), P("fsdp", None), P("fsdp", None), P("fsdp", None),
        ),
        check_vma=False,
    )
```

```python
import functools

import jax
import jax.numpy as jnp
from jax import lax
from jax.experimental import pallas as pl
from jax.experimental.pallas import tpu as pltpu
from jax.sharding import PartitionSpec as P

EPS = 1e-06
SCALE = 0.125
LANES = 128
VMEM_LIMIT = 60 << 20
F32 = jnp.float32
BF16 = jnp.bfloat16


MESH = pl.DeviceIdType.MESH
ANY = pl.BlockSpec(memory_space=pltpu.HBM)


def rms_scale(values):
    return lax.rsqrt(jnp.mean(values * values, axis=-1, keepdims=True) + EPS)


def norm_back(grad_normed, values, scale_values, gain_values):
    scaled = grad_normed * gain_values
    cubed = scale_values * scale_values * scale_values
    return scale_values * scaled - values * cubed * jnp.mean(
        scaled * values, axis=-1, keepdims=True
    )


def dot(left, right):
    return lax.dot_general(
        left, right, (((1,), (0,)), ((), ())), preferred_element_type=F32
    )


def left_product(left, right):
    return lax.dot_general(
        left, right, (((0,), (0,)), ((), ())), preferred_element_type=F32
    )


def right_product(left, right):
    return lax.dot_general(
        left, right, (((1,), (1,)), ((), ())), preferred_element_type=F32
    )


def split_three(values):
    high = values.astype(BF16).astype(F32)
    rest = values - high
    middle = rest.astype(BF16).astype(F32)
    return high, middle, rest - middle


def lane_ids(rows, lanes=LANES):
    return lax.broadcasted_iota(jnp.int32, (rows, lanes), 1)


def pick_lane(values, lanes, index):
    return jnp.sum(jnp.where(lanes == index, values, 0.0), axis=-1, keepdims=True)


def turns(rows, chunk, unroll=False):
    def decorate(body):
        @pl.loop(0, rows // chunk, unroll=rows // chunk if unroll else None)
        def _(turn):
            body(pl.ds(pl.multiple_of(turn * chunk, chunk), chunk))

    return decorate


def fill_mask(chunk, pos_row, pos_col, seg_row, seg_col, mask):
    @turns(mask.shape[0], chunk)
    def _(part):
        allowed = (pos_row[0:1, :] <= pos_col[part, :]) & (seg_row[0:1, :] == seg_col[part, :])
        mask[part, :] = jnp.where(allowed, 0.0, -jnp.inf)


def fill_prefix(chunk, heads, pos_row, pos_col, logits, prefix):
    rows = prefix.shape[0]
    log_forget = jax.nn.log_sigmoid(jnp.where(lane_ids(rows) < heads, logits, 0.0))
    high, middle, low = split_three(log_forget)

    @turns(rows, chunk)
    def _(part):
        before = jnp.where(pos_row[0:1, :] <= pos_col[part, :], 1.0, 0.0).astype(BF16)
        prefix[part, :] = (
            dot(before, high.astype(BF16)) + dot(before, middle.astype(BF16)) + dot(before, low.astype(BF16))
        )


def attend_block(
    head, chunk, index, query, key, value, gate, gains, mask, prefix,
    gated, attended, wide_query, wide_key, wide_value,
):
    rows = mask.shape[0]
    lanes = lane_ids(rows)
    half = lane_ids(rows, head)
    short = lane_ids(chunk, head)
    for side in range(LANES // head):
        here = slice(side * head, (side + 1) * head)
        column = pick_lane(prefix[...], lanes, (LANES // head) * index + side)
        high, middle, low = split_three(column)
        wide = jnp.where(half == 1, high, 0.0)
        wide = jnp.where(half == 2, middle, wide)
        wide = jnp.where(half == 3, low, wide)
        query_rest = jnp.where((half >= 4) & (half < 7), 1.0, wide)
        wide = jnp.where(half == 4, -high, 0.0)
        wide = jnp.where(half == 5, -middle, wide)
        wide = jnp.where(half == 6, -low, wide)
        ones = ((half >= 1) & (half < 4)) | ((half >= 7) & (half < 10))
        key_rest = jnp.where(ones, 1.0, wide)
        raw = query[:, here]
        normed = (raw * rms_scale(raw) * gains[0:1, here]).astype(BF16)
        wide_query[side, :, 0:head] = (normed.astype(F32) * SCALE).astype(BF16)
        wide_query[side, :, head:LANES] = query_rest.astype(BF16)
        raw = key[:, here]
        wide_key[side, :, 0:head] = (raw * rms_scale(raw) * gains[1:2, here]).astype(BF16)
        wide_key[side, :, head:LANES] = key_rest.astype(BF16)
        wide_value[side, :, 0:head] = value[:, here].astype(BF16)
        wide_value[side, :, head:LANES] = jnp.where(half < 3, 1.0, 0.0).astype(BF16)

        @turns(rows, chunk, unroll=True)
        def _(part):
            scores = right_product(wide_query[side, part, :], wide_key[side]) + mask[part, :]
            expos = jnp.exp(scores)
            total = jnp.sum(expos, axis=-1, keepdims=True)
            result = dot(expos.astype(BF16), wide_value[side])[:, 0:head] / total
            attended[part, here] = result
            gated[part, here] = (result * jax.nn.sigmoid(gate(part)[:, here])).astype(BF16)
            high, middle, low = split_three(-jnp.log(total))
            rest = wide_query[side, part, head:LANES].astype(F32)
            rest = jnp.where(short == 7, high, rest)
            rest = jnp.where(short == 8, middle, rest)
            rest = jnp.where(short == 9, low, rest)
            wide_query[side, part, head:LANES] = rest.astype(BF16)


def attend_kernel(
    head, chunk, heads,
    pos_row, pos_col, seg_row, seg_col, bias, gains, query, key, value, gate, forget,
    gated, attended, wide_query, wide_key, wide_value,
    mask, prefix,
):
    @pl.when(pl.program_id(0) == 0)
    def _():
        fill_mask(chunk, pos_row, pos_col, seg_row, seg_col, mask)
        fill_prefix(chunk, heads, pos_row, pos_col, forget[...] + bias[0:1, :], prefix)

    attend_block(
        head, chunk, pl.program_id(0), query, key, value, lambda part: gate[part, :], gains, mask, prefix,
        gated, attended.at[0], wide_query, wide_key, wide_value,
    )


def attend_back_kernel(
    head, chunk, width, heads, ranks, shards,
    pos_row, pos_col, seg_row, seg_col, bias, gains, query, key, gate, forget,
    attended, wide_query, wide_key, wide_value, grad_gated, *rest,
):
    if ranks:
        aside, normed, out_grad, blocks, grad_project, small, aside_in, late, share, forget_grad = rest[:10]
        mask, wide_grad, grad_query, grad_key, grad_value, grad_prefix = rest[10:16]
        normed_in, out_in, aside_own, blocks_in, side_in, kept, from_below, from_above = rest[16:24]
        late_all, load_sem, save_sem = rest[24:27]
        sems = rest[27:29]
        over_shards = ShardSum(shards, blocks_in, side_in, kept, from_below, from_above, rest[29:])

        def loads():
            own = rows_of(aside, lax.axis_index("ctx"), aside_in.shape[1])
            for n, pair in enumerate(((normed, normed_in), (out_grad, out_in), (own, aside_own))):
                yield pltpu.make_async_copy(*pair, load_sem.at[n])

    else:
        grad_project, small, mask, wide_grad, grad_query, grad_key, grad_value, grad_prefix = rest
    step = pl.program_id(0)
    steps = pl.num_programs(0)

    def aside_copies():
        send_sem, recv_sem = sems
        rank = lax.axis_index("ctx")
        size = aside_in.shape[1]
        for distance in range(1, ranks):
            other = rank ^ distance
            yield to_rank(
                rows_of(aside, other, size), aside_in.at[rank],
                send_sem.at[distance - 1], recv_sem.at[distance - 1], other,
            )

    def sum_stage(hook):
        if not ranks:
            return
        now = (LANES // head) * step + hook
        for stage in range(over_shards.layers - 1):

            @pl.when(now == 2 + 2 * stage)
            def _():
                if stage == 0:
                    over_shards.presum()
                else:
                    over_shards.receive(stage - 1)
                over_shards.send(stage)

    if ranks:

        @pl.when(step == 0)
        def _():
            rank = lax.axis_index("ctx")
            greet([{"ctx": rank ^ distance} for distance in range(1, ranks)], over_shards)
            early = pltpu.make_async_copy(blocks, blocks_in, load_sem.at[4])
            early.start()
            for copy in aside_copies():
                copy.start()
            for copy in loads():
                copy.start()
            early.wait()
            over_shards.start()

    rows = query.shape[0]
    lanes = lane_ids(rows)
    half = lane_ids(rows, head)

    @pl.when(step == 0)
    def _():
        @pl.loop(0, rows // chunk)
        def _(turn):
            part = pl.ds(pl.multiple_of(turn * chunk, chunk), chunk)
            after = pos_row[0:1, :] >= pos_col[part, :]
            same = seg_row[0:1, :] == seg_col[part, :]
            mask[part, :] = jnp.where(after & same, 0.0, -jnp.inf)
        grad_prefix[...] = jnp.zeros_like(grad_prefix)
        small[...] = jnp.zeros_like(small)

    for side in range(LANES // head):
        sum_stage(side)
        here = pl.ds(side * head, head)

        def column(part):
            return pl.ds(pl.multiple_of(part * width + step * LANES, LANES), LANES)

        sig = jax.nn.sigmoid(gate[:, here])
        grad_in = grad_gated[:, here]
        result = attended[0, :, here]
        grad_result = (grad_in * sig).astype(BF16)
        grad_gate = (grad_in * result * sig * (1.0 - sig)).astype(BF16)
        inner = -jnp.sum(grad_result.astype(F32) * result, axis=-1, keepdims=True)
        high, middle, low = split_three(inner)
        rest = jnp.where(half == 0, high, 0.0)
        rest = jnp.where(half == 1, middle, rest)
        rest = jnp.where(half == 2, low, rest)
        wide_grad[:, 0:head] = grad_result
        wide_grad[:, head:LANES] = rest.astype(BF16)
        grad_query[...] = jnp.zeros_like(grad_query)
        @turns(rows, chunk, unroll=True)
        def _(part):
            scores = right_product(wide_key[side, part, :], wide_query[side]) + mask[part, :]
            probs = jnp.exp(scores)
            outer = right_product(wide_value[side, part, :], wide_grad[...])
            grad_scores = (probs * outer).astype(BF16)
            grad_key[part, :] = dot(grad_scores, wide_query[side])
            grad_value[part, :] = dot(probs.astype(BF16), wide_grad[...])
            grad_query[...] += left_product(wide_key[side, part, :], grad_scores)
        from_query = grad_query[...].T
        from_key = grad_key[...]
        change = pick_lane(from_query, lanes, head + 1) - pick_lane(from_key, lanes, head + 4)
        grad_prefix[...] += jnp.where(lanes == (LANES // head) * step + side, change, 0.0)

        raw = query[:, here]
        scale_raw = rms_scale(raw)
        grad_normed = from_query[:, 0:head] * SCALE
        grad_raw_query = norm_back(grad_normed, raw, scale_raw, gains[0:1, here])
        small[0:1, here] += jnp.sum(grad_normed * raw * scale_raw, axis=0, keepdims=True)
        raw = key[:, here]
        scale_raw = rms_scale(raw)
        grad_normed = from_key[:, 0:head]
        grad_raw_key = norm_back(grad_normed, raw, scale_raw, gains[1:2, here])
        small[1:2, here] += jnp.sum(grad_normed * raw * scale_raw, axis=0, keepdims=True)
        wide_grad[:, here] = grad_gate
        for part_id, piece in enumerate(
            (grad_raw_query.astype(BF16), grad_raw_key.astype(BF16), grad_value[:, 0:head].astype(BF16), grad_gate)
        ):
            if side == 0:
                grad_project[:, column(part_id)] = jnp.concatenate([piece, piece], axis=1)
            else:
                keep = grad_project[:, column(part_id)]
                both = jnp.concatenate([piece, piece], axis=1)
                grad_project[:, column(part_id)] = jnp.where(lanes < head, keep, both)

    @pl.when(step == steps - 1)
    def _():
        high, middle, low = split_three(grad_prefix[...])
        short = lane_ids(chunk)

        @pl.loop(0, rows // chunk)
        def _(turn):
            part = pl.ds(pl.multiple_of(turn * chunk, chunk), chunk)
            after = jnp.where(pos_row[0:1, :] >= pos_col[part, :], 1.0, 0.0).astype(BF16)
            total = dot(after, high.astype(BF16)) + dot(after, middle.astype(BF16)) + dot(after, low.astype(BF16))
            grad_logit = total * jax.nn.sigmoid(-(forget[part, :] + bias[0:1, :]))
            grad_logit = jnp.where(short < heads, grad_logit, 0.0).astype(BF16)
            grad_project[part, 4 * width : 4 * width + LANES] = grad_logit
            small[2:3, :] += jnp.sum(grad_logit.astype(F32), axis=0, keepdims=True)

        if ranks:
            for copy in loads():
                copy.wait()
            keep = pltpu.make_async_copy(aside_own, aside_in.at[lax.axis_index("ctx")], load_sem.at[3])
            keep.start()
            late_stages = [n for n in range(over_shards.layers - 1) if 2 + 2 * n >= heads]
            for stage in late_stages:
                over_shards.receive(stage - 1)
                over_shards.send(stage)
            ends = 4 * width, 4 * width + out_grad.shape[1]
            late_all[:, ends[0] : ends[1]] = out_in[...]
            piece = 2 * LANES

            def save(turn, size=piece):
                cols = pl.ds(pl.multiple_of(turn * piece, LANES), size)
                return pltpu.make_async_copy(late_all.at[:, cols], late.at[:, cols], save_sem.at[turn])

            count = 4 * width // piece
            rest_save = pltpu.make_async_copy(
                late_all.at[:, pl.ds(ends[0], late.shape[1] - ends[0])],
                late.at[:, pl.ds(ends[0], late.shape[1] - ends[0])],
                save_sem.at[count],
            )

            def product(into, cols):
                @turns(late.shape[0], 3 * chunk if late.shape[0] % (3 * chunk) == 0 else chunk)
                def _(part):
                    late_all[part, into] = dot(normed_in[part, :], grad_project[:, cols]).astype(BF16)

            rest_save.start()
            turned = grad_project[:, ends[0] : ends[0] + LANES].astype(F32).T[0:8, :]
            forget_grad[...] = right_product(turned.astype(BF16), normed_in[...])

            @pl.loop(0, count)
            def _(turn):
                cols = pl.ds(pl.multiple_of(turn * piece, LANES), piece)
                product(cols, cols)
                save(turn).start()

            for copy in aside_copies():
                copy.wait()
            keep.wait()
            over_shards.receive(over_shards.layers - 2)
            share[...] = kept[over_shards.layer]
            over_shards.sent()
            rest_save.wait()

            @pl.loop(0, count)
            def _(turn):
                save(turn).wait()


def pick_chunk(rows):
    return 256 if rows % 256 == 0 else 128


def whole(shape):
    return pl.BlockSpec(shape, lambda step: tuple(0 for _ in shape))


def attend(project, places, bias, gains, head, width, heads):
    rows = project.shape[0]
    steps = width // LANES
    per = LANES // head
    chunk = pick_chunk(rows)

    def part(index):
        return pl.BlockSpec((rows, LANES), lambda step: (0, index * steps + step))

    own = pl.BlockSpec((rows, LANES), lambda step: (0, step))
    wide = pl.BlockSpec((per, rows, LANES), lambda step: (step, 0, 0))
    forget = pl.BlockSpec((rows, LANES), lambda step: (0, 4 * steps))
    wide_shape = jax.ShapeDtypeStruct((per * steps, rows, LANES), BF16)
    return pl.pallas_call(
        functools.partial(attend_kernel, head, chunk, heads),
        grid=(steps,),
        in_specs=[whole(p.shape) for p in places] + [whole(bias.shape), whole(gains.shape)]
        + [part(0), part(1), part(2), part(3), forget],
        out_specs=[own, pl.BlockSpec((1, rows, LANES), lambda step: (step, 0, 0)), wide, wide, wide],
        out_shape=[
            jax.ShapeDtypeStruct((rows, width), BF16),
            jax.ShapeDtypeStruct((steps, rows, LANES), F32),
            wide_shape, wide_shape, wide_shape,
        ],
        scratch_shapes=[pltpu.VMEM((rows, rows), F32), pltpu.VMEM((rows, LANES), F32)],
        compiler_params=pltpu.CompilerParams(vmem_limit_bytes=VMEM_LIMIT),
        name="attend",
    )(*places, bias, gains, project, project, project, project, project)


def attend_back(project, places, bias, gains, attended, wides, grad_gated, beside, ranks, shards, head, width, heads):
    rows = project.shape[0]
    steps = width // LANES
    per = LANES // head
    chunk = pick_chunk(rows)

    def part(index):
        return pl.BlockSpec((rows, LANES), lambda step: (0, index * steps + step))

    own = pl.BlockSpec((rows, LANES), lambda step: (0, step))
    block = pl.BlockSpec((1, rows, LANES), lambda step: (step, 0, 0))
    wide = pl.BlockSpec((per, rows, LANES), lambda step: (step, 0, 0))
    forget = pl.BlockSpec((rows, LANES), lambda step: (0, 4 * steps))
    total = 4 * width + LANES
    out_specs = [whole((rows, total)), whole((8, LANES))]
    out_shape = [jax.ShapeDtypeStruct((rows, total), BF16), jax.ShapeDtypeStruct((8, LANES), F32)]
    scratch = [
        pltpu.VMEM((rows, rows), F32),
        pltpu.VMEM((rows, LANES), BF16),
        pltpu.VMEM((LANES, rows), F32),
        pltpu.VMEM((rows, LANES), F32),
        pltpu.VMEM((rows, LANES), F32),
        pltpu.VMEM((rows, LANES), F32),
    ]
    if ranks:
        aside, normed, out_grad, blocks = beside
        share = (blocks.shape[0] // shards, blocks.shape[1])
        sum_blocks, sum_sems = shard_sum_scratch(shards, *share)
        model, late_cols = normed.shape[0], 4 * width + out_grad.shape[1]
        out_specs += [ANY, ANY, whole(share), whole((8, model))]
        out_shape += [
            jax.ShapeDtypeStruct((ranks, aside.shape[0] // ranks, aside.shape[1]), BF16),
            jax.ShapeDtypeStruct((model, late_cols), BF16),
            jax.ShapeDtypeStruct(share, BF16),
            jax.ShapeDtypeStruct((8, model), F32),
        ]
        scratch += [
            pltpu.VMEM(normed.shape, BF16),
            pltpu.VMEM(out_grad.shape, BF16),
            pltpu.VMEM((aside.shape[0] // ranks, aside.shape[1]), BF16),
            pltpu.VMEM(blocks.shape, BF16),
            *sum_blocks,
            pltpu.VMEM((model, late_cols), BF16),
            pltpu.SemaphoreType.DMA((5,)),
            pltpu.SemaphoreType.DMA((4 * width // (2 * LANES) + 1,)),
            pltpu.SemaphoreType.DMA((ranks - 1,)),
            pltpu.SemaphoreType.DMA((ranks - 1,)),
            *sum_sems,
        ]
    return pl.pallas_call(
        functools.partial(attend_back_kernel, head, chunk, width, heads, ranks, shards),
        grid=(steps,),
        in_specs=[whole(p.shape) for p in places] + [whole(bias.shape), whole(gains.shape)]
        + [part(0), part(1), part(3), forget, block, wide, wide, wide, own] + [ANY] * len(beside),
        out_specs=out_specs,
        out_shape=out_shape,
        scratch_shapes=scratch,
        compiler_params=pltpu.CompilerParams(
            collective_id=5 if ranks else None, has_side_effects=ranks > 0, vmem_limit_bytes=VMEM_LIMIT
        ),
        name="attend_back",
    )(*places, bias, gains, project, project, project, project, attended, *wides, grad_gated, *beside)


def greet(peers, line=None):
    barrier = pltpu.get_barrier_semaphore()
    if line is not None:
        peers = peers + [line.sibling]
    for peer in peers:
        pl.semaphore_signal(barrier, inc=1, device_id=peer, device_id_type=MESH)
    if line is not None:
        for there, peer in ((line.has_above, line.above), (line.has_below, line.below)):

            @pl.when(there)
            def _():
                pl.semaphore_signal(barrier, inc=1, device_id=peer, device_id_type=MESH)

    count = len(peers)
    if line is not None:
        last = line.layers - 1
        count = count + (1 - line.layer // last) + (line.layer + last) // line.layers
    pl.semaphore_wait(barrier, count)


class Line:
    def __init__(self, shards, source, target, sems):
        self.shard = lax.axis_index("fsdp")
        self.layers = shards // 2
        self.layer, self.core = self.shard // 2, self.shard % 2
        self.sibling = {"fsdp": self.shard ^ 1}
        self.above, self.below = {"fsdp": self.shard + 2}, {"fsdp": self.shard - 2}
        self.has_above, self.has_below = self.layer < self.layers - 1, self.layer > 0
        self.source, self.target = source, target
        self.rows = target.shape[0] // shards
        self.line_send, self.line_recv, self.side_send, self.side_recv, self.own_sem = sems

    def block(self, owner):
        return rows_of(self.target, owner, self.rows)

    def line(self, owner_layer, peer, way, own=False):
        here = self.block(owner_layer * 2 + self.core)
        return pltpu.make_async_remote_copy(
            self.source if own else here, here, self.line_send.at[way, owner_layer], self.line_recv.at[owner_layer],
            device_id=peer, device_id_type=MESH,
        )

    def side(self, owner_layer, owner_core, own=False):
        here = self.block(owner_layer * 2 + owner_core)
        return pltpu.make_async_remote_copy(
            self.source if own else here, here, self.side_send.at[owner_layer], self.side_recv.at[owner_layer],
            device_id=self.sibling, device_id_type=MESH,
        )

    def start(self):
        own = self.source is not None

        @pl.when(self.has_above)
        def _():
            self.line(self.layer, self.above, 0, own).start()

        @pl.when(self.has_below)
        def _():
            self.line(self.layer, self.below, 1, own).start()

        self.side(self.layer, self.core, own).start()
        if own:
            self.keep = pltpu.make_async_copy(self.source, self.block(self.shard), self.own_sem)
            self.keep.start()

    def step(self, distance):
        lower, upper = self.layer - distance, self.layer + distance

        @pl.when(lower >= 0)
        def _():
            self.line(lower, self.below, 1).wait_recv()

            @pl.when(self.has_above)
            def _():
                self.line(lower, self.above, 0).start()

            self.side(lower, self.core).start()

        @pl.when(upper < self.layers)
        def _():
            self.line(upper, self.above, 0).wait_recv()

            @pl.when(self.has_below)
            def _():
                self.line(upper, self.below, 1).start()

            self.side(upper, self.core).start()

    def from_side(self, owner_layer):
        self.side(owner_layer, 1 - self.core).wait_recv()

    def finish(self):
        self.keep.wait()
        for owner_layer in range(self.layers):
            self.from_side(owner_layer)
        self.sent()

    def sent(self):
        for owner_layer in range(self.layers):
            self.side(owner_layer, self.core).wait_send()

            @pl.when(self.has_above & (owner_layer <= self.layer))
            def _():
                self.line(owner_layer, self.above, 0).wait_send()

            @pl.when(self.has_below & (owner_layer >= self.layer))
            def _():
                self.line(owner_layer, self.below, 1).wait_send()

    def near_finish(self):
        self.keep.wait()
        self.from_side(self.layer)
        self.side(self.layer, self.core).wait_send()

        @pl.when(self.has_below)
        def _():
            self.line(self.layer - 1, self.below, 1).wait_recv()
            self.line(self.layer, self.below, 1).wait_send()

        @pl.when(self.has_above)
        def _():
            self.line(self.layer + 1, self.above, 0).wait_recv()
            self.line(self.layer, self.above, 0).wait_send()

    def near_load(self, near, sems, number):
        if number == 0:
            chip = 2 * self.rows
            source, target = rows_of(near, self.layer, chip), rows_of(self.target, self.layer, chip)
        else:
            owner = self.shard + (-2, 2)[number - 1]
            source, target = rows_of(near, owner, self.rows), self.block(owner)
        return pltpu.make_async_copy(source, target, sems.at[number])

    def near_start(self, near, sems):
        self.near_load(near, sems, 0).start()

        @pl.when(self.has_below)
        def _():
            self.near_load(near, sems, 1).start()

        @pl.when(self.has_above)
        def _():
            self.near_load(near, sems, 2).start()

    def resume(self, near, sems):
        @pl.when(self.has_below)
        def _():
            self.near_load(near, sems, 1).wait()

            @pl.when(self.has_above)
            def _():
                self.line(self.layer - 1, self.above, 0).start()

            self.side(self.layer - 1, self.core).start()

        @pl.when(self.has_above)
        def _():
            self.near_load(near, sems, 2).wait()

            @pl.when(self.has_below)
            def _():
                self.line(self.layer + 1, self.below, 1).start()

            self.side(self.layer + 1, self.core).start()

    def resumed_sent(self):
        for owner_layer in range(self.layers):

            @pl.when(owner_layer != self.layer)
            def _():
                self.side(owner_layer, self.core).wait_send()

            @pl.when(self.has_above & (owner_layer < self.layer))
            def _():
                self.line(owner_layer, self.above, 0).wait_send()

            @pl.when(self.has_below & (owner_layer > self.layer))
            def _():
                self.line(owner_layer, self.below, 1).wait_send()


def line_scratch(shards):
    layers = shards // 2
    return [
        pltpu.SemaphoreType.DMA((2, layers)),
        pltpu.SemaphoreType.DMA((layers,)),
        pltpu.SemaphoreType.DMA((layers,)),
        pltpu.SemaphoreType.DMA((layers,)),
        pltpu.SemaphoreType.DMA,
    ]


class Relay:
    def __init__(self, rank, source, place, send_sem, recv_sem, own_sem):
        self.rank, self.source, self.place = rank, source, place
        self.send_sem, self.recv_sem, self.own_sem = send_sem, recv_sem, own_sem

    def copy(self, number):
        me = self.rank
        source, place, distance = (
            lambda: (self.source(0), self.place(me, 0), 1),
            lambda: (self.source(1), self.place(me, 1), 2),
            lambda: (self.source(1), self.place(me, 1), 1),
            lambda: (self.source(0), self.place(me, 0), 2),
            lambda: (self.place(me ^ 1, 0), self.place(me ^ 1, 0), 2),
            lambda: (self.place(me ^ 2, 1), self.place(me ^ 2, 1), 1),
        )[number]()
        return pltpu.make_async_remote_copy(
            source, place, self.send_sem.at[number], self.recv_sem.at[number],
            device_id={"ctx": me ^ distance}, device_id_type=MESH,
        )

    def own(self, h):
        return pltpu.make_async_copy(self.source(h), self.place(self.rank, h), self.own_sem.at[h])

    def start(self, keep=True):
        for number in range(4):
            self.copy(number).start()
        if keep:
            for h in range(2):
                self.own(h).start()

    def forward(self):
        for number in range(2):
            self.copy(number).wait_recv()
            self.copy(number + 4).start()

    def arrive(self):
        for number in range(2, 6):
            self.copy(number).wait_recv()

    def finish(self, arrive=True, keep=True):
        if keep:
            for h in range(2):
                self.own(h).wait()
        if arrive:
            self.arrive()
        for number in range(6):
            self.copy(number).wait_send()


def rows_of(ref, index, size):
    return ref.at[pl.ds(pl.multiple_of(index * size, 16), size), :]


def cols_of(ref, index, size):
    return ref.at[:, pl.ds(pl.multiple_of(index * size, LANES), size)]


def relay_ops(mode, rank, source, target, sems):
    rows, cols = source.shape
    half = rows // 2

    def part(h):
        return source.at[pl.ds(h * half, half), :]

    def place(block, h):
        if mode == "gather_rows":
            return target.at[pl.ds(pl.multiple_of(block * rows + h * half, 16), half), :]
        if mode == "gather_cols":
            return target.at[pl.ds(h * half, half), pl.ds(pl.multiple_of(block * cols, LANES), cols)]
        return target.at[block, pl.ds(h * half, half), :]

    return Relay(rank, part, place, *sems)


VMEM_WHOLE = pl.BlockSpec(memory_space=pltpu.VMEM)


def to_rank(source, target, send, recv, other):
    return pltpu.make_async_remote_copy(
        source, target, send, recv, device_id={"ctx": other}, device_id_type=MESH
    )


FRONT_LOADS = 6
FRONT_SAVES = 12


def front_kernel(
    shards, head, heads, width, piece, chunk,
    tokens, cotangent, weight, weight_out, other, down, forget_weight, norm_gains, qk_gains, segments, order, forget_bias,
    inputs, grad_low, w_in, w_out, w_gate_up, normed, project, gated, attended, wide_query, wide_key, wide_value,
    mixed, down_near, normed_two, turned, gain_rows, pos_row, pos_col, seg_row, seg_col, bias, gains,
    weight_all, other_all, out_all, own_x, own_g, own_in, own_pick, own_out, x_all, in_all, hn_all, proj_all, mask, prefix,
    gated_all, attended_all, query_all, key_all, value_all, out_cols, scale_one, y_own, own_down,
    mixed_all, h2_all, turned_all,
    send_sem, recv_sem, own_sem, load_sem, save_sem, *line_sems,
):
    rank = lax.axis_index("ctx")
    ranks = lax.axis_size("ctx")
    model = weight.shape[1] // 4
    rows = x_all.shape[0]
    steps = width // LANES
    tail_at = 4 * width
    loads = [
        pltpu.make_async_copy(a, b, load_sem.at[n])
        for n, (a, b) in enumerate(
            (
                (weight, weight_all), (other, other_all), (weight_out, out_all), (tokens, own_x), (cotangent, own_g),
                (rows_of(down, rank, own_down.shape[0]), own_down),
            )
        )
    ]
    saves = [
        pltpu.make_async_copy(a, b, save_sem.at[n])
        for n, (a, b) in enumerate(
            (
                (x_all, inputs), (in_all, w_in), (hn_all, normed), (proj_all, project), (query_all, wide_query),
                (key_all, wide_key), (value_all, wide_value), (attended_all, attended), (gated_all, gated),
                (mixed_all, mixed), (h2_all, normed_two), (turned_all, turned),
            )
        )
    ]
    for copy in loads:
        copy.start()
    per = len(line_sems) // 4
    in_line = Line(shards, own_in, in_all, line_sems[:per])
    out_line = Line(shards, own_out, out_cols, line_sems[per : 2 * per])
    up_line = Line(shards, own_pick, w_gate_up, line_sems[2 * per : 3 * per])
    down_line = Line(shards, own_down, down_near, line_sems[3 * per :])
    greet([{"ctx": rank ^ 1}, {"ctx": rank ^ 2}], in_line)

    def sems(n):
        return send_sem.at[n], recv_sem.at[n], own_sem.at[n]

    first = relay_ops("gather_rows", rank, own_x, x_all, sems(0))
    second = relay_ops("gather_rows", rank, own_g, grad_low, sems(1))

    def cols(start, size):
        return pl.ds(pl.multiple_of(start, LANES), size)

    loads[0].wait()
    for i in range(4):
        own_in[:, i * width : (i + 1) * width] = weight_all[:, cols(i * model + rank * width, width)]
    total_heads = forget_weight.shape[0]
    from_head = lax.broadcasted_iota(jnp.int32, (total_heads, LANES), 0)
    to_lane = lax.broadcasted_iota(jnp.int32, (total_heads, LANES), 1)
    chosen = jnp.where((to_lane < heads) & (from_head == rank * heads + to_lane), 1.0, 0.0).astype(BF16)
    from_gain = lax.broadcasted_iota(jnp.int32, (2, LANES), 0)
    to_lane = lax.broadcasted_iota(jnp.int32, (2, LANES), 1)
    chosen_gain = jnp.where(to_lane == heads + from_gain, 1.0, 0.0).astype(BF16)
    tail = left_product(forget_weight[...], chosen) + left_product(norm_gains[...], chosen_gain)
    own_in[:, tail_at : tail_at + LANES] = tail.astype(BF16)
    in_line.start()
    loads[3].wait()
    first.start()
    loads[1].wait()
    for i in range(own_pick.shape[1] // piece):
        own_pick[:, i * piece : (i + 1) * piece] = other_all[:, cols((i * ranks + rank) * piece, piece)]
    loads[2].wait()
    own_out[...] = out_all[:, cols(rank * width, width)]
    count = order.shape[1]
    length = rows // count
    row_ids = lax.broadcasted_iota(jnp.int32, (rows, LANES), 0)
    lane_id = lax.broadcasted_iota(jnp.int32, (8, rows), 1)
    tall = jnp.zeros((rows, LANES), jnp.int32)
    flat = jnp.zeros((8, rows), jnp.int32)
    for block in range(count):
        start = order[0, block] * length - block * length
        tall = jnp.where((row_ids >= block * length) & (row_ids < (block + 1) * length), row_ids + start, tall)
        flat = jnp.where((lane_id >= block * length) & (lane_id < (block + 1) * length), lane_id + start, flat)
    pos_col[...] = tall[:, 0:1].astype(F32)
    pos_row[...] = flat[0:1, :].astype(F32)
    true_segments = segments[0:1, :].astype(F32)

    @turns(rows, chunk)
    def _(part):
        true_place = lax.broadcasted_iota(jnp.int32, (chunk, rows), 1).astype(F32)
        own_place = true_place == pos_col[part, :]
        seg_col[part, :] = jnp.sum(jnp.where(own_place, true_segments, 0.0), axis=-1, keepdims=True)

    seg_row[...] = jnp.broadcast_to(seg_col[...], (rows, LANES)).T[0:1, :]
    lane = lax.broadcasted_iota(jnp.int32, (1, LANES), 1)
    bias_row = jnp.zeros((1, LANES), F32)
    for index in range(heads):
        bias_row = jnp.where(lane == index, forget_bias[0, rank * heads + index], bias_row)
    bias[...] = bias_row
    for side in range(LANES // head):
        gains[:, side * head : (side + 1) * head] = qk_gains[...]
    fill_mask(chunk, pos_row, pos_col, seg_row, seg_col, mask)
    proj_all[...] = jnp.zeros_like(proj_all)
    gain_rows[...] = jnp.zeros_like(gain_rows)
    first.forward()
    loads[4].wait()
    second.start()
    in_line.step(1)
    first.finish()
    saves[0].start()

    @turns(rows, chunk)
    def _(part):
        values = x_all[part, :].astype(F32)
        scale_one[part, :] = jnp.broadcast_to(rms_scale(values), (chunk, LANES))

    def consume(layer):
        in_line.from_side(layer)
        size = 2 * in_line.rows
        here = cols(layer * size, size)
        tail_block = in_all[here, tail_at : tail_at + LANES].astype(F32).T
        gain_rows[0:1, here] = tail_block[heads : heads + 1, :]
        gain_rows[1:2, here] = tail_block[heads + 1 : heads + 2, :]

        @turns(rows, chunk)
        def _(part):
            values = x_all[part, here].astype(F32) * scale_one[part, 0:1] * gain_rows[0:1, here]
            hn_all[here, part] = values.T.astype(BF16)
            proj_all[part, :] += dot(values.astype(BF16), in_all[here, :])

    def consume_at(distance):
        lower, upper = in_line.layer - distance, in_line.layer + distance

        @pl.when(lower >= 0)
        def _():
            consume(lower)

        @pl.when(upper < in_line.layers)
        def _():
            consume(upper)

    in_line.keep.wait()
    consume(in_line.layer)
    consume_at(1)
    second.forward()
    for distance in range(2, in_line.layers):
        in_line.step(distance)
        if distance == in_line.layers - 1:
            out_line.start()
            up_line.start()
        consume_at(distance)

    for n in (1, 2, 3):
        saves[n].start()
    out_line.step(1)
    fill_prefix(chunk, heads, pos_row, pos_col, proj_all[:, tail_at : tail_at + LANES] + bias[0:1, :], prefix)

    def share(index):
        block = rank * steps + index
        half = rows // 2

        def source(h):
            return gated_all.at[block, pl.ds(h * half, half), :]

        def place(owner, h):
            return gated_all.at[owner * steps + index, pl.ds(h * half, half), :]

        return Relay(rank, source, place, send_sem.at[2 + index], recv_sem.at[2 + index], None)

    per_block = LANES // head

    @pl.loop(0, steps)
    def _(index):
        def lanes_of(part_id):
            return proj_all[:, cols(part_id * width + index * LANES, LANES)]

        def gate(part):
            return proj_all[part, cols(3 * width + index * LANES, LANES)]

        group = pl.ds(index * per_block, per_block)
        attend_block(
            head, chunk, index, lanes_of(0), lanes_of(1), lanes_of(2), gate, gains, mask, prefix,
            gated_all.at[rank * steps + index], attended_all.at[index],
            query_all.at[group], key_all.at[group], value_all.at[group],
        )
        share(index).start(keep=False)

        @pl.when(index == 0)
        def _():
            out_line.step(2)

        @pl.when(index > 0)
        def _():
            share(index - 1).forward()

    up_line.step(1)
    out_line.step(3)
    share(steps - 1).forward()
    for n in (4, 5, 6, 7):
        saves[n].start()
    for index in range(steps):
        share(index).arrive()
    saves[8].start()
    out_line.keep.wait()
    for layer in range(out_line.layers):
        out_line.from_side(layer)
    save_out = pltpu.make_async_copy(out_cols, w_out, save_sem.at[len(saves)])
    save_out.start()

    third = relay_ops("gather_cols", rank, y_own, mixed_all, sems(2 + steps))

    @turns(rows, chunk)
    def _(part):
        total = x_all[part, cols(rank * width, width)].astype(F32)
        for block in range(gated_all.shape[0]):
            total = total + dot(gated_all[block, part, :], out_cols[block * LANES : (block + 1) * LANES, :])
        y_own[part, :] = total.astype(BF16)

    third.start()
    third.forward()
    up_line.step(2)
    loads[5].wait()
    down_line.start()
    third.finish()
    saves[9].start()

    @turns(rows, chunk)
    def _(part):
        values = mixed_all[part, :].astype(F32)
        low = values * rms_scale(values) * gain_rows[1:2, :]
        h2_all[part, :] = low.astype(BF16)
        turned_all[:, part] = low.T.astype(BF16)

    saves[10].start()
    saves[11].start()
    for distance in range(3, up_line.layers):
        up_line.step(distance)
    up_line.finish()
    down_line.near_finish()
    out_line.sent()
    in_line.sent()
    second.finish()
    for index in range(steps):
        share(index).finish(arrive=False, keep=False)
    for copy in saves:
        copy.wait()
    save_out.wait()


def front(
    collective_id, ranks, shards, head, heads, width, piece,
    tokens, cotangent, weight, weight_out, other, down, forget_weight, norm_gains, qk_gains, segments, order, forget_bias,
):
    own_rows, model = tokens.shape
    rows = ranks * own_rows
    chunk = pick_chunk(rows)
    steps, shard_rows = width // LANES, weight.shape[0]
    wide_in = 4 * width + LANES
    other_cols = other.shape[1] // ranks
    wide = (heads, rows, LANES)
    shape, vmem = jax.ShapeDtypeStruct, pltpu.VMEM
    return pl.pallas_call(
        functools.partial(front_kernel, shards, head, heads, width, piece, chunk),
        in_specs=[ANY] * 6 + [VMEM_WHOLE] * 4 + [pl.BlockSpec(memory_space=pltpu.SMEM)] * 2,
        out_specs=[ANY] * 16 + [VMEM_WHOLE] * 7,
        out_shape=[
            shape((rows, model), BF16),
            shape((rows, model), BF16),
            shape((model, wide_in), BF16),
            shape((model, width), BF16),
            shape((model, other_cols), BF16),
            shape((model, rows), BF16),
            shape((rows, wide_in), F32),
            shape((ranks * steps, rows, LANES), BF16),
            shape((steps, rows, LANES), F32),
            shape(wide, BF16), shape(wide, BF16), shape(wide, BF16),
            shape((rows, model), BF16),
            shape((shards * (down.shape[0] // ranks), model), BF16),
            shape((rows, model), BF16),
            shape((model, rows), BF16),
            shape((8, model), F32),
            shape((1, rows), F32), shape((rows, 1), F32), shape((1, rows), F32), shape((rows, 1), F32),
            shape((1, LANES), F32),
            shape((2, LANES), F32),
        ],
        scratch_shapes=[
            vmem(weight.shape, BF16),
            vmem(other.shape, BF16),
            vmem(weight_out.shape, BF16),
            vmem(tokens.shape, BF16),
            vmem(cotangent.shape, BF16),
            vmem((shard_rows, wide_in), BF16),
            vmem((shard_rows, other_cols), BF16),
            vmem((shard_rows, width), BF16),
            vmem((rows, model), BF16),
            vmem((model, wide_in), BF16),
            vmem((model, rows), BF16),
            vmem((rows, wide_in), F32),
            vmem((rows, rows), F32),
            vmem((rows, LANES), F32),
            vmem((ranks * steps, rows, LANES), BF16),
            vmem((steps, rows, LANES), F32),
            vmem(wide, BF16), vmem(wide, BF16), vmem(wide, BF16),
            vmem((model, width), BF16),
            vmem((rows, LANES), F32),
            vmem((rows, width), BF16),
            vmem((down.shape[0] // ranks, model), BF16),
            vmem((rows, model), BF16),
            vmem((rows, model), BF16),
            vmem((model, rows), BF16),
            pltpu.SemaphoreType.DMA((3 + steps, 6)),
            pltpu.SemaphoreType.DMA((3 + steps, 6)),
            pltpu.SemaphoreType.DMA((3 + steps, 2)),
            pltpu.SemaphoreType.DMA((FRONT_LOADS,)),
            pltpu.SemaphoreType.DMA((FRONT_SAVES + 1,)),
        ]
        + 4 * line_scratch(shards),
        compiler_params=pltpu.CompilerParams(
            collective_id=collective_id, has_side_effects=True, vmem_limit_bytes=VMEM_LIMIT
        ),
        cost_estimate=pl.CostEstimate(flops=0, bytes_accessed=300 << 20, transcendentals=0),
        name="front",
    )(
        tokens, cotangent, weight, weight_out, other, down, forget_weight, norm_gains, qk_gains, segments, order, forget_bias
    )


def ffn_kernel(
    shards, chunk,
    normed, turned_from, w_gate_up, cotangent, down_near,
    w_down, hidden, grad_gate_up, grad_weight, grad_down,
    weight_in, cotangent_in, gates, ups, hn, turned, acts, grads, weight_out, down_out,
    load_sem, save_sem, tile_sem, near_sem, *line_sems,
):
    size = gates.shape[1]
    rows, model = normed.shape
    tile = 2 * w_down.shape[0] // shards
    loads = [
        pltpu.make_async_copy(a, b, load_sem.at[n])
        for n, (a, b) in enumerate(
            ((normed, hn), (w_gate_up, weight_in), (cotangent, cotangent_in), (turned_from, turned))
        )
    ]
    saves = [
        pltpu.make_async_copy(a, b, save_sem.at[n])
        for n, (a, b) in enumerate(
            ((acts, hidden), (down_out, grad_down))
        )
    ]
    line = Line(shards, None, w_down, line_sems)
    line.near_start(down_near, near_sem)
    for copy in loads:
        copy.start()
    greet([], line)
    line.resume(down_near, near_sem)
    loads[0].wait()
    loads[1].wait()

    def span(turn, start=0):
        return pl.ds(pl.multiple_of(start + turn * tile, LANES), tile)

    def activate(turn):
        gate = dot(hn[...], weight_in[:, span(turn)])
        up = dot(hn[...], weight_in[:, span(turn, size)])
        gates[:, span(turn)] = gate
        ups[:, span(turn)] = up
        acts[:, span(turn)] = (jax.nn.silu(gate) * up).astype(BF16)

    def down_grad(turn):
        down_out[span(turn), :] = left_product(acts[:, span(turn)], cotangent_in[...]).astype(BF16)

    count = size // tile
    pl.loop(0, count)(activate)
    saves[0].start()
    loads[2].wait()
    loads[3].wait()
    line.near_load(down_near, near_sem, 0).wait()

    def consume(turn):
        grad = right_product(cotangent_in[...], w_down[span(turn), :])
        gate, up = gates[:, span(turn)], ups[:, span(turn)]
        sig = jax.nn.sigmoid(gate)
        grads[:, span(turn)] = (grad * up * sig * (1.0 + gate * (1.0 - sig))).astype(BF16)
        grads[:, span(turn, size)] = (grad * gate * sig).astype(BF16)

        for start in (0, size):
            here = span(turn, start)

            @turns(model, 3 * chunk if model % (3 * chunk) == 0 else chunk)
            def _(part):
                weight_out[part, here] = dot(turned[part, :], grads[:, here]).astype(BF16)

        for copy in tile_saves(turn):
            copy.start()

    def tile_saves(turn):
        for n, start in enumerate((0, size)):
            here = span(turn, start)
            yield pltpu.make_async_copy(grads.at[:, here], grad_gate_up.at[:, here], tile_sem.at[turn, 2 * n])
            yield pltpu.make_async_copy(weight_out.at[:, here], grad_weight.at[:, here], tile_sem.at[turn, 2 * n + 1])

    def consume_at(distance):
        lower, upper = line.layer - distance, line.layer + distance

        @pl.when(lower >= 0)
        def _():
            line.from_side(lower)
            consume(lower)

        @pl.when(upper < line.layers)
        def _():
            line.from_side(upper)
            consume(upper)

    line.step(2)
    consume(line.layer)
    consume_at(1)
    pl.loop(0, count)(down_grad)
    saves[1].start()
    for distance in range(3, line.layers):
        line.step(distance)
    for distance in range(2, line.layers):
        consume_at(distance)
    line.resumed_sent()
    for copy in saves:
        copy.wait()

    @pl.loop(0, count)
    def _(turn):
        for copy in tile_saves(turn):
            copy.wait()


def ffn(collective_id, shards, normed, turned, w_gate_up, cotangent, down_near):
    rows, model = normed.shape
    size = w_gate_up.shape[1] // 2
    shape, vmem = jax.ShapeDtypeStruct, pltpu.VMEM
    return pl.pallas_call(
        functools.partial(ffn_kernel, shards, pick_chunk(rows)),
        in_specs=[ANY] * 5,
        out_specs=[VMEM_WHOLE] + [ANY] * 4,
        out_shape=[
            shape((size, model), BF16),
            shape((rows, size), BF16),
            shape((rows, 2 * size), BF16),
            shape((model, 2 * size), BF16),
            shape((size, model), BF16),
        ],
        scratch_shapes=[
            vmem(w_gate_up.shape, BF16),
            vmem((rows, model), BF16),
            vmem((rows, size), F32),
            vmem((rows, size), F32),
            vmem((rows, model), BF16),
            vmem((model, rows), BF16),
            vmem((rows, size), BF16),
            vmem((rows, 2 * size), BF16),
            vmem((model, 2 * size), BF16),
            vmem((size, model), BF16),
            pltpu.SemaphoreType.DMA((4,)),
            pltpu.SemaphoreType.DMA((2,)),
            pltpu.SemaphoreType.DMA((shards // 2, 4)),
            pltpu.SemaphoreType.DMA((3,)),
        ]
        + line_scratch(shards),
        compiler_params=pltpu.CompilerParams(
            collective_id=collective_id, has_side_effects=True, vmem_limit_bytes=VMEM_LIMIT
        ),
        cost_estimate=pl.CostEstimate(flops=0, bytes_accessed=100 << 20, transcendentals=0),
        name="ffn",
    )(normed, turned, w_gate_up, cotangent, down_near)


class ShardSum:
    def __init__(self, shards, blocks, side_in, kept, from_below, from_above, sems):
        self.shard = lax.axis_index("fsdp")
        self.layers = shards // 2
        self.layer, self.core = self.shard // 2, self.shard % 2
        self.sibling = {"fsdp": self.shard ^ 1}
        self.above, self.below = {"fsdp": self.shard + 2}, {"fsdp": self.shard - 2}
        self.has_above, self.has_below = self.layer < self.layers - 1, self.layer > 0
        self.blocks, self.side_in, self.kept = blocks, side_in, kept
        self.from_below, self.from_above = from_below, from_above
        self.rows = kept.shape[1]
        self.side_send, self.side_recv, self.up_send, self.up_recv, self.down_send, self.down_recv = sems

    def side(self, layer):
        return pltpu.make_async_remote_copy(
            rows_of(self.blocks, 2 * layer + 1 - self.core, self.rows), self.side_in.at[layer],
            self.side_send.at[layer], self.side_recv.at[layer], device_id=self.sibling, device_id_type=MESH,
        )

    def start(self):
        for layer in range(self.layers):
            self.side(layer).start()

    def presum(self):
        for layer in range(self.layers):
            self.side(layer).wait_recv()
            own = rows_of(self.blocks, 2 * layer + self.core, self.rows)[...].astype(F32)
            self.kept[layer] = (own + self.side_in[layer].astype(F32)).astype(BF16)

    def up(self, stage):
        return pltpu.make_async_remote_copy(
            self.kept.at[self.layers - 1 - stage + self.layer], self.from_below.at[stage],
            self.up_send.at[stage], self.up_recv.at[stage], device_id=self.above, device_id_type=MESH,
        )

    def down(self, stage):
        return pltpu.make_async_remote_copy(
            self.kept.at[stage - self.layers + 1 + self.layer], self.from_above.at[stage],
            self.down_send.at[stage], self.down_recv.at[stage], device_id=self.below, device_id_type=MESH,
        )

    def each_sent(self, stage, what):
        @pl.when(self.has_above & (self.layer <= stage))
        def _():
            what(self.up(stage))

        @pl.when(self.has_below & (self.layers - 1 - self.layer <= stage))
        def _():
            what(self.down(stage))

    def send(self, stage):
        self.each_sent(stage, lambda copy: copy.start())

    def receive(self, stage):
        def add(target, arrived):
            self.kept[target] = (self.kept[target].astype(F32) + arrived[stage].astype(F32)).astype(BF16)

        @pl.when(self.has_below & (self.layer - 1 <= stage))
        def _():
            pltpu.make_async_remote_copy(
                self.from_below.at[stage], self.from_below.at[stage], self.up_send.at[stage], self.up_recv.at[stage],
                device_id=self.below, device_id_type=MESH,
            ).wait_recv()
            add(self.layers - 2 - stage + self.layer, self.from_below)

        @pl.when(self.has_above & (self.layers - 2 - self.layer <= stage))
        def _():
            pltpu.make_async_remote_copy(
                self.from_above.at[stage], self.from_above.at[stage], self.down_send.at[stage],
                self.down_recv.at[stage], device_id=self.above, device_id_type=MESH,
            ).wait_recv()
            add(stage - self.layers + 2 + self.layer, self.from_above)

    def sent(self):
        for layer in range(self.layers):
            self.side(layer).wait_send()
        for stage in range(self.layers - 1):
            self.each_sent(stage, lambda copy: copy.wait_send())


def shard_sum_scratch(shards, rows, cols):
    layers = shards // 2
    few, all_layers = pltpu.SemaphoreType.DMA((layers - 1,)), pltpu.SemaphoreType.DMA((layers,))
    block = pltpu.VMEM((layers, rows, cols), BF16)
    part = pltpu.VMEM((layers - 1, rows, cols), BF16)
    return [block, block, part, part], [all_layers, all_layers, few, few, few, few]


class Fold:
    def __init__(self, rank, piece, first, between, second, send_sem, recv_sem):
        self.rank, self.piece, self.first, self.between, self.second = rank, piece, first, between, second
        self.send_sem, self.recv_sem = send_sem, recv_sem

    def copy(self, number):
        me = self.rank
        source, target, distance = (
            lambda: (self.piece(me ^ 1, 0), self.first(0, 0), 1),
            lambda: (self.piece(me ^ 3, 0), self.first(1, 0), 1),
            lambda: (self.piece(me ^ 2, 1), self.first(0, 1), 2),
            lambda: (self.piece(me ^ 3, 1), self.first(1, 1), 2),
            lambda: (self.between(0), self.second(0), 2),
            lambda: (self.between(1), self.second(1), 1),
        )[number]()
        return to_rank(source, target, self.send_sem.at[number], self.recv_sem.at[number], me ^ distance)

    def start(self):
        for number in range(4):
            self.copy(number).start()

    def pass_on(self):
        for h, distance in ((0, 2), (1, 1)):
            self.copy(2 * h).wait_recv()
            self.copy(2 * h + 1).wait_recv()
            own = self.piece(self.rank ^ distance, h)[...].astype(F32)
            self.between(h)[...] = (own + self.first(1, h)[...].astype(F32)).astype(BF16)
            self.copy(4 + h).start()

    def total(self, h):
        self.copy(4 + h).wait_recv()
        own = self.piece(self.rank, h)[...].astype(F32)
        return own + self.first(0, h)[...].astype(F32) + self.second(h)[...].astype(F32)

    def sent(self):
        for number in range(6):
            self.copy(number).wait_send()


def middle_kernel(
    ranks,
    grad_gate_up, w_gate_up, mixed, cotangent, w_out, hidden, w_down, gated, gain,
    mixed_grad, gated_grad, gain_grad, down_part, out_grad,
    grad_in, weight_in, mixed_in, cotangent_in, out_in, hidden_in, down_in, gated_in, low_grad, down_all, out_all,
    wide, first_out, first_in, first_between, first_end, second_out, second_in, second_between, second_end,
    load_sem, save_sem, first_send, first_recv, second_send, second_recv,
):
    rank = lax.axis_index("ctx")
    rows = mixed.shape[0] // ranks
    model, width = w_out.shape
    tile = 512
    loads = [
        pltpu.make_async_copy(a, b, load_sem.at[n])
        for n, (a, b) in enumerate(
            (
                (w_gate_up, weight_in), (grad_gate_up, grad_in), (mixed, mixed_in), (cotangent, cotangent_in),
                (w_out, out_in), (hidden, hidden_in), (w_down, down_in), (gated, gated_in),
            )
        )
    ]
    saves = [
        pltpu.make_async_copy(down_all, down_part, save_sem.at[0]),
        pltpu.make_async_copy(out_all, out_grad, save_sem.at[1]),
    ]
    for copy in loads:
        copy.start()
    greet([{"ctx": rank ^ distance} for distance in range(1, ranks)])
    gain_grad[...] = jnp.zeros_like(gain_grad)
    for copy in loads[:2]:
        copy.wait()

    def part(turn):
        return pl.ds(pl.multiple_of(turn * rows, 16), rows)

    half = rows // 2

    def fold(out, into, between, end, send_sem, recv_sem):
        def make(turn):
            def at(h):
                return pl.ds(pl.multiple_of(turn * rows + h * half, 16), half)

            return Fold(
                rank,
                lambda index, h: out.at[index, at(h), :],
                lambda slot, h: into.at[slot, at(h), :],
                lambda h: between.at[at(h), :],
                lambda h: end.at[at(h), :],
                send_sem.at[turn],
                recv_sem.at[turn],
            )

        return make

    first = fold(first_out, first_in, first_between, first_end, first_send, first_recv)
    second = fold(second_out, second_in, second_between, second_end, second_send, second_recv)

    def compute(turn):
        here = part(turn)

        @pl.loop(0, model // tile)
        def _(step):
            cols = pl.ds(pl.multiple_of(step * tile, tile), tile)
            wide[:, cols] = right_product(grad_in[here, :], weight_in[cols, :])

        @pl.when(turn == 0)
        def _():
            for copy in loads[2:5]:
                copy.wait()

        values = mixed_in[here, :].astype(F32)
        scale = rms_scale(values)
        grad = wide[...]
        gain_grad[0:1, :] += jnp.sum(grad * values * scale, axis=0, keepdims=True)
        back = norm_back(grad, values, scale, gain[1:2, :]).astype(BF16)
        for index in range(ranks):
            first_out[index, here, :] = back[:, index * width : (index + 1) * width]
        first(turn).start()

    def project(turn):
        here = part(turn)
        for h in range(2):
            at = pl.ds(pl.multiple_of(turn * rows + h * half, 16), half)
            total = cotangent_in[at, pl.ds(pl.multiple_of(rank * width, LANES), width)].astype(F32)
            total = total + first(turn).total(h)
            mixed_grad[at, :] = total
            low_grad[at, :] = total.astype(BF16)
        for index in range(ranks):
            second_out[index, here, :] = right_product(
                low_grad[here, :], out_in[index * width : (index + 1) * width, :]
            ).astype(BF16)
        second(turn).start()

    def collect(turn):
        for h in range(2):
            at = pl.ds(pl.multiple_of(turn * rows + h * half, 16), half)
            gated_grad[at, :] = second(turn).total(h)

    def aside(turn):
        @pl.when(turn == ranks)
        def _():
            for copy in loads[5:8]:
                copy.wait()

            @pl.loop(0, model // tile)
            def _(step):
                cols = pl.ds(pl.multiple_of(step * tile, tile), tile)
                down_all[:, cols] = dot(hidden_in[...], down_in[:, cols]).astype(BF16)

            saves[0].start()

        @pl.when(turn == ranks + 2)
        def _():
            @pl.loop(0, gated_in.shape[0])
            def _(block):
                out_all[pl.ds(pl.multiple_of(block * LANES, LANES), LANES), :] = left_product(
                    gated_in[block], low_grad[...]
                ).astype(BF16)

            saves[1].start()

    @pl.loop(0, ranks + 4)
    def _(turn):
        stages = (
            compute, lambda t: first(t).pass_on(), project, lambda t: second(t).pass_on(), collect,
        )
        for lag, stage in enumerate(stages):
            if lag == 4:
                aside(turn)

            @pl.when((turn >= lag) & (turn < ranks + lag))
            def _():
                stage(turn - lag)

    @pl.loop(0, ranks)
    def _(turn):
        first(turn).sent()
        second(turn).sent()

    for copy in saves:
        copy.wait()


def middle(
    collective_id, ranks, grad_gate_up, w_gate_up, mixed, cotangent, w_out, hidden, w_down, gated, gain
):
    rows, model = mixed.shape
    width = w_out.shape[1]
    flat = pltpu.VMEM((rows, width), BF16)
    blocks = [pltpu.VMEM((ranks, rows, width), BF16), pltpu.VMEM((2, rows, width), BF16), flat, flat]
    sems = pltpu.SemaphoreType.DMA((ranks, 6))
    return pl.pallas_call(
        functools.partial(middle_kernel, ranks),
        in_specs=[ANY] * 8 + [VMEM_WHOLE],
        out_specs=[VMEM_WHOLE] * 3 + [ANY] * 2,
        out_shape=[
            jax.ShapeDtypeStruct((rows, width), F32),
            jax.ShapeDtypeStruct((rows, width), F32),
            jax.ShapeDtypeStruct((8, model), F32),
            jax.ShapeDtypeStruct((rows, model), BF16),
            jax.ShapeDtypeStruct((model, width), BF16),
        ],
        scratch_shapes=[
            pltpu.VMEM(grad_gate_up.shape, BF16),
            pltpu.VMEM(w_gate_up.shape, BF16),
            pltpu.VMEM(mixed.shape, BF16),
            pltpu.VMEM(cotangent.shape, BF16),
            pltpu.VMEM(w_out.shape, BF16),
            pltpu.VMEM(hidden.shape, BF16),
            pltpu.VMEM(w_down.shape, BF16),
            pltpu.VMEM(gated.shape, BF16),
            pltpu.VMEM((rows, width), BF16),
            pltpu.VMEM((rows, model), BF16),
            pltpu.VMEM((model, width), BF16),
            pltpu.VMEM((rows // ranks, model), F32),
            *blocks, *blocks,
            pltpu.SemaphoreType.DMA((8,)),
            pltpu.SemaphoreType.DMA((2,)),
            sems, sems, sems, sems,
        ],
        compiler_params=pltpu.CompilerParams(
            collective_id=collective_id, has_side_effects=True, vmem_limit_bytes=VMEM_LIMIT
        ),
        cost_estimate=pl.CostEstimate(flops=0, bytes_accessed=150 << 20, transcendentals=0),
        name="middle",
    )(grad_gate_up, w_gate_up, mixed, cotangent, w_out, hidden, w_down, gated, gain)


def last_kernel(
    ranks, shards,
    grad_project, w_in, inputs, aside, pieces, mixed, share, mixed_grad, gain, gain_two_grad, small, segments, forget_grad,
    tokens_grad, block_out, total_sums, parts, aside_all, share_all,
    grad_in, weight_in, inputs_in, aside_in, pieces_in, mixed_in, wide, out, into, between, end, sums_out, sums_in,
    share_in, load_sem, send_sem, recv_sem, sums_send, sums_recv, aside_send, aside_recv, aside_own,
):
    rank = lax.axis_index("ctx")
    rows = inputs.shape[0] // ranks
    model, width = inputs.shape[1], mixed_grad.shape[1]
    tile = 512
    loads = [
        pltpu.make_async_copy(a, b, load_sem.at[n])
        for n, (a, b) in enumerate(
            (
                (aside, aside_in), (w_in, weight_in), (grad_project, grad_in), (inputs, inputs_in),
                (pieces, pieces_in), (rows_of(mixed, rank, rows), mixed_in), (share, share_in),
            )
        )
    ]
    for copy in loads:
        copy.start()
    greet([{"ctx": rank ^ distance} for distance in range(1, ranks)])
    relay, share_relay = [
        relay_ops("stack", rank, a, b, (aside_send.at[n], aside_recv.at[n], aside_own.at[n]))
        for n, (a, b) in enumerate(((aside_in, aside_all), (share_in, share_all)))
    ]
    loads[6].wait()
    share_relay.start()
    loads[0].wait()
    relay.start()
    sums_out[...] = jnp.zeros_like(sums_out)
    sums_out[1:2, :] = gain_two_grad[0:1, :]
    sums_out[2:3, 0:LANES] = small[0:1, :]
    sums_out[2:3, LANES : 2 * LANES] = small[1:2, :]
    for index in range(ranks):
        sums_out[3 + index : 4 + index, 0:LANES] = jnp.where(rank == index, small[2:3, :], 0.0)
    for copy in loads[1:4]:
        copy.wait()

    half = rows // 2

    def at(h):
        return pl.ds(h * half, half)

    fold = Fold(
        rank,
        lambda index, h: out.at[index, at(h), :],
        lambda slot, h: into.at[slot, at(h), :],
        lambda h: between.at[at(h), :],
        lambda h: end.at[at(h), :],
        send_sem,
        recv_sem,
    )

    def send_sums(distance):
        return to_rank(
            sums_out, sums_in.at[distance], sums_send.at[distance - 1], sums_recv.at[distance - 1], rank ^ distance
        )

    def compute(other):
        here = pl.ds(pl.multiple_of(other * rows, 16), rows)

        @pl.loop(0, model // tile)
        def _(step):
            cols = pl.ds(pl.multiple_of(step * tile, tile), tile)
            wide[:, cols] = right_product(grad_in[here, :], weight_in[cols, :])

        values = inputs_in[here, :].astype(F32)
        scale = rms_scale(values)
        grad = wide[...]
        sums_out[0:1, :] += jnp.sum(grad * values * scale, axis=0, keepdims=True)
        wide[...] = norm_back(grad, values, scale, gain[0:1, :])
        own = pl.ds(pl.multiple_of(rank * width, LANES), width)
        wide[:, own] += mixed_grad[here, :]
        out[other] = wide[...].astype(BF16)

    @pl.loop(1, ranks)
    def _(turn):
        compute(rank ^ (ranks - turn))

        @pl.when(turn == 2)
        def _():
            for number in (2, 3):
                fold.copy(number).start()

        @pl.when(turn == 3)
        def _():
            for number in (0, 1):
                fold.copy(number).start()

    share_relay.forward()
    for copy in loads[4:6]:
        copy.wait()
    own = pl.ds(pl.multiple_of(rank * rows, 16), rows)
    result = mixed_in[...].astype(F32)
    for index in range(ranks):
        result = result + pieces_in[index].astype(F32)
    block_out[...] = result.astype(BF16)
    branch = result - inputs_in[own, :].astype(F32)
    valid = jnp.where(segments[own, :] >= 0.0, 1.0, 0.0)
    lane = lax.broadcasted_iota(jnp.int32, (1, LANES), 1)
    stats = jnp.zeros((1, LANES), F32)
    for index, values in enumerate((result, branch)):
        total = jnp.sum(valid * jnp.sum(values * values, axis=-1, keepdims=True), axis=0, keepdims=True)
        stats = jnp.where(lane == index, total, stats)
    sums_out[7:8, 0:LANES] = stats
    compute(rank)
    for distance in range(1, ranks):
        send_sums(distance).start()
    relay.forward()
    fold.pass_on()
    for h in range(2):
        tokens_grad[at(h), :] = fold.total(h).astype(BF16)
    total = sums_out[...]
    for distance in range(1, ranks):
        send_sums(distance).wait_recv()
        total = total + sums_in[distance]
    total_sums[...] = total
    share = model // shards
    parts[...] = jnp.zeros_like(parts)
    for index in range(shards):
        parts[index, 0:2, 0:share] = total[0:2, index * share : (index + 1) * share]
        parts[index, 2:8, :] = total[2:8, 0 : parts.shape[2]]
        parts[index, 8:16, 0:share] = forget_grad[:, index * share : (index + 1) * share]
    fold.sent()
    for distance in range(1, ranks):
        send_sums(distance).wait_send()
    relay.finish()
    share_relay.finish()


def last_moves(
    collective_id, ranks, shards,
    grad_project, w_in, inputs, aside, pieces, mixed, share, mixed_grad, gain, gain_two_grad, small, segments,
    forget_grad,
):
    rows, model = inputs.shape
    own = (rows // ranks, model)
    flat = pltpu.VMEM(own, BF16)
    blocks = [pltpu.VMEM((ranks,) + own, BF16), pltpu.VMEM((2,) + own, BF16), flat, flat]
    sems = pltpu.SemaphoreType.DMA((ranks - 1,))
    return pl.pallas_call(
        functools.partial(last_kernel, ranks, shards),
        in_specs=[ANY] * 7 + [VMEM_WHOLE] * 6,
        out_specs=[VMEM_WHOLE] * 4 + [ANY] * 2,
        out_shape=[
            jax.ShapeDtypeStruct(own, BF16),
            jax.ShapeDtypeStruct(own, BF16),
            jax.ShapeDtypeStruct((8, model), F32),
            jax.ShapeDtypeStruct((shards, 16, max(2 * LANES, -(-model // shards // LANES) * LANES)), F32),
            jax.ShapeDtypeStruct((ranks,) + aside.shape, BF16),
            jax.ShapeDtypeStruct((ranks,) + share.shape, BF16),
        ],
        scratch_shapes=[
            pltpu.VMEM(grad_project.shape, BF16),
            pltpu.VMEM(w_in.shape, BF16),
            pltpu.VMEM(inputs.shape, BF16),
            pltpu.VMEM(aside.shape, BF16),
            pltpu.VMEM(pieces.shape, BF16),
            pltpu.VMEM(own, BF16),
            pltpu.VMEM(own, F32),
            *blocks,
            pltpu.VMEM((8, model), F32),
            pltpu.VMEM((ranks, 8, model), F32),
            pltpu.VMEM(share.shape, BF16),
            pltpu.SemaphoreType.DMA((7,)),
            pltpu.SemaphoreType.DMA((6,)),
            pltpu.SemaphoreType.DMA((6,)),
            sems, sems,
            pltpu.SemaphoreType.DMA((2, 6)),
            pltpu.SemaphoreType.DMA((2, 6)),
            pltpu.SemaphoreType.DMA((2, 2)),
        ],
        compiler_params=pltpu.CompilerParams(
            collective_id=collective_id, has_side_effects=True, vmem_limit_bytes=VMEM_LIMIT
        ),
        cost_estimate=pl.CostEstimate(flops=0, bytes_accessed=150 << 20, transcendentals=0),
        name="last_moves",
    )(grad_project, w_in, inputs, aside, pieces, mixed, share, mixed_grad, gain, gain_two_grad, small, segments, forget_grad)


def finish_kernel(
    ranks, shards, late, parts, late_all, part_sum, forget_all,
    late_in, into, load_sem, send_sem, recv_sem, own_sem, part_send, part_recv, forget_send, forget_recv,
):
    rank = lax.axis_index("ctx")
    shard = lax.axis_index("fsdp")
    load = pltpu.make_async_copy(late, late_in, load_sem.at[0])
    load.start()
    relay = relay_ops("stack", rank, late_in, late_all, (send_sem, recv_sem, own_sem))
    greet(
        [{"ctx": rank ^ distance} for distance in range(1, ranks)]
        + [{"fsdp": shard ^ distance} for distance in range(1, shards)]
    )
    load.wait()
    relay.start()

    def send(distance):
        other = shard ^ distance
        return pltpu.make_async_remote_copy(
            parts.at[other], into.at[distance], part_send.at[distance - 1], part_recv.at[distance - 1],
            device_id={"fsdp": other}, device_id_type=MESH,
        )

    def send_forget(distance):
        return to_rank(
            forget_all.at[rank], forget_all.at[rank], forget_send.at[distance - 1], forget_recv.at[distance - 1],
            rank ^ distance,
        )

    for distance in range(1, shards):
        send(distance).start()
    total = parts[shard]
    for distance in range(1, shards):
        send(distance).wait_recv()
        total = total + into[distance]
    part_sum[...] = total
    forget_all[rank] = total[8:16, :]
    for distance in range(1, ranks):
        send_forget(distance).start()
    relay.forward()
    for distance in range(1, ranks):
        send_forget(distance).wait()
    for distance in range(1, shards):
        send(distance).wait_send()
    relay.finish()


def finish_moves(collective_id, ranks, shards, late, parts):
    sems = pltpu.SemaphoreType.DMA((shards - 1,))
    return pl.pallas_call(
        functools.partial(finish_kernel, ranks, shards),
        in_specs=[ANY, VMEM_WHOLE],
        out_specs=[ANY, VMEM_WHOLE, VMEM_WHOLE],
        out_shape=[
            jax.ShapeDtypeStruct((ranks,) + late.shape, BF16),
            jax.ShapeDtypeStruct(parts.shape[1:], F32),
            jax.ShapeDtypeStruct((ranks, 8, parts.shape[2]), F32),
        ],
        scratch_shapes=[
            pltpu.VMEM(late.shape, BF16),
            pltpu.VMEM(parts.shape, F32),
            pltpu.SemaphoreType.DMA((1,)),
            pltpu.SemaphoreType.DMA((6,)),
            pltpu.SemaphoreType.DMA((6,)),
            pltpu.SemaphoreType.DMA((2,)),
            sems, sems,
            pltpu.SemaphoreType.DMA((ranks - 1,)),
            pltpu.SemaphoreType.DMA((ranks - 1,)),
        ],
        compiler_params=pltpu.CompilerParams(
            collective_id=collective_id, has_side_effects=True, vmem_limit_bytes=VMEM_LIMIT
        ),
        cost_estimate=pl.CostEstimate(flops=0, bytes_accessed=50 << 20, transcendentals=0),
        name="finish_moves",
    )(late, parts)


def spread_kernel(pieces, *refs):
    source, targets = refs[0], refs[1:]
    ranks = source.shape[0]
    for target, (piece, first, count) in zip(targets, pieces):
        for block in range(count):
            for index in range(ranks):
                target[:, pl.ds((block * ranks + index) * piece, piece)] = source[
                    index, :, pl.ds(first + block * piece, piece)
                ].astype(F32)


def spread_cols(source, *pieces):
    ranks, rows, cols = source.shape
    if any(piece % LANES or first % LANES for piece, first, _ in pieces):
        return [
            jnp.concatenate(
                [
                    source[c, :, first + i * piece : first + (i + 1) * piece]
                    for i in range(count)
                    for c in range(ranks)
                ],
                axis=1,
            ).astype(F32)
            for piece, first, count in pieces
        ]
    part = rows // 4 if rows % 64 == 0 else rows
    widths = [count * ranks * piece for piece, _, count in pieces]
    return pl.pallas_call(
        functools.partial(spread_kernel, pieces),
        grid=(rows // part,),
        in_specs=[pl.BlockSpec((ranks, part, cols), lambda step: (0, step, 0))],
        out_specs=[pl.BlockSpec((part, w), lambda step: (step, 0)) for w in widths],
        out_shape=[jax.ShapeDtypeStruct((rows, w), F32) for w in widths],
        compiler_params=pltpu.CompilerParams(vmem_limit_bytes=VMEM_LIMIT),
        cost_estimate=pl.CostEstimate(flops=0, bytes_accessed=rows * sum(widths) * 6, transcendentals=0),
        name="spread_cols",
    )(source)


def spread_early_kernel(piece, gate_up, down, gate_up_out, down_out):
    ranks = gate_up.shape[0]
    for block in range(gate_up.shape[2] // piece):
        for index in range(ranks):
            gate_up_out[:, (block * ranks + index) * piece : (block * ranks + index + 1) * piece] = gate_up[
                index, :, block * piece : (block + 1) * piece
            ].astype(F32)
    size = down.shape[1]
    for index in range(down.shape[0]):
        down_out[index * size : (index + 1) * size, :] = down[index].astype(F32)


def spread_early(gate_up, down, piece):
    ranks, rows, cols = gate_up.shape
    _, down_rows, model = down.shape
    steps = 2
    part, each = rows // steps, ranks // steps
    return pl.pallas_call(
        functools.partial(spread_early_kernel, piece),
        grid=(steps,),
        in_specs=[
            pl.BlockSpec((ranks, part, cols), lambda step: (0, step, 0)),
            pl.BlockSpec((each, down_rows, model), lambda step: (step, 0, 0)),
        ],
        out_specs=[
            pl.BlockSpec((part, ranks * cols), lambda step: (step, 0)),
            pl.BlockSpec((each * down_rows, model), lambda step: (step, 0)),
        ],
        out_shape=[
            jax.ShapeDtypeStruct((rows, ranks * cols), F32),
            jax.ShapeDtypeStruct((ranks * down_rows, model), F32),
        ],
        compiler_params=pltpu.CompilerParams(vmem_limit_bytes=VMEM_LIMIT),
        cost_estimate=pl.CostEstimate(
            flops=0, bytes_accessed=6 * ranks * (rows * cols + down_rows * model), transcendentals=0
        ),
        name="spread_early",
    )(gate_up, down)


def unpack_kernel(
    width, heads, head, late, forget_all, sums, totals, segments, first_rows, second_rows,
    in_out, out_out, first_out, second_out, forget_out, gains, bias, qk, rms,
):
    ranks = late.shape[0]
    first = 4 * width
    for block in range(4):
        for index in range(ranks):
            in_out[:, (block * ranks + index) * width : (block * ranks + index + 1) * width] = late[
                index, :, block * width : (block + 1) * width
            ].astype(F32)
    first_out[...] = first_rows[...]
    second_out[...] = second_rows[...]
    lane = lax.broadcasted_iota(jnp.int32, (LANES, ranks * heads), 0)
    place = lax.broadcasted_iota(jnp.int32, (LANES, ranks * heads), 1)
    biases = jnp.zeros((8, ranks * heads), F32)
    for index in range(ranks):
        chosen = (lane < heads) & (place == index * heads + lane)
        out_out[:, index * width : (index + 1) * width] = late[index, :, first : first + width].astype(F32)
        forget_out[index * heads : (index + 1) * heads, :] = forget_all[index, 0:heads, 0 : forget_out.shape[1]]
        row = jnp.broadcast_to(sums[3 + index : 4 + index, 0:LANES], (8, LANES))
        for part in split_three(row):
            biases = biases + dot(part.astype(BF16), jnp.where(chosen, 1.0, 0.0).astype(BF16))
    gains[...] = sums[0:2, 0 : gains.shape[1]]
    bias[...] = biases[0:1, :]
    for row in range(2):
        qk[row : row + 1, :] = sum(
            sums[2:3, row * LANES + side * head : row * LANES + (side + 1) * head] for side in range(LANES // head)
        )
    count = jnp.sum(jnp.where(segments[...] >= 0, 1.0, 0.0), axis=-1, keepdims=True)
    rms[...] = jnp.sqrt(totals[7:8, 0:2] / (count * totals.shape[1]))


def unpack(late, forget_all, sums, totals, segments, first_rows, second_rows, width, heads, head):
    ranks, rows, cols = late.shape
    part = rows // 2

    def block(lanes):
        return pl.BlockSpec((part, lanes), lambda step: (step, 0))

    share = rows
    shape = jax.ShapeDtypeStruct
    return pl.pallas_call(
        functools.partial(unpack_kernel, width, heads, head),
        grid=(rows // part,),
        in_specs=[
            pl.BlockSpec((ranks, part, cols), lambda step: (0, step, 0)),
        ]
        + [whole(a.shape) for a in (forget_all, sums, totals, segments)]
        + [block(first_rows.shape[1])] * 2,
        out_specs=[block(4 * ranks * width), block(ranks * width)] + [block(first_rows.shape[1])] * 2
        + [whole(a) for a in ((ranks * heads, rows), (2, share), (1, ranks * heads), (2, head), (1, 2))],
        out_shape=[
            shape((rows, 4 * ranks * width), F32),
            shape((rows, ranks * width), F32),
            shape(first_rows.shape, BF16),
            shape(second_rows.shape, BF16),
            shape((ranks * heads, rows), F32),
            shape((2, share), F32),
            shape((1, ranks * heads), F32),
            shape((2, head), F32),
            shape((1, 2), F32),
        ],
        compiler_params=pltpu.CompilerParams(vmem_limit_bytes=VMEM_LIMIT),
        cost_estimate=pl.CostEstimate(flops=0, bytes_accessed=ranks * rows * cols * 6, transcendentals=0),
        name="unpack",
    )(late, forget_all, sums, totals, segments, first_rows, second_rows)


class Native:
    def __init__(self, ranks):
        self.ranks = ranks

    def begin(self, tokens, cotangent, weight, tail, other, piece, width, padded):
        rank, model = lax.axis_index("ctx"), tokens.shape[1]
        parts = [lax.dynamic_slice_in_dim(weight, i * model + rank * width, width, 1) for i in range(4)]
        parts = [jnp.pad(part, ((0, 0), (0, padded - width))) for part in parts]
        cols = other.shape[1] // self.ranks
        picks = [
            lax.dynamic_slice_in_dim(other, (i * self.ranks + rank) * piece, piece, 1) for i in range(cols // piece)
        ]
        return (
            lax.all_gather(tokens, "ctx", axis=0, tiled=True),
            lax.all_gather(cotangent, "ctx", axis=0, tiled=True),
            lax.all_gather(jnp.concatenate(parts + [tail], axis=1), "fsdp", axis=0, tiled=True),
            jnp.concatenate(picks, axis=1),
        )

    def gather_cols(self, array, piece):
        return lax.all_gather(array, "ctx", axis=1, tiled=True), lax.all_gather(piece, "fsdp", axis=0, tiled=True)


def body(
    tokens, block_order, segment_ids, norm_gains, attn_in_weight, forget_weight, forget_bias,
    qk_gains, out_weight, gate_up_weight, down_weight, out_grad,
):
    ranks = lax.axis_size("ctx")
    shards = lax.axis_size("fsdp")
    rank = lax.axis_index("ctx")
    row_count, model_width = tokens.shape[1], tokens.shape[2]
    head_count, head_dim = forget_bias.shape[0], qk_gains.shape[1]
    local_heads = head_count // ranks
    width = local_heads * head_dim
    padded = -(-width // LANES) * LANES
    seq_order = block_order[0]
    seq_len = segment_ids.shape[1]
    block_len = seq_len // seq_order.shape[0]
    hidden_piece = down_weight.shape[0] // ranks
    hidden = hidden_piece * shards
    plain = ranks == 4 and shards & (shards - 1) == 0 and width == padded
    comm = Native(ranks)

    def slab(array, start, size, axis):
        return lax.dynamic_slice_in_dim(array, start, size, axis)

    def widen(array):
        return jnp.pad(array, ((0, 0), (0, padded - width))) if padded > width else array

    if plain:
        (
            inputs, grad_low, w_in, w_out, w_gate_up, normed, project, gated_all, attended,
            wide_query, wide_key, wide_value, mixed_low, down_near, normed_two, turned, gain_rows, *places_all,
            bias, head_gains,
        ) = front(
            0, ranks, shards, head_dim, local_heads, width, hidden_piece,
            tokens[0], out_grad[0], attn_in_weight, out_weight, gate_up_weight, down_weight, forget_weight.T,
            norm_gains, qk_gains, segment_ids, block_order, forget_bias[None],
        )
        w_down, hidden_act, grad_gate_up, early_grad, down_part_grad = ffn(
            1, shards, normed_two, turned, w_gate_up, grad_low, down_near
        )
    else:
        tail = jnp.concatenate(
            [
                slab(forget_weight, rank * local_heads, local_heads, 1),
                norm_gains.T,
                jnp.zeros((attn_in_weight.shape[0], LANES - local_heads - 2), BF16),
            ],
            axis=1,
        )
        offsets = jnp.arange(block_len, dtype=jnp.int32)
        blocks = jnp.arange(seq_order.shape[0], dtype=jnp.int32)
        places = (seq_order[:, None] * block_len + offsets[None]).reshape(-1)
        by_block = segment_ids[0].reshape(-1, block_len)
        chosen = seq_order[:, None, None] == blocks[None, :, None]
        segments = jnp.sum(jnp.where(chosen, by_block[None], 0), axis=1).reshape(-1)
        places, segments = places.astype(F32), segments.astype(F32)
        places_all = (places[None, :], places[:, None], segments[None, :], segments[:, None])
        bias = jnp.pad(slab(forget_bias, rank * local_heads, local_heads, 0), (0, LANES - local_heads))[None]
        head_gains = jnp.tile(qk_gains, (1, LANES // head_dim))
        down_piece = slab(down_weight, rank * hidden_piece, hidden_piece, 0)
        inputs, grad_low, w_in, gate_up_piece = comm.begin(
            tokens[0], out_grad[0], attn_in_weight, tail, gate_up_weight, hidden_piece, width, padded
        )
        w_gate_up = lax.all_gather(gate_up_piece, "fsdp", axis=0, tiled=True)
        gain_cols = w_in[:, 4 * padded : 4 * padded + LANES].astype(F32).T
        gain_one = gain_cols[local_heads]
        gain_two = gain_cols[local_heads + 1]
        wide_inputs = inputs.astype(F32)
        scale_one = rms_scale(wide_inputs)
        normed = (wide_inputs * scale_one * gain_one).astype(BF16)
        project = dot(normed, w_in)
        gated, attended, wide_query, wide_key, wide_value = attend(
            project, places_all, bias, head_gains, head_dim, padded, local_heads
        )
        gated_all, w_out = comm.gather_cols(gated[:, :width], slab(out_weight, rank * width, width, 1))
        mixed_cols = slab(inputs, rank * width, width, 1).astype(F32) + dot(gated_all, w_out)
        mixed_low, w_down = comm.gather_cols(mixed_cols.astype(BF16), down_piece)
        mixed = mixed_low.astype(F32)
        scale_two = rms_scale(mixed)
        normed_two = (mixed * scale_two * gain_two).astype(BF16)
        gate_up = dot(normed_two, w_gate_up)
        gate_part, up_part = gate_up[:, :hidden], gate_up[:, hidden:]
        gate_sigmoid = jax.nn.sigmoid(gate_part)
        silu = gate_part * gate_sigmoid
        hidden_act = (silu * up_part).astype(BF16)
        grad_hidden = right_product(grad_low, w_down)
        grad_gate = grad_hidden * up_part * gate_sigmoid * (1.0 + gate_part * (1.0 - gate_sigmoid))
        grad_gate_up = jnp.concatenate([grad_gate, grad_hidden * silu], axis=1).astype(BF16)
        down_part_grad = left_product(hidden_act, grad_low).astype(BF16)
        gate_up_grad = left_product(normed_two, grad_gate_up).astype(BF16)
        down_part = dot(hidden_act, w_down).astype(BF16)

    def own_rows(array):
        return slab(array, rank * row_count, row_count, 0)

    def reduce_shards(array):
        return lax.psum_scatter(array.astype(BF16), "fsdp", scatter_dimension=0, tiled=True)

    if plain:
        early_share = (reduce_shards(early_grad),)
    else:
        early_share = (reduce_shards(down_part_grad), reduce_shards(gate_up_grad))
    if plain:
        grad_mixed_cols, grad_gated, gain_two_grad, down_part, out_part = middle(
            3, ranks, grad_gate_up, w_gate_up, mixed_low, grad_low, w_out, hidden_act, w_down, gated_all,
            gain_rows,
        )
    else:
        grad_normed_two = right_product(grad_gate_up, w_gate_up)
        gain_two_grad = jnp.sum(grad_normed_two * mixed * scale_two, axis=0)
        grad_mixed_part = norm_back(grad_normed_two, mixed, scale_two, gain_two).astype(BF16)
        grad_mixed_cols = slab(grad_low, rank * width, width, 1).astype(F32) + lax.psum_scatter(
            grad_mixed_part, "ctx", scatter_dimension=1, tiled=True
        ).astype(F32)
        grad_branch = grad_mixed_cols.astype(BF16)
        grad_gated = widen(
            lax.psum_scatter(
                right_product(grad_branch, w_out).astype(BF16), "ctx", scatter_dimension=1, tiled=True
            ).astype(F32)
        )
    grad_project, small, *rest = attend_back(
        project, places_all, bias, head_gains, attended, (wide_query, wide_key, wide_value),
        grad_gated, (down_part, normed, out_part, down_part_grad) if plain else (), ranks if plain else 0, shards, head_dim, padded, local_heads,
    )
    if plain:
        down_pieces, late, down_share, forget_grad = rest
    else:
        in_part = left_product(normed, grad_project).astype(BF16)
        out_part = left_product(gated_all, grad_branch).astype(BF16)
        late = jnp.concatenate([in_part[:, : 4 * padded], out_part, in_part[:, 4 * padded :]], axis=1)
    late, early_share = lax.optimization_barrier((late, early_share))
    late_share = reduce_shards(late)

    if plain:
        tokens_grad, block_out, sums, parts, early_own, down_own = last_moves(
            4, ranks, shards, grad_project, w_in, inputs, early_share[0], down_pieces, mixed_low, down_share,
            grad_mixed_cols,             gain_rows, gain_two_grad, small, places_all[3], forget_grad,
        )
        late_own, piece_sum, forget_all = finish_moves(6, ranks, shards, late_share, parts)
        gate_up_out, down_out = spread_early(early_own, down_own, hidden_piece)
    else:
        grad_normed = right_product(grad_project, w_in)
        gain_one_grad = jnp.sum(grad_normed * wide_inputs * scale_one, axis=0)
        in_own = jnp.arange(model_width, dtype=jnp.int32) // width == rank
        grad_inputs = norm_back(grad_normed, wide_inputs, scale_one, gain_one) + jnp.where(
            in_own[None], jnp.tile(grad_mixed_cols, (1, ranks)), 0.0
        )
        down_sum = lax.psum_scatter(down_part, "ctx", scatter_dimension=0, tiled=True).astype(F32)
        tokens_grad = lax.psum_scatter(grad_inputs.astype(BF16), "ctx", scatter_dimension=0, tiled=True)[None]
        own_bias = jnp.where(jnp.arange(ranks, dtype=jnp.int32)[:, None] == rank, small[2:3], 0.0)
        small_rows = jnp.concatenate([small[0:2].reshape(1, -1), jnp.pad(own_bias, ((0, 0), (0, LANES)))], axis=0)
        sums = jnp.concatenate(
            [
                jnp.stack([gain_one_grad, gain_two_grad]),
                jnp.pad(small_rows, ((0, 0), (0, model_width - 2 * LANES))),
            ],
            axis=0,
        )
        sums = lax.psum(sums, "ctx")
        down_own, gate_up_own = [lax.all_gather(a, "ctx", axis=0, tiled=False) for a in early_share]
        down_out = down_own.astype(F32).reshape(down_weight.shape)
        gate_up_out = spread_cols(gate_up_own, (hidden_piece, 0, 2 * shards))[0]
        result = own_rows(mixed_low).astype(F32) + down_sum
        block_out = result.astype(BF16)[None]
        branch = result - own_rows(inputs).astype(F32)
        own_valid = own_rows(places_all[3][:, 0] >= 0).astype(F32)
        totals = lax.psum(
            jnp.stack(
                [
                    jnp.sum(own_valid * jnp.sum(result * result, axis=-1)),
                    jnp.sum(own_valid * jnp.sum(branch * branch, axis=-1)),
                ]
            ),
            "ctx",
        )
        share = model_width // shards
        room = 2 * LANES
        gain_pieces = sums[0:2].reshape(2, shards, share).transpose(1, 0, 2)
        gain_pieces = jnp.pad(gain_pieces, ((0, 0), (0, 0), (0, room - share)))
        others = jnp.broadcast_to(sums[None, 2 : 3 + ranks, :room], (shards, 1 + ranks, room))
        piece_sum = lax.psum_scatter(
            jnp.concatenate([gain_pieces, others], axis=1), "fsdp", scatter_dimension=0, tiled=False
        )
        late_own = lax.all_gather(late_share, "ctx", axis=0, tiled=False)
    if plain:
        in_out, out_out, tokens_grad, block_out, forget_out, gains_sum, bias_sum, qk_sum, rms = unpack(
            late_own, forget_all, piece_sum, sums, segment_ids, tokens_grad, block_out, width, local_heads, head_dim
        )
        tokens_grad, block_out = tokens_grad[None], block_out[None]
        bias_sum, forget_out = bias_sum[0], forget_out.T
    else:
        share = model_width // shards
        valid_count = jnp.sum((segment_ids[0] >= 0).astype(F32)) * model_width
        in_out = jnp.concatenate(
            [late_own[c, :, i * padded : i * padded + width] for i in range(4) for c in range(ranks)], axis=1
        ).astype(F32)
        out_out = jnp.concatenate(
            [late_own[c, :, 4 * padded : 4 * padded + width] for c in range(ranks)], axis=1
        ).astype(F32)
        last = 4 * padded + width
        forget_out = jnp.concatenate(
            [late_own[c, :, last : last + local_heads] for c in range(ranks)], axis=1
        ).astype(F32)
        gains_sum = piece_sum[0:2, :share]
        bias_sum = piece_sum[3 : 3 + ranks, :local_heads].reshape(-1)
        qk_sum = piece_sum[2, : 2 * LANES].reshape(2, LANES // head_dim, head_dim).sum(axis=1)
        rms = jnp.sqrt(totals / valid_count)[None]
    return (
        block_out, tokens_grad, gains_sum, in_out, forget_out, bias_sum, qk_sum,
        out_out, gate_up_out, down_out, rms,
    )


def solution(mesh):
    rows = P("fsdp", "ctx", None)
    return jax.shard_map(
        body,
        mesh=mesh,
        in_specs=(
            rows, P("fsdp", None), P("fsdp", None), P(None, "fsdp"), P("fsdp", None), P("fsdp", None),
            P(), P(), P("fsdp", None), P("fsdp", None), P("fsdp", None), rows,
        ),
        out_specs=(
            rows, rows, P(None, "fsdp"), P("fsdp", None), P("fsdp", None), P(), P(),
            P("fsdp", None), P("fsdp", None), P("fsdp", None), P("fsdp", None),
        ),
        check_vma=False,
    )
```
